32 devices in a mesh: dp: 8 (over y, x, core), mp: 4 (over z).
Axes of the slice: x: 2, y: 2, z: 4, core: 2. Of those that a mesh axis runs over, the one named last changes fastest.
Arguments:
- mel_pair: bfloat16 [16384, 200], P('dp'), may hold values from -6 to 6
- text_ids: int32 [16384], P('dp'), may hold values from 0 to 2545
- clip_lengths: int32 [8, 4], P('dp'), may hold values from 1 to 1024, 2048 in all within a row
- t_index: int32 [8, 4], P('dp'), may hold values from 0 to 999
- txt_table: bfloat16 [2546, 512], replicated, may hold values from -6 to 6
- txt_conv: float32 [2, 7, 512], replicated, may hold values from -2 to 2
- txt_vec: float32 [2, 3, 512], replicated, may hold values from -1.75 to 1.75
- txt_gain: float32 [2, 512], replicated, may hold values from 0.5 to 1.5
- txt_up: bfloat16 [2, 512, 1024], replicated, may hold values from -0.25 to 0.25
- txt_hid: float32 [2, 3, 1024], replicated, may hold values from -1.75 to 1.75
- txt_down: bfloat16 [2, 1024, 512], replicated, may hold values from -0.1875 to 0.1875
- emb_mel: bfloat16 [200, 1024], replicated, may hold values from -0.21875 to 0.21875
- emb_text: bfloat16 [512, 1024], replicated, may hold values from -0.21875 to 0.21875
- emb_bias: float32 [1024], replicated, may hold values from -1.75 to 1.75
- pos_conv: bfloat16 [2, 31, 64, 1024], P(None, None, None, 'mp'), may hold values from -0.125 to 0.125
- pos_bias: float32 [2, 1024], P(None, 'mp'), may hold values from -1.75 to 1.75
- time_w1: bfloat16 [256, 1024], replicated, may hold values from -0.375 to 0.375
- time_bias: float32 [2, 1024], replicated, may hold values from -1.75 to 1.75
- time_w2: bfloat16 [1024, 1024], replicated, may hold values from -0.1875 to 0.1875
- ada_w: bfloat16 [1024, 6144], replicated, may hold values from -0.1875 to 0.1875
- ada_b: float32 [6144], replicated, may hold values from -1.75 to 1.75
- qkv_w: bfloat16 [3, 1024, 1024], P(None, None, 'mp'), may hold values from -0.1875 to 0.1875
- qkv_b: float32 [3, 1024], P(None, 'mp'), may hold values from -1.75 to 1.75
- out_w: bfloat16 [1024, 1024], P('mp'), may hold values from -0.75 to 0.75
- out_b: float32 [1024], replicated, may hold values from -1.75 to 1.75
- ff_w1: bfloat16 [1024, 2048], P(None, 'mp'), may hold values from -0.1875 to 0.1875
- ff_b1: float32 [2048], P('mp'), may hold values from -1.75 to 1.75
- ff_w2: bfloat16 [2048, 1024], P('mp'), may hold values from -0.125 to 0.125
- ff_b2: float32 [1024], replicated, may hold values from -1.75 to 1.75
- out_grad: bfloat16 [16384, 1024], P('dp'), may hold values from -6 to 6
Outputs:
- out: float32 [16384, 1024], P('dp')
- mel_grad: float32 [16384, 200], P('dp')
- grad_txt_table: float32 [2546, 512], P(None, ('dp', 'mp'))
- grad_txt_conv: float32 [2, 7, 512], P(None, None, ('dp', 'mp'))
- grad_txt_vec: float32 [2, 3, 512], P(None, None, ('dp', 'mp'))
- grad_txt_gain: float32 [2, 512], P(None, ('dp', 'mp'))
- grad_txt_up: float32 [2, 512, 1024], P(None, None, ('dp', 'mp'))
- grad_txt_hid: float32 [2, 3, 1024], P(None, None, ('dp', 'mp'))
- grad_txt_down: float32 [2, 1024, 512], P(None, None, ('dp', 'mp'))
- grad_emb_mel: float32 [200, 1024], P(None, 'dp')
- grad_emb_text: float32 [512, 1024], P(None, 'dp')
- grad_emb_bias: float32 [1024], P('dp')
- grad_pos_conv: float32 [2, 31, 64, 1024], P(None, None, None, ('mp', 'dp'))
- grad_pos_bias: float32 [2, 1024], P(None, ('mp', 'dp'))
- grad_time_w1: float32 [256, 1024], P(None, 'dp')
- grad_time_bias: float32 [2, 1024], P(None, 'dp')
- grad_time_w2: float32 [1024, 1024], P(None, 'dp')
- grad_ada_w: float32 [1024, 6144], P(None, 'dp')
- grad_ada_b: float32 [6144], P('dp')
- grad_qkv_w: float32 [3, 1024, 1024], P(None, 'dp', 'mp')
- grad_qkv_b: float32 [3, 1024], P(None, ('mp', 'dp'))
- grad_out_w: float32 [1024, 1024], P('mp', 'dp')
- grad_out_b: float32 [1024], P('dp')
- grad_ff_w1: float32 [1024, 2048], P('dp', 'mp')
- grad_ff_b1: float32 [2048], P(('mp', 'dp'))
- grad_ff_w2: float32 [2048, 1024], P('mp', 'dp')
- grad_ff_b2: float32 [1024], P('dp')
The draws below stay inside these ranges and needn't reach their ends.
Inputs may be any that keep to these rules, and one draw needn't show every extreme that they name: `clip_lengths`: A group's 4 clips fill its 2048 frames; one clip of every group has exactly 1024 frames.
All inputs are finite; a program needn't handle non-finite values.
Results may differ from the reference program's by a relative error of at most 0.02.
Values may be sent and summed in bfloat16 or wider, within the bound.
A program may use at most 768 MiB of HBM per device.

```python
import math
from functools import partial
import jax
import jax.numpy as jnp
import numpy as np
from jax import lax

D = 1024
HEAD_DIM = 64
FF = 2048
MEL = 100
TD = 512
TH = 1024
VOCAB = 2546
TS = 256
KERNEL = 7
POS_K = 31
POS_G = 16
TB = 2
SEGS = 4
CLIP_MAX = 1024
FR = 2048
GROUPS = 8
FRAMES = 16384


def set_ends(values, rng, low, top_value):
    longest = values.shape.index(max(values.shape))
    spots = []
    for shift in (0, 1):
        where = [jax.random.randint(jax.random.fold_in(rng, axis), (), 0, length) for axis, length in enumerate(values.shape)]
        where[longest] = (where[longest] + shift) % values.shape[longest]
        spots.append(tuple(where))
    return values.at[spots[0]].set(low).at[spots[1]].set(top_value)


def steps_of(own_key, extent, split, least, high):
    loudness = 1.0
    for dim, shards_of in split:
        steps = jax.random.uniform(jax.random.fold_in(jax.random.fold_in(own_key, 6), dim), (shards_of,), jnp.float32, least / len(split), high / len(split))
        loudness = loudness * jnp.repeat(jnp.exp(steps), extent[dim] // shards_of).reshape((-1,) + (1,) * (len(extent) - 1 - dim))
    return loudness


def rank_table(amount, skew):
    weights = [(1 << 20) // math.isqrt(standing ** skew) + 1 for standing in range(1, amount + 1)]
    scale = 1 + sum(weights) // (1 << 30)
    return np.cumsum(np.array([max(1, weight // scale) for weight in weights]))


def ranked_ids(stream_key, dims, number_of, skew):
    table = rank_table(number_of, skew)
    lot = jax.random.randint(jax.random.fold_in(stream_key, 1), dims, 0, int(table[number_of - 1]))
    grade = jnp.searchsorted(jnp.asarray(table, jnp.int32), lot, side="right")
    return jax.random.permutation(jax.random.fold_in(stream_key, 2), number_of)[grade].astype(jnp.int32)


def split_up(count, total, reach, skew):
    portions = [(1 << 20) // math.isqrt(grade ** skew) + 1 for grade in range(2, count + 1)]
    surplus, holding = total - reach - (count - 1), [1] * (count - 1)
    while surplus > 0:
        free = [i for i in range(count - 1) if holding[i] < reach]
        mass, budget = sum([portions[i] for i in free]), surplus
        for i in free:
            more = min(reach - holding[i], max(1, budget * portions[i] // mass), surplus)
            holding[i] = holding[i] + more
            surplus = surplus - more
    return np.array([reach] + holding)


def ragged(stream_key, number_of, total, bound, skew):
    if number_of == 2:
        one = jax.random.randint(stream_key, (), max(1, total - bound), min(bound, total - 1) + 1)
        return jnp.stack([one, total - one])
    sizes = jnp.asarray(split_up(number_of, total, bound, skew), jnp.int32)
    twos = (number_of - 1) // 2
    giver, taker = sizes[1:1 + 2 * twos:2], sizes[2:2 + 2 * twos:2]
    margin = jnp.minimum(giver - 1, bound - taker)
    moved = jax.random.randint(jax.random.fold_in(stream_key, 1), (twos,), 0, 1 << 20) % (margin + 1)
    sizes = sizes.at[1:1 + 2 * twos:2].set(giver - moved).at[2:2 + 2 * twos:2].set(taker + moved)
    return sizes[jax.random.permutation(jax.random.fold_in(stream_key, 2), number_of)]


def normal_values(own_key, dims, scale, reach, cuts=(), held_as=jnp.bfloat16):
    array = scale * jax.random.normal(own_key, dims, jnp.float32)
    if cuts:
        array = array * steps_of(own_key, dims, cuts, -0.22, 0.18)
    return jnp.clip(array, -reach, reach).astype(held_as)


def setup_inputs(seed: int = 0) -> dict:
    streams_of = jax.random.split(jax.random.key(seed), 31)
    return {
        "mel_pair": normal_values(streams_of[0], (FRAMES, 2 * MEL), 1.0, 6.0, ((0, 8),)),
        "text_ids": set_ends(ranked_ids(streams_of[1], (FRAMES,), VOCAB, 2), jax.random.fold_in(streams_of[1], 3), 0, VOCAB - 1).astype(jnp.int32),
        "clip_lengths": jax.vmap(lambda own: ragged(own, SEGS, FR, CLIP_MAX, 2))(jax.random.split(streams_of[2], GROUPS)).reshape((GROUPS, SEGS)).astype(jnp.int32),
        "t_index": set_ends(jax.random.randint(streams_of[3], (GROUPS, SEGS), 0, 1000), jax.random.fold_in(streams_of[3], 1), 0, 999).astype(jnp.int32),
        "txt_table": normal_values(streams_of[4], (VOCAB, TD), 1.0, 6.0),
        "txt_conv": normal_values(streams_of[5], (TB, KERNEL, TD), KERNEL ** -0.5, 2.0, (), jnp.float32),
        "txt_vec": normal_values(streams_of[6], (TB, 3, TD), 0.3, 1.75, (), jnp.float32),
        "txt_gain": jnp.clip(1.0 + 0.1 * jax.random.normal(streams_of[7], (TB, TD), jnp.float32), 0.5, 1.5),
        "txt_up": normal_values(streams_of[8], (TB, TD, TH), TD ** -0.5, 0.25),
        "txt_hid": normal_values(streams_of[9], (TB, 3, TH), 0.3, 1.75, (), jnp.float32),
        "txt_down": normal_values(streams_of[10], (TB, TH, TD), TH ** -0.5, 0.1875),
        "emb_mel": normal_values(streams_of[11], (2 * MEL, D), (2 * MEL + TD) ** -0.5, 0.21875),
        "emb_text": normal_values(streams_of[12], (TD, D), (2 * MEL + TD) ** -0.5, 0.21875),
        "emb_bias": normal_values(streams_of[13], (D,), 0.3, 1.75, (), jnp.float32),
        "pos_conv": normal_values(streams_of[14], (2, POS_K, D // POS_G, D), (POS_K * (D // POS_G)) ** -0.5, 0.125, ((3, 4),)),
        "pos_bias": normal_values(streams_of[15], (2, D), 0.3, 1.75, ((1, 4),), jnp.float32),
        "time_w1": normal_values(streams_of[16], (TS, D), TS ** -0.5, 0.375),
        "time_bias": normal_values(streams_of[17], (2, D), 0.3, 1.75, (), jnp.float32),
        "time_w2": normal_values(streams_of[18], (D, D), D ** -0.5, 0.1875),
        "ada_w": normal_values(streams_of[19], (D, 6 * D), D ** -0.5, 0.1875),
        "ada_b": normal_values(streams_of[20], (6 * D,), 0.3, 1.75, (), jnp.float32),
        "qkv_w": normal_values(streams_of[21], (3, D, D), D ** -0.5, 0.1875, ((2, 4),)),
        "qkv_b": normal_values(streams_of[22], (3, D), 0.3, 1.75, ((1, 4),), jnp.float32),
        "out_w": normal_values(streams_of[23], (D, D), HEAD_DIM ** -0.5, 0.75, ((0, 4),)),
        "out_b": normal_values(streams_of[24], (D,), 0.3, 1.75, (), jnp.float32),
        "ff_w1": normal_values(streams_of[25], (D, FF), D ** -0.5, 0.1875, ((1, 4),)),
        "ff_b1": normal_values(streams_of[26], (FF,), 0.3, 1.75, ((0, 4),), jnp.float32),
        "ff_w2": normal_values(streams_of[27], (FF, D), FF ** -0.5, 0.125, ((0, 4),)),
        "ff_b2": normal_values(streams_of[28], (D,), 0.3, 1.75, (), jnp.float32),
        "out_grad": normal_values(streams_of[29], (FRAMES, D), 1.0, 6.0, ((0, 8),)),
    }


@jax.custom_vjp
def low(v):
    return lax.optimization_barrier(v.astype(jnp.bfloat16)).astype(jnp.float32)

@jax.custom_vjp
def low_back(v):
    return v

def low_keep(v):
    return (low(v), None)

def low_pass(kept, grad):
    return (grad,)

def back_keep(v):
    return (v, None)

def back_low(kept, grad):
    return (low(grad),)
low.defvjp(low_keep, low_pass)
low_back.defvjp(back_keep, back_low)
highest = lax.Precision.HIGHEST
weight_names = ('txt_table', 'txt_conv', 'txt_vec', 'txt_gain', 'txt_up', 'txt_hid', 'txt_down', 'emb_mel', 'emb_text', 'emb_bias', 'pos_conv', 'pos_bias', 'time_w1', 'time_bias', 'time_w2', 'ada_w', 'ada_b', 'qkv_w', 'qkv_b', 'out_w', 'out_b', 'ff_w1', 'ff_b1', 'ff_w2', 'ff_b2')

def matmul(left, right):
    return jnp.dot(left, right, precision=highest)

def precise(left, right):
    return jnp.dot(left, right, precision=highest)

def layer_norm(values):
    centred = values - lax.optimization_barrier(jnp.mean(values, axis=-1, keepdims=True))
    variance = lax.optimization_barrier(jnp.mean(centred * centred, axis=-1, keepdims=True))
    return centred * lax.rsqrt(variance + 1e-06)

def clip_layout(lengths, row_count):
    clip_ends = jnp.cumsum(lengths).astype(jnp.int32)
    starts = (clip_ends - lengths).astype(jnp.int32)
    frames = jnp.arange(row_count, dtype=jnp.int32)
    member = (frames[:, None] >= starts[None, :]) & (frames[:, None] < clip_ends[None, :])
    member_int = member.astype(jnp.int32)
    clip_index = jnp.arange(lengths.shape[0], dtype=jnp.int32)
    segment = lax.optimization_barrier(jnp.sum(member_int * clip_index[None, :], axis=1)).astype(jnp.int32)
    position = (frames - lax.optimization_barrier(jnp.sum(member_int * starts[None, :], axis=1))).astype(jnp.int32)
    return (member.astype(jnp.float32), segment, position, starts)

def neighbour(values, segment, offset):
    row_count = values.shape[0]
    reach_rows = abs(offset)
    padded = jnp.pad(values, ((reach_rows, reach_rows), (0, 0)))
    seg_padded = jnp.pad(segment, (reach_rows, reach_rows), constant_values=-1)
    moved_rows = lax.slice_in_dim(padded, reach_rows + offset, reach_rows + offset + row_count, axis=0)
    moved_seg = lax.slice_in_dim(seg_padded, reach_rows + offset, reach_rows + offset + row_count, axis=0)
    keep_row = (moved_seg == segment) & (segment >= 0)
    return jnp.where(keep_row[:, None], moved_rows, 0.0)

def mish_act(values):
    softplus = jnp.maximum(values, 0.0) + jnp.log1p(jnp.exp(-jnp.abs(values)))
    return values * jnp.tanh(softplus)

def text_block(hidden, segment, onehot, conv_kernel, vec_small, scale_vec, up_weight, vec_big, down_weight):
    tap_count = conv_kernel.shape[0]
    mixture = vec_small[0] + jnp.zeros_like(hidden)
    for tap_index in range(tap_count):
        mixture = mixture + conv_kernel[tap_index] * neighbour(hidden, segment, tap_index - tap_count // 2)
    normed = layer_norm(mixture) * scale_vec + vec_small[1]
    upper_pre = low_back(matmul(low(normed), up_weight)) + vec_big[0]
    active = jax.nn.gelu(upper_pre, approximate=False)
    squares = precise(onehot.T, active * active)
    col_norms = jnp.sqrt(jnp.maximum(squares, 1.0))
    norm_ratio = col_norms / (lax.optimization_barrier(jnp.mean(col_norms, axis=-1, keepdims=True)) + 1e-06)
    grn_out = vec_big[1] * (active * precise(onehot, norm_ratio)) + vec_big[2] + active
    return hidden + low_back(matmul(low(grn_out), down_weight)) + vec_small[2]

def refine_text(weights, token_ids, segment, onehot):
    hidden = jnp.take(weights['txt_table'], token_ids, axis=0)
    for block_index in range(weights['txt_conv'].shape[0]):
        hidden = text_block(hidden, segment, onehot, weights['txt_conv'][block_index], weights['txt_vec'][block_index], weights['txt_gain'][block_index], weights['txt_up'][block_index], weights['txt_hid'][block_index], weights['txt_down'][block_index])
    return low(hidden)

def position_conv(source, segment, kernel):
    row_count, feature_width = source.shape
    tap_count, group_width = (kernel.shape[0], kernel.shape[1])
    group_count = feature_width // group_width
    stacked = jnp.stack([neighbour(source, segment, tap_index - tap_count // 2) for tap_index in range(tap_count)], axis=1)
    stacked = stacked.reshape(row_count, tap_count, group_count, group_width)
    kernel_view = kernel.reshape(tap_count, group_width, group_count, group_width)
    return jnp.einsum('tkgi,kigo->tgo', stacked, kernel_view, precision=highest).reshape(row_count, feature_width)

def position_embed(weights, source, segment):
    conv_entry = low_back(low(source))
    first_out = low(mish_act(low_back(position_conv(conv_entry, segment, weights['pos_conv'][0])) + weights['pos_bias'][0]))
    return low(mish_act(low_back(position_conv(first_out, segment, weights['pos_conv'][1])) + weights['pos_bias'][1]))

def time_sinusoid(time_steps, full_width):
    half_width = full_width // 2
    frequency = jnp.exp(jnp.arange(half_width, dtype=jnp.float32) * (-math.log(10000.0) / (half_width - 1)))
    angles = time_steps.astype(jnp.float32)[:, None] * frequency[None, :]
    return jnp.concatenate([jnp.sin(angles), jnp.cos(angles)], axis=-1)

def time_embed(weights, time_steps):
    sinusoid = time_sinusoid(time_steps, weights['time_w1'].shape[0])
    act_one = jax.nn.silu(precise(sinusoid, weights['time_w1']) + weights['time_bias'][0])
    time_vec = precise(act_one, weights['time_w2']) + weights['time_bias'][1]
    return precise(jax.nn.silu(time_vec), weights['ada_w']) + weights['ada_b']

def rotary(position, head_dim):
    inverse = jnp.exp(jnp.arange(0, head_dim, 2, dtype=jnp.float32) * (-math.log(10000.0) / head_dim))
    angles = position.astype(jnp.float32)[:, None] * inverse[None, :]
    return (jnp.cos(angles), jnp.sin(angles))

def rotate(values, cosine, sine_table):
    row_count, head_count, head_width = values.shape
    pair_view = values.reshape(row_count, head_count, head_width // 2, 2)
    first_half = pair_view[..., 0]
    second_half = pair_view[..., 1]
    cos_rows = cosine[:, None, :]
    sin_rows = sine_table[:, None, :]
    turned = jnp.stack([first_half * cos_rows - second_half * sin_rows, second_half * cos_rows + first_half * sin_rows], axis=-1)
    return turned.reshape(row_count, head_count, head_width)

def attend_block(queries, seg_block, key_rows, value_rows, segment):
    score_scale = queries.shape[-1] ** (-0.5)
    scores = low_back(jnp.einsum('qhd,khd->hqk', queries, key_rows, precision=highest)) * score_scale
    allowed = (seg_block[:, None] == segment[None, :])[None]
    scores = jnp.where(allowed, scores, -1e+30)
    row_top = lax.optimization_barrier(jnp.max(scores, axis=-1, keepdims=True))
    exponent = jnp.exp(scores - row_top)
    attn_probs = low(exponent / lax.optimization_barrier(jnp.sum(exponent, axis=-1, keepdims=True)))
    return low(low_back(jnp.einsum('hqk,khd->qhd', attn_probs, value_rows, precision=highest)))

def attention(qkv_weight, qkv_bias, out_weight, normed, segment, position, head_dim):
    row_count = normed.shape[0]
    feature_width = qkv_weight.shape[2]
    head_count = feature_width // head_dim
    cosine, sine_table = rotary(position, head_dim)

    def project(which_part):
        return (low_back(matmul(normed, qkv_weight[which_part])) + qkv_bias[which_part]).reshape(row_count, head_count, head_dim)
    queries = low(rotate(project(0), cosine, sine_table))
    key_rows = low(rotate(project(1), cosine, sine_table))
    value_rows = low(project(2))
    block_rows = min(512, row_count)
    block_count = row_count // block_rows
    step_fn = jax.checkpoint(partial(attend_block, key_rows=key_rows, value_rows=value_rows, segment=segment))
    attended = lax.map(lambda pieces: step_fn(pieces[0], pieces[1]), (queries.reshape(block_count, block_rows, head_count, head_dim), segment.reshape(block_count, block_rows)))
    return matmul(attended.reshape(row_count, feature_width), out_weight)

def expand(onehot, modulation, which_part, feature_width):
    return precise(onehot, modulation[:, which_part * feature_width:(which_part + 1) * feature_width])

def modulate(state, onehot, modulation, shift_part, scale_part):
    feature_width = state.shape[1]
    return low(layer_norm(state) * (1.0 + expand(onehot, modulation, scale_part, feature_width)) + expand(onehot, modulation, shift_part, feature_width))

def group_forward(weights, mel_in, token_ids, lengths, time_steps):
    row_count = mel_in.shape[0]
    onehot, segment, position, starts = clip_layout(lengths, row_count)
    text_rows = refine_text(weights, token_ids, segment, onehot)
    start_embed = low_back(matmul(low(mel_in), weights['emb_mel']) + matmul(text_rows, weights['emb_text'])) + weights['emb_bias']
    state_one = start_embed + position_embed(weights, start_embed, segment)
    modulation = time_embed(weights, time_steps)
    feature_width = state_one.shape[1]
    normed_one = modulate(state_one, onehot, modulation, 0, 1)
    attended = low_back(attention(weights['qkv_w'], weights['qkv_b'], weights['out_w'], normed_one, segment, position, HEAD_DIM)) + weights['out_b']
    state_two = state_one + expand(onehot, modulation, 2, feature_width) * attended
    normed_two = modulate(state_two, onehot, modulation, 3, 4)
    ff_inner = low(jax.nn.gelu(low_back(matmul(normed_two, weights['ff_w1'])) + weights['ff_b1'], approximate=True))
    ff_out = low_back(matmul(ff_inner, weights['ff_w2'])) + weights['ff_b2']
    return state_two + expand(onehot, modulation, 5, feature_width) * ff_out

def reference(mel_pair, text_ids, clip_lengths, t_index, txt_table, txt_conv, txt_vec, txt_gain, txt_up, txt_hid, txt_down, emb_mel, emb_text, emb_bias, pos_conv, pos_bias, time_w1, time_bias, time_w2, ada_w, ada_b, qkv_w, qkv_b, out_w, out_b, ff_w1, ff_b1, ff_w2, ff_b2, out_grad):
    given = (txt_table, txt_conv, txt_vec, txt_gain, txt_up, txt_hid, txt_down, emb_mel, emb_text, emb_bias, pos_conv, pos_bias, time_w1, time_bias, time_w2, ada_w, ada_b, qkv_w, qkv_b, out_w, out_b, ff_w1, ff_b1, ff_w2, ff_b2)
    weights = {name_key: array_in.astype(jnp.float32) for name_key, array_in in zip(weight_names, given)}
    mel_rows = mel_pair.astype(jnp.float32).reshape(GROUPS, FR, 2 * MEL)
    id_rows = text_ids.reshape(GROUPS, FR)
    cot_rows = out_grad.astype(jnp.float32).reshape(GROUPS, FR, D)
    zeros_tree = jax.tree.map(jnp.zeros_like, weights)

    def one_group(running, packed):
        mel_now, ids_now, length_now, steps_now, cot_now = packed

        def forward(weights_in, mel_value):
            return group_forward(weights_in, mel_value, ids_now, length_now, steps_now)
        result, pullback = jax.vjp(forward, weights, mel_now)
        grad_weights, grad_mel = pullback(cot_now)
        return (jax.tree.map(jnp.add, running, grad_weights), (result, grad_mel))
    totals, (outputs, mel_grads) = lax.scan(one_group, zeros_tree, (mel_rows, id_rows, clip_lengths, t_index, cot_rows))
    return (outputs.reshape(FRAMES, D), mel_grads.reshape(FRAMES, 2 * MEL), totals['txt_table'], totals['txt_conv'], totals['txt_vec'], totals['txt_gain'], totals['txt_up'], totals['txt_hid'], totals['txt_down'], totals['emb_mel'], totals['emb_text'], totals['emb_bias'], totals['pos_conv'], totals['pos_bias'], totals['time_w1'], totals['time_bias'], totals['time_w2'], totals['ada_w'], totals['ada_b'], totals['qkv_w'], totals['qkv_b'], totals['out_w'], totals['out_b'], totals['ff_w1'], totals['ff_b1'], totals['ff_w2'], totals['ff_b2'])
```

```python
from functools import partial
import math

import jax
import jax.numpy as jnp
from jax import lax
from jax.experimental import pallas as pl
from jax.experimental.pallas import tpu as pltpu
from jax.sharding import PartitionSpec as P

HEAD_DIM = 64
GAP = 16
HALO = 8
BF = jnp.bfloat16
F32 = jnp.float32
highest = lax.Precision.HIGHEST
NN = (((1,), (0,)), ((), ()))
NT = (((1,), (1,)), ((), ()))
TN = (((0,), (0,)), ((), ()))


def dot(left, right, dims=NN):
    return lax.dot_general(left.astype(BF), right.astype(BF), dims, preferred_element_type=F32)


def precise(left, right, dims=NN):
    one = lax.reduce_precision(left, 8, 7)
    two = lax.reduce_precision(left - one, 8, 7)
    three = left - one - two
    rows = left.shape[0]
    stacked = jnp.concatenate([one, two, three], axis=0).astype(BF)
    product = lax.dot_general(stacked, right, dims, preferred_element_type=F32)
    return product[:rows] + product[rows : 2 * rows] + product[2 * rows :]


@jax.custom_vjp
def expand(onehot, parts):
    return sum(onehot[:, c : c + 1] * parts[c : c + 1] for c in range(parts.shape[0]))


def expand_ahead(onehot, parts):
    return expand(onehot, parts), onehot


def expand_behind(onehot, grad):
    return None, jnp.dot(onehot.T, grad, precision=highest)


expand.defvjp(expand_ahead, expand_behind)


def silu_slope(values):
    sigmoid_val = jax.nn.sigmoid(values)
    return sigmoid_val * (1.0 + values * (1.0 - sigmoid_val))


def layer_norm(values):
    centred = values - jnp.mean(values, axis=-1, keepdims=True)
    variance = jnp.mean(centred * centred, axis=-1, keepdims=True)
    return centred * lax.rsqrt(variance + 1e-06)


def mish(values):
    grown = jnp.exp(jnp.minimum(values, 20.0))
    wide = grown * (grown + 2.0)
    return values * (wide / (wide + 2.0))


def mish_slope(values):
    grown = jnp.exp(jnp.minimum(values, 20.0))
    wide = grown * (grown + 2.0)
    under = 1.0 / (wide + 2.0)
    return wide * under + values * (4.0 * grown * (1.0 + grown) * under * under)


def conv_norm(hidden, segment, conv, vec, gain):
    taps = conv.shape[0]
    reach = taps // 2
    rows = hidden.shape[0]
    padded = jnp.pad(hidden, ((reach, reach), (0, 0)))
    seg_padded = jnp.pad(segment, (reach, reach), constant_values=-1)
    mixture = vec[0]
    for tap in range(taps):
        keep = (seg_padded[tap : tap + rows] == segment) & (segment >= 0)
        mixture = mixture + conv[tap] * jnp.where(keep[:, None], padded[tap : tap + rows], 0.0)
    return layer_norm(mixture) * gain + vec[1]


def activate(pre, bias):
    return jax.nn.gelu(pre + bias, approximate=False)


def clip_squares(own, active):
    return jnp.dot(own.T, active * active, precision=highest)


def respond(active, squares, onehot, scale, shift):
    norms = jnp.sqrt(jnp.maximum(squares, 1.0))
    ratio = norms / (jnp.mean(norms, axis=-1, keepdims=True) + 1e-06)
    return scale * (active * expand(onehot, ratio)) + shift + active


def text_ahead(hidden, segment, onehot, own, conv, vec, gain, up, hid, down, axis):
    normed, norm_pull = jax.vjp(
        lambda h, c, v, g: conv_norm(h, segment, c, v, g), hidden, conv, vec, gain
    )
    normed = normed.astype(BF)
    active, act_pull = jax.vjp(activate, dot(normed, up), hid[0])
    squares, square_pull = jax.vjp(lambda a: clip_squares(own, a), active)
    squares = lax.psum(squares, axis)
    grown, respond_pull = jax.vjp(
        lambda a, s, g, b: respond(a, s, onehot, g, b), active, squares, hid[1], hid[2]
    )
    grown = grown.astype(BF)
    result = hidden + dot(grown, down) + vec[2]
    return result, (norm_pull, normed, act_pull, square_pull, respond_pull, grown)


def text_behind(kept, grad, up, down, axis):
    norm_pull, normed, act_pull, square_pull, respond_pull, grown = kept
    grad_low = grad.astype(BF)
    g_out = jnp.sum(grad, axis=0)
    g_down = dot(grad_low, grown, TN)
    grad_active, grad_squares, g_scale, g_shift = respond_pull(dot(grad_low, down, NT))
    grad_squares = lax.psum(grad_squares, axis)
    grad_active = grad_active + square_pull(grad_squares)[0]
    grad_pre, g_bias = act_pull(grad_active)
    pre_low = grad_pre.astype(BF)
    g_up = dot(pre_low, normed, TN)
    grad_hidden, g_conv, g_vec, g_gain = norm_pull(dot(pre_low, up, NT))
    g_vec = g_vec.at[2].add(g_out)
    return (
        grad + grad_hidden,
        (g_conv, g_vec, g_gain, g_up, jnp.stack([g_bias, g_scale, g_shift]), g_down),
    )


def spread(values, starts, ends):
    rows = values.shape[0]
    clips = starts.shape[0]
    at = jnp.arange(rows, dtype=jnp.int32)
    total = rows + GAP * clips + 2 * GAP
    out = None
    for c in range(clips):
        keep = (at >= starts[c]) & (at < ends[c])
        part = jnp.where(keep[:, None], values, 0)
        lead = GAP + GAP * c
        part = jnp.pad(part, ((lead, total - lead - rows), (0, 0)))
        out = part if out is None else out + part
    return out


def gather_back(values, starts, ends):
    clips = starts.shape[0]
    rows = values.shape[0] - GAP * clips
    at = jnp.arange(rows, dtype=jnp.int32)
    out = None
    for c in range(clips):
        keep = (at >= starts[c]) & (at < ends[c])
        part = jnp.where(keep[:, None], values[GAP * c : GAP * c + rows], 0)
        out = part if out is None else out + part
    return out


def conv_kernel(taps, x_ref, w_ref, o_ref):
    rows = o_ref.shape[0]
    first = GAP - taps // 2
    columns = [x_ref[first + k : first + k + rows, :].astype(BF) for k in range(taps)]
    o_ref[...] = jnp.dot(
        jnp.concatenate(columns, axis=1), w_ref[...], preferred_element_type=F32
    )


def conv_chunk(rows):
    for size in (528, 352, 256, 128, 64, 32, 16):
        if rows % size == 0:
            return size
    return rows


def apply_conv(spread_rows, weight, taps):
    rows = spread_rows.shape[0] - 2 * GAP
    width = spread_rows.shape[1]
    chunk = conv_chunk(rows)
    return pl.pallas_call(
        partial(conv_kernel, taps),
        out_shape=jax.ShapeDtypeStruct((rows, width), F32),
        grid=(rows // chunk,),
        in_specs=[
            pl.BlockSpec((pl.Element(chunk + 2 * GAP), pl.Element(width)), lambda i: (i * chunk, 0)),
            pl.BlockSpec(weight.shape, lambda i: (0, 0), pipeline_mode=pl.Buffered(1)),
        ],
        out_specs=pl.BlockSpec((chunk, width), lambda i: (i, 0)),
        compiler_params=pltpu.CompilerParams(vmem_limit_bytes=48 << 20),
        cost_estimate=pl.CostEstimate(
            flops=2 * rows * taps * width * width, bytes_accessed=8 << 20, transcendentals=0
        ),
    )(spread_rows, weight)


def conv_grad_kernel(taps, group, x_ref, g_ref, o_ref):
    rows, width = g_ref.shape
    first = GAP - taps // 2
    turned = g_ref[...].T.astype(BF)

    @pl.when(pl.program_id(0) == 0)
    def _():
        o_ref[...] = jnp.zeros_like(o_ref)

    for k in range(taps):
        window = x_ref[first + k : first + k + rows, :].astype(BF)
        product = jnp.dot(turned, window, preferred_element_type=F32)
        for g in range(width // group):
            own = slice(g * group, (g + 1) * group)
            o_ref[own, k * group : (k + 1) * group] += product[own, own]


def conv_grad(spread_rows, grads, taps, group):
    rows, width = grads.shape
    chunk = conv_chunk(rows)
    return pl.pallas_call(
        partial(conv_grad_kernel, taps, group),
        out_shape=jax.ShapeDtypeStruct((width, taps * group), F32),
        grid=(rows // chunk,),
        in_specs=[
            pl.BlockSpec((pl.Element(chunk + 2 * GAP), pl.Element(width)), lambda i: (i * chunk, 0)),
            pl.BlockSpec((chunk, width), lambda i: (i, 0)),
        ],
        out_specs=pl.BlockSpec((width, taps * group), lambda i: (0, 0)),
        compiler_params=pltpu.CompilerParams(vmem_limit_bytes=48 << 20),
        cost_estimate=pl.CostEstimate(
            flops=2 * rows * taps * width * width, bytes_accessed=8 << 20, transcendentals=0
        ),
    )(spread_rows, grads)


def block_diagonal(weight, turned):
    taps, group, width = weight.shape
    groups = width // group
    parts = weight.reshape(taps, group, groups, group)
    if turned:
        parts = parts[::-1].transpose(0, 3, 2, 1)
    eye = jnp.eye(groups, dtype=weight.dtype)
    full = parts[:, None] * eye[None, :, None, :, None]
    return full.reshape(taps * groups * group, groups * group)


def pair_split(columns):
    lead = columns.shape[:-1]
    pairs = columns.reshape(*lead, columns.shape[-1] // 2, 2)
    return jnp.concatenate([pairs[..., 0], pairs[..., 1]], axis=-1)


def pair_merge(columns):
    half = columns.shape[-1] // 2
    return jnp.stack([columns[..., :half], columns[..., half:]], axis=-1).reshape(columns.shape)


def head_masks(width):
    heads = width // HEAD_DIM
    lane = lax.broadcasted_iota(jnp.int32, (1, width), 1)
    half = HEAD_DIM // 2
    paired = [((lane % (width // 2)) // half) == h for h in range(heads)]
    plain = [(lane // HEAD_DIM) == h for h in range(heads)]
    return heads, paired, plain


def attend_kernel(bounds, q_ref, k_ref, v_ref, sq_ref, sk_ref, o_ref, full_ref, lse_ref):
    i = pl.program_id(0)
    q = q_ref[...]
    rows, width = q.shape
    heads, paired, plain = head_masks(width)
    scale = HEAD_DIM**-0.5
    q_heads = [jnp.where(paired[h], q, jnp.zeros_like(q)) for h in range(heads)]
    sq = sq_ref[...]

    def step(kb, carry):
        tops, sums, acc = carry
        k, v = k_ref[kb], v_ref[kb]
        same = sq == sk_ref[kb]
        new_tops, new_sums = [], []
        decay, extra = None, None
        for h in range(heads):
            scores = lax.dot_general(q_heads[h], k, NT, preferred_element_type=F32) * scale
            scores = jnp.where(same, scores, -1e30)
            top = jnp.maximum(tops[h], jnp.max(scores, axis=-1, keepdims=True))
            fade = jnp.exp(tops[h] - top)
            weight = jnp.exp(scores - top)
            new_tops.append(top)
            new_sums.append(fade * sums[h] + jnp.sum(weight, axis=-1, keepdims=True))
            v_head = jnp.where(plain[h], v, jnp.zeros_like(v))
            part = jnp.dot(weight.astype(BF), v_head, preferred_element_type=F32)
            extra = part if extra is None else extra + part
            decay = fade * jnp.ones((1, width), F32) if h == 0 else jnp.where(plain[h], fade, decay)
        return tuple(new_tops), tuple(new_sums), acc * decay + extra

    start = (
        tuple(jnp.full((rows, 1), -1e30, F32) for _ in range(heads)),
        tuple(jnp.zeros((rows, 1), F32) for _ in range(heads)),
        jnp.zeros((rows, width), F32),
    )
    tops, sums, acc = lax.fori_loop(bounds[i, 0], bounds[i, 1], step, start)
    lane = lax.broadcasted_iota(jnp.int32, (1, lse_ref.shape[1]), 1)
    share = jnp.ones((rows, width), F32)
    logs = jnp.zeros((rows, lse_ref.shape[1]), F32)
    for h in range(heads):
        share = jnp.where(plain[h], 1.0 / sums[h], share)
        logs = jnp.where(lane == h, tops[h] + jnp.log(sums[h]), logs)
    full = acc * share
    full_ref[...] = full
    o_ref[...] = full.astype(BF)
    lse_ref[...] = logs


def attend(qkv, seg_rows, seg_blocks, bounds, block):
    shards, _, rows, width = qkv.shape
    total = shards * rows
    per = rows // block
    grid_spec = pltpu.PrefetchScalarGridSpec(
        num_scalar_prefetch=1,
        grid=(total // block,),
        in_specs=[
            pl.BlockSpec((None, None, block, width), lambda i, b: (i // per, 0, i % per, 0)),
            pl.BlockSpec((shards, None, rows, width), lambda i, b: (0, 1, 0, 0)),
            pl.BlockSpec((shards, None, rows, width), lambda i, b: (0, 2, 0, 0)),
            pl.BlockSpec((block, 1), lambda i, b: (i, 0)),
            pl.BlockSpec((shards, 1, rows), lambda i, b: (0, 0, 0)),
        ],
        out_specs=[
            pl.BlockSpec((block, width), lambda i, b: (i, 0)),
            pl.BlockSpec((block, width), lambda i, b: (i, 0)),
            pl.BlockSpec((block, 128), lambda i, b: (i, 0)),
        ],
    )
    return pl.pallas_call(
        attend_kernel,
        out_shape=[
            jax.ShapeDtypeStruct((total, width), BF),
            jax.ShapeDtypeStruct((total, width), F32),
            jax.ShapeDtypeStruct((total, 128), F32),
        ],
        grid_spec=grid_spec,
        compiler_params=pltpu.CompilerParams(vmem_limit_bytes=48 << 20),
        cost_estimate=pl.CostEstimate(
            flops=8 * total * total * width, bytes_accessed=8 << 20, transcendentals=0
        ),
    )(bounds, qkv, qkv, qkv, seg_rows, seg_blocks)


def unrotate(values, cos, sin):
    half = values.shape[1] // 2
    even, odd = values[:, :half], values[:, half:]
    return jnp.concatenate([even * cos + odd * sin, odd * cos - even * sin], axis=1)


def attend_back_kernel(
    bounds, q_ref, k_ref, v_ref, full_ref, lse_ref, do_ref, sq_ref, sk_ref, cos_ref, sin_ref,
    out_ref, dk_ref, dv_ref,
):
    i = pl.program_id(0)
    q, do = q_ref[...], do_ref[...]
    rows, width = q.shape
    shards, _, shard_rows, _ = out_ref.shape
    per = shard_rows // rows
    heads, paired, plain = head_masks(width)
    scale = HEAD_DIM**-0.5

    @pl.when(i == 0)
    def _():
        dk_ref[...] = jnp.zeros_like(dk_ref)
        dv_ref[...] = jnp.zeros_like(dv_ref)

    zero = jnp.zeros_like(q)
    q_heads = [jnp.where(paired[h], q, zero) for h in range(heads)]
    do_heads = [jnp.where(plain[h], do, zero) for h in range(heads)]
    product = do.astype(F32) * full_ref[...]
    deltas = [jnp.sum(jnp.where(plain[h], product, 0.0), axis=-1, keepdims=True) for h in range(heads)]
    logs = [lse_ref[:, h : h + 1] for h in range(heads)]
    sq = sq_ref[...]

    def step(kb, dq):
        k, v = k_ref[kb], v_ref[kb]
        same = sq == sk_ref[kb]
        dk, dv = dk_ref[kb], dv_ref[kb]
        for h in range(heads):
            scores = lax.dot_general(q_heads[h], k, NT, preferred_element_type=F32) * scale
            weight = jnp.where(same, jnp.exp(scores - logs[h]), 0.0)
            dp = lax.dot_general(do_heads[h], v, NT, preferred_element_type=F32)
            ds = (weight * (dp - deltas[h]) * scale).astype(BF)
            dv = dv + lax.dot_general(weight.astype(BF), do_heads[h], TN, preferred_element_type=F32)
            dk = dk + lax.dot_general(ds, q_heads[h], TN, preferred_element_type=F32)
            k_head = jnp.where(paired[h], k, jnp.zeros_like(k))
            dq = dq + jnp.dot(ds, k_head, preferred_element_type=F32)
        dk_ref[kb] = dk
        dv_ref[kb] = dv
        return dq

    dq = lax.fori_loop(bounds[i, 0], bounds[i, 1], step, jnp.zeros((rows, width), F32))
    here = pl.ds(pl.multiple_of(i * rows, rows), rows)
    inside = pl.ds(pl.multiple_of((i % per) * rows, rows), rows)
    out_ref[i // per, 0, inside, :] = unrotate(dq, cos_ref[here, :], sin_ref[here, :]).astype(BF)

    @pl.when(i == pl.num_programs(0) - 1)
    def _():
        for s in range(shards):
            own = slice(s * shard_rows, (s + 1) * shard_rows)
            out_ref[s, 1] = unrotate(dk_ref[s], cos_ref[own, :], sin_ref[own, :]).astype(BF)
            out_ref[s, 2] = dv_ref[s].astype(BF)


def attend_back(qkv, full, logs, grads, seg_rows, seg_blocks, cos, sin, bounds, block):
    shards, _, rows, width = qkv.shape
    total = shards * rows
    per = rows // block
    grid_spec = pltpu.PrefetchScalarGridSpec(
        num_scalar_prefetch=1,
        grid=(total // block,),
        in_specs=[
            pl.BlockSpec((None, None, block, width), lambda i, b: (i // per, 0, i % per, 0)),
            pl.BlockSpec((shards, None, rows, width), lambda i, b: (0, 1, 0, 0)),
            pl.BlockSpec((shards, None, rows, width), lambda i, b: (0, 2, 0, 0)),
            pl.BlockSpec((block, width), lambda i, b: (i, 0)),
            pl.BlockSpec((block, 128), lambda i, b: (i, 0)),
            pl.BlockSpec((block, width), lambda i, b: (i, 0)),
            pl.BlockSpec((block, 1), lambda i, b: (i, 0)),
            pl.BlockSpec((shards, 1, rows), lambda i, b: (0, 0, 0)),
            pl.BlockSpec((total, width // 2), lambda i, b: (0, 0)),
            pl.BlockSpec((total, width // 2), lambda i, b: (0, 0)),
        ],
        out_specs=pl.BlockSpec((shards, 3, rows, width), lambda i, b: (0, 0, 0, 0)),
        scratch_shapes=[
            pltpu.VMEM((shards, rows, width), F32),
            pltpu.VMEM((shards, rows, width), F32),
        ],
    )
    return pl.pallas_call(
        attend_back_kernel,
        out_shape=jax.ShapeDtypeStruct((shards, 3, rows, width), BF),
        grid_spec=grid_spec,
        compiler_params=pltpu.CompilerParams(vmem_limit_bytes=48 << 20),
        cost_estimate=pl.CostEstimate(
            flops=20 * total * total * width, bytes_accessed=16 << 20, transcendentals=0
        ),
    )(bounds, qkv, qkv, qkv, full, logs, grads, seg_rows, seg_blocks, cos, sin)


def exchange(values, axis):
    return lax.all_to_all(values, axis, 0, 0)


def local(
    mel_pair, text_ids, clip_lengths, t_index,
    txt_table, txt_conv, txt_vec, txt_gain, txt_up, txt_hid, txt_down,
    emb_mel, emb_text, emb_bias, pos_conv, pos_bias,
    time_w1, time_bias, time_w2, ada_w, ada_b,
    qkv_w, qkv_b, out_w, out_b, ff_w1, ff_b1, ff_w2, ff_b2, out_grad,
):
    total = mel_pair.shape[0]
    width = emb_mel.shape[1]
    shards, groups = lax.axis_size("mp"), lax.axis_size("dp")
    rank, place = lax.axis_index("mp"), lax.axis_index("dp")
    rows = total // shards
    cols = width // shards
    clips = clip_lengths.shape[1]
    first = rank * rows
    taps = pos_conv.shape[1]
    group = pos_conv.shape[2]

    def spread_slice(weight, axis):
        piece = weight.shape[axis] // groups
        return lax.dynamic_slice_in_dim(weight, place * piece, piece, axis)

    def gather(piece, axis):
        return lax.all_gather(lax.all_gather(piece, "mp"), "dp", axis=axis, tiled=True)

    qkv_piece = spread_slice(qkv_w, 1)
    qkv_piece = jnp.concatenate([pair_split(qkv_piece[:2]), qkv_piece[2:]], axis=0)
    qkv_full = gather(qkv_piece, 2)
    out_full = gather(spread_slice(out_w, 0), 1).reshape(width, width)
    w1_full = lax.all_gather(
        lax.all_gather(spread_slice(ff_w1, 0), "mp", axis=1, tiled=True), "dp", axis=0, tiled=True
    )
    w2_full = gather(spread_slice(ff_w2, 0), 1).reshape(-1, width)
    small = jnp.concatenate([pair_split(qkv_b[:2]), qkv_b[2:]], axis=0)
    qkv_bias = lax.all_gather(small, "mp")
    b1_full = lax.all_gather(ff_b1, "mp", tiled=True)
    all_steps = lax.all_gather(t_index, "dp", tiled=True).reshape(-1)

    lengths = clip_lengths[0]
    clip_index = jnp.arange(clips, dtype=jnp.int32)
    ends = jnp.sum(jnp.where(clip_index[:, None] >= clip_index[None, :], lengths[None, :], 0), axis=1)
    starts = ends - lengths
    frames = jnp.arange(total, dtype=jnp.int32)
    member = (frames[:, None] >= starts[None, :]) & (frames[:, None] < ends[None, :])
    segment = jnp.sum(member * clip_index[None, :], axis=1).astype(jnp.int32)
    position = frames - jnp.sum(member * starts[None, :], axis=1)
    ext = rows + 2 * HALO
    ids = lax.dynamic_slice_in_dim(jnp.pad(text_ids, (HALO, HALO)), first, ext)
    seg_ext = lax.dynamic_slice_in_dim(jnp.pad(segment, (HALO, HALO), constant_values=-1), first, ext)
    hot_ext = (seg_ext[:, None] == clip_index[None, :]).astype(F32)
    ext_index = jnp.arange(ext, dtype=jnp.int32)
    inside = (ext_index >= HALO) & (ext_index < HALO + rows)
    own_ext = jnp.where(inside[:, None], hot_ext, 0.0)
    hot = hot_ext[HALO : HALO + rows]

    def time_path(steps):
        half = time_w1.shape[0] // 2
        frequency = jnp.exp(jnp.arange(half, dtype=F32) * (-math.log(10000.0) / (half - 1)))
        angles = steps.astype(F32)[:, None] * frequency[None, :]
        sinusoid = jnp.concatenate([jnp.sin(angles), jnp.cos(angles)], axis=-1)
        pre_one = precise(sinusoid, time_w1) + time_bias[0]
        act_one = jax.nn.silu(pre_one)
        time_vec = precise(act_one, time_w2) + time_bias[1]
        return sinusoid, pre_one, act_one, time_vec, jax.nn.silu(time_vec)

    mod = precise(time_path(t_index[0])[4], ada_w) + ada_b

    hidden = jnp.take(txt_table, ids, axis=0).astype(F32)
    kept = []
    blocks = txt_conv.shape[0]
    for b in range(blocks):
        hidden, saved = text_ahead(
            hidden, seg_ext, hot_ext, own_ext, txt_conv[b], txt_vec[b], txt_gain[b],
            txt_up[b], txt_hid[b], txt_down[b], "mp",
        )
        kept.append(saved)
    text = hidden[HALO : HALO + rows].astype(BF)

    mel = lax.dynamic_slice_in_dim(mel_pair, first, rows)
    x0 = dot(mel, emb_mel) + dot(text, emb_text) + emb_bias

    def to_channels(values):
        blocks_of = values.reshape(rows, shards, cols).transpose(1, 0, 2)
        return exchange(blocks_of, "mp").reshape(total, cols)

    def to_rows(values):
        return exchange(values.reshape(shards, rows, cols), "mp").transpose(1, 0, 2).reshape(rows, width)

    spread_in = spread(to_channels(x0.astype(BF)).astype(F32), starts, ends)
    real = spread(jnp.ones((total, 1), F32), starts, ends)
    pre_a = apply_conv(spread_in, block_diagonal(pos_conv[0], False), taps) + pos_bias[0]
    y_a = jnp.pad(
        jnp.where(real[GAP:-GAP] > 0, mish(pre_a), 0.0).astype(BF).astype(F32), ((GAP, GAP), (0, 0))
    )
    pre_b = apply_conv(y_a, block_diagonal(pos_conv[1], False), taps) + pos_bias[1]
    c_pos = to_rows(gather_back(mish(pre_b).astype(BF), starts, ends))
    x1 = x0 + c_pos.astype(F32)

    def modulate(state, mod_in, shift_part, scale_part):
        scale = expand(hot, mod_in[:, scale_part * width : (scale_part + 1) * width])
        shift = expand(hot, mod_in[:, shift_part * width : (shift_part + 1) * width])
        return layer_norm(state) * (1.0 + scale) + shift

    n1, n1_pull = jax.vjp(lambda s, m: modulate(s, m, 0, 1), x1, mod)
    n1 = n1.astype(BF)
    half = HEAD_DIM // 2
    inverse = jnp.exp(jnp.arange(0, HEAD_DIM, 2, dtype=F32) * (-math.log(10000.0) / HEAD_DIM))
    angles = position.astype(F32)[:, None] * jnp.tile(inverse, cols // HEAD_DIM)[None, :]
    cos, sin = jnp.cos(angles), jnp.sin(angles)
    cos_own = lax.dynamic_slice_in_dim(cos, first, rows)
    sin_own = lax.dynamic_slice_in_dim(sin, first, rows)
    projected = []
    for s in range(shards):
        for p in range(3):
            value = dot(n1, qkv_full[s, p]) + qkv_bias[s, p]
            if p < 2:
                even, odd = value[:, : cols // 2], value[:, cols // 2 :]
                value = jnp.concatenate(
                    [even * cos_own - odd * sin_own, odd * cos_own + even * sin_own], axis=1
                )
            projected.append(value.astype(BF))
    qkv = jnp.stack(projected).reshape(shards, 3, rows, cols)
    qkv = exchange(qkv, "mp")
    block = 256
    heads_of = segment[::block]
    tails_of = segment[block - 1 :: block]
    low_key = jnp.sum(jnp.where(heads_of[:, None] == clip_index, starts[None, :], 0), axis=1)
    high_key = jnp.sum(jnp.where(tails_of[:, None] == clip_index, ends[None, :], 0), axis=1)
    bounds = jnp.stack([low_key // rows, (high_key + rows - 1) // rows], axis=1).astype(jnp.int32)
    seg_rows = segment[:, None]
    seg_blocks = segment.reshape(shards, 1, rows)
    o, o_full, logs = attend(qkv, seg_rows, seg_blocks, bounds, block)
    o_rows = to_rows(o)

    def residual(state, mod_in, summed, bias, part):
        return state + expand(hot, mod_in[:, part * width : (part + 1) * width]) * (summed + bias)

    x2, att_pull = jax.vjp(
        lambda s, m, a, b: residual(s, m, a, b, 2), x1, mod, dot(o_rows, out_full), out_b
    )

    n2, n2_pull = jax.vjp(lambda s, m: modulate(s, m, 3, 4), x2, mod)
    n2 = n2.astype(BF)
    r, r_pull = jax.vjp(
        lambda v, b: jax.nn.gelu(v + b, approximate=True), dot(n2, w1_full), b1_full
    )
    r = r.astype(BF)
    out, ff_pull = jax.vjp(lambda s, m, a, b: residual(s, m, a, b, 5), x2, mod, dot(r, w2_full), ff_b2)
    result = lax.all_gather(out.astype(BF), "mp", tiled=True).astype(F32)

    grad = lax.dynamic_slice_in_dim(out_grad, first, rows).astype(F32)
    dx2, dmod_a, df, g_ff_b2 = ff_pull(grad)
    df = df.astype(BF)
    g_ff_w2 = dot(df, r, TN)
    dh, g_ff_b1 = r_pull(dot(df, w2_full, NT))
    g_ff_b1 = jnp.sum(dh.astype(BF).astype(F32), axis=0)
    dh = dh.astype(BF)
    g_ff_w1 = dot(n2, dh, TN)
    more, dmod_b = n2_pull(dot(dh, w1_full, NT))
    dx2 = dx2 + more

    def by_rank(matrix):
        return matrix.reshape(matrix.shape[0], shards, -1)

    def scatter(matrix):
        part = lax.psum_scatter(matrix.astype(BF), "dp", scatter_dimension=0, tiled=True)
        return lax.psum_scatter(part, "mp", scatter_dimension=1, tiled=True).astype(F32)

    ff_pair = jnp.concatenate([by_rank(g_ff_w1), by_rank(g_ff_w2)], axis=2)
    ff_pair = scatter(ff_pair.reshape(width, -1))
    ff_cols = ff_w1.shape[1]
    o_ff_w1, o_ff_w2 = ff_pair[:, :ff_cols], ff_pair[:, ff_cols:].T

    dx1, dmod_c, da, g_out_b = att_pull(dx2)
    da = da.astype(BF)
    g_out_w = dot(da, o_rows, TN)
    do = to_channels(dot(da, out_full, NT).astype(BF))
    dqkv = attend_back(qkv, o_full, logs, do, seg_rows, seg_blocks, cos, sin, bounds, block)
    dqkv = exchange(dqkv, "mp").transpose(2, 0, 1, 3).reshape(rows, 3 * width)
    g_qkv_w = dot(n1, dqkv, TN)
    g_qkv_b = jnp.sum(dqkv.astype(F32), axis=0).reshape(shards, 3, cols)
    w_all = qkv_full.transpose(2, 0, 1, 3).reshape(width, 3 * width)
    more, dmod_d = n1_pull(dot(dqkv, w_all, NT))
    dx1 = dx1 + more
    at_pair = jnp.concatenate([by_rank(g_qkv_w), by_rank(g_out_w)], axis=2)
    at_pair = scatter(at_pair.reshape(width, -1))
    g_qkv = at_pair[:, : 3 * cols].reshape(-1, 3, cols).transpose(1, 0, 2)
    o_qkv_w = jnp.concatenate([pair_merge(g_qkv[:2]), g_qkv[2:]], axis=0)
    o_out_w = at_pair[:, 3 * cols :].T

    dmod = dmod_a + dmod_b + dmod_c + dmod_d
    dmod_all = jnp.sum(
        lax.all_gather(lax.all_gather(dmod, "mp"), "dp"), axis=1
    ).reshape(groups * clips, -1)

    slope_b = gather_back(mish_slope(pre_b), starts, ends)
    dy_b = to_channels(dx1.astype(BF)).astype(F32) * slope_b
    g_pos_b = jnp.sum(dy_b, axis=0)
    dy_b = spread(dy_b.astype(BF).astype(F32), starts, ends)
    dy_a = apply_conv(dy_b, block_diagonal(pos_conv[1], True), taps) * mish_slope(pre_a)
    dy_a = jnp.where(real[GAP:-GAP] > 0, dy_a, 0.0)
    g_pos_a = jnp.sum(dy_a, axis=0)
    dy_a = jnp.pad(dy_a.astype(BF).astype(F32), ((GAP, GAP), (0, 0)))
    dc = gather_back(
        apply_conv(dy_a, block_diagonal(pos_conv[0], True), taps).astype(BF), starts, ends
    )
    dx0_full = dx1 + to_rows(dc).astype(F32)
    g_conv = jnp.concatenate(
        [conv_grad(spread_in, dy_a[GAP:-GAP], taps, group), conv_grad(y_a, dy_b[GAP:-GAP], taps, group)],
        axis=1,
    )
    g_conv = lax.psum_scatter(g_conv.astype(BF), "dp", scatter_dimension=0, tiled=True)
    o_pos_conv = g_conv.astype(F32).T.reshape(2, taps, group, -1)

    g_emb_bias = jnp.sum(dx0_full, axis=0)
    dx0 = dx0_full.astype(BF)
    mel_grad = lax.all_gather(dot(dx0, emb_mel, NT).astype(BF), "mp", tiled=True).astype(F32)
    g_emb = jnp.concatenate([dot(dx0, text, TN), dot(dx0, mel, TN)], axis=1)
    g_emb = lax.psum_scatter(g_emb.astype(BF), "dp", scatter_dimension=0, tiled=True)
    g_emb = lax.psum(g_emb, "mp").astype(F32)
    text_width = text.shape[1]
    o_emb_text, o_emb_mel = g_emb[:, :text_width].T, g_emb[:, text_width:].T

    dtext = jnp.pad(dot(dx0, emb_text, NT), ((HALO, HALO), (0, 0)))
    text_grads = [None] * blocks
    for b in reversed(range(blocks)):
        dtext, text_grads[b] = text_behind(kept[b], dtext, txt_up[b], txt_down[b], "mp")
    vocab = txt_table.shape[0]
    chosen = (ids[:, None] == jnp.arange(vocab, dtype=jnp.int32)[None, :]).astype(BF)
    g_table = dot(dtext, chosen, TN)

    def scatter_rows(matrix):
        part = lax.psum_scatter(matrix.astype(BF), "dp", scatter_dimension=0, tiled=True)
        return lax.psum_scatter(part, "mp", scatter_dimension=0, tiled=True).astype(F32)

    ups = scatter_rows(jnp.concatenate([text_grads[b][3] for b in range(blocks)], axis=1))
    downs = scatter_rows(
        jnp.concatenate([text_grads[b][5] for b in range(blocks)] + [g_table], axis=1)
    )
    hidden_width = txt_up.shape[2]
    o_up = ups.T.reshape(blocks, text_width, -1)
    o_down = downs[:, : blocks * hidden_width].T.reshape(blocks, hidden_width, -1)
    o_table = downs[:, blocks * hidden_width :].T

    def placed(values):
        full = jnp.zeros((shards,) + values.shape, F32)
        return lax.dynamic_update_slice_in_dim(full, values[None], rank, 0)

    g_pos_bias = placed(jnp.stack([g_pos_a, g_pos_b])).transpose(1, 0, 2).reshape(2, width)
    g_qkv_b = jnp.concatenate([pair_merge(g_qkv_b[:, :2]), g_qkv_b[:, 2:]], axis=1)
    g_qkv_b = g_qkv_b.transpose(1, 0, 2).reshape(3, width)
    small = [
        jnp.stack([g[0] for g in text_grads]), jnp.stack([g[1] for g in text_grads]),
        jnp.stack([g[2] for g in text_grads]), jnp.stack([g[4] for g in text_grads]),
        g_emb_bias, g_pos_bias, g_qkv_b, g_out_b, g_ff_b1, g_ff_b2,
    ]
    packed = lax.psum(jnp.concatenate([s.reshape(-1) for s in small]), ("dp", "mp"))
    unpacked, at = [], 0
    for s in small:
        unpacked.append(packed[at : at + s.size].reshape(s.shape))
        at += s.size
    both, crossed = place * shards + rank, rank * groups + place
    everyone = groups * shards

    def own(values, index, parts):
        piece = values.shape[-1] // parts
        return lax.dynamic_slice_in_dim(values, index * piece, piece, values.ndim - 1)

    sinusoid, pre_one, act_one, time_vec, act_two = time_path(all_steps)
    de = precise(dmod_all, ada_w, NT) * silu_slope(time_vec)
    dpre = precise(de, time_w2, NT) * silu_slope(pre_one)

    def outer(left, right):
        return lax.dot_general(left, own(right, place, groups), TN, precision=highest)

    return (
        result,
        mel_grad,
        o_table,
        own(unpacked[0], both, everyone),
        own(unpacked[1], both, everyone),
        own(unpacked[2], both, everyone),
        o_up,
        own(unpacked[3], both, everyone),
        o_down,
        o_emb_mel,
        o_emb_text,
        own(unpacked[4], place, groups),
        o_pos_conv,
        own(unpacked[5], crossed, everyone),
        outer(sinusoid, dpre),
        own(jnp.stack([jnp.sum(dpre, axis=0), jnp.sum(de, axis=0)]), place, groups),
        outer(act_one, de),
        outer(act_two, dmod_all),
        own(jnp.sum(dmod_all, axis=0), place, groups),
        o_qkv_w,
        own(unpacked[6], crossed, everyone),
        o_out_w,
        own(unpacked[7], place, groups),
        o_ff_w1,
        own(unpacked[8], crossed, everyone),
        o_ff_w2,
        own(unpacked[9], place, groups),
    )


def solution(mesh):
    both, crossed = ("dp", "mp"), ("mp", "dp")
    placed = (
        P("dp", None), P("dp"), P("dp", None), P("dp", None),
        P(), P(), P(), P(), P(), P(), P(), P(), P(), P(),
        P(None, None, None, "mp"), P(None, "mp"),
        P(), P(), P(), P(), P(),
        P(None, None, "mp"), P(None, "mp"), P("mp", None), P(),
        P(None, "mp"), P("mp"), P("mp", None), P(),
        P("dp", None),
    )
    given = (
        P("dp", None), P("dp", None),
        P(None, both), P(None, None, both), P(None, None, both), P(None, both),
        P(None, None, both), P(None, None, both), P(None, None, both),
        P(None, "dp"), P(None, "dp"), P("dp"),
        P(None, None, None, crossed), P(None, crossed),
        P(None, "dp"), P(None, "dp"), P(None, "dp"), P(None, "dp"), P("dp"),
        P(None, "dp", "mp"), P(None, crossed), P("mp", "dp"), P("dp"),
        P("dp", "mp"), P(crossed), P("mp", "dp"), P("dp"),
    )
    return jax.shard_map(local, mesh=mesh, in_specs=placed, out_specs=given, check_vma=False)
```

```python
from functools import partial
import math

import jax
import jax.numpy as jnp
from jax import lax
from jax.experimental import pallas as pl
from jax.experimental.pallas import tpu as pltpu
from jax.sharding import PartitionSpec as P

HEAD_DIM = 64
GAP = 16
HALO = 8
BF = jnp.bfloat16
F32 = jnp.float32
highest = lax.Precision.HIGHEST
NN = (((1,), (0,)), ((), ()))
NT = (((1,), (1,)), ((), ()))
TN = (((0,), (0,)), ((), ()))


def dot(left, right, dims=NN):
    return lax.dot_general(left.astype(BF), right.astype(BF), dims, preferred_element_type=F32)


def precise(left, right, dims=NN):
    one = lax.reduce_precision(left, 8, 7)
    two = lax.reduce_precision(left - one, 8, 7)
    three = left - one - two
    rows = left.shape[0]
    stacked = jnp.concatenate([one, two, three], axis=0).astype(BF)
    product = lax.dot_general(stacked, right, dims, preferred_element_type=F32)
    return product[:rows] + product[rows : 2 * rows] + product[2 * rows :]


@jax.custom_vjp
def expand(onehot, parts):
    return sum(onehot[:, c : c + 1] * parts[c : c + 1] for c in range(parts.shape[0]))


def expand_ahead(onehot, parts):
    return expand(onehot, parts), onehot


def expand_behind(onehot, grad):
    return None, jnp.dot(onehot.T, grad, precision=highest)


expand.defvjp(expand_ahead, expand_behind)


def silu_slope(values):
    sigmoid_val = jax.nn.sigmoid(values)
    return sigmoid_val * (1.0 + values * (1.0 - sigmoid_val))


def layer_norm(values):
    centred = values - jnp.mean(values, axis=-1, keepdims=True)
    variance = jnp.mean(centred * centred, axis=-1, keepdims=True)
    return centred * lax.rsqrt(variance + 1e-06)


def mish(values):
    grown = jnp.exp(jnp.minimum(values, 20.0))
    wide = grown * (grown + 2.0)
    return values * (wide / (wide + 2.0))


def mish_slope(values):
    grown = jnp.exp(jnp.minimum(values, 20.0))
    wide = grown * (grown + 2.0)
    under = 1.0 / (wide + 2.0)
    return wide * under + values * (4.0 * grown * (1.0 + grown) * under * under)


def sum_kernel(axis, size, x_ref, o_ref, slots, send_sems, recv_sems):
    me = lax.axis_index(axis)
    barrier = pltpu.get_barrier_semaphore()
    peers = [lax.rem(me + step, size) for step in range(1, size)]
    for peer in peers:
        pl.semaphore_signal(
            barrier, inc=1, device_id={axis: peer}, device_id_type=pl.DeviceIdType.MESH
        )
    pl.semaphore_wait(barrier, size - 1)
    for step, peer in enumerate(peers):
        pltpu.make_async_remote_copy(
            src_ref=x_ref,
            dst_ref=slots.at[me],
            send_sem=send_sems.at[step],
            recv_sem=recv_sems.at[me],
            device_id={axis: peer},
            device_id_type=pl.DeviceIdType.MESH,
        ).start()
    slots[me] = x_ref[...]
    for step, peer in enumerate(peers):
        copy = pltpu.make_async_remote_copy(
            src_ref=x_ref,
            dst_ref=slots.at[peer],
            send_sem=send_sems.at[step],
            recv_sem=recv_sems.at[peer],
            device_id={axis: peer},
            device_id_type=pl.DeviceIdType.MESH,
        )
        copy.wait_send()
        copy.wait_recv()
    total = slots[0]
    for device in range(1, size):
        total = total + slots[device]
    o_ref[...] = total


def small_sum(values, axis, name):
    size = lax.axis_size(axis)
    whole = pl.BlockSpec(memory_space=pltpu.VMEM)
    return pl.pallas_call(
        partial(sum_kernel, axis, size),
        out_shape=jax.ShapeDtypeStruct(values.shape, F32),
        in_specs=[whole],
        out_specs=whole,
        scratch_shapes=[
            pltpu.VMEM((size,) + values.shape, F32),
            pltpu.SemaphoreType.DMA((size - 1,)),
            pltpu.SemaphoreType.DMA((size,)),
        ],
        compiler_params=pltpu.CompilerParams(
            collective_id=name, has_side_effects=True, vmem_limit_bytes=16 << 20
        ),
    )(values)


def conv_norm(hidden, segment, conv, vec, gain):
    taps = conv.shape[0]
    reach = taps // 2
    rows = hidden.shape[0]
    padded = jnp.pad(hidden, ((reach, reach), (0, 0)))
    seg_padded = jnp.pad(segment, (reach, reach), constant_values=-1)
    mixture = vec[0]
    for tap in range(taps):
        keep = (seg_padded[tap : tap + rows] == segment) & (segment >= 0)
        mixture = mixture + conv[tap] * jnp.where(keep[:, None], padded[tap : tap + rows], 0.0)
    return layer_norm(mixture) * gain + vec[1]


def activate(pre, bias):
    return jax.nn.gelu(pre + bias, approximate=False)


def clip_squares(own, active):
    return jnp.dot(own.T, active * active, precision=highest)


def respond(active, squares, onehot, scale, shift):
    norms = jnp.sqrt(jnp.maximum(squares, 1.0))
    ratio = norms / (jnp.mean(norms, axis=-1, keepdims=True) + 1e-06)
    return scale * (active * expand(onehot, ratio)) + shift + active


def text_ahead(hidden, segment, onehot, own, conv, vec, gain, up, hid, down):
    normed, norm_pull = jax.vjp(
        lambda h, c, v, g: conv_norm(h, segment, c, v, g), hidden, conv, vec, gain
    )
    normed = normed.astype(BF)
    active, act_pull = jax.vjp(activate, dot(normed, up), hid[0])
    squares, square_pull = jax.vjp(lambda a: clip_squares(own, a), active)
    squares = small_sum(squares, "mp", 1)
    grown, respond_pull = jax.vjp(
        lambda a, s, g, b: respond(a, s, onehot, g, b), active, squares, hid[1], hid[2]
    )
    grown = grown.astype(BF)
    result = hidden + dot(grown, down) + vec[2]
    return result, (norm_pull, normed, act_pull, square_pull, respond_pull, grown)


def text_behind(kept, grad, up, down, extra):
    norm_pull, normed, act_pull, square_pull, respond_pull, grown = kept
    grad_low = grad.astype(BF)
    g_out = jnp.sum(grad, axis=0)
    g_down = dot(grad_low, grown, TN)
    grad_active, grad_squares, g_scale, g_shift = respond_pull(dot(grad_low, down, NT))
    if extra is None:
        grad_squares = small_sum(grad_squares, "mp", 1)
    else:
        joined = small_sum(jnp.concatenate([grad_squares, extra], axis=1), "mp", 2)
        grad_squares, extra = joined[:, : grad_squares.shape[1]], joined[:, grad_squares.shape[1] :]
    grad_active = grad_active + square_pull(grad_squares)[0]
    grad_pre, g_bias = act_pull(grad_active)
    pre_low = grad_pre.astype(BF)
    g_up = dot(pre_low, normed, TN)
    grad_hidden, g_conv, g_vec, g_gain = norm_pull(dot(pre_low, up, NT))
    g_vec = g_vec.at[2].add(g_out)
    return (
        grad + grad_hidden,
        (g_conv, g_vec, g_gain, g_up, jnp.stack([g_bias, g_scale, g_shift]), g_down),
        extra,
    )


def spread(values, starts, ends):
    rows = values.shape[0]
    clips = starts.shape[0]
    at = jnp.arange(rows, dtype=jnp.int32)
    total = rows + GAP * clips + 2 * GAP
    out = None
    for c in range(clips):
        keep = (at >= starts[c]) & (at < ends[c])
        part = jnp.where(keep[:, None], values, 0)
        lead = GAP + GAP * c
        part = jnp.pad(part, ((lead, total - lead - rows), (0, 0)))
        out = part if out is None else out + part
    return out


def gather_back(values, starts, ends):
    clips = starts.shape[0]
    rows = values.shape[0] - GAP * clips
    at = jnp.arange(rows, dtype=jnp.int32)
    out = None
    for c in range(clips):
        keep = (at >= starts[c]) & (at < ends[c])
        part = jnp.where(keep[:, None], values[GAP * c : GAP * c + rows], 0)
        out = part if out is None else out + part
    return out


def conv_kernel(taps, turned, x_ref, w_ref, o_ref, full_ref):
    rows, width = o_ref.shape
    group = w_ref.shape[1]
    first = GAP - taps // 2

    @pl.when(pl.program_id(0) == 0)
    def _():
        lane = lax.broadcasted_iota(jnp.int32, (group, width), 1) // group
        for k in range(taps):
            tap = w_ref[taps - 1 - k if turned else k]
            for g in range(width // group):
                piece = jnp.where(lane == g, tap, jnp.zeros_like(tap))
                if turned:
                    full_ref[g * group : (g + 1) * group, k * width : (k + 1) * width] = piece
                else:
                    full_ref[k * width + g * group : k * width + (g + 1) * group, :] = piece

    columns = [x_ref[first + k : first + k + rows, :].astype(BF) for k in range(taps)]
    o_ref[...] = lax.dot_general(
        jnp.concatenate(columns, axis=1),
        full_ref[...],
        NT if turned else NN,
        preferred_element_type=F32,
    )


def conv_chunk(rows):
    for size in (528, 352, 256, 128, 64, 32, 16):
        if rows % size == 0:
            return size
    return rows


def apply_conv(spread_rows, weight, turned):
    rows = spread_rows.shape[0] - 2 * GAP
    width = spread_rows.shape[1]
    taps, group = weight.shape[:2]
    chunk = conv_chunk(rows)
    return pl.pallas_call(
        partial(conv_kernel, taps, turned),
        out_shape=jax.ShapeDtypeStruct((rows, width), F32),
        grid=(rows // chunk,),
        in_specs=[
            pl.BlockSpec((pl.Element(chunk + 2 * GAP), pl.Element(width)), lambda i: (i * chunk, 0)),
            pl.BlockSpec(weight.shape, lambda i: (0, 0, 0), pipeline_mode=pl.Buffered(1)),
        ],
        out_specs=pl.BlockSpec((chunk, width), lambda i: (i, 0)),
        scratch_shapes=[
            pltpu.VMEM((width, taps * width) if turned else (taps * width, width), BF)
        ],
        compiler_params=pltpu.CompilerParams(vmem_limit_bytes=48 << 20),
        cost_estimate=pl.CostEstimate(
            flops=2 * rows * taps * width * width, bytes_accessed=8 << 20, transcendentals=0
        ),
    )(spread_rows, weight)


def conv_grad_kernel(taps, group, x_ref, g_ref, o_ref):
    rows, width = g_ref.shape
    first = GAP - taps // 2
    turned = g_ref[...].T.astype(BF)

    @pl.when(pl.program_id(0) == 0)
    def _():
        o_ref[...] = jnp.zeros_like(o_ref)

    for k in range(taps):
        window = x_ref[first + k : first + k + rows, :].astype(BF)
        product = jnp.dot(turned, window, preferred_element_type=F32)
        for g in range(width // group):
            own = slice(g * group, (g + 1) * group)
            o_ref[own, k * group : (k + 1) * group] += product[own, own]


def conv_grad(spread_rows, grads, taps, group):
    rows, width = grads.shape
    chunk = conv_chunk(rows)
    return pl.pallas_call(
        partial(conv_grad_kernel, taps, group),
        out_shape=jax.ShapeDtypeStruct((width, taps * group), F32),
        grid=(rows // chunk,),
        in_specs=[
            pl.BlockSpec((pl.Element(chunk + 2 * GAP), pl.Element(width)), lambda i: (i * chunk, 0)),
            pl.BlockSpec((chunk, width), lambda i: (i, 0)),
        ],
        out_specs=pl.BlockSpec((width, taps * group), lambda i: (0, 0)),
        compiler_params=pltpu.CompilerParams(vmem_limit_bytes=48 << 20),
        cost_estimate=pl.CostEstimate(
            flops=2 * rows * taps * width * width, bytes_accessed=8 << 20, transcendentals=0
        ),
    )(spread_rows, grads)


def pair_split(columns):
    lead = columns.shape[:-1]
    pairs = columns.reshape(*lead, columns.shape[-1] // 2, 2)
    return jnp.concatenate([pairs[..., 0], pairs[..., 1]], axis=-1)


def pair_merge(columns):
    half = columns.shape[-1] // 2
    return jnp.stack([columns[..., :half], columns[..., half:]], axis=-1).reshape(columns.shape)


def head_masks(width):
    heads = width // HEAD_DIM
    lane = lax.broadcasted_iota(jnp.int32, (1, width), 1)
    half = HEAD_DIM // 2
    paired = [((lane % (width // 2)) // half) == h for h in range(heads)]
    plain = [(lane // HEAD_DIM) == h for h in range(heads)]
    return heads, paired, plain


def attend_kernel(bounds, q_ref, k_ref, v_ref, sq_ref, sk_ref, o_ref, full_ref, lse_ref):
    i = pl.program_id(0)
    q = q_ref[...]
    rows, width = q.shape
    heads, paired, plain = head_masks(width)
    scale = HEAD_DIM**-0.5
    q_heads = [jnp.where(paired[h], q, jnp.zeros_like(q)) for h in range(heads)]
    sq = sq_ref[...]

    def step(kb, carry):
        tops, sums, acc = carry
        k, v = k_ref[kb], v_ref[kb]
        same = sq == sk_ref[kb]
        new_tops, new_sums = [], []
        decay, extra = None, None
        for h in range(heads):
            scores = lax.dot_general(q_heads[h], k, NT, preferred_element_type=F32) * scale
            scores = jnp.where(same, scores, -1e30)
            top = jnp.maximum(tops[h], jnp.max(scores, axis=-1, keepdims=True))
            fade = jnp.exp(tops[h] - top)
            weight = jnp.exp(scores - top)
            new_tops.append(top)
            new_sums.append(fade * sums[h] + jnp.sum(weight, axis=-1, keepdims=True))
            v_head = jnp.where(plain[h], v, jnp.zeros_like(v))
            part = jnp.dot(weight.astype(BF), v_head, preferred_element_type=F32)
            extra = part if extra is None else extra + part
            decay = fade * jnp.ones((1, width), F32) if h == 0 else jnp.where(plain[h], fade, decay)
        return tuple(new_tops), tuple(new_sums), acc * decay + extra

    start = (
        tuple(jnp.full((rows, 1), -1e30, F32) for _ in range(heads)),
        tuple(jnp.zeros((rows, 1), F32) for _ in range(heads)),
        jnp.zeros((rows, width), F32),
    )
    tops, sums, acc = lax.fori_loop(bounds[i, 0], bounds[i, 1], step, start)
    lane = lax.broadcasted_iota(jnp.int32, (1, lse_ref.shape[1]), 1)
    share = jnp.ones((rows, width), F32)
    logs = jnp.zeros((rows, lse_ref.shape[1]), F32)
    for h in range(heads):
        share = jnp.where(plain[h], 1.0 / sums[h], share)
        logs = jnp.where(lane == h, tops[h] + jnp.log(sums[h]), logs)
    full = acc * share
    full_ref[...] = full
    o_ref[...] = full.astype(BF)
    lse_ref[...] = logs


def attend(qkv, seg_rows, seg_blocks, bounds, block):
    shards, _, rows, width = qkv.shape
    total = shards * rows
    per = rows // block
    grid_spec = pltpu.PrefetchScalarGridSpec(
        num_scalar_prefetch=1,
        grid=(total // block,),
        in_specs=[
            pl.BlockSpec((None, None, block, width), lambda i, b: (i // per, 0, i % per, 0)),
            pl.BlockSpec((shards, None, rows, width), lambda i, b: (0, 1, 0, 0)),
            pl.BlockSpec((shards, None, rows, width), lambda i, b: (0, 2, 0, 0)),
            pl.BlockSpec((block, 1), lambda i, b: (i, 0)),
            pl.BlockSpec((shards, 1, rows), lambda i, b: (0, 0, 0)),
        ],
        out_specs=[
            pl.BlockSpec((block, width), lambda i, b: (i, 0)),
            pl.BlockSpec((block, width), lambda i, b: (i, 0)),
            pl.BlockSpec((block, 128), lambda i, b: (i, 0)),
        ],
    )
    return pl.pallas_call(
        attend_kernel,
        out_shape=[
            jax.ShapeDtypeStruct((total, width), BF),
            jax.ShapeDtypeStruct((total, width), F32),
            jax.ShapeDtypeStruct((total, 128), F32),
        ],
        grid_spec=grid_spec,
        compiler_params=pltpu.CompilerParams(vmem_limit_bytes=48 << 20),
        cost_estimate=pl.CostEstimate(
            flops=8 * total * total * width, bytes_accessed=8 << 20, transcendentals=0
        ),
    )(bounds, qkv, qkv, qkv, seg_rows, seg_blocks)


def unrotate(values, cos, sin):
    half = values.shape[1] // 2
    even, odd = values[:, :half], values[:, half:]
    return jnp.concatenate([even * cos + odd * sin, odd * cos - even * sin], axis=1)


def attend_back_kernel(
    bounds, q_ref, k_ref, v_ref, full_ref, lse_ref, do_ref, sq_ref, sk_ref, cos_ref, sin_ref,
    out_ref, dk_ref, dv_ref,
):
    i = pl.program_id(0)
    q, do = q_ref[...], do_ref[...]
    rows, width = q.shape
    shards, _, shard_rows, _ = out_ref.shape
    per = shard_rows // rows
    heads, paired, plain = head_masks(width)
    scale = HEAD_DIM**-0.5

    @pl.when(i == 0)
    def _():
        dk_ref[...] = jnp.zeros_like(dk_ref)
        dv_ref[...] = jnp.zeros_like(dv_ref)

    zero = jnp.zeros_like(q)
    q_heads = [jnp.where(paired[h], q, zero) for h in range(heads)]
    do_heads = [jnp.where(plain[h], do, zero) for h in range(heads)]
    product = do.astype(F32) * full_ref[...]
    deltas = [jnp.sum(jnp.where(plain[h], product, 0.0), axis=-1, keepdims=True) for h in range(heads)]
    logs = [lse_ref[:, h : h + 1] for h in range(heads)]
    sq = sq_ref[...]

    def step(kb, dq):
        k, v = k_ref[kb], v_ref[kb]
        same = sq == sk_ref[kb]
        dk, dv = dk_ref[kb], dv_ref[kb]
        for h in range(heads):
            scores = lax.dot_general(q_heads[h], k, NT, preferred_element_type=F32) * scale
            weight = jnp.where(same, jnp.exp(scores - logs[h]), 0.0)
            dp = lax.dot_general(do_heads[h], v, NT, preferred_element_type=F32)
            ds = (weight * (dp - deltas[h]) * scale).astype(BF)
            dv = dv + lax.dot_general(weight.astype(BF), do_heads[h], TN, preferred_element_type=F32)
            dk = dk + lax.dot_general(ds, q_heads[h], TN, preferred_element_type=F32)
            k_head = jnp.where(paired[h], k, jnp.zeros_like(k))
            dq = dq + jnp.dot(ds, k_head, preferred_element_type=F32)
        dk_ref[kb] = dk
        dv_ref[kb] = dv
        return dq

    dq = lax.fori_loop(bounds[i, 0], bounds[i, 1], step, jnp.zeros((rows, width), F32))
    here = pl.ds(pl.multiple_of(i * rows, rows), rows)
    inside = pl.ds(pl.multiple_of((i % per) * rows, rows), rows)
    out_ref[i // per, 0, inside, :] = unrotate(dq, cos_ref[here, :], sin_ref[here, :]).astype(BF)

    @pl.when(i == pl.num_programs(0) - 1)
    def _():
        for s in range(shards):
            own = slice(s * shard_rows, (s + 1) * shard_rows)
            out_ref[s, 1] = unrotate(dk_ref[s], cos_ref[own, :], sin_ref[own, :]).astype(BF)
            out_ref[s, 2] = dv_ref[s].astype(BF)


def attend_back(qkv, full, logs, grads, seg_rows, seg_blocks, cos, sin, bounds, block):
    shards, _, rows, width = qkv.shape
    total = shards * rows
    per = rows // block
    grid_spec = pltpu.PrefetchScalarGridSpec(
        num_scalar_prefetch=1,
        grid=(total // block,),
        in_specs=[
            pl.BlockSpec((None, None, block, width), lambda i, b: (i // per, 0, i % per, 0)),
            pl.BlockSpec((shards, None, rows, width), lambda i, b: (0, 1, 0, 0)),
            pl.BlockSpec((shards, None, rows, width), lambda i, b: (0, 2, 0, 0)),
            pl.BlockSpec((block, width), lambda i, b: (i, 0)),
            pl.BlockSpec((block, 128), lambda i, b: (i, 0)),
            pl.BlockSpec((block, width), lambda i, b: (i, 0)),
            pl.BlockSpec((block, 1), lambda i, b: (i, 0)),
            pl.BlockSpec((shards, 1, rows), lambda i, b: (0, 0, 0)),
            pl.BlockSpec((total, width // 2), lambda i, b: (0, 0)),
            pl.BlockSpec((total, width // 2), lambda i, b: (0, 0)),
        ],
        out_specs=pl.BlockSpec((shards, 3, rows, width), lambda i, b: (0, 0, 0, 0)),
        scratch_shapes=[
            pltpu.VMEM((shards, rows, width), F32),
            pltpu.VMEM((shards, rows, width), F32),
        ],
    )
    return pl.pallas_call(
        attend_back_kernel,
        out_shape=jax.ShapeDtypeStruct((shards, 3, rows, width), BF),
        grid_spec=grid_spec,
        compiler_params=pltpu.CompilerParams(vmem_limit_bytes=48 << 20),
        cost_estimate=pl.CostEstimate(
            flops=20 * total * total * width, bytes_accessed=16 << 20, transcendentals=0
        ),
    )(bounds, qkv, qkv, qkv, full, logs, grads, seg_rows, seg_blocks, cos, sin)


def exchange(values, axis):
    return lax.all_to_all(values, axis, 0, 0)


def local(
    mel_pair, text_ids, clip_lengths, t_index,
    txt_table, txt_conv, txt_vec, txt_gain, txt_up, txt_hid, txt_down,
    emb_mel, emb_text, emb_bias, pos_conv, pos_bias,
    time_w1, time_bias, time_w2, ada_w, ada_b,
    qkv_w, qkv_b, out_w, out_b, ff_w1, ff_b1, ff_w2, ff_b2, out_grad,
):
    total = mel_pair.shape[0]
    width = emb_mel.shape[1]
    shards, groups = lax.axis_size("mp"), lax.axis_size("dp")
    rank, place = lax.axis_index("mp"), lax.axis_index("dp")
    rows = total // shards
    cols = width // shards
    clips = clip_lengths.shape[1]
    first = rank * rows
    taps = pos_conv.shape[1]
    group = pos_conv.shape[2]

    def spread_slice(weight, axis):
        piece = weight.shape[axis] // groups
        return lax.dynamic_slice_in_dim(weight, place * piece, piece, axis)

    def to_all(piece, axis_name="mp"):
        size = lax.axis_size(axis_name)
        return lax.all_to_all(jnp.broadcast_to(piece[None], (size,) + piece.shape), axis_name, 0, 0)

    def gather(piece, axis):
        return lax.all_gather(to_all(piece), "dp", axis=axis, tiled=True)

    qkv_piece = spread_slice(qkv_w, 1)
    qkv_piece = jnp.concatenate([pair_split(qkv_piece[:2]), qkv_piece[2:]], axis=0)
    qkv_full = gather(qkv_piece, 2)
    out_full = gather(spread_slice(out_w, 0), 1).reshape(width, width)
    w1_piece = to_all(spread_slice(ff_w1, 0)).transpose(1, 0, 2)
    w1_full = lax.all_gather(w1_piece.reshape(w1_piece.shape[0], -1), "dp", axis=0, tiled=True)
    w2_full = gather(spread_slice(ff_w2, 0), 1).reshape(-1, width)
    small = jnp.concatenate([pair_split(qkv_b[:2]), qkv_b[2:]], axis=0)
    small = jnp.concatenate([small, ff_b1.reshape(-1, cols)], axis=0)
    small = to_all(small)
    qkv_bias = small[:, :3]
    b1_full = small[:, 3:].reshape(-1)
    all_steps = lax.all_gather(t_index, "dp", tiled=True).reshape(-1)

    lengths = clip_lengths[0]
    clip_index = jnp.arange(clips, dtype=jnp.int32)
    ends = jnp.sum(jnp.where(clip_index[:, None] >= clip_index[None, :], lengths[None, :], 0), axis=1)
    starts = ends - lengths
    frames = jnp.arange(total, dtype=jnp.int32)
    member = (frames[:, None] >= starts[None, :]) & (frames[:, None] < ends[None, :])
    segment = jnp.sum(member * clip_index[None, :], axis=1).astype(jnp.int32)
    position = frames - jnp.sum(member * starts[None, :], axis=1)
    ext = rows + 2 * HALO
    ids = lax.dynamic_slice_in_dim(jnp.pad(text_ids, (HALO, HALO)), first, ext)
    seg_ext = lax.dynamic_slice_in_dim(jnp.pad(segment, (HALO, HALO), constant_values=-1), first, ext)
    hot_ext = (seg_ext[:, None] == clip_index[None, :]).astype(F32)
    ext_index = jnp.arange(ext, dtype=jnp.int32)
    inside = (ext_index >= HALO) & (ext_index < HALO + rows)
    own_ext = jnp.where(inside[:, None], hot_ext, 0.0)
    hot = hot_ext[HALO : HALO + rows]

    def time_path(steps):
        half = time_w1.shape[0] // 2
        frequency = jnp.exp(jnp.arange(half, dtype=F32) * (-math.log(10000.0) / (half - 1)))
        angles = steps.astype(F32)[:, None] * frequency[None, :]
        sinusoid = jnp.concatenate([jnp.sin(angles), jnp.cos(angles)], axis=-1)
        pre_one = precise(sinusoid, time_w1) + time_bias[0]
        act_one = jax.nn.silu(pre_one)
        time_vec = precise(act_one, time_w2) + time_bias[1]
        return sinusoid, pre_one, act_one, time_vec, jax.nn.silu(time_vec)

    mod = precise(time_path(t_index[0])[4], ada_w) + ada_b

    hidden = jnp.take(txt_table, ids, axis=0).astype(F32)
    kept = []
    blocks = txt_conv.shape[0]
    for b in range(blocks):
        hidden, saved = text_ahead(
            hidden, seg_ext, hot_ext, own_ext, txt_conv[b], txt_vec[b], txt_gain[b],
            txt_up[b], txt_hid[b], txt_down[b],
        )
        kept.append(saved)
    text = hidden[HALO : HALO + rows].astype(BF)

    mel = lax.dynamic_slice_in_dim(mel_pair, first, rows)
    x0 = dot(mel, emb_mel) + dot(text, emb_text) + emb_bias

    def to_channels(values):
        blocks_of = values.reshape(rows, shards, cols).transpose(1, 0, 2)
        return exchange(blocks_of, "mp").reshape(total, cols)

    def to_rows(values):
        return exchange(values.reshape(shards, rows, cols), "mp").transpose(1, 0, 2).reshape(rows, width)

    spread_in = spread(to_channels(x0.astype(BF)).astype(F32), starts, ends)
    real = spread(jnp.ones((total, 1), F32), starts, ends)
    pre_a = apply_conv(spread_in, pos_conv[0], False) + pos_bias[0]
    y_a = jnp.pad(
        jnp.where(real[GAP:-GAP] > 0, mish(pre_a), 0.0).astype(BF).astype(F32), ((GAP, GAP), (0, 0))
    )
    pre_b = apply_conv(y_a, pos_conv[1], False) + pos_bias[1]
    c_pos = to_rows(gather_back(mish(pre_b).astype(BF), starts, ends))
    x1 = x0 + c_pos.astype(F32)

    def modulate(state, mod_in, shift_part, scale_part):
        scale = expand(hot, mod_in[:, scale_part * width : (scale_part + 1) * width])
        shift = expand(hot, mod_in[:, shift_part * width : (shift_part + 1) * width])
        return layer_norm(state) * (1.0 + scale) + shift

    n1, n1_pull = jax.vjp(lambda s, m: modulate(s, m, 0, 1), x1, mod)
    n1 = n1.astype(BF)
    half = HEAD_DIM // 2
    inverse = jnp.exp(jnp.arange(0, HEAD_DIM, 2, dtype=F32) * (-math.log(10000.0) / HEAD_DIM))
    angles = position.astype(F32)[:, None] * jnp.tile(inverse, cols // HEAD_DIM)[None, :]
    cos, sin = jnp.cos(angles), jnp.sin(angles)
    cos_own = lax.dynamic_slice_in_dim(cos, first, rows)
    sin_own = lax.dynamic_slice_in_dim(sin, first, rows)
    projected = []
    for s in range(shards):
        for p in range(3):
            value = dot(n1, qkv_full[s, p]) + qkv_bias[s, p]
            if p < 2:
                even, odd = value[:, : cols // 2], value[:, cols // 2 :]
                value = jnp.concatenate(
                    [even * cos_own - odd * sin_own, odd * cos_own + even * sin_own], axis=1
                )
            projected.append(value.astype(BF))
    qkv = jnp.stack(projected).reshape(shards, 3, rows, cols)
    qkv = exchange(qkv, "mp")
    block = 256
    heads_of = segment[::block]
    tails_of = segment[block - 1 :: block]
    low_key = jnp.sum(jnp.where(heads_of[:, None] == clip_index, starts[None, :], 0), axis=1)
    high_key = jnp.sum(jnp.where(tails_of[:, None] == clip_index, ends[None, :], 0), axis=1)
    bounds = jnp.stack([low_key // rows, (high_key + rows - 1) // rows], axis=1).astype(jnp.int32)
    seg_rows = segment[:, None]
    seg_blocks = segment.reshape(shards, 1, rows)
    o, o_full, logs = attend(qkv, seg_rows, seg_blocks, bounds, block)
    o_rows = to_rows(o)

    def residual(state, mod_in, summed, bias, part):
        return state + expand(hot, mod_in[:, part * width : (part + 1) * width]) * (summed + bias)

    x2, att_pull = jax.vjp(
        lambda s, m, a, b: residual(s, m, a, b, 2), x1, mod, dot(o_rows, out_full), out_b
    )

    n2, n2_pull = jax.vjp(lambda s, m: modulate(s, m, 3, 4), x2, mod)
    n2 = n2.astype(BF)
    r, r_pull = jax.vjp(
        lambda v, b: jax.nn.gelu(v + b, approximate=True), dot(n2, w1_full), b1_full
    )
    r = r.astype(BF)
    out, ff_pull = jax.vjp(lambda s, m, a, b: residual(s, m, a, b, 5), x2, mod, dot(r, w2_full), ff_b2)
    result = to_all(out.astype(BF)).reshape(total, width).astype(F32)

    grad = lax.dynamic_slice_in_dim(out_grad, first, rows).astype(F32)
    dx2, dmod_a, df, g_ff_b2 = ff_pull(grad)
    df = df.astype(BF)
    g_ff_w2 = dot(df, r, TN)
    dh, g_ff_b1 = r_pull(dot(df, w2_full, NT))
    g_ff_b1 = jnp.sum(dh.astype(BF).astype(F32), axis=0)
    dh = dh.astype(BF)
    g_ff_w1 = dot(n2, dh, TN)
    more, dmod_b = n2_pull(dot(dh, w1_full, NT))
    dx2 = dx2 + more

    def send_dp(matrix):
        parts = matrix.astype(BF).reshape(groups, matrix.shape[0] // groups, matrix.shape[1])
        return lax.all_to_all(parts, "dp", 0, 0)

    def total_of(received):
        return jnp.sum(received.astype(F32), axis=0)

    def by_rank(matrix):
        return matrix.reshape(matrix.shape[0], shards, -1).transpose(1, 0, 2)

    def send_mp(parts):
        return lax.all_to_all(parts.astype(BF), "mp", 0, 0)

    sent_w1, sent_w2 = send_dp(g_ff_w1), send_dp(g_ff_w2)

    dx1, dmod_c, da, g_out_b = att_pull(dx2)
    da = da.astype(BF)
    g_out_w = dot(da, o_rows, TN)
    do = to_channels(dot(da, out_full, NT).astype(BF))
    dqkv = attend_back(qkv, o_full, logs, do, seg_rows, seg_blocks, cos, sin, bounds, block)
    dqkv = exchange(dqkv, "mp").transpose(2, 0, 1, 3).reshape(rows, 3 * width)
    g_qkv_w = dot(n1, dqkv, TN)
    g_qkv_b = jnp.sum(dqkv.astype(F32), axis=0).reshape(shards, 3, cols)
    w_all = qkv_full.transpose(2, 0, 1, 3).reshape(width, 3 * width)
    more, dmod_d = n1_pull(dot(dqkv, w_all, NT))
    dx1 = dx1 + more
    sent_w1, sent_w2, dx1 = lax.optimization_barrier((sent_w1, sent_w2, dx1))
    ff_pair = jnp.concatenate([by_rank(total_of(sent_w1)), by_rank(total_of(sent_w2))], axis=2)
    ff_pair = send_mp(ff_pair)
    sent_qkv, sent_out = send_dp(g_qkv_w), send_dp(g_out_w)

    dmod = dmod_a + dmod_b + dmod_c + dmod_d

    slope_b = gather_back(mish_slope(pre_b), starts, ends)
    dy_b = to_channels(dx1.astype(BF)).astype(F32) * slope_b
    g_pos_b = jnp.sum(dy_b, axis=0)
    dy_b = spread(dy_b.astype(BF).astype(F32), starts, ends)
    dy_a = apply_conv(dy_b, pos_conv[1], True) * mish_slope(pre_a)
    dy_a = jnp.where(real[GAP:-GAP] > 0, dy_a, 0.0)
    g_pos_a = jnp.sum(dy_a, axis=0)
    dy_a = jnp.pad(dy_a.astype(BF).astype(F32), ((GAP, GAP), (0, 0)))
    dc = gather_back(
        apply_conv(dy_a, pos_conv[0], True).astype(BF), starts, ends
    )
    dx0_full = dx1 + to_rows(dc).astype(F32)
    g_conv = jnp.concatenate(
        [conv_grad(spread_in, dy_a[GAP:-GAP], taps, group), conv_grad(y_a, dy_b[GAP:-GAP], taps, group)],
        axis=1,
    )
    sent_qkv, sent_out, ff_pair, dx0_full = lax.optimization_barrier(
        (sent_qkv, sent_out, ff_pair, dx0_full)
    )
    ff_pair = total_of(ff_pair)
    ff_cols = ff_w1.shape[1]
    o_ff_w1, o_ff_w2 = ff_pair[:, :ff_cols], ff_pair[:, ff_cols:].T
    at_pair = jnp.concatenate([by_rank(total_of(sent_qkv)), by_rank(total_of(sent_out))], axis=2)
    at_pair = send_mp(at_pair)
    sent_conv = send_dp(g_conv)

    g_emb_bias = jnp.sum(dx0_full, axis=0)
    dx0 = dx0_full.astype(BF)
    mel_grad = to_all(dot(dx0, emb_mel, NT).astype(BF)).reshape(total, -1).astype(F32)
    g_emb = jnp.concatenate([dot(dx0, text, TN), dot(dx0, mel, TN)], axis=1)
    sent_emb = send_dp(g_emb)
    text_width = text.shape[1]

    dtext = jnp.pad(dot(dx0, emb_text, NT), ((HALO, HALO), (0, 0)))
    text_grads = [None] * blocks
    extra = dmod
    sent_up, sent_down = [None] * blocks, [None] * blocks
    for b in reversed(range(blocks)):
        dtext, text_grads[b], summed = text_behind(kept[b], dtext, txt_up[b], txt_down[b], extra)
        if extra is not None:
            dmod_all = lax.all_gather(summed, "dp", tiled=True)
        extra = None
        sent_up[b], sent_down[b] = send_dp(text_grads[b][3]), send_dp(text_grads[b][5])
        if b == blocks - 1:
            at_pair, sent_conv, sent_emb, dtext = lax.optimization_barrier(
                (at_pair, sent_conv, sent_emb, dtext)
            )
            at_pair = total_of(at_pair)
            g_emb = total_of(to_all(total_of(sent_emb).astype(BF)))
    g_qkv = at_pair[:, : 3 * cols].reshape(-1, 3, cols).transpose(1, 0, 2)
    o_qkv_w = jnp.concatenate([pair_merge(g_qkv[:2]), g_qkv[2:]], axis=0)
    o_out_w = at_pair[:, 3 * cols :].T
    o_pos_conv = total_of(sent_conv).T.reshape(2, taps, group, -1)
    o_emb_text, o_emb_mel = g_emb[:, :text_width].T, g_emb[:, text_width:].T
    vocab = txt_table.shape[0]
    wide = -(-vocab // 128) * 128
    chosen = (ids[:, None] == jnp.arange(wide, dtype=jnp.int32)[None, :]).astype(BF)
    sent_table = send_dp(dot(dtext, chosen, TN))

    def rows_by_rank(matrix):
        return matrix.reshape(shards, matrix.shape[0] // shards, -1)

    ups = send_mp(rows_by_rank(jnp.concatenate([total_of(v) for v in sent_up], axis=1)))
    downs = send_mp(
        rows_by_rank(jnp.concatenate([total_of(v) for v in sent_down + [sent_table]], axis=1))
    )
    hidden_width = txt_up.shape[2]
    downs = total_of(downs)
    o_up = total_of(ups).T.reshape(blocks, text_width, -1)
    o_down = downs[:, : blocks * hidden_width].T.reshape(blocks, hidden_width, -1)
    o_table = downs[:, blocks * hidden_width :].T[:vocab]

    def placed(values):
        full = jnp.zeros((shards,) + values.shape, F32)
        return lax.dynamic_update_slice_in_dim(full, values[None], rank, 0)

    g_pos_bias = placed(jnp.stack([g_pos_a, g_pos_b])).transpose(1, 0, 2).reshape(2, width)
    g_qkv_b = jnp.concatenate([pair_merge(g_qkv_b[:, :2]), g_qkv_b[:, 2:]], axis=1)
    g_qkv_b = g_qkv_b.transpose(1, 0, 2).reshape(3, width)
    small = [
        jnp.stack([g[0] for g in text_grads]), jnp.stack([g[1] for g in text_grads]),
        jnp.stack([g[2] for g in text_grads]), jnp.stack([g[4] for g in text_grads]),
        g_emb_bias, g_pos_bias, g_qkv_b, g_out_b, g_ff_b1, g_ff_b2,
    ]
    packed = jnp.concatenate([s.reshape(-1) for s in small]).reshape(8, -1)
    packed = small_sum(small_sum(packed, "mp", 3), "dp", 4).reshape(-1)
    unpacked, at = [], 0
    for s in small:
        unpacked.append(packed[at : at + s.size].reshape(s.shape))
        at += s.size
    both, crossed = place * shards + rank, rank * groups + place
    everyone = groups * shards

    def own(values, index, parts):
        piece = values.shape[-1] // parts
        return lax.dynamic_slice_in_dim(values, index * piece, piece, values.ndim - 1)

    sinusoid, pre_one, act_one, time_vec, act_two = time_path(all_steps)
    de = precise(dmod_all, ada_w, NT) * silu_slope(time_vec)
    dpre = precise(de, time_w2, NT) * silu_slope(pre_one)

    def outer(left, right):
        return lax.dot_general(left, own(right, place, groups), TN, precision=highest)

    return (
        result,
        mel_grad,
        o_table,
        own(unpacked[0], both, everyone),
        own(unpacked[1], both, everyone),
        own(unpacked[2], both, everyone),
        o_up,
        own(unpacked[3], both, everyone),
        o_down,
        o_emb_mel,
        o_emb_text,
        own(unpacked[4], place, groups),
        o_pos_conv,
        own(unpacked[5], crossed, everyone),
        outer(sinusoid, dpre),
        own(jnp.stack([jnp.sum(dpre, axis=0), jnp.sum(de, axis=0)]), place, groups),
        outer(act_one, de),
        outer(act_two, dmod_all),
        own(jnp.sum(dmod_all, axis=0), place, groups),
        o_qkv_w,
        own(unpacked[6], crossed, everyone),
        o_out_w,
        own(unpacked[7], place, groups),
        o_ff_w1,
        own(unpacked[8], crossed, everyone),
        o_ff_w2,
        own(unpacked[9], place, groups),
    )


def solution(mesh):
    both, crossed = ("dp", "mp"), ("mp", "dp")
    placed = (
        P("dp", None), P("dp"), P("dp", None), P("dp", None),
        P(), P(), P(), P(), P(), P(), P(), P(), P(), P(),
        P(None, None, None, "mp"), P(None, "mp"),
        P(), P(), P(), P(), P(),
        P(None, None, "mp"), P(None, "mp"), P("mp", None), P(),
        P(None, "mp"), P("mp"), P("mp", None), P(),
        P("dp", None),
    )
    given = (
        P("dp", None), P("dp", None),
        P(None, both), P(None, None, both), P(None, None, both), P(None, both),
        P(None, None, both), P(None, None, both), P(None, None, both),
        P(None, "dp"), P(None, "dp"), P("dp"),
        P(None, None, None, crossed), P(None, crossed),
        P(None, "dp"), P(None, "dp"), P(None, "dp"), P(None, "dp"), P("dp"),
        P(None, "dp", "mp"), P(None, crossed), P("mp", "dp"), P("dp"),
        P("dp", "mp"), P(crossed), P("mp", "dp"), P("dp"),
    )
    return jax.shard_map(local, mesh=mesh, in_specs=placed, out_specs=given, check_vma=False)
```

```python
from functools import partial
import math

import jax
import jax.numpy as jnp
from jax import lax
from jax.experimental import pallas as pl
from jax.experimental.pallas import tpu as pltpu
from jax.sharding import PartitionSpec as P

HEAD_DIM = 64
GAP = 16
HALO = 8
BF = jnp.bfloat16
F32 = jnp.float32
highest = lax.Precision.HIGHEST
NN = (((1,), (0,)), ((), ()))
NT = (((1,), (1,)), ((), ()))
TN = (((0,), (0,)), ((), ()))


def dot(left, right, dims=NN):
    return lax.dot_general(left.astype(BF), right.astype(BF), dims, preferred_element_type=F32)


def precise(left, right, dims=NN):
    one = lax.reduce_precision(left, 8, 7)
    two = lax.reduce_precision(left - one, 8, 7)
    three = left - one - two
    rows = left.shape[0]
    stacked = jnp.concatenate([one, two, three], axis=0).astype(BF)
    product = lax.dot_general(stacked, right, dims, preferred_element_type=F32)
    return product[:rows] + product[rows : 2 * rows] + product[2 * rows :]


@jax.custom_vjp
def expand(onehot, parts):
    return sum(onehot[:, c : c + 1] * parts[c : c + 1] for c in range(parts.shape[0]))


def expand_ahead(onehot, parts):
    return expand(onehot, parts), onehot


def expand_behind(onehot, grad):
    return None, jnp.dot(onehot.T, grad, precision=highest)


expand.defvjp(expand_ahead, expand_behind)


def silu_slope(values):
    sigmoid_val = jax.nn.sigmoid(values)
    return sigmoid_val * (1.0 + values * (1.0 - sigmoid_val))


def layer_norm(values):
    centred = values - jnp.mean(values, axis=-1, keepdims=True)
    variance = jnp.mean(centred * centred, axis=-1, keepdims=True)
    return centred * lax.rsqrt(variance + 1e-06)


def mish(values):
    grown = jnp.exp(jnp.minimum(values, 20.0))
    wide = grown * (grown + 2.0)
    return values * (wide / (wide + 2.0))


def mish_slope(values):
    grown = jnp.exp(jnp.minimum(values, 20.0))
    wide = grown * (grown + 2.0)
    under = 1.0 / (wide + 2.0)
    return wide * under + values * (4.0 * grown * (1.0 + grown) * under * under)


def sum_kernel(axis, size, x_ref, o_ref, slots, send_sems, recv_sems):
    me = lax.axis_index(axis)
    barrier = pltpu.get_barrier_semaphore()
    peers = [lax.rem(me + step, size) for step in range(1, size)]
    for peer in peers:
        pl.semaphore_signal(
            barrier, inc=1, device_id={axis: peer}, device_id_type=pl.DeviceIdType.MESH
        )
    pl.semaphore_wait(barrier, size - 1)
    for step, peer in enumerate(peers):
        pltpu.make_async_remote_copy(
            src_ref=x_ref,
            dst_ref=slots.at[me],
            send_sem=send_sems.at[step],
            recv_sem=recv_sems.at[me],
            device_id={axis: peer},
            device_id_type=pl.DeviceIdType.MESH,
        ).start()
    slots[me] = x_ref[...]
    for step, peer in enumerate(peers):
        copy = pltpu.make_async_remote_copy(
            src_ref=x_ref,
            dst_ref=slots.at[peer],
            send_sem=send_sems.at[step],
            recv_sem=recv_sems.at[peer],
            device_id={axis: peer},
            device_id_type=pl.DeviceIdType.MESH,
        )
        copy.wait_send()
        copy.wait_recv()
    total = slots[0]
    for device in range(1, size):
        total = total + slots[device]
    o_ref[...] = total


def small_sum(values, axis, name):
    size = lax.axis_size(axis)
    whole = pl.BlockSpec(memory_space=pltpu.VMEM)
    return pl.pallas_call(
        partial(sum_kernel, axis, size),
        out_shape=jax.ShapeDtypeStruct(values.shape, F32),
        in_specs=[whole],
        out_specs=whole,
        scratch_shapes=[
            pltpu.VMEM((size,) + values.shape, F32),
            pltpu.SemaphoreType.DMA((size - 1,)),
            pltpu.SemaphoreType.DMA((size,)),
        ],
        compiler_params=pltpu.CompilerParams(
            collective_id=name, has_side_effects=True, vmem_limit_bytes=16 << 20
        ),
    )(values)


def last_kernel(dp, mp, n_all, n_mp, n_both, *refs):
    n_in = n_all + n_mp + n_both
    ins, outs, rest = refs[:n_in], refs[n_in : 2 * n_in], refs[2 * n_in :]
    first, second = rest[:n_in], rest[n_in : n_in + n_all]
    middle = rest[n_in + n_all : n_in + 2 * n_all]
    send_one, recv_one, send_two, recv_two, own_sems = rest[n_in + 2 * n_all :]
    me = {"dp": lax.axis_index("dp"), "mp": lax.axis_index("mp")}
    sizes = {"dp": dp, "mp": mp}
    peers = {
        axis: [lax.rem(me[axis] + step, sizes[axis]) for step in range(1, sizes[axis])]
        for axis in sizes
    }
    mesh_id = pl.DeviceIdType.MESH
    barrier = pltpu.get_barrier_semaphore()
    for axis in sizes:
        for peer in peers[axis]:
            pl.semaphore_signal(barrier, inc=1, device_id={axis: peer}, device_id_type=mesh_id)
    pl.semaphore_wait(barrier, dp + mp - 2)

    def send(source, slots, send_sem, recv_sems, index, axis, peer, step, mine):
        return pltpu.make_async_remote_copy(
            src_ref=source,
            dst_ref=slots.at[mine],
            send_sem=send_sem.at[index, step],
            recv_sem=recv_sems.at[index, mine],
            device_id={axis: peer},
            device_id_type=mesh_id,
        )

    def source_of(t, axis, device):
        return ins[t] if t >= n_all + n_mp else ins[t].at[device]

    axes = ["dp"] * n_all + ["mp"] * (n_mp + n_both)
    local = []
    for t in range(n_in):
        axis = axes[t]
        for step, peer in enumerate(peers[axis]):
            send(
                source_of(t, axis, peer), first[t], send_one, recv_one, t, axis, peer, step, me[axis]
            ).start()
        copy = pltpu.make_async_copy(
            source_of(t, axis, me[axis]), first[t].at[me[axis]], own_sems.at[t]
        )
        copy.start()
        local.append(copy)

    def arrived(slots, send_sem, recv_sems, index, axis):
        for step, peer in enumerate(peers[axis]):
            copy = send(slots.at[peer], slots, send_sem, recv_sems, index, axis, peer, step, peer)
            copy.wait_send()
            copy.wait_recv()

    def total(slots, size):
        value = slots[0].astype(F32)
        for device in range(1, size):
            value = value + slots[device].astype(F32)
        return value

    for t in range(n_all):
        local[t].wait()
        arrived(first[t], send_one, recv_one, t, "dp")
        value = total(first[t], dp)
        if t < n_all - 1:
            rows = value.shape[0] // mp
            for z in range(mp):
                middle[t][z] = value[z * rows : (z + 1) * rows].astype(middle[t].dtype)
        else:
            middle[t][...] = value
        for step, peer in enumerate(peers["mp"]):
            source = middle[t].at[peer] if t < n_all - 1 else middle[t]
            send(source, second[t], send_two, recv_two, t, "mp", peer, step, me["mp"]).start()
        if t < n_all - 1:
            second[t][me["mp"]] = middle[t][me["mp"]]
        else:
            second[t][me["mp"]] = value
    for t in range(n_all, n_in):
        local[t].wait()
        arrived(first[t], send_one, recv_one, t, "mp")
        outs[t][...] = total(first[t], mp)
    for t in range(n_all):
        arrived(second[t], send_two, recv_two, t, "mp")
        outs[t][...] = total(second[t], mp)


def last_sums(over_all, small, over_mp, both):
    dp, mp = lax.axis_size("dp"), lax.axis_size("mp")
    ins = list(over_all) + [small] + list(over_mp) + list(both)
    n_all, n_mp, n_both = len(over_all) + 1, len(over_mp), len(both)
    outs, first, second, middle = [], [], [], []
    for t, value in enumerate(ins):
        if t < n_all - 1:
            rows, columns = value.shape[1] // mp, value.shape[2]
            outs.append((rows, columns))
            first.append(pltpu.VMEM(value.shape, value.dtype))
            second.append(pltpu.VMEM((mp, rows, columns), value.dtype))
            middle.append(pltpu.VMEM((mp, rows, columns), value.dtype))
        elif t == n_all - 1:
            outs.append(value.shape[1:])
            first.append(pltpu.VMEM(value.shape, value.dtype))
            second.append(pltpu.VMEM((mp,) + value.shape[1:], value.dtype))
            middle.append(pltpu.VMEM(value.shape[1:], value.dtype))
        elif t < n_all + n_mp:
            outs.append(value.shape[1:])
            first.append(pltpu.VMEM(value.shape, value.dtype))
        else:
            outs.append(value.shape)
            first.append(pltpu.VMEM((mp,) + value.shape, value.dtype))
    most = max(dp, mp)
    dma = pltpu.SemaphoreType.DMA
    return pl.pallas_call(
        partial(last_kernel, dp, mp, n_all, n_mp, n_both),
        out_shape=[jax.ShapeDtypeStruct(shape, F32) for shape in outs],
        in_specs=[pl.BlockSpec(memory_space=pl.ANY)] * len(ins),
        out_specs=[pl.BlockSpec(memory_space=pltpu.VMEM)] * len(ins),
        scratch_shapes=first
        + second
        + middle
        + [
            dma((len(ins), most)),
            dma((len(ins), most)),
            dma((n_all, mp)),
            dma((n_all, mp)),
            dma((len(ins),)),
        ],
        compiler_params=pltpu.CompilerParams(
            collective_id=3, has_side_effects=True, vmem_limit_bytes=48 << 20
        ),
    )(*ins)


def conv_norm(hidden, segment, conv, vec, gain):
    taps = conv.shape[0]
    reach = taps // 2
    rows = hidden.shape[0]
    padded = jnp.pad(hidden, ((reach, reach), (0, 0)))
    seg_padded = jnp.pad(segment, (reach, reach), constant_values=-1)
    mixture = vec[0]
    for tap in range(taps):
        keep = (seg_padded[tap : tap + rows] == segment) & (segment >= 0)
        mixture = mixture + conv[tap] * jnp.where(keep[:, None], padded[tap : tap + rows], 0.0)
    return layer_norm(mixture) * gain + vec[1]


def activate(pre, bias):
    return jax.nn.gelu(pre + bias, approximate=False)


def clip_squares(own, active):
    return jnp.dot(own.T, active * active, precision=highest)


def respond(active, squares, onehot, scale, shift):
    norms = jnp.sqrt(jnp.maximum(squares, 1.0))
    ratio = norms / (jnp.mean(norms, axis=-1, keepdims=True) + 1e-06)
    return scale * (active * expand(onehot, ratio)) + shift + active


def text_ahead(hidden, segment, onehot, own, conv, vec, gain, up, hid, down):
    normed, norm_pull = jax.vjp(
        lambda h, c, v, g: conv_norm(h, segment, c, v, g), hidden, conv, vec, gain
    )
    normed = normed.astype(BF)
    active, act_pull = jax.vjp(activate, dot(normed, up), hid[0])
    squares, square_pull = jax.vjp(lambda a: clip_squares(own, a), active)
    squares = small_sum(squares, "mp", 1)
    grown, respond_pull = jax.vjp(
        lambda a, s, g, b: respond(a, s, onehot, g, b), active, squares, hid[1], hid[2]
    )
    grown = grown.astype(BF)
    result = hidden + dot(grown, down) + vec[2]
    return result, (norm_pull, normed, act_pull, square_pull, respond_pull, grown)


def text_behind(kept, grad, up, down, extra):
    norm_pull, normed, act_pull, square_pull, respond_pull, grown = kept
    grad_low = grad.astype(BF)
    g_out = jnp.sum(grad, axis=0)
    g_down = dot(grad_low, grown, TN)
    grad_active, grad_squares, g_scale, g_shift = respond_pull(dot(grad_low, down, NT))
    if extra is None:
        grad_squares = small_sum(grad_squares, "mp", 1)
    else:
        joined = small_sum(jnp.concatenate([grad_squares, extra], axis=1), "mp", 2)
        grad_squares, extra = joined[:, : grad_squares.shape[1]], joined[:, grad_squares.shape[1] :]
    grad_active = grad_active + square_pull(grad_squares)[0]
    grad_pre, g_bias = act_pull(grad_active)
    pre_low = grad_pre.astype(BF)
    g_up = dot(pre_low, normed, TN)
    grad_hidden, g_conv, g_vec, g_gain = norm_pull(dot(pre_low, up, NT))
    g_vec = g_vec.at[2].add(g_out)
    return (
        grad + grad_hidden,
        (g_conv, g_vec, g_gain, g_up, jnp.stack([g_bias, g_scale, g_shift]), g_down),
        extra,
    )


def spread(values, starts, ends):
    rows = values.shape[0]
    clips = starts.shape[0]
    at = jnp.arange(rows, dtype=jnp.int32)
    total = rows + GAP * clips + 2 * GAP
    out = None
    for c in range(clips):
        keep = (at >= starts[c]) & (at < ends[c])
        part = jnp.where(keep[:, None], values, 0)
        lead = GAP + GAP * c
        part = jnp.pad(part, ((lead, total - lead - rows), (0, 0)))
        out = part if out is None else out + part
    return out


def gather_back(values, starts, ends):
    clips = starts.shape[0]
    rows = values.shape[0] - GAP * clips
    at = jnp.arange(rows, dtype=jnp.int32)
    out = None
    for c in range(clips):
        keep = (at >= starts[c]) & (at < ends[c])
        part = jnp.where(keep[:, None], values[GAP * c : GAP * c + rows], 0)
        out = part if out is None else out + part
    return out


def conv_kernel(taps, turned, x_ref, w_ref, o_ref, full_ref):
    rows, width = o_ref.shape
    group = w_ref.shape[1]
    first = GAP - taps // 2

    @pl.when(pl.program_id(0) == 0)
    def _():
        lane = lax.broadcasted_iota(jnp.int32, (group, width), 1) // group
        for k in range(taps):
            tap = w_ref[taps - 1 - k if turned else k]
            for g in range(width // group):
                piece = jnp.where(lane == g, tap, jnp.zeros_like(tap))
                if turned:
                    full_ref[g * group : (g + 1) * group, k * width : (k + 1) * width] = piece
                else:
                    full_ref[k * width + g * group : k * width + (g + 1) * group, :] = piece

    columns = [x_ref[first + k : first + k + rows, :].astype(BF) for k in range(taps)]
    o_ref[...] = lax.dot_general(
        jnp.concatenate(columns, axis=1),
        full_ref[...],
        NT if turned else NN,
        preferred_element_type=F32,
    )


def conv_chunk(rows):
    for size in (528, 352, 256, 128, 64, 32, 16):
        if rows % size == 0:
            return size
    return rows


def apply_conv(spread_rows, weight, turned):
    rows = spread_rows.shape[0] - 2 * GAP
    width = spread_rows.shape[1]
    taps, group = weight.shape[:2]
    chunk = conv_chunk(rows)
    return pl.pallas_call(
        partial(conv_kernel, taps, turned),
        out_shape=jax.ShapeDtypeStruct((rows, width), F32),
        grid=(rows // chunk,),
        in_specs=[
            pl.BlockSpec((pl.Element(chunk + 2 * GAP), pl.Element(width)), lambda i: (i * chunk, 0)),
            pl.BlockSpec(weight.shape, lambda i: (0, 0, 0), pipeline_mode=pl.Buffered(1)),
        ],
        out_specs=pl.BlockSpec((chunk, width), lambda i: (i, 0)),
        scratch_shapes=[
            pltpu.VMEM((width, taps * width) if turned else (taps * width, width), BF)
        ],
        compiler_params=pltpu.CompilerParams(vmem_limit_bytes=48 << 20),
        cost_estimate=pl.CostEstimate(
            flops=2 * rows * taps * width * width, bytes_accessed=8 << 20, transcendentals=0
        ),
    )(spread_rows, weight)


def conv_grad_kernel(taps, group, x_ref, g_ref, o_ref):
    rows, width = g_ref.shape
    first = GAP - taps // 2
    turned = g_ref[...].T.astype(BF)

    @pl.when(pl.program_id(0) == 0)
    def _():
        o_ref[...] = jnp.zeros_like(o_ref)

    for k in range(taps):
        window = x_ref[first + k : first + k + rows, :].astype(BF)
        product = jnp.dot(turned, window, preferred_element_type=F32)
        for g in range(width // group):
            own = slice(g * group, (g + 1) * group)
            o_ref[own, k * group : (k + 1) * group] += product[own, own]


def conv_grad(spread_rows, grads, taps, group):
    rows, width = grads.shape
    chunk = conv_chunk(rows)
    return pl.pallas_call(
        partial(conv_grad_kernel, taps, group),
        out_shape=jax.ShapeDtypeStruct((width, taps * group), F32),
        grid=(rows // chunk,),
        in_specs=[
            pl.BlockSpec((pl.Element(chunk + 2 * GAP), pl.Element(width)), lambda i: (i * chunk, 0)),
            pl.BlockSpec((chunk, width), lambda i: (i, 0)),
        ],
        out_specs=pl.BlockSpec((width, taps * group), lambda i: (0, 0)),
        compiler_params=pltpu.CompilerParams(vmem_limit_bytes=48 << 20),
        cost_estimate=pl.CostEstimate(
            flops=2 * rows * taps * width * width, bytes_accessed=8 << 20, transcendentals=0
        ),
    )(spread_rows, grads)


def pair_split(columns):
    lead = columns.shape[:-1]
    pairs = columns.reshape(*lead, columns.shape[-1] // 2, 2)
    return jnp.concatenate([pairs[..., 0], pairs[..., 1]], axis=-1)


def pair_merge(columns):
    half = columns.shape[-1] // 2
    return jnp.stack([columns[..., :half], columns[..., half:]], axis=-1).reshape(columns.shape)


def head_masks(width):
    heads = width // HEAD_DIM
    lane = lax.broadcasted_iota(jnp.int32, (1, width), 1)
    half = HEAD_DIM // 2
    paired = [((lane % (width // 2)) // half) == h for h in range(heads)]
    plain = [(lane // HEAD_DIM) == h for h in range(heads)]
    return heads, paired, plain


def attend_kernel(bounds, q_ref, k_ref, v_ref, sq_ref, sk_ref, o_ref, full_ref, lse_ref):
    i = pl.program_id(0)
    q = q_ref[...]
    rows, width = q.shape
    heads, paired, plain = head_masks(width)
    scale = HEAD_DIM**-0.5
    q_heads = [jnp.where(paired[h], q, jnp.zeros_like(q)) for h in range(heads)]
    sq = sq_ref[...]

    def step(kb, carry):
        tops, sums, acc = carry
        k, v = k_ref[kb], v_ref[kb]
        same = sq == sk_ref[kb]
        new_tops, new_sums = [], []
        decay, extra = None, None
        for h in range(heads):
            scores = lax.dot_general(q_heads[h], k, NT, preferred_element_type=F32) * scale
            scores = jnp.where(same, scores, -1e30)
            top = jnp.maximum(tops[h], jnp.max(scores, axis=-1, keepdims=True))
            fade = jnp.exp(tops[h] - top)
            weight = jnp.exp(scores - top)
            new_tops.append(top)
            new_sums.append(fade * sums[h] + jnp.sum(weight, axis=-1, keepdims=True))
            v_head = jnp.where(plain[h], v, jnp.zeros_like(v))
            part = jnp.dot(weight.astype(BF), v_head, preferred_element_type=F32)
            extra = part if extra is None else extra + part
            decay = fade * jnp.ones((1, width), F32) if h == 0 else jnp.where(plain[h], fade, decay)
        return tuple(new_tops), tuple(new_sums), acc * decay + extra

    start = (
        tuple(jnp.full((rows, 1), -1e30, F32) for _ in range(heads)),
        tuple(jnp.zeros((rows, 1), F32) for _ in range(heads)),
        jnp.zeros((rows, width), F32),
    )
    tops, sums, acc = lax.fori_loop(bounds[i, 0], bounds[i, 1], step, start)
    lane = lax.broadcasted_iota(jnp.int32, (1, lse_ref.shape[1]), 1)
    share = jnp.ones((rows, width), F32)
    logs = jnp.zeros((rows, lse_ref.shape[1]), F32)
    for h in range(heads):
        share = jnp.where(plain[h], 1.0 / sums[h], share)
        logs = jnp.where(lane == h, tops[h] + jnp.log(sums[h]), logs)
    full = acc * share
    full_ref[...] = full
    o_ref[...] = full.astype(BF)
    lse_ref[...] = logs


def attend(qkv, seg_rows, seg_blocks, bounds, block):
    shards, _, rows, width = qkv.shape
    total = shards * rows
    per = rows // block
    grid_spec = pltpu.PrefetchScalarGridSpec(
        num_scalar_prefetch=1,
        grid=(total // block,),
        in_specs=[
            pl.BlockSpec((None, None, block, width), lambda i, b: (i // per, 0, i % per, 0)),
            pl.BlockSpec((shards, None, rows, width), lambda i, b: (0, 1, 0, 0)),
            pl.BlockSpec((shards, None, rows, width), lambda i, b: (0, 2, 0, 0)),
            pl.BlockSpec((block, 1), lambda i, b: (i, 0)),
            pl.BlockSpec((shards, 1, rows), lambda i, b: (0, 0, 0)),
        ],
        out_specs=[
            pl.BlockSpec((block, width), lambda i, b: (i, 0)),
            pl.BlockSpec((block, width), lambda i, b: (i, 0)),
            pl.BlockSpec((block, 128), lambda i, b: (i, 0)),
        ],
    )
    return pl.pallas_call(
        attend_kernel,
        out_shape=[
            jax.ShapeDtypeStruct((total, width), BF),
            jax.ShapeDtypeStruct((total, width), F32),
            jax.ShapeDtypeStruct((total, 128), F32),
        ],
        grid_spec=grid_spec,
        compiler_params=pltpu.CompilerParams(vmem_limit_bytes=48 << 20),
        cost_estimate=pl.CostEstimate(
            flops=8 * total * total * width, bytes_accessed=8 << 20, transcendentals=0
        ),
    )(bounds, qkv, qkv, qkv, seg_rows, seg_blocks)


def unrotate(values, cos, sin):
    half = values.shape[1] // 2
    even, odd = values[:, :half], values[:, half:]
    return jnp.concatenate([even * cos + odd * sin, odd * cos - even * sin], axis=1)


def attend_back_kernel(
    bounds, q_ref, k_ref, v_ref, full_ref, lse_ref, do_ref, sq_ref, sk_ref, cos_ref, sin_ref,
    out_ref, dk_ref, dv_ref,
):
    i = pl.program_id(0)
    q, do = q_ref[...], do_ref[...]
    rows, width = q.shape
    shards, _, shard_rows, _ = out_ref.shape
    per = shard_rows // rows
    heads, paired, plain = head_masks(width)
    scale = HEAD_DIM**-0.5

    @pl.when(i == 0)
    def _():
        dk_ref[...] = jnp.zeros_like(dk_ref)
        dv_ref[...] = jnp.zeros_like(dv_ref)

    zero = jnp.zeros_like(q)
    q_heads = [jnp.where(paired[h], q, zero) for h in range(heads)]
    do_heads = [jnp.where(plain[h], do, zero) for h in range(heads)]
    product = do.astype(F32) * full_ref[...]
    deltas = [jnp.sum(jnp.where(plain[h], product, 0.0), axis=-1, keepdims=True) for h in range(heads)]
    logs = [lse_ref[:, h : h + 1] for h in range(heads)]
    sq = sq_ref[...]

    def step(kb, dq):
        k, v = k_ref[kb], v_ref[kb]
        same = sq == sk_ref[kb]
        dk, dv = dk_ref[kb], dv_ref[kb]
        for h in range(heads):
            scores = lax.dot_general(q_heads[h], k, NT, preferred_element_type=F32) * scale
            weight = jnp.where(same, jnp.exp(scores - logs[h]), 0.0)
            dp = lax.dot_general(do_heads[h], v, NT, preferred_element_type=F32)
            ds = (weight * (dp - deltas[h]) * scale).astype(BF)
            dv = dv + lax.dot_general(weight.astype(BF), do_heads[h], TN, preferred_element_type=F32)
            dk = dk + lax.dot_general(ds, q_heads[h], TN, preferred_element_type=F32)
            k_head = jnp.where(paired[h], k, jnp.zeros_like(k))
            dq = dq + jnp.dot(ds, k_head, preferred_element_type=F32)
        dk_ref[kb] = dk
        dv_ref[kb] = dv
        return dq

    dq = lax.fori_loop(bounds[i, 0], bounds[i, 1], step, jnp.zeros((rows, width), F32))
    here = pl.ds(pl.multiple_of(i * rows, rows), rows)
    inside = pl.ds(pl.multiple_of((i % per) * rows, rows), rows)
    out_ref[i // per, 0, inside, :] = unrotate(dq, cos_ref[here, :], sin_ref[here, :]).astype(BF)

    @pl.when(i == pl.num_programs(0) - 1)
    def _():
        for s in range(shards):
            own = slice(s * shard_rows, (s + 1) * shard_rows)
            out_ref[s, 1] = unrotate(dk_ref[s], cos_ref[own, :], sin_ref[own, :]).astype(BF)
            out_ref[s, 2] = dv_ref[s].astype(BF)


def attend_back(qkv, full, logs, grads, seg_rows, seg_blocks, cos, sin, bounds, block):
    shards, _, rows, width = qkv.shape
    total = shards * rows
    per = rows // block
    grid_spec = pltpu.PrefetchScalarGridSpec(
        num_scalar_prefetch=1,
        grid=(total // block,),
        in_specs=[
            pl.BlockSpec((None, None, block, width), lambda i, b: (i // per, 0, i % per, 0)),
            pl.BlockSpec((shards, None, rows, width), lambda i, b: (0, 1, 0, 0)),
            pl.BlockSpec((shards, None, rows, width), lambda i, b: (0, 2, 0, 0)),
            pl.BlockSpec((block, width), lambda i, b: (i, 0)),
            pl.BlockSpec((block, 128), lambda i, b: (i, 0)),
            pl.BlockSpec((block, width), lambda i, b: (i, 0)),
            pl.BlockSpec((block, 1), lambda i, b: (i, 0)),
            pl.BlockSpec((shards, 1, rows), lambda i, b: (0, 0, 0)),
            pl.BlockSpec((total, width // 2), lambda i, b: (0, 0)),
            pl.BlockSpec((total, width // 2), lambda i, b: (0, 0)),
        ],
        out_specs=pl.BlockSpec((shards, 3, rows, width), lambda i, b: (0, 0, 0, 0)),
        scratch_shapes=[
            pltpu.VMEM((shards, rows, width), F32),
            pltpu.VMEM((shards, rows, width), F32),
        ],
    )
    return pl.pallas_call(
        attend_back_kernel,
        out_shape=jax.ShapeDtypeStruct((shards, 3, rows, width), BF),
        grid_spec=grid_spec,
        compiler_params=pltpu.CompilerParams(vmem_limit_bytes=48 << 20),
        cost_estimate=pl.CostEstimate(
            flops=20 * total * total * width, bytes_accessed=16 << 20, transcendentals=0
        ),
    )(bounds, qkv, qkv, qkv, full, logs, grads, seg_rows, seg_blocks, cos, sin)


def exchange(values, axis):
    return lax.all_to_all(values, axis, 0, 0)


def local(
    mel_pair, text_ids, clip_lengths, t_index,
    txt_table, txt_conv, txt_vec, txt_gain, txt_up, txt_hid, txt_down,
    emb_mel, emb_text, emb_bias, pos_conv, pos_bias,
    time_w1, time_bias, time_w2, ada_w, ada_b,
    qkv_w, qkv_b, out_w, out_b, ff_w1, ff_b1, ff_w2, ff_b2, out_grad,
):
    total = mel_pair.shape[0]
    width = emb_mel.shape[1]
    shards, groups = lax.axis_size("mp"), lax.axis_size("dp")
    rank, place = lax.axis_index("mp"), lax.axis_index("dp")
    rows = total // shards
    cols = width // shards
    clips = clip_lengths.shape[1]
    first = rank * rows
    taps = pos_conv.shape[1]
    group = pos_conv.shape[2]

    def spread_slice(weight, axis):
        piece = weight.shape[axis] // groups
        return lax.dynamic_slice_in_dim(weight, place * piece, piece, axis)

    def to_all(piece, axis_name="mp"):
        size = lax.axis_size(axis_name)
        return lax.all_to_all(jnp.broadcast_to(piece[None], (size,) + piece.shape), axis_name, 0, 0)

    def gather(piece, axis):
        return lax.all_gather(to_all(piece), "dp", axis=axis, tiled=True)

    qkv_piece = spread_slice(qkv_w, 1)
    qkv_piece = jnp.concatenate([pair_split(qkv_piece[:2]), qkv_piece[2:]], axis=0)
    qkv_full = gather(qkv_piece, 2)
    out_full = gather(spread_slice(out_w, 0), 1).reshape(width, width)
    w1_piece = to_all(spread_slice(ff_w1, 0)).transpose(1, 0, 2)
    w1_full = lax.all_gather(w1_piece.reshape(w1_piece.shape[0], -1), "dp", axis=0, tiled=True)
    w2_full = gather(spread_slice(ff_w2, 0), 1).reshape(-1, width)
    small = jnp.concatenate([pair_split(qkv_b[:2]), qkv_b[2:]], axis=0)
    small = jnp.concatenate([small, ff_b1.reshape(-1, cols)], axis=0)
    small = to_all(small)
    qkv_bias = small[:, :3]
    b1_full = small[:, 3:].reshape(-1)
    all_steps = lax.all_gather(t_index, "dp", tiled=True).reshape(-1)

    lengths = clip_lengths[0]
    clip_index = jnp.arange(clips, dtype=jnp.int32)
    ends = jnp.sum(jnp.where(clip_index[:, None] >= clip_index[None, :], lengths[None, :], 0), axis=1)
    starts = ends - lengths
    frames = jnp.arange(total, dtype=jnp.int32)
    member = (frames[:, None] >= starts[None, :]) & (frames[:, None] < ends[None, :])
    segment = jnp.sum(member * clip_index[None, :], axis=1).astype(jnp.int32)
    position = frames - jnp.sum(member * starts[None, :], axis=1)
    ext = rows + 2 * HALO
    ids = lax.dynamic_slice_in_dim(jnp.pad(text_ids, (HALO, HALO)), first, ext)
    seg_ext = lax.dynamic_slice_in_dim(jnp.pad(segment, (HALO, HALO), constant_values=-1), first, ext)
    hot_ext = (seg_ext[:, None] == clip_index[None, :]).astype(F32)
    ext_index = jnp.arange(ext, dtype=jnp.int32)
    inside = (ext_index >= HALO) & (ext_index < HALO + rows)
    own_ext = jnp.where(inside[:, None], hot_ext, 0.0)
    hot = hot_ext[HALO : HALO + rows]

    def time_path(steps):
        half = time_w1.shape[0] // 2
        frequency = jnp.exp(jnp.arange(half, dtype=F32) * (-math.log(10000.0) / (half - 1)))
        angles = steps.astype(F32)[:, None] * frequency[None, :]
        sinusoid = jnp.concatenate([jnp.sin(angles), jnp.cos(angles)], axis=-1)
        pre_one = precise(sinusoid, time_w1) + time_bias[0]
        act_one = jax.nn.silu(pre_one)
        time_vec = precise(act_one, time_w2) + time_bias[1]
        return sinusoid, pre_one, act_one, time_vec, jax.nn.silu(time_vec)

    mod = precise(time_path(t_index[0])[4], ada_w) + ada_b

    hidden = jnp.take(txt_table, ids, axis=0).astype(F32)
    kept = []
    blocks = txt_conv.shape[0]
    for b in range(blocks):
        hidden, saved = text_ahead(
            hidden, seg_ext, hot_ext, own_ext, txt_conv[b], txt_vec[b], txt_gain[b],
            txt_up[b], txt_hid[b], txt_down[b],
        )
        kept.append(saved)
    text = hidden[HALO : HALO + rows].astype(BF)

    mel = lax.dynamic_slice_in_dim(mel_pair, first, rows)
    x0 = dot(mel, emb_mel) + dot(text, emb_text) + emb_bias

    def to_channels(values):
        blocks_of = values.reshape(rows, shards, cols).transpose(1, 0, 2)
        return exchange(blocks_of, "mp").reshape(total, cols)

    def to_rows(values):
        return exchange(values.reshape(shards, rows, cols), "mp").transpose(1, 0, 2).reshape(rows, width)

    spread_in = spread(to_channels(x0.astype(BF)).astype(F32), starts, ends)
    real = spread(jnp.ones((total, 1), F32), starts, ends)
    pre_a = apply_conv(spread_in, pos_conv[0], False) + pos_bias[0]
    y_a = jnp.pad(
        jnp.where(real[GAP:-GAP] > 0, mish(pre_a), 0.0).astype(BF).astype(F32), ((GAP, GAP), (0, 0))
    )
    pre_b = apply_conv(y_a, pos_conv[1], False) + pos_bias[1]
    c_pos = to_rows(gather_back(mish(pre_b).astype(BF), starts, ends))
    x1 = x0 + c_pos.astype(F32)

    def modulate(state, mod_in, shift_part, scale_part):
        scale = expand(hot, mod_in[:, scale_part * width : (scale_part + 1) * width])
        shift = expand(hot, mod_in[:, shift_part * width : (shift_part + 1) * width])
        return layer_norm(state) * (1.0 + scale) + shift

    n1, n1_pull = jax.vjp(lambda s, m: modulate(s, m, 0, 1), x1, mod)
    n1 = n1.astype(BF)
    half = HEAD_DIM // 2
    inverse = jnp.exp(jnp.arange(0, HEAD_DIM, 2, dtype=F32) * (-math.log(10000.0) / HEAD_DIM))
    angles = position.astype(F32)[:, None] * jnp.tile(inverse, cols // HEAD_DIM)[None, :]
    cos, sin = jnp.cos(angles), jnp.sin(angles)
    cos_own = lax.dynamic_slice_in_dim(cos, first, rows)
    sin_own = lax.dynamic_slice_in_dim(sin, first, rows)
    projected = []
    for s in range(shards):
        for p in range(3):
            value = dot(n1, qkv_full[s, p]) + qkv_bias[s, p]
            if p < 2:
                even, odd = value[:, : cols // 2], value[:, cols // 2 :]
                value = jnp.concatenate(
                    [even * cos_own - odd * sin_own, odd * cos_own + even * sin_own], axis=1
                )
            projected.append(value.astype(BF))
    qkv = jnp.stack(projected).reshape(shards, 3, rows, cols)
    qkv = exchange(qkv, "mp")
    block = 256
    heads_of = segment[::block]
    tails_of = segment[block - 1 :: block]
    low_key = jnp.sum(jnp.where(heads_of[:, None] == clip_index, starts[None, :], 0), axis=1)
    high_key = jnp.sum(jnp.where(tails_of[:, None] == clip_index, ends[None, :], 0), axis=1)
    bounds = jnp.stack([low_key // rows, (high_key + rows - 1) // rows], axis=1).astype(jnp.int32)
    seg_rows = segment[:, None]
    seg_blocks = segment.reshape(shards, 1, rows)
    o, o_full, logs = attend(qkv, seg_rows, seg_blocks, bounds, block)
    o_rows = to_rows(o)

    def residual(state, mod_in, summed, bias, part):
        return state + expand(hot, mod_in[:, part * width : (part + 1) * width]) * (summed + bias)

    x2, att_pull = jax.vjp(
        lambda s, m, a, b: residual(s, m, a, b, 2), x1, mod, dot(o_rows, out_full), out_b
    )

    n2, n2_pull = jax.vjp(lambda s, m: modulate(s, m, 3, 4), x2, mod)
    n2 = n2.astype(BF)
    r, r_pull = jax.vjp(
        lambda v, b: jax.nn.gelu(v + b, approximate=True), dot(n2, w1_full), b1_full
    )
    r = r.astype(BF)
    out, ff_pull = jax.vjp(lambda s, m, a, b: residual(s, m, a, b, 5), x2, mod, dot(r, w2_full), ff_b2)
    result = to_all(out.astype(BF)).reshape(total, width).astype(F32)

    grad = lax.dynamic_slice_in_dim(out_grad, first, rows).astype(F32)
    dx2, dmod_a, df, g_ff_b2 = ff_pull(grad)
    df = df.astype(BF)
    g_ff_w2 = dot(df, r, TN)
    dh, g_ff_b1 = r_pull(dot(df, w2_full, NT))
    g_ff_b1 = jnp.sum(dh.astype(BF).astype(F32), axis=0)
    dh = dh.astype(BF)
    g_ff_w1 = dot(n2, dh, TN)
    more, dmod_b = n2_pull(dot(dh, w1_full, NT))
    dx2 = dx2 + more

    def for_dp(matrix):
        return matrix.astype(BF).reshape(groups, matrix.shape[0] // groups, matrix.shape[1])

    def by_rank(matrix):
        return matrix.reshape(matrix.shape[0], shards, -1).transpose(1, 0, 2)

    def scatter_dp(matrix):
        return lax.psum_scatter(matrix.astype(BF), "dp", scatter_dimension=0, tiled=True)

    sent_w1, sent_w2 = scatter_dp(g_ff_w1), scatter_dp(g_ff_w2)

    dx1, dmod_c, da, g_out_b = att_pull(dx2)
    da = da.astype(BF)
    g_out_w = dot(da, o_rows, TN)
    do = to_channels(dot(da, out_full, NT).astype(BF))
    dqkv = attend_back(qkv, o_full, logs, do, seg_rows, seg_blocks, cos, sin, bounds, block)
    dqkv = exchange(dqkv, "mp").transpose(2, 0, 1, 3).reshape(rows, 3 * width)
    sent_w1, sent_w2, dqkv = lax.optimization_barrier((sent_w1, sent_w2, dqkv))
    g_qkv_w = dot(n1, dqkv, TN)
    g_qkv_b = jnp.sum(dqkv.astype(F32), axis=0).reshape(shards, 3, cols)
    w_all = qkv_full.transpose(2, 0, 1, 3).reshape(width, 3 * width)
    more, dmod_d = n1_pull(dot(dqkv, w_all, NT))
    dx1 = dx1 + more
    ff_pair = jnp.concatenate([by_rank(sent_w1), by_rank(sent_w2)], axis=2)
    sent_qkv, sent_out = scatter_dp(g_qkv_w), scatter_dp(g_out_w)

    dmod = dmod_a + dmod_b + dmod_c + dmod_d

    slope_b = gather_back(mish_slope(pre_b), starts, ends)
    dy_b = to_channels(dx1.astype(BF)).astype(F32) * slope_b
    g_pos_b = jnp.sum(dy_b, axis=0)
    dy_b = spread(dy_b.astype(BF).astype(F32), starts, ends)
    dy_a = apply_conv(dy_b, pos_conv[1], True) * mish_slope(pre_a)
    dy_a = jnp.where(real[GAP:-GAP] > 0, dy_a, 0.0)
    g_pos_a = jnp.sum(dy_a, axis=0)
    dy_a = jnp.pad(dy_a.astype(BF).astype(F32), ((GAP, GAP), (0, 0)))
    dc = gather_back(
        apply_conv(dy_a, pos_conv[0], True).astype(BF), starts, ends
    )
    dx0_full = dx1 + to_rows(dc).astype(F32)
    g_conv = jnp.concatenate(
        [conv_grad(spread_in, dy_a[GAP:-GAP], taps, group), conv_grad(y_a, dy_b[GAP:-GAP], taps, group)],
        axis=1,
    )
    sent_qkv, sent_out, dx0_full = lax.optimization_barrier((sent_qkv, sent_out, dx0_full))
    at_pair = jnp.concatenate([by_rank(sent_qkv), by_rank(sent_out)], axis=2)
    sent_conv = scatter_dp(g_conv)

    g_emb_bias = jnp.sum(dx0_full, axis=0)
    dx0 = dx0_full.astype(BF)
    mel_grad = to_all(dot(dx0, emb_mel, NT).astype(BF)).reshape(total, -1).astype(F32)
    g_emb = jnp.concatenate([dot(dx0, text, TN), dot(dx0, mel, TN)], axis=1)
    sent_emb = scatter_dp(g_emb)
    text_width = text.shape[1]

    dtext = jnp.pad(dot(dx0, emb_text, NT), ((HALO, HALO), (0, 0)))
    text_grads = [None] * blocks
    extra = dmod
    for b in reversed(range(blocks)):
        dtext, text_grads[b], summed = text_behind(kept[b], dtext, txt_up[b], txt_down[b], extra)
        if extra is not None:
            dmod_all = lax.all_gather(summed, "dp", tiled=True)
            sent_conv, dtext = lax.optimization_barrier((sent_conv, dtext))
        extra = None
    sent_emb, dtext = lax.optimization_barrier((sent_emb, dtext))
    vocab = txt_table.shape[0]
    wide = -(-vocab // 128) * 128
    chosen = (ids[:, None] == jnp.arange(wide, dtype=jnp.int32)[None, :]).astype(BF)
    g_table = dot(dtext, chosen, TN)
    hidden_width = txt_up.shape[2]

    def placed(values):
        full = jnp.zeros((shards,) + values.shape, F32)
        return lax.dynamic_update_slice_in_dim(full, values[None], rank, 0)

    g_pos_bias = placed(jnp.stack([g_pos_a, g_pos_b])).transpose(1, 0, 2).reshape(2, width)
    g_qkv_b = jnp.concatenate([pair_merge(g_qkv_b[:, :2]), g_qkv_b[:, 2:]], axis=1)
    g_qkv_b = g_qkv_b.transpose(1, 0, 2).reshape(3, width)
    small = [
        (jnp.stack([g[0] for g in text_grads]), "both"),
        (jnp.stack([g[1] for g in text_grads]), "both"),
        (jnp.stack([g[2] for g in text_grads]), "both"),
        (jnp.stack([g[4] for g in text_grads]), "both"),
        (g_emb_bias, "dp"),
        (g_pos_bias, "crossed"),
        (g_qkv_b, "crossed"),
        (g_out_b, "dp"),
        (g_ff_b1, "crossed"),
        (g_ff_b2, "dp"),
    ]
    packed = []
    for value, kind in small:
        lead = value.size // value.shape[-1]
        if kind == "crossed":
            value = value.reshape(lead, shards, groups, -1).transpose(2, 0, 1, 3)
        else:
            value = value.reshape(lead, groups, -1).transpose(1, 0, 2)
        packed.append(value.reshape(groups, -1))
    packed = jnp.concatenate(packed, axis=1)
    length = packed.shape[1]
    packed = jnp.pad(packed, ((0, 0), (0, -length % 1024))).reshape(groups, -1, 128)
    table_sum, up0, up1, down0, down1, packed, ff_pair, at_pair, g_emb = last_sums(
        [for_dp(g_table)]
        + [for_dp(text_grads[b][3]) for b in range(blocks)]
        + [for_dp(text_grads[b][5]) for b in range(blocks)],
        packed,
        [ff_pair, at_pair],
        [sent_emb],
    )
    packed = packed.reshape(-1)
    unpacked, at = [], 0
    for value, kind in small:
        size = value.size // groups
        piece = packed[at : at + size]
        at += size
        if kind == "dp":
            unpacked.append(piece.reshape(value.shape[:-1] + (-1,)))
        else:
            piece = piece.reshape(value.size // value.shape[-1], shards, -1)
            piece = lax.dynamic_slice_in_dim(piece, rank, 1, 1)
            unpacked.append(piece.reshape(value.shape[:-1] + (-1,)))
    o_table = table_sum[:, :vocab].T
    o_up = jnp.stack([up0.T, up1.T])
    o_down = jnp.stack([down0.T, down1.T])
    ff_cols = ff_w1.shape[1]
    o_ff_w1, o_ff_w2 = ff_pair[:, :ff_cols], ff_pair[:, ff_cols:].T
    g_qkv = at_pair[:, : 3 * cols].reshape(-1, 3, cols).transpose(1, 0, 2)
    o_qkv_w = jnp.concatenate([pair_merge(g_qkv[:2]), g_qkv[2:]], axis=0)
    o_out_w = at_pair[:, 3 * cols :].T
    o_pos_conv = sent_conv.astype(F32).T.reshape(2, taps, group, -1)
    o_emb_text, o_emb_mel = g_emb[:, :text_width].T, g_emb[:, text_width:].T

    def own(values, index, parts):
        piece = values.shape[-1] // parts
        return lax.dynamic_slice_in_dim(values, index * piece, piece, values.ndim - 1)

    sinusoid, pre_one, act_one, time_vec, act_two = time_path(all_steps)
    de = precise(dmod_all, ada_w, NT) * silu_slope(time_vec)
    dpre = precise(de, time_w2, NT) * silu_slope(pre_one)

    def outer(left, right):
        return lax.dot_general(left, own(right, place, groups), TN, precision=highest)

    return (
        result,
        mel_grad,
        o_table,
        unpacked[0],
        unpacked[1],
        unpacked[2],
        o_up,
        unpacked[3],
        o_down,
        o_emb_mel,
        o_emb_text,
        unpacked[4],
        o_pos_conv,
        unpacked[5],
        outer(sinusoid, dpre),
        own(jnp.stack([jnp.sum(dpre, axis=0), jnp.sum(de, axis=0)]), place, groups),
        outer(act_one, de),
        outer(act_two, dmod_all),
        own(jnp.sum(dmod_all, axis=0), place, groups),
        o_qkv_w,
        unpacked[6],
        o_out_w,
        unpacked[7],
        o_ff_w1,
        unpacked[8],
        o_ff_w2,
        unpacked[9],
    )


def solution(mesh):
    both, crossed = ("dp", "mp"), ("mp", "dp")
    placed = (
        P("dp", None), P("dp"), P("dp", None), P("dp", None),
        P(), P(), P(), P(), P(), P(), P(), P(), P(), P(),
        P(None, None, None, "mp"), P(None, "mp"),
        P(), P(), P(), P(), P(),
        P(None, None, "mp"), P(None, "mp"), P("mp", None), P(),
        P(None, "mp"), P("mp"), P("mp", None), P(),
        P("dp", None),
    )
    given = (
        P("dp", None), P("dp", None),
        P(None, both), P(None, None, both), P(None, None, both), P(None, both),
        P(None, None, both), P(None, None, both), P(None, None, both),
        P(None, "dp"), P(None, "dp"), P("dp"),
        P(None, None, None, crossed), P(None, crossed),
        P(None, "dp"), P(None, "dp"), P(None, "dp"), P(None, "dp"), P("dp"),
        P(None, "dp", "mp"), P(None, crossed), P("mp", "dp"), P("dp"),
        P("dp", "mp"), P(crossed), P("mp", "dp"), P("dp"),
    )
    return jax.shard_map(local, mesh=mesh, in_specs=placed, out_specs=given, check_vma=False)
```

```python
from functools import partial
import math

import jax
import jax.numpy as jnp
from jax import lax
from jax.experimental import pallas as pl
from jax.experimental.pallas import tpu as pltpu
from jax.sharding import PartitionSpec as P

HEAD_DIM = 64
GAP = 16
HALO = 8
BF = jnp.bfloat16
F32 = jnp.float32
highest = lax.Precision.HIGHEST
NN = (((1,), (0,)), ((), ()))
NT = (((1,), (1,)), ((), ()))
TN = (((0,), (0,)), ((), ()))


def dot(left, right, dims=NN):
    return lax.dot_general(left.astype(BF), right.astype(BF), dims, preferred_element_type=F32)


def precise(left, right, dims=NN):
    one = lax.reduce_precision(left, 8, 7)
    two = lax.reduce_precision(left - one, 8, 7)
    three = left - one - two
    rows = left.shape[0]
    stacked = jnp.concatenate([one, two, three], axis=0).astype(BF)
    product = lax.dot_general(stacked, right, dims, preferred_element_type=F32)
    return product[:rows] + product[rows : 2 * rows] + product[2 * rows :]


@jax.custom_vjp
def expand(onehot, parts):
    return sum(onehot[:, c : c + 1] * parts[c : c + 1] for c in range(parts.shape[0]))


def expand_ahead(onehot, parts):
    return expand(onehot, parts), onehot


def expand_behind(onehot, grad):
    return None, jnp.dot(onehot.T, grad, precision=highest)


expand.defvjp(expand_ahead, expand_behind)


def silu_slope(values):
    sigmoid_val = jax.nn.sigmoid(values)
    return sigmoid_val * (1.0 + values * (1.0 - sigmoid_val))


def layer_norm(values):
    centred = values - jnp.mean(values, axis=-1, keepdims=True)
    variance = jnp.mean(centred * centred, axis=-1, keepdims=True)
    return centred * lax.rsqrt(variance + 1e-06)


def mish(values):
    grown = jnp.exp(jnp.minimum(values, 20.0))
    wide = grown * (grown + 2.0)
    return values * (wide / (wide + 2.0))


def mish_slope(values):
    grown = jnp.exp(jnp.minimum(values, 20.0))
    wide = grown * (grown + 2.0)
    under = 1.0 / (wide + 2.0)
    return wide * under + values * (4.0 * grown * (1.0 + grown) * under * under)


def sum_kernel(axis, size, x_ref, o_ref, slots, send_sems, recv_sems):
    me = lax.axis_index(axis)
    barrier = pltpu.get_barrier_semaphore()
    peers = [lax.rem(me + step, size) for step in range(1, size)]
    for peer in peers:
        pl.semaphore_signal(
            barrier, inc=1, device_id={axis: peer}, device_id_type=pl.DeviceIdType.MESH
        )
    pl.semaphore_wait(barrier, size - 1)
    for step, peer in enumerate(peers):
        pltpu.make_async_remote_copy(
            src_ref=x_ref,
            dst_ref=slots.at[me],
            send_sem=send_sems.at[step],
            recv_sem=recv_sems.at[me],
            device_id={axis: peer},
            device_id_type=pl.DeviceIdType.MESH,
        ).start()
    slots[me] = x_ref[...]
    for step, peer in enumerate(peers):
        copy = pltpu.make_async_remote_copy(
            src_ref=x_ref,
            dst_ref=slots.at[peer],
            send_sem=send_sems.at[step],
            recv_sem=recv_sems.at[peer],
            device_id={axis: peer},
            device_id_type=pl.DeviceIdType.MESH,
        )
        copy.wait_send()
        copy.wait_recv()
    total = slots[0]
    for device in range(1, size):
        total = total + slots[device]
    o_ref[...] = total


def small_sum(values, axis, name):
    size = lax.axis_size(axis)
    whole = pl.BlockSpec(memory_space=pltpu.VMEM)
    return pl.pallas_call(
        partial(sum_kernel, axis, size),
        out_shape=jax.ShapeDtypeStruct(values.shape, F32),
        in_specs=[whole],
        out_specs=whole,
        scratch_shapes=[
            pltpu.VMEM((size,) + values.shape, F32),
            pltpu.SemaphoreType.DMA((size - 1,)),
            pltpu.SemaphoreType.DMA((size,)),
        ],
        compiler_params=pltpu.CompilerParams(
            collective_id=name, has_side_effects=True, vmem_limit_bytes=16 << 20
        ),
    )(values)


def last_kernel(dp, mp, n_all, n_mp, n_both, n_gather, *refs):
    n_in = n_all + n_mp + n_both + n_gather
    ins, outs, rest = refs[:n_in], refs[n_in : 2 * n_in], list(refs[2 * n_in :])

    def take(count):
        return [rest.pop(0) for _ in range(count)]

    own, pair, joint, chip_slots, middle, slots = (
        take(n_all), take(n_all), take(n_all), take(n_all), take(n_all), take(n_in)
    )
    pair_send, pair_recv, chip_send, chip_recv, mp_send, mp_recv, own_sems = rest
    me, z = lax.axis_index("dp"), lax.axis_index("mp")
    chips = dp // 2
    core, chip = lax.rem(me, 2), me // 2
    partner = me + 1 - 2 * core
    other_chips = [lax.rem(chip + step, chips) for step in range(1, chips)]
    other_z = [lax.rem(z + step, mp) for step in range(1, mp)]
    mesh_id = pl.DeviceIdType.MESH
    barrier = pltpu.get_barrier_semaphore()
    greeted = (
        [{"dp": partner}]
        + [{"dp": 2 * q + core} for q in other_chips]
        + [{"mp": peer} for peer in other_z]
    )
    for device in greeted:
        pl.semaphore_signal(barrier, inc=1, device_id=device, device_id_type=mesh_id)
    pl.semaphore_wait(barrier, chips + mp - 1)

    def to_partner(t):
        return pltpu.make_async_remote_copy(
            src_ref=ins[t].at[:, 1 - core],
            dst_ref=pair[t],
            send_sem=pair_send.at[t],
            recv_sem=pair_recv.at[t],
            device_id={"dp": partner},
            device_id_type=mesh_id,
        )

    def to_chip(t, step, mine):
        q = other_chips[step]
        return pltpu.make_async_remote_copy(
            src_ref=joint[t].at[q],
            dst_ref=chip_slots[t].at[mine],
            send_sem=chip_send.at[t, step],
            recv_sem=chip_recv.at[t, mine],
            device_id={"dp": 2 * q + core},
            device_id_type=mesh_id,
        )

    def to_z(t, step, mine):
        peer = other_z[step]
        if t < n_all - 1:
            source = middle[t].at[peer]
        elif t == n_all - 1:
            source = middle[t]
        else:
            source = ins[t].at[peer] if t < n_all + n_mp else ins[t]
        return pltpu.make_async_remote_copy(
            src_ref=source,
            dst_ref=slots[t].at[mine],
            send_sem=mp_send.at[t, step],
            recv_sem=mp_recv.at[t, mine],
            device_id={"mp": peer},
            device_id_type=mesh_id,
        )

    local = []
    for t in range(n_all):
        to_partner(t).start()
        copy = pltpu.make_async_copy(ins[t].at[:, core], own[t], own_sems.at[t])
        copy.start()
        local.append(copy)
    for t in range(n_all, n_in):
        for step in range(mp - 1):
            to_z(t, step, z).start()
        source = ins[t].at[z] if t < n_all + n_mp else ins[t]
        copy = pltpu.make_async_copy(source, slots[t].at[z], own_sems.at[t])
        copy.start()
        local.append(copy)

    def total(ref, size):
        value = ref[0].astype(F32)
        for device in range(1, size):
            value = value + ref[device].astype(F32)
        return value

    for t in range(n_all):
        local[t].wait()
        copy = to_partner(t)
        copy.wait_send()
        copy.wait_recv()
        for q in range(chips):
            value = own[t][q].astype(F32) + pair[t][q].astype(F32)
            joint[t][q] = value.astype(joint[t].dtype)
        for step in range(chips - 1):
            to_chip(t, step, chip).start()
        chip_slots[t][chip] = joint[t][chip]
    for t in range(n_all):
        for step in range(chips - 1):
            copy = to_chip(t, step, other_chips[step])
            copy.wait_send()
            copy.wait_recv()
        value = total(chip_slots[t], chips)
        if t < n_all - 1:
            rows = value.shape[0] // mp
            for device in range(mp):
                part = value[device * rows : (device + 1) * rows]
                middle[t][device] = part.astype(middle[t].dtype)
            slots[t][z] = middle[t][z]
        else:
            middle[t][...] = value
            slots[t][z] = value
        for step in range(mp - 1):
            to_z(t, step, z).start()
    for t in list(range(n_all, n_in)) + list(range(n_all)):
        if t >= n_all:
            local[t].wait()
        for step in range(mp - 1):
            copy = to_z(t, step, other_z[step])
            copy.wait_send()
            copy.wait_recv()
        if t < n_in - n_gather:
            outs[t][...] = total(slots[t], mp)
        else:
            outs[t][...] = slots[t][...].astype(F32)


def last_sums(over_all, small, over_mp, both, gathered):
    dp, mp = lax.axis_size("dp"), lax.axis_size("mp")
    chips = dp // 2
    everywhere = [v.reshape((chips, 2) + v.shape[1:]) for v in list(over_all) + [small]]
    ins = everywhere + list(over_mp) + list(both) + list(gathered)
    n_all, n_mp, n_both, n_gather = len(everywhere), len(over_mp), len(both), len(gathered)
    halves = [pltpu.VMEM((chips,) + v.shape[2:], v.dtype) for v in everywhere]
    outs, middle, slots = [], [], []
    for t, value in enumerate(ins):
        if t < n_all - 1:
            shape = (value.shape[2] // mp, value.shape[3])
            middle.append(pltpu.VMEM((mp,) + shape, value.dtype))
        elif t == n_all - 1:
            shape = value.shape[2:]
            middle.append(pltpu.VMEM(shape, value.dtype))
        else:
            shape = value.shape[1:] if t < n_all + n_mp else value.shape
        slots.append(pltpu.VMEM((mp,) + shape, value.dtype))
        outs.append((mp,) + shape if t >= len(ins) - n_gather else shape)
    dma = pltpu.SemaphoreType.DMA
    return pl.pallas_call(
        partial(last_kernel, dp, mp, n_all, n_mp, n_both, n_gather),
        out_shape=[jax.ShapeDtypeStruct(shape, F32) for shape in outs],
        in_specs=[pl.BlockSpec(memory_space=pl.ANY)] * len(ins),
        out_specs=[pl.BlockSpec(memory_space=pltpu.VMEM)] * len(ins),
        scratch_shapes=halves * 4
        + middle
        + slots
        + [
            dma((n_all,)),
            dma((n_all,)),
            dma((n_all, chips)),
            dma((n_all, chips)),
            dma((len(ins), mp)),
            dma((len(ins), mp)),
            dma((len(ins),)),
        ],
        compiler_params=pltpu.CompilerParams(
            collective_id=3, has_side_effects=True, vmem_limit_bytes=56 << 20
        ),
    )(*ins)


def conv_norm(hidden, segment, conv, vec, gain):
    taps = conv.shape[0]
    reach = taps // 2
    rows = hidden.shape[0]
    padded = jnp.pad(hidden, ((reach, reach), (0, 0)))
    seg_padded = jnp.pad(segment, (reach, reach), constant_values=-1)
    mixture = vec[0]
    for tap in range(taps):
        keep = (seg_padded[tap : tap + rows] == segment) & (segment >= 0)
        mixture = mixture + conv[tap] * jnp.where(keep[:, None], padded[tap : tap + rows], 0.0)
    return layer_norm(mixture) * gain + vec[1]


def activate(pre, bias):
    return jax.nn.gelu(pre + bias, approximate=False)


def clip_squares(own, active):
    return jnp.dot(own.T, active * active, precision=highest)


def respond(active, squares, onehot, scale, shift):
    norms = jnp.sqrt(jnp.maximum(squares, 1.0))
    ratio = norms / (jnp.mean(norms, axis=-1, keepdims=True) + 1e-06)
    return scale * (active * expand(onehot, ratio)) + shift + active


def text_ahead(hidden, segment, onehot, own, conv, vec, gain, up, hid, down):
    normed, norm_pull = jax.vjp(
        lambda h, c, v, g: conv_norm(h, segment, c, v, g), hidden, conv, vec, gain
    )
    normed = normed.astype(BF)
    active, act_pull = jax.vjp(activate, dot(normed, up), hid[0])
    squares, square_pull = jax.vjp(lambda a: clip_squares(own, a), active)
    squares = small_sum(squares, "mp", 1)
    grown, respond_pull = jax.vjp(
        lambda a, s, g, b: respond(a, s, onehot, g, b), active, squares, hid[1], hid[2]
    )
    grown = grown.astype(BF)
    result = hidden + dot(grown, down) + vec[2]
    return result, (norm_pull, normed, act_pull, square_pull, respond_pull, grown)


def text_behind(kept, grad, up, down, extra):
    norm_pull, normed, act_pull, square_pull, respond_pull, grown = kept
    grad_low = grad.astype(BF)
    g_out = jnp.sum(grad, axis=0)
    g_down = dot(grad_low, grown, TN)
    grad_active, grad_squares, g_scale, g_shift = respond_pull(dot(grad_low, down, NT))
    if extra is None:
        grad_squares = small_sum(grad_squares, "mp", 1)
    else:
        joined = small_sum(jnp.concatenate([grad_squares, extra], axis=1), "mp", 2)
        grad_squares, extra = joined[:, : grad_squares.shape[1]], joined[:, grad_squares.shape[1] :]
    grad_active = grad_active + square_pull(grad_squares)[0]
    grad_pre, g_bias = act_pull(grad_active)
    pre_low = grad_pre.astype(BF)
    g_up = dot(pre_low, normed, TN)
    grad_hidden, g_conv, g_vec, g_gain = norm_pull(dot(pre_low, up, NT))
    g_vec = g_vec.at[2].add(g_out)
    return (
        grad + grad_hidden,
        (g_conv, g_vec, g_gain, g_up, jnp.stack([g_bias, g_scale, g_shift]), g_down),
        extra,
    )


def spread(values, starts, ends):
    rows = values.shape[0]
    clips = starts.shape[0]
    at = jnp.arange(rows, dtype=jnp.int32)
    total = rows + GAP * clips + 2 * GAP
    out = None
    for c in range(clips):
        keep = (at >= starts[c]) & (at < ends[c])
        part = jnp.where(keep[:, None], values, 0)
        lead = GAP + GAP * c
        part = jnp.pad(part, ((lead, total - lead - rows), (0, 0)))
        out = part if out is None else out + part
    return out


def gather_back(values, starts, ends):
    clips = starts.shape[0]
    rows = values.shape[0] - GAP * clips
    at = jnp.arange(rows, dtype=jnp.int32)
    out = None
    for c in range(clips):
        keep = (at >= starts[c]) & (at < ends[c])
        part = jnp.where(keep[:, None], values[GAP * c : GAP * c + rows], 0)
        out = part if out is None else out + part
    return out


def conv_kernel(taps, turned, x_ref, w_ref, o_ref, full_ref):
    rows, width = o_ref.shape
    group = w_ref.shape[1]
    first = GAP - taps // 2

    @pl.when(pl.program_id(0) == 0)
    def _():
        lane = lax.broadcasted_iota(jnp.int32, (group, width), 1) // group
        for k in range(taps):
            tap = w_ref[taps - 1 - k if turned else k]
            for g in range(width // group):
                piece = jnp.where(lane == g, tap, jnp.zeros_like(tap))
                if turned:
                    full_ref[g * group : (g + 1) * group, k * width : (k + 1) * width] = piece
                else:
                    full_ref[k * width + g * group : k * width + (g + 1) * group, :] = piece

    columns = [x_ref[first + k : first + k + rows, :].astype(BF) for k in range(taps)]
    o_ref[...] = lax.dot_general(
        jnp.concatenate(columns, axis=1),
        full_ref[...],
        NT if turned else NN,
        preferred_element_type=F32,
    )


def conv_chunk(rows):
    for size in (528, 352, 256, 128, 64, 32, 16):
        if rows % size == 0:
            return size
    return rows


def apply_conv(spread_rows, weight, turned):
    rows = spread_rows.shape[0] - 2 * GAP
    width = spread_rows.shape[1]
    taps, group = weight.shape[:2]
    chunk = conv_chunk(rows)
    return pl.pallas_call(
        partial(conv_kernel, taps, turned),
        out_shape=jax.ShapeDtypeStruct((rows, width), F32),
        grid=(rows // chunk,),
        in_specs=[
            pl.BlockSpec((pl.Element(chunk + 2 * GAP), pl.Element(width)), lambda i: (i * chunk, 0)),
            pl.BlockSpec(weight.shape, lambda i: (0, 0, 0), pipeline_mode=pl.Buffered(1)),
        ],
        out_specs=pl.BlockSpec((chunk, width), lambda i: (i, 0)),
        scratch_shapes=[
            pltpu.VMEM((width, taps * width) if turned else (taps * width, width), BF)
        ],
        compiler_params=pltpu.CompilerParams(vmem_limit_bytes=48 << 20),
        cost_estimate=pl.CostEstimate(
            flops=2 * rows * taps * width * width, bytes_accessed=8 << 20, transcendentals=0
        ),
    )(spread_rows, weight)


def conv_grad_kernel(taps, group, x_ref, g_ref, o_ref):
    rows, width = g_ref.shape
    first = GAP - taps // 2
    turned = g_ref[...].T.astype(BF)

    @pl.when(pl.program_id(0) == 0)
    def _():
        o_ref[...] = jnp.zeros_like(o_ref)

    for k in range(taps):
        window = x_ref[first + k : first + k + rows, :].astype(BF)
        product = jnp.dot(turned, window, preferred_element_type=F32)
        for g in range(width // group):
            own = slice(g * group, (g + 1) * group)
            o_ref[own, k * group : (k + 1) * group] += product[own, own]


def conv_grad(spread_rows, grads, taps, group):
    rows, width = grads.shape
    chunk = conv_chunk(rows)
    return pl.pallas_call(
        partial(conv_grad_kernel, taps, group),
        out_shape=jax.ShapeDtypeStruct((width, taps * group), F32),
        grid=(rows // chunk,),
        in_specs=[
            pl.BlockSpec((pl.Element(chunk + 2 * GAP), pl.Element(width)), lambda i: (i * chunk, 0)),
            pl.BlockSpec((chunk, width), lambda i: (i, 0)),
        ],
        out_specs=pl.BlockSpec((width, taps * group), lambda i: (0, 0)),
        compiler_params=pltpu.CompilerParams(vmem_limit_bytes=48 << 20),
        cost_estimate=pl.CostEstimate(
            flops=2 * rows * taps * width * width, bytes_accessed=8 << 20, transcendentals=0
        ),
    )(spread_rows, grads)


LANES = 128


def pair_split(columns):
    pairs = columns.reshape(*columns.shape[:-1], -1, LANES // 2, 2)
    return jnp.swapaxes(pairs, -1, -2).reshape(columns.shape)


def pair_merge(columns):
    pairs = columns.reshape(*columns.shape[:-1], -1, 2, LANES // 2)
    return jnp.swapaxes(pairs, -1, -2).reshape(columns.shape)


def project_kernel(x_ref, w_ref, b_ref, cos_ref, sin_ref, *out_refs):
    cos, sin = cos_ref[...], sin_ref[...]
    for p in range(3):
        value = jnp.dot(x_ref[...], w_ref[p], preferred_element_type=F32) + b_ref[p : p + 1, :]
        for at, out_ref in enumerate(out_refs):
            piece = value[:, at * LANES : (at + 1) * LANES]
            if p < 2:
                piece = piece * cos + pltpu.roll(piece, LANES // 2, 1) * sin
            out_ref[p] = piece.astype(BF)


def project(normed, weight, bias, cos, sin):
    rows = normed.shape[0]
    shards, _, width, cols = weight.shape
    parts = cols // LANES
    return pl.pallas_call(
        project_kernel,
        out_shape=[jax.ShapeDtypeStruct((shards, 3, rows, LANES), BF)] * parts,
        grid=(shards,),
        in_specs=[
            pl.BlockSpec((rows, width), lambda i: (0, 0)),
            pl.BlockSpec((None, 3, width, cols), lambda i: (i, 0, 0, 0)),
            pl.BlockSpec((None, 3, cols), lambda i: (i, 0, 0)),
            pl.BlockSpec((rows, LANES), lambda i: (0, 0)),
            pl.BlockSpec((rows, LANES), lambda i: (0, 0)),
        ],
        out_specs=[pl.BlockSpec((None, 3, rows, LANES), lambda i: (i, 0, 0, 0))] * parts,
        compiler_params=pltpu.CompilerParams(vmem_limit_bytes=32 << 20),
        cost_estimate=pl.CostEstimate(
            flops=6 * rows * width * width, bytes_accessed=10 << 20, transcendentals=0
        ),
    )(normed, weight, bias, cos, sin)


def head_masks(width):
    heads = width // HEAD_DIM
    lane = lax.broadcasted_iota(jnp.int32, (1, width), 1)
    half = HEAD_DIM // 2
    paired = [((lane % (width // 2)) // half) == h for h in range(heads)]
    plain = [(lane // HEAD_DIM) == h for h in range(heads)]
    return heads, paired, plain


def attend_kernel(bounds, q_ref, k_ref, v_ref, sq_ref, sk_ref, o_ref, full_ref, lse_ref):
    i = pl.program_id(0)
    q = q_ref[...]
    rows, width = q.shape
    heads, paired, plain = head_masks(width)
    scale = HEAD_DIM**-0.5
    q_heads = [jnp.where(paired[h], q, jnp.zeros_like(q)) for h in range(heads)]
    sq = sq_ref[...]

    def step(kb, carry):
        tops, sums, acc = carry
        k, v = k_ref[kb], v_ref[kb]
        same = sq == sk_ref[kb]
        new_tops, new_sums = [], []
        decay, extra = None, None
        for h in range(heads):
            scores = lax.dot_general(q_heads[h], k, NT, preferred_element_type=F32) * scale
            scores = jnp.where(same, scores, -1e30)
            top = jnp.maximum(tops[h], jnp.max(scores, axis=-1, keepdims=True))
            fade = jnp.exp(tops[h] - top)
            weight = jnp.exp(scores - top)
            new_tops.append(top)
            new_sums.append(fade * sums[h] + jnp.sum(weight, axis=-1, keepdims=True))
            v_head = jnp.where(plain[h], v, jnp.zeros_like(v))
            part = jnp.dot(weight.astype(BF), v_head, preferred_element_type=F32)
            extra = part if extra is None else extra + part
            decay = fade * jnp.ones((1, width), F32) if h == 0 else jnp.where(plain[h], fade, decay)
        return tuple(new_tops), tuple(new_sums), acc * decay + extra

    start = (
        tuple(jnp.full((rows, 1), -1e30, F32) for _ in range(heads)),
        tuple(jnp.zeros((rows, 1), F32) for _ in range(heads)),
        jnp.zeros((rows, width), F32),
    )
    tops, sums, acc = lax.fori_loop(bounds[i, 0], bounds[i, 1], step, start)
    lane = lax.broadcasted_iota(jnp.int32, (1, lse_ref.shape[1]), 1)
    share = jnp.ones((rows, width), F32)
    logs = jnp.zeros((rows, lse_ref.shape[1]), F32)
    for h in range(heads):
        share = jnp.where(plain[h], 1.0 / sums[h], share)
        logs = jnp.where(lane == h, tops[h] + jnp.log(sums[h]), logs)
    full = acc * share
    full_ref[...] = full
    o_ref[...] = full.astype(BF)
    lse_ref[...] = logs


def attend(qkv, seg_rows, seg_blocks, bounds, block):
    shards, _, rows, width = qkv.shape
    total = shards * rows
    per = rows // block
    grid_spec = pltpu.PrefetchScalarGridSpec(
        num_scalar_prefetch=1,
        grid=(total // block,),
        in_specs=[
            pl.BlockSpec((None, None, block, width), lambda i, b: (i // per, 0, i % per, 0)),
            pl.BlockSpec((shards, None, rows, width), lambda i, b: (0, 1, 0, 0)),
            pl.BlockSpec((shards, None, rows, width), lambda i, b: (0, 2, 0, 0)),
            pl.BlockSpec((block, 1), lambda i, b: (i, 0)),
            pl.BlockSpec((shards, 1, rows), lambda i, b: (0, 0, 0)),
        ],
        out_specs=[
            pl.BlockSpec((block, width), lambda i, b: (i, 0)),
            pl.BlockSpec((block, width), lambda i, b: (i, 0)),
            pl.BlockSpec((block, 128), lambda i, b: (i, 0)),
        ],
    )
    return pl.pallas_call(
        attend_kernel,
        out_shape=[
            jax.ShapeDtypeStruct((total, width), BF),
            jax.ShapeDtypeStruct((total, width), F32),
            jax.ShapeDtypeStruct((total, 128), F32),
        ],
        grid_spec=grid_spec,
        compiler_params=pltpu.CompilerParams(vmem_limit_bytes=48 << 20),
        cost_estimate=pl.CostEstimate(
            flops=4 * total * total * width, bytes_accessed=8 << 20, transcendentals=0
        ),
    )(bounds, qkv, qkv, qkv, seg_rows, seg_blocks)


def unrotate(values, cos, sin):
    return values * cos - pltpu.roll(values, LANES // 2, 1) * sin


def attend_back_kernel(
    bounds, q_ref, k_ref, v_ref, full_ref, lse_ref, do_ref, sq_ref, sk_ref, cos_ref, sin_ref,
    out_ref, dk_ref, dv_ref,
):
    i = pl.program_id(0)
    q, do = q_ref[...], do_ref[...]
    rows, width = q.shape
    shards, _, shard_rows, _ = out_ref.shape
    per = shard_rows // rows
    heads, paired, plain = head_masks(width)
    scale = HEAD_DIM**-0.5

    @pl.when(i == 0)
    def _():
        dk_ref[...] = jnp.zeros_like(dk_ref)
        dv_ref[...] = jnp.zeros_like(dv_ref)

    zero = jnp.zeros_like(q)
    q_heads = [jnp.where(paired[h], q, zero) for h in range(heads)]
    do_heads = [jnp.where(plain[h], do, zero) for h in range(heads)]
    product = do.astype(F32) * full_ref[...]
    deltas = [jnp.sum(jnp.where(plain[h], product, 0.0), axis=-1, keepdims=True) for h in range(heads)]
    logs = [lse_ref[:, h : h + 1] for h in range(heads)]
    sq = sq_ref[...]

    def step(kb, dq):
        k, v = k_ref[kb], v_ref[kb]
        same = sq == sk_ref[kb]
        dk, dv = dk_ref[kb], dv_ref[kb]
        for h in range(heads):
            scores = lax.dot_general(q_heads[h], k, NT, preferred_element_type=F32) * scale
            weight = jnp.where(same, jnp.exp(scores - logs[h]), 0.0)
            dp = lax.dot_general(do_heads[h], v, NT, preferred_element_type=F32)
            ds = (weight * (dp - deltas[h]) * scale).astype(BF)
            dv = dv + lax.dot_general(weight.astype(BF), do_heads[h], TN, preferred_element_type=F32)
            dk = dk + lax.dot_general(ds, q_heads[h], TN, preferred_element_type=F32)
            k_head = jnp.where(paired[h], k, jnp.zeros_like(k))
            dq = dq + jnp.dot(ds, k_head, preferred_element_type=F32)
        dk_ref[kb] = dk
        dv_ref[kb] = dv
        return dq

    dq = lax.fori_loop(bounds[i, 0], bounds[i, 1], step, jnp.zeros((rows, width), F32))
    here = pl.ds(pl.multiple_of(i * rows, rows), rows)
    inside = pl.ds(pl.multiple_of((i % per) * rows, rows), rows)
    out_ref[i // per, 0, inside, :] = unrotate(dq, cos_ref[here, :], sin_ref[here, :]).astype(BF)

    @pl.when(i == pl.num_programs(0) - 1)
    def _():
        for s in range(shards):
            own = slice(s * shard_rows, (s + 1) * shard_rows)
            out_ref[s, 1] = unrotate(dk_ref[s], cos_ref[own, :], sin_ref[own, :]).astype(BF)
            out_ref[s, 2] = dv_ref[s].astype(BF)


def attend_back(qkv, full, logs, grads, seg_rows, seg_blocks, cos, sin, bounds, block):
    shards, _, rows, width = qkv.shape
    total = shards * rows
    per = rows // block
    grid_spec = pltpu.PrefetchScalarGridSpec(
        num_scalar_prefetch=1,
        grid=(total // block,),
        in_specs=[
            pl.BlockSpec((None, None, block, width), lambda i, b: (i // per, 0, i % per, 0)),
            pl.BlockSpec((shards, None, rows, width), lambda i, b: (0, 1, 0, 0)),
            pl.BlockSpec((shards, None, rows, width), lambda i, b: (0, 2, 0, 0)),
            pl.BlockSpec((block, width), lambda i, b: (i, 0)),
            pl.BlockSpec((block, 128), lambda i, b: (i, 0)),
            pl.BlockSpec((block, width), lambda i, b: (i, 0)),
            pl.BlockSpec((block, 1), lambda i, b: (i, 0)),
            pl.BlockSpec((shards, 1, rows), lambda i, b: (0, 0, 0)),
            pl.BlockSpec((total, width), lambda i, b: (0, 0)),
            pl.BlockSpec((total, width), lambda i, b: (0, 0)),
        ],
        out_specs=pl.BlockSpec((shards, 3, rows, width), lambda i, b: (0, 0, 0, 0)),
        scratch_shapes=[
            pltpu.VMEM((shards, rows, width), F32),
            pltpu.VMEM((shards, rows, width), F32),
        ],
    )
    return pl.pallas_call(
        attend_back_kernel,
        out_shape=jax.ShapeDtypeStruct((shards, 3, rows, width), BF),
        grid_spec=grid_spec,
        compiler_params=pltpu.CompilerParams(vmem_limit_bytes=48 << 20),
        cost_estimate=pl.CostEstimate(
            flops=10 * total * total * width, bytes_accessed=16 << 20, transcendentals=0
        ),
    )(bounds, qkv, qkv, qkv, full, logs, grads, seg_rows, seg_blocks, cos, sin)


def exchange(values, axis):
    return lax.all_to_all(values, axis, 0, 0)


def local(
    mel_pair, text_ids, clip_lengths, t_index,
    txt_table, txt_conv, txt_vec, txt_gain, txt_up, txt_hid, txt_down,
    emb_mel, emb_text, emb_bias, pos_conv, pos_bias,
    time_w1, time_bias, time_w2, ada_w, ada_b,
    qkv_w, qkv_b, out_w, out_b, ff_w1, ff_b1, ff_w2, ff_b2, out_grad,
):
    total = mel_pair.shape[0]
    width = emb_mel.shape[1]
    shards, groups = lax.axis_size("mp"), lax.axis_size("dp")
    rank, place = lax.axis_index("mp"), lax.axis_index("dp")
    rows = total // shards
    cols = width // shards
    clips = clip_lengths.shape[1]
    first = rank * rows
    taps = pos_conv.shape[1]
    group = pos_conv.shape[2]

    def spread_slice(weight, axis):
        piece = weight.shape[axis] // groups
        return lax.dynamic_slice_in_dim(weight, place * piece, piece, axis)

    def to_all(piece, axis_name="mp"):
        size = lax.axis_size(axis_name)
        return lax.all_to_all(jnp.broadcast_to(piece[None], (size,) + piece.shape), axis_name, 0, 0)

    def gather(piece, axis):
        return lax.all_gather(piece, "dp", axis=axis, tiled=True)

    def three(values):
        one = lax.reduce_precision(values, 8, 7)
        two = lax.reduce_precision(values - one, 8, 7)
        return jnp.concatenate([one, two, values - one - two], axis=0).astype(BF)

    qkv_piece = spread_slice(qkv_w, 1)
    qkv_piece = jnp.concatenate([pair_split(qkv_piece[:2]), qkv_piece[2:]], axis=0)
    in_rows = qkv_piece.shape[1]
    biases = jnp.concatenate(
        [pair_split(qkv_b[:2]), qkv_b[2:], ff_b1.reshape(-1, cols)], axis=0
    )
    bias_rows = biases.shape[0]
    biases = three(biases)
    biases = jnp.pad(biases, ((0, -biases.shape[0] % 16), (0, 0)))
    received = to_all(jnp.concatenate([qkv_piece.reshape(3 * in_rows, cols), biases], axis=0))
    qkv_full = gather(received[:, : 3 * in_rows].reshape(shards, 3, in_rows, cols), 2)
    biases = received[:, 3 * in_rows :].astype(F32)
    biases = sum(biases[:, i * bias_rows : (i + 1) * bias_rows] for i in range(3))
    qkv_bias = biases[:, :3]
    b1_full = biases[:, 3:].reshape(-1)
    out_piece, w2_piece, w1_piece = spread_slice(out_w, 0), spread_slice(ff_w2, 0), spread_slice(ff_w1, 0)
    w1_shape = w1_piece.shape
    cut = [out_piece.shape[0], out_piece.shape[0] + w2_piece.shape[0]]
    received = to_all(jnp.concatenate([out_piece, w2_piece, w1_piece.reshape(-1, width)], axis=0))
    out_full = gather(received[:, : cut[0]], 1).reshape(width, width)
    w1_piece = received[:, cut[1] :].reshape((shards,) + w1_shape).transpose(1, 0, 2)
    w1_full = gather(w1_piece.reshape(w1_shape[0], -1), 0)
    w2_full = gather(received[:, cut[0] : cut[1]], 1).reshape(-1, width)
    all_steps = lax.all_gather(t_index, "dp", tiled=True).reshape(-1)

    lengths = clip_lengths[0]
    clip_index = jnp.arange(clips, dtype=jnp.int32)
    ends = jnp.sum(jnp.where(clip_index[:, None] >= clip_index[None, :], lengths[None, :], 0), axis=1)
    starts = ends - lengths
    frames = jnp.arange(total, dtype=jnp.int32)
    member = (frames[:, None] >= starts[None, :]) & (frames[:, None] < ends[None, :])
    segment = jnp.sum(member * clip_index[None, :], axis=1).astype(jnp.int32)
    position = frames - jnp.sum(member * starts[None, :], axis=1)
    ext = rows + 2 * HALO
    ids = lax.dynamic_slice_in_dim(jnp.pad(text_ids, (HALO, HALO)), first, ext)
    seg_ext = lax.dynamic_slice_in_dim(jnp.pad(segment, (HALO, HALO), constant_values=-1), first, ext)
    hot_ext = (seg_ext[:, None] == clip_index[None, :]).astype(F32)
    ext_index = jnp.arange(ext, dtype=jnp.int32)
    inside = (ext_index >= HALO) & (ext_index < HALO + rows)
    own_ext = jnp.where(inside[:, None], hot_ext, 0.0)
    hot = hot_ext[HALO : HALO + rows]

    def time_path(steps):
        half = time_w1.shape[0] // 2
        frequency = jnp.exp(jnp.arange(half, dtype=F32) * (-math.log(10000.0) / (half - 1)))
        angles = steps.astype(F32)[:, None] * frequency[None, :]
        sinusoid = jnp.concatenate([jnp.sin(angles), jnp.cos(angles)], axis=-1)
        pre_one = precise(sinusoid, time_w1) + time_bias[0]
        act_one = jax.nn.silu(pre_one)
        time_vec = precise(act_one, time_w2) + time_bias[1]
        return sinusoid, pre_one, act_one, time_vec, jax.nn.silu(time_vec)

    mod = precise(time_path(t_index[0])[4], ada_w) + ada_b

    hidden = jnp.take(txt_table, ids, axis=0).astype(F32)
    kept = []
    blocks = txt_conv.shape[0]
    for b in range(blocks):
        hidden, saved = text_ahead(
            hidden, seg_ext, hot_ext, own_ext, txt_conv[b], txt_vec[b], txt_gain[b],
            txt_up[b], txt_hid[b], txt_down[b],
        )
        kept.append(saved)
    text = hidden[HALO : HALO + rows].astype(BF)

    mel = lax.dynamic_slice_in_dim(mel_pair, first, rows)
    x0 = dot(mel, emb_mel) + dot(text, emb_text) + emb_bias

    def to_channels(values):
        blocks_of = values.reshape(rows, shards, cols).transpose(1, 0, 2)
        return exchange(blocks_of, "mp").reshape(total, cols)

    def to_rows(values):
        return exchange(values.reshape(shards, rows, cols), "mp").transpose(1, 0, 2).reshape(rows, width)

    spread_in = spread(to_channels(x0.astype(BF)).astype(F32), starts, ends)
    real = spread(jnp.ones((total, 1), F32), starts, ends)
    pre_a = apply_conv(spread_in, pos_conv[0], False) + pos_bias[0]
    y_a = jnp.pad(
        jnp.where(real[GAP:-GAP] > 0, mish(pre_a), 0.0).astype(BF).astype(F32), ((GAP, GAP), (0, 0))
    )
    pre_b = apply_conv(y_a, pos_conv[1], False) + pos_bias[1]
    c_pos = to_rows(gather_back(mish(pre_b).astype(BF), starts, ends))
    x1 = x0 + c_pos.astype(F32)

    def modulate(state, mod_in, shift_part, scale_part):
        scale = expand(hot, mod_in[:, scale_part * width : (scale_part + 1) * width])
        shift = expand(hot, mod_in[:, shift_part * width : (shift_part + 1) * width])
        return layer_norm(state) * (1.0 + scale) + shift

    n1, n1_pull = jax.vjp(lambda s, m: modulate(s, m, 0, 1), x1, mod)
    n1 = n1.astype(BF)
    inverse = jnp.exp(jnp.arange(0, HEAD_DIM, 2, dtype=F32) * (-math.log(10000.0) / HEAD_DIM))
    angles = position.astype(F32)[:, None] * jnp.tile(inverse, LANES // inverse.shape[0])[None, :]
    cos = jnp.cos(angles)
    sin = jnp.sin(angles) * jnp.where(jnp.arange(LANES) < LANES // 2, -1.0, 1.0)
    cos_own = lax.dynamic_slice_in_dim(cos, first, rows)
    sin_own = lax.dynamic_slice_in_dim(sin, first, rows)
    parts = range(cols // LANES)
    qkv = [exchange(v, "mp") for v in project(n1, qkv_full, qkv_bias, cos_own, sin_own)]
    block = 256
    heads_of = segment[::block]
    tails_of = segment[block - 1 :: block]
    low_key = jnp.sum(jnp.where(heads_of[:, None] == clip_index, starts[None, :], 0), axis=1)
    high_key = jnp.sum(jnp.where(tails_of[:, None] == clip_index, ends[None, :], 0), axis=1)
    bounds = jnp.stack([low_key // rows, (high_key + rows - 1) // rows], axis=1).astype(jnp.int32)
    seg_rows = segment[:, None]
    seg_blocks = segment.reshape(shards, 1, rows)
    attended = [attend(qkv[h], seg_rows, seg_blocks, bounds, block) for h in parts]
    o_rows = jnp.stack([exchange(a[0].reshape(shards, rows, LANES), "mp") for a in attended])
    o_rows = o_rows.transpose(2, 1, 0, 3).reshape(rows, width)

    def residual(state, mod_in, summed, bias, part):
        return state + expand(hot, mod_in[:, part * width : (part + 1) * width]) * (summed + bias)

    x2, att_pull = jax.vjp(
        lambda s, m, a, b: residual(s, m, a, b, 2), x1, mod, dot(o_rows, out_full), out_b
    )

    n2, n2_pull = jax.vjp(lambda s, m: modulate(s, m, 3, 4), x2, mod)
    n2 = n2.astype(BF)
    r, r_pull = jax.vjp(
        lambda v, b: jax.nn.gelu(v + b, approximate=True), dot(n2, w1_full), b1_full
    )
    r = r.astype(BF)
    out, ff_pull = jax.vjp(lambda s, m, a, b: residual(s, m, a, b, 5), x2, mod, dot(r, w2_full), ff_b2)

    grad = lax.dynamic_slice_in_dim(out_grad, first, rows).astype(F32)
    dx2, dmod_a, df, g_ff_b2 = ff_pull(grad)
    df = df.astype(BF)
    g_ff_w2 = dot(df, r, TN)
    dh, g_ff_b1 = r_pull(dot(df, w2_full, NT))
    g_ff_b1 = jnp.sum(dh.astype(BF).astype(F32), axis=0)
    dh = dh.astype(BF)
    g_ff_w1 = dot(n2, dh, TN)
    more, dmod_b = n2_pull(dot(dh, w1_full, NT))
    dx2 = dx2 + more

    def for_dp(matrix):
        return matrix.astype(BF).reshape(groups, matrix.shape[0] // groups, matrix.shape[1])

    def by_rank(matrix):
        return matrix.reshape(matrix.shape[0], shards, -1).transpose(1, 0, 2)

    def scatter_dp(matrix):
        return lax.psum_scatter(matrix.astype(BF), "dp", scatter_dimension=0, tiled=True)

    sent_w1, sent_w2 = scatter_dp(g_ff_w1), scatter_dp(g_ff_w2)

    dx1, dmod_c, da, g_out_b = att_pull(dx2)
    da = da.astype(BF)
    g_out_w = dot(da, o_rows, TN)
    do = dot(da, out_full, NT).astype(BF).reshape(rows, shards, -1, LANES)
    dqkv = []
    for h in parts:
        do_part = exchange(do[:, :, h].transpose(1, 0, 2), "mp").reshape(total, LANES)
        d_part = attend_back(
            qkv[h], attended[h][1], attended[h][2], do_part, seg_rows, seg_blocks, cos, sin, bounds, block
        )
        dqkv.append(exchange(d_part, "mp"))
    result = lax.all_gather(out.astype(BF), "mp", tiled=True)
    result, dqkv = lax.optimization_barrier((result, dqkv))
    result = result.astype(F32)
    dqkv = jnp.stack(dqkv).transpose(3, 1, 2, 0, 4).reshape(rows, 3 * width)
    g_qkv_w = dot(n1, dqkv, TN)
    g_qkv_b = jnp.sum(dqkv.astype(F32), axis=0).reshape(shards, 3, cols)
    w_all = qkv_full.transpose(2, 0, 1, 3).reshape(width, 3 * width)
    more, dmod_d = n1_pull(dot(dqkv, w_all, NT))
    dx1 = dx1 + more
    sent_w1, sent_w2, dx1 = lax.optimization_barrier((sent_w1, sent_w2, dx1))
    ff_pair = jnp.concatenate([by_rank(sent_w1), by_rank(sent_w2)], axis=2)
    sent_qkv, sent_out = scatter_dp(g_qkv_w), scatter_dp(g_out_w)

    dmod = dmod_a + dmod_b + dmod_c + dmod_d

    slope_b = gather_back(mish_slope(pre_b), starts, ends)
    dy_b = to_channels(dx1.astype(BF)).astype(F32) * slope_b
    g_pos_b = jnp.sum(dy_b, axis=0)
    dy_b = spread(dy_b.astype(BF).astype(F32), starts, ends)
    dy_a = apply_conv(dy_b, pos_conv[1], True) * mish_slope(pre_a)
    dy_a = jnp.where(real[GAP:-GAP] > 0, dy_a, 0.0)
    g_pos_a = jnp.sum(dy_a, axis=0)
    dy_a = jnp.pad(dy_a.astype(BF).astype(F32), ((GAP, GAP), (0, 0)))
    dc = gather_back(
        apply_conv(dy_a, pos_conv[0], True).astype(BF), starts, ends
    )
    ff_got, dc = lax.optimization_barrier((exchange(ff_pair, "mp"), dc))
    dx0_full = dx1 + to_rows(dc).astype(F32)
    g_conv = jnp.concatenate(
        [conv_grad(spread_in, dy_a[GAP:-GAP], taps, group), conv_grad(y_a, dy_b[GAP:-GAP], taps, group)],
        axis=1,
    )
    sent_qkv, sent_out, dx0_full = lax.optimization_barrier((sent_qkv, sent_out, dx0_full))
    at_pair = jnp.concatenate([by_rank(sent_qkv), by_rank(sent_out)], axis=2)
    sent_conv = scatter_dp(g_conv)

    g_emb_bias = jnp.sum(dx0_full, axis=0)
    dx0 = dx0_full.astype(BF)
    mel_grad = dot(dx0, emb_mel, NT).astype(BF)
    g_emb = jnp.concatenate([dot(dx0, text, TN), dot(dx0, mel, TN)], axis=1)
    sent_emb = scatter_dp(g_emb)
    text_width = text.shape[1]

    dtext = jnp.pad(dot(dx0, emb_text, NT), ((HALO, HALO), (0, 0)))
    text_grads = [None] * blocks
    extra = dmod
    at_got, dtext = lax.optimization_barrier((exchange(at_pair, "mp"), dtext))
    for b in reversed(range(blocks)):
        dtext, text_grads[b], summed = text_behind(kept[b], dtext, txt_up[b], txt_down[b], extra)
        if extra is not None:
            dmod_all = lax.all_gather(summed, "dp", tiled=True)
            sent_conv, dtext = lax.optimization_barrier((sent_conv, dtext))
        extra = None
    sent_emb, dtext = lax.optimization_barrier((sent_emb, dtext))
    vocab = txt_table.shape[0]
    wide = -(-vocab // 128) * 128
    chosen = (ids[:, None] == jnp.arange(wide, dtype=jnp.int32)[None, :]).astype(BF)
    g_table = dot(dtext, chosen, TN)
    hidden_width = txt_up.shape[2]

    def placed(values):
        full = jnp.zeros((shards,) + values.shape, F32)
        return lax.dynamic_update_slice_in_dim(full, values[None], rank, 0)

    g_pos_bias = placed(jnp.stack([g_pos_a, g_pos_b])).transpose(1, 0, 2).reshape(2, width)
    g_qkv_b = jnp.concatenate([pair_merge(g_qkv_b[:, :2]), g_qkv_b[:, 2:]], axis=1)
    g_qkv_b = g_qkv_b.transpose(1, 0, 2).reshape(3, width)
    small = [
        (jnp.stack([g[0] for g in text_grads]), "both"),
        (jnp.stack([g[1] for g in text_grads]), "both"),
        (jnp.stack([g[2] for g in text_grads]), "both"),
        (jnp.stack([g[4] for g in text_grads]), "both"),
        (g_emb_bias, "dp"),
        (g_pos_bias, "crossed"),
        (g_qkv_b, "crossed"),
        (g_out_b, "dp"),
        (g_ff_b1, "crossed"),
        (g_ff_b2, "dp"),
    ]
    packed = []
    for value, kind in small:
        lead = value.size // value.shape[-1]
        if kind == "crossed":
            value = value.reshape(lead, shards, groups, -1).transpose(2, 0, 1, 3)
        else:
            value = value.reshape(lead, groups, -1).transpose(1, 0, 2)
        packed.append(value.reshape(groups, -1))
    packed = jnp.concatenate(packed, axis=1)
    length = packed.shape[1]
    packed = jnp.pad(packed, ((0, 0), (0, -length % 1024))).reshape(groups, -1, 128)
    table_sum, up0, up1, down0, down1, packed, g_emb, mel_grad = last_sums(
        [for_dp(g_table)]
        + [for_dp(text_grads[b][3]) for b in range(blocks)]
        + [for_dp(text_grads[b][5]) for b in range(blocks)],
        packed,
        [],
        [sent_emb],
        [mel_grad],
    )
    mel_grad = mel_grad.reshape(total, -1)
    packed = packed.reshape(-1)
    unpacked, at = [], 0
    for value, kind in small:
        size = value.size // groups
        piece = packed[at : at + size]
        at += size
        if kind == "dp":
            unpacked.append(piece.reshape(value.shape[:-1] + (-1,)))
        else:
            piece = piece.reshape(value.size // value.shape[-1], shards, -1)
            piece = lax.dynamic_slice_in_dim(piece, rank, 1, 1)
            unpacked.append(piece.reshape(value.shape[:-1] + (-1,)))
    o_table = table_sum[:, :vocab].T
    o_up = jnp.stack([up0.T, up1.T])
    o_down = jnp.stack([down0.T, down1.T])
    ff_pair, at_pair = (jnp.sum(v.astype(F32), axis=0) for v in (ff_got, at_got))
    ff_cols = ff_w1.shape[1]
    o_ff_w1, o_ff_w2 = ff_pair[:, :ff_cols], ff_pair[:, ff_cols:].T
    g_qkv = at_pair[:, : 3 * cols].reshape(-1, 3, cols).transpose(1, 0, 2)
    o_qkv_w = jnp.concatenate([pair_merge(g_qkv[:2]), g_qkv[2:]], axis=0)
    o_out_w = at_pair[:, 3 * cols :].T
    o_pos_conv = sent_conv.astype(F32).T.reshape(2, taps, group, -1)
    o_emb_text, o_emb_mel = g_emb[:, :text_width].T, g_emb[:, text_width:].T

    def own(values, index, parts):
        piece = values.shape[-1] // parts
        return lax.dynamic_slice_in_dim(values, index * piece, piece, values.ndim - 1)

    sinusoid, pre_one, act_one, time_vec, act_two = time_path(all_steps)
    de = precise(dmod_all, ada_w, NT) * silu_slope(time_vec)
    dpre = precise(de, time_w2, NT) * silu_slope(pre_one)

    def outer(left, right):
        return lax.dot_general(left, own(right, place, groups), TN, precision=highest)

    return (
        result,
        mel_grad,
        o_table,
        unpacked[0],
        unpacked[1],
        unpacked[2],
        o_up,
        unpacked[3],
        o_down,
        o_emb_mel,
        o_emb_text,
        unpacked[4],
        o_pos_conv,
        unpacked[5],
        outer(sinusoid, dpre),
        own(jnp.stack([jnp.sum(dpre, axis=0), jnp.sum(de, axis=0)]), place, groups),
        outer(act_one, de),
        outer(act_two, dmod_all),
        own(jnp.sum(dmod_all, axis=0), place, groups),
        o_qkv_w,
        unpacked[6],
        o_out_w,
        unpacked[7],
        o_ff_w1,
        unpacked[8],
        o_ff_w2,
        unpacked[9],
    )


def solution(mesh):
    both, crossed = ("dp", "mp"), ("mp", "dp")
    placed = (
        P("dp", None), P("dp"), P("dp", None), P("dp", None),
        P(), P(), P(), P(), P(), P(), P(), P(), P(), P(),
        P(None, None, None, "mp"), P(None, "mp"),
        P(), P(), P(), P(), P(),
        P(None, None, "mp"), P(None, "mp"), P("mp", None), P(),
        P(None, "mp"), P("mp"), P("mp", None), P(),
        P("dp", None),
    )
    given = (
        P("dp", None), P("dp", None),
        P(None, both), P(None, None, both), P(None, None, both), P(None, both),
        P(None, None, both), P(None, None, both), P(None, None, both),
        P(None, "dp"), P(None, "dp"), P("dp"),
        P(None, None, None, crossed), P(None, crossed),
        P(None, "dp"), P(None, "dp"), P(None, "dp"), P(None, "dp"), P("dp"),
        P(None, "dp", "mp"), P(None, crossed), P("mp", "dp"), P("dp"),
        P("dp", "mp"), P(crossed), P("mp", "dp"), P("dp"),
    )
    return jax.shard_map(local, mesh=mesh, in_specs=placed, out_specs=given, check_vma=False)
```

```python
from functools import partial
import math

import jax
import jax.numpy as jnp
from jax import lax
from jax.experimental import pallas as pl
from jax.experimental.pallas import tpu as pltpu
from jax.sharding import PartitionSpec as P

HEAD_DIM = 64
GAP = 16
HALO = 8
BF = jnp.bfloat16
F32 = jnp.float32
highest = lax.Precision.HIGHEST
NN = (((1,), (0,)), ((), ()))
NT = (((1,), (1,)), ((), ()))
TN = (((0,), (0,)), ((), ()))


def dot(left, right, dims=NN):
    return lax.dot_general(left.astype(BF), right.astype(BF), dims, preferred_element_type=F32)


def precise(left, right, dims=NN):
    one = lax.reduce_precision(left, 8, 7)
    two = lax.reduce_precision(left - one, 8, 7)
    three = left - one - two
    rows = left.shape[0]
    stacked = jnp.concatenate([one, two, three], axis=0).astype(BF)
    product = lax.dot_general(stacked, right, dims, preferred_element_type=F32)
    return product[:rows] + product[rows : 2 * rows] + product[2 * rows :]


@jax.custom_vjp
def expand(onehot, parts):
    return sum(onehot[:, c : c + 1] * parts[c : c + 1] for c in range(parts.shape[0]))


def expand_ahead(onehot, parts):
    return expand(onehot, parts), onehot


def expand_behind(onehot, grad):
    return None, jnp.dot(onehot.T, grad, precision=highest)


expand.defvjp(expand_ahead, expand_behind)


def silu_slope(values):
    sigmoid_val = jax.nn.sigmoid(values)
    return sigmoid_val * (1.0 + values * (1.0 - sigmoid_val))


def layer_norm(values):
    centred = values - jnp.mean(values, axis=-1, keepdims=True)
    variance = jnp.mean(centred * centred, axis=-1, keepdims=True)
    return centred * lax.rsqrt(variance + 1e-06)


def mish(values):
    grown = jnp.exp(jnp.minimum(values, 20.0))
    wide = grown * (grown + 2.0)
    return values * (wide / (wide + 2.0))


def mish_slope(values):
    grown = jnp.exp(jnp.minimum(values, 20.0))
    wide = grown * (grown + 2.0)
    under = 1.0 / (wide + 2.0)
    return wide * under + values * (4.0 * grown * (1.0 + grown) * under * under)


def sum_kernel(axis, size, x_ref, o_ref, slots, send_sems, recv_sems):
    me = lax.axis_index(axis)
    barrier = pltpu.get_barrier_semaphore()
    peers = [lax.rem(me + step, size) for step in range(1, size)]
    for peer in peers:
        pl.semaphore_signal(
            barrier, inc=1, device_id={axis: peer}, device_id_type=pl.DeviceIdType.MESH
        )
    pl.semaphore_wait(barrier, size - 1)
    for step, peer in enumerate(peers):
        pltpu.make_async_remote_copy(
            src_ref=x_ref,
            dst_ref=slots.at[me],
            send_sem=send_sems.at[step],
            recv_sem=recv_sems.at[me],
            device_id={axis: peer},
            device_id_type=pl.DeviceIdType.MESH,
        ).start()
    slots[me] = x_ref[...]
    for step, peer in enumerate(peers):
        copy = pltpu.make_async_remote_copy(
            src_ref=x_ref,
            dst_ref=slots.at[peer],
            send_sem=send_sems.at[step],
            recv_sem=recv_sems.at[peer],
            device_id={axis: peer},
            device_id_type=pl.DeviceIdType.MESH,
        )
        copy.wait_send()
        copy.wait_recv()
    total = slots[0]
    for device in range(1, size):
        total = total + slots[device]
    o_ref[...] = total


def small_sum(values, axis, name):
    size = lax.axis_size(axis)
    whole = pl.BlockSpec(memory_space=pltpu.VMEM)
    return pl.pallas_call(
        partial(sum_kernel, axis, size),
        out_shape=jax.ShapeDtypeStruct(values.shape, F32),
        in_specs=[whole],
        out_specs=whole,
        scratch_shapes=[
            pltpu.VMEM((size,) + values.shape, F32),
            pltpu.SemaphoreType.DMA((size - 1,)),
            pltpu.SemaphoreType.DMA((size,)),
        ],
        compiler_params=pltpu.CompilerParams(
            collective_id=name, has_side_effects=True, vmem_limit_bytes=16 << 20
        ),
    )(values)


def last_kernel(dp, mp, n_all, n_mp, n_both, n_gather, *refs):
    n_in = n_all + n_mp + n_both + n_gather
    ins, outs, rest = refs[:n_in], refs[n_in : 2 * n_in], list(refs[2 * n_in :])

    def take(count):
        return [rest.pop(0) for _ in range(count)]

    own, pair, joint, chip_slots, middle, slots = (
        take(n_all), take(n_all), take(n_all), take(n_all), take(n_all), take(n_in)
    )
    pair_send, pair_recv, chip_send, chip_recv, mp_send, mp_recv, own_sems = rest
    me, z = lax.axis_index("dp"), lax.axis_index("mp")
    chips = dp // 2
    core, chip = lax.rem(me, 2), me // 2
    partner = me + 1 - 2 * core
    other_chips = [lax.rem(chip + step, chips) for step in range(1, chips)]
    other_z = [lax.rem(z + step, mp) for step in range(1, mp)]
    mesh_id = pl.DeviceIdType.MESH
    barrier = pltpu.get_barrier_semaphore()
    greeted = (
        [{"dp": partner}]
        + [{"dp": 2 * q + core} for q in other_chips]
        + [{"mp": peer} for peer in other_z]
    )
    for device in greeted:
        pl.semaphore_signal(barrier, inc=1, device_id=device, device_id_type=mesh_id)
    pl.semaphore_wait(barrier, chips + mp - 1)

    def to_partner(t):
        return pltpu.make_async_remote_copy(
            src_ref=ins[t].at[:, 1 - core],
            dst_ref=pair[t],
            send_sem=pair_send.at[t],
            recv_sem=pair_recv.at[t],
            device_id={"dp": partner},
            device_id_type=mesh_id,
        )

    def to_chip(t, step, mine):
        q = other_chips[step]
        return pltpu.make_async_remote_copy(
            src_ref=joint[t].at[q],
            dst_ref=chip_slots[t].at[mine],
            send_sem=chip_send.at[t, step],
            recv_sem=chip_recv.at[t, mine],
            device_id={"dp": 2 * q + core},
            device_id_type=mesh_id,
        )

    def to_z(t, step, mine):
        peer = other_z[step]
        if t < n_all - 1:
            source = middle[t].at[peer]
        elif t == n_all - 1:
            source = middle[t]
        else:
            source = ins[t].at[peer] if t < n_all + n_mp else ins[t]
        return pltpu.make_async_remote_copy(
            src_ref=source,
            dst_ref=slots[t].at[mine],
            send_sem=mp_send.at[t, step],
            recv_sem=mp_recv.at[t, mine],
            device_id={"mp": peer},
            device_id_type=mesh_id,
        )

    local = []
    for t in range(n_all):
        to_partner(t).start()
        copy = pltpu.make_async_copy(ins[t].at[:, core], own[t], own_sems.at[t])
        copy.start()
        local.append(copy)
    for t in range(n_all, n_in):
        for step in range(mp - 1):
            to_z(t, step, z).start()
        source = ins[t].at[z] if t < n_all + n_mp else ins[t]
        copy = pltpu.make_async_copy(source, slots[t].at[z], own_sems.at[t])
        copy.start()
        local.append(copy)

    def total(ref, size):
        value = ref[0].astype(F32)
        for device in range(1, size):
            value = value + ref[device].astype(F32)
        return value

    for t in range(n_all):
        local[t].wait()
        copy = to_partner(t)
        copy.wait_send()
        copy.wait_recv()
        for q in range(chips):
            value = own[t][q].astype(F32) + pair[t][q].astype(F32)
            joint[t][q] = value.astype(joint[t].dtype)
        for step in range(chips - 1):
            to_chip(t, step, chip).start()
        chip_slots[t][chip] = joint[t][chip]
    for t in range(n_all):
        for step in range(chips - 1):
            copy = to_chip(t, step, other_chips[step])
            copy.wait_send()
            copy.wait_recv()
        value = total(chip_slots[t], chips)
        if t < n_all - 1:
            rows = value.shape[0] // mp
            for device in range(mp):
                part = value[device * rows : (device + 1) * rows]
                middle[t][device] = part.astype(middle[t].dtype)
            slots[t][z] = middle[t][z]
        else:
            middle[t][...] = value
            slots[t][z] = value
        for step in range(mp - 1):
            to_z(t, step, z).start()
    for t in list(range(n_all, n_in)) + list(range(n_all)):
        if t >= n_all:
            local[t].wait()
        for step in range(mp - 1):
            copy = to_z(t, step, other_z[step])
            copy.wait_send()
            copy.wait_recv()
        if t < n_in - n_gather:
            outs[t][...] = total(slots[t], mp)
        else:
            outs[t][...] = slots[t][...].astype(F32)


def last_sums(over_all, small, over_mp, both, gathered):
    dp, mp = lax.axis_size("dp"), lax.axis_size("mp")
    chips = dp // 2
    everywhere = [v.reshape((chips, 2) + v.shape[1:]) for v in list(over_all) + [small]]
    ins = everywhere + list(over_mp) + list(both) + list(gathered)
    n_all, n_mp, n_both, n_gather = len(everywhere), len(over_mp), len(both), len(gathered)
    halves = [pltpu.VMEM((chips,) + v.shape[2:], v.dtype) for v in everywhere]
    outs, middle, slots = [], [], []
    for t, value in enumerate(ins):
        if t < n_all - 1:
            shape = (value.shape[2] // mp, value.shape[3])
            middle.append(pltpu.VMEM((mp,) + shape, value.dtype))
        elif t == n_all - 1:
            shape = value.shape[2:]
            middle.append(pltpu.VMEM(shape, value.dtype))
        else:
            shape = value.shape[1:] if t < n_all + n_mp else value.shape
        slots.append(pltpu.VMEM((mp,) + shape, value.dtype))
        outs.append((mp,) + shape if t >= len(ins) - n_gather else shape)
    dma = pltpu.SemaphoreType.DMA
    return pl.pallas_call(
        partial(last_kernel, dp, mp, n_all, n_mp, n_both, n_gather),
        out_shape=[jax.ShapeDtypeStruct(shape, F32) for shape in outs],
        in_specs=[pl.BlockSpec(memory_space=pl.ANY)] * len(ins),
        out_specs=[pl.BlockSpec(memory_space=pltpu.VMEM)] * len(ins),
        scratch_shapes=halves * 4
        + middle
        + slots
        + [
            dma((n_all,)),
            dma((n_all,)),
            dma((n_all, chips)),
            dma((n_all, chips)),
            dma((len(ins), mp)),
            dma((len(ins), mp)),
            dma((len(ins),)),
        ],
        compiler_params=pltpu.CompilerParams(
            collective_id=3, has_side_effects=True, vmem_limit_bytes=56 << 20
        ),
    )(*ins)


def conv_norm(hidden, segment, conv, vec, gain):
    taps = conv.shape[0]
    reach = taps // 2
    rows = hidden.shape[0]
    padded = jnp.pad(hidden, ((reach, reach), (0, 0)))
    seg_padded = jnp.pad(segment, (reach, reach), constant_values=-1)
    mixture = vec[0]
    for tap in range(taps):
        keep = (seg_padded[tap : tap + rows] == segment) & (segment >= 0)
        mixture = mixture + conv[tap] * jnp.where(keep[:, None], padded[tap : tap + rows], 0.0)
    return layer_norm(mixture) * gain + vec[1]


def activate(pre, bias):
    return jax.nn.gelu(pre + bias, approximate=False)


def clip_squares(own, active):
    return jnp.dot(own.T, active * active, precision=highest)


def respond(active, squares, onehot, scale, shift):
    norms = jnp.sqrt(jnp.maximum(squares, 1.0))
    ratio = norms / (jnp.mean(norms, axis=-1, keepdims=True) + 1e-06)
    return scale * (active * expand(onehot, ratio)) + shift + active


def text_ahead(hidden, segment, onehot, own, conv, vec, gain, up, hid, down):
    normed, norm_pull = jax.vjp(
        lambda h, c, v, g: conv_norm(h, segment, c, v, g), hidden, conv, vec, gain
    )
    normed = normed.astype(BF)
    active, act_pull = jax.vjp(activate, dot(normed, up), hid[0])
    squares, square_pull = jax.vjp(lambda a: clip_squares(own, a), active)
    squares = small_sum(squares, "mp", 1)
    grown, respond_pull = jax.vjp(
        lambda a, s, g, b: respond(a, s, onehot, g, b), active, squares, hid[1], hid[2]
    )
    grown = grown.astype(BF)
    result = hidden + dot(grown, down) + vec[2]
    return result, (norm_pull, normed, act_pull, square_pull, respond_pull, grown)


def text_behind(kept, grad, up, down, extra):
    norm_pull, normed, act_pull, square_pull, respond_pull, grown = kept
    grad_low = grad.astype(BF)
    g_out = jnp.sum(grad, axis=0)
    g_down = dot(grad_low, grown, TN)
    grad_active, grad_squares, g_scale, g_shift = respond_pull(dot(grad_low, down, NT))
    if extra is None:
        grad_squares = small_sum(grad_squares, "mp", 1)
    else:
        joined = small_sum(jnp.concatenate([grad_squares, extra], axis=1), "mp", 2)
        grad_squares, extra = joined[:, : grad_squares.shape[1]], joined[:, grad_squares.shape[1] :]
    grad_active = grad_active + square_pull(grad_squares)[0]
    grad_pre, g_bias = act_pull(grad_active)
    pre_low = grad_pre.astype(BF)
    g_up = dot(pre_low, normed, TN)
    grad_hidden, g_conv, g_vec, g_gain = norm_pull(dot(pre_low, up, NT))
    g_vec = g_vec.at[2].add(g_out)
    return (
        grad + grad_hidden,
        (g_conv, g_vec, g_gain, g_up, jnp.stack([g_bias, g_scale, g_shift]), g_down),
        extra,
    )


def spread(values, starts, ends):
    rows = values.shape[0]
    clips = starts.shape[0]
    at = lax.broadcasted_iota(jnp.int32, values.shape, 0)
    total = rows + GAP * clips + 2 * GAP
    out = None
    for c in range(clips):
        part = jnp.where((at >= starts[c]) & (at < ends[c]), values, 0)
        lead = GAP + GAP * c
        part = jnp.pad(part, ((lead, total - lead - rows), (0, 0)))
        out = part if out is None else out + part
    return out


def only_clips(values, starts, ends):
    at = lax.broadcasted_iota(jnp.int32, values.shape, 0)
    keep = None
    for c in range(starts.shape[0]):
        inside = (at >= starts[c] + GAP * c) & (at < ends[c] + GAP * c)
        keep = inside if keep is None else keep | inside
    return jnp.where(keep, values, 0.0)


def gather_back(values, starts, ends):
    clips = starts.shape[0]
    rows = values.shape[0] - GAP * clips
    at = lax.broadcasted_iota(jnp.int32, (rows, values.shape[1]), 0)
    out = values[:rows]
    for c in range(1, clips):
        out = jnp.where(at >= starts[c], values[GAP * c : GAP * c + rows], out)
    return out


def conv_kernel(taps, turned, x_ref, w_ref, o_ref, full_ref):
    rows, width = o_ref.shape
    group = w_ref.shape[1]
    first = GAP - taps // 2

    @pl.when(pl.program_id(0) == 0)
    def _():
        lane = lax.broadcasted_iota(jnp.int32, (group, width), 1) // group
        for k in range(taps):
            tap = w_ref[taps - 1 - k if turned else k]
            for g in range(width // group):
                piece = jnp.where(lane == g, tap, jnp.zeros_like(tap))
                if turned:
                    full_ref[g * group : (g + 1) * group, k * width : (k + 1) * width] = piece
                else:
                    full_ref[k * width + g * group : k * width + (g + 1) * group, :] = piece

    columns = [x_ref[first + k : first + k + rows, :].astype(BF) for k in range(taps)]
    o_ref[...] = lax.dot_general(
        jnp.concatenate(columns, axis=1),
        full_ref[...],
        NT if turned else NN,
        preferred_element_type=F32,
    )


def conv_chunk(rows):
    for size in (528, 352, 256, 128, 64, 32, 16):
        if rows % size == 0:
            return size
    return rows


def apply_conv(spread_rows, weight, turned):
    rows = spread_rows.shape[0] - 2 * GAP
    width = spread_rows.shape[1]
    taps, group = weight.shape[:2]
    chunk = conv_chunk(rows)
    return pl.pallas_call(
        partial(conv_kernel, taps, turned),
        out_shape=jax.ShapeDtypeStruct((rows, width), F32),
        grid=(rows // chunk,),
        in_specs=[
            pl.BlockSpec((pl.Element(chunk + 2 * GAP), pl.Element(width)), lambda i: (i * chunk, 0)),
            pl.BlockSpec(weight.shape, lambda i: (0, 0, 0), pipeline_mode=pl.Buffered(1)),
        ],
        out_specs=pl.BlockSpec((chunk, width), lambda i: (i, 0)),
        scratch_shapes=[
            pltpu.VMEM((width, taps * width) if turned else (taps * width, width), BF)
        ],
        compiler_params=pltpu.CompilerParams(vmem_limit_bytes=48 << 20),
        cost_estimate=pl.CostEstimate(
            flops=2 * rows * taps * width * width, bytes_accessed=8 << 20, transcendentals=0
        ),
    )(spread_rows, weight)


def conv_grad_kernel(taps, group, x_ref, g_ref, o_ref):
    rows, width = g_ref.shape
    first = GAP - taps // 2
    turned = g_ref[...].T.astype(BF)

    @pl.when(pl.program_id(0) == 0)
    def _():
        o_ref[...] = jnp.zeros_like(o_ref)

    for k in range(taps):
        window = x_ref[first + k : first + k + rows, :].astype(BF)
        product = jnp.dot(turned, window, preferred_element_type=F32)
        for g in range(width // group):
            own = slice(g * group, (g + 1) * group)
            o_ref[own, k * group : (k + 1) * group] += product[own, own]


def conv_grad(spread_rows, grads, taps, group):
    rows, width = grads.shape
    chunk = conv_chunk(rows)
    return pl.pallas_call(
        partial(conv_grad_kernel, taps, group),
        out_shape=jax.ShapeDtypeStruct((width, taps * group), F32),
        grid=(rows // chunk,),
        in_specs=[
            pl.BlockSpec((pl.Element(chunk + 2 * GAP), pl.Element(width)), lambda i: (i * chunk, 0)),
            pl.BlockSpec((chunk, width), lambda i: (i, 0)),
        ],
        out_specs=pl.BlockSpec((width, taps * group), lambda i: (0, 0)),
        compiler_params=pltpu.CompilerParams(vmem_limit_bytes=48 << 20),
        cost_estimate=pl.CostEstimate(
            flops=2 * rows * taps * width * width, bytes_accessed=8 << 20, transcendentals=0
        ),
    )(spread_rows, grads)


LANES = 128


def pair_split(columns):
    pairs = columns.reshape(*columns.shape[:-1], -1, LANES // 2, 2)
    return jnp.swapaxes(pairs, -1, -2).reshape(columns.shape)


def pair_merge(columns):
    pairs = columns.reshape(*columns.shape[:-1], -1, 2, LANES // 2)
    return jnp.swapaxes(pairs, -1, -2).reshape(columns.shape)


def project_kernel(x_ref, w_ref, b_ref, cos_ref, sin_ref, *out_refs):
    cos, sin = cos_ref[...], sin_ref[...]
    for p in range(3):
        value = jnp.dot(x_ref[...], w_ref[p], preferred_element_type=F32) + b_ref[p : p + 1, :]
        for at, out_ref in enumerate(out_refs):
            piece = value[:, at * LANES : (at + 1) * LANES]
            if p < 2:
                piece = piece * cos + pltpu.roll(piece, LANES // 2, 1) * sin
            out_ref[p] = piece.astype(BF)


def project(normed, weight, bias, cos, sin):
    rows = normed.shape[0]
    shards, _, width, cols = weight.shape
    parts = cols // LANES
    return pl.pallas_call(
        project_kernel,
        out_shape=[jax.ShapeDtypeStruct((shards, 3, rows, LANES), BF)] * parts,
        grid=(shards,),
        in_specs=[
            pl.BlockSpec((rows, width), lambda i: (0, 0)),
            pl.BlockSpec((None, 3, width, cols), lambda i: (i, 0, 0, 0)),
            pl.BlockSpec((None, 3, cols), lambda i: (i, 0, 0)),
            pl.BlockSpec((rows, LANES), lambda i: (0, 0)),
            pl.BlockSpec((rows, LANES), lambda i: (0, 0)),
        ],
        out_specs=[pl.BlockSpec((None, 3, rows, LANES), lambda i: (i, 0, 0, 0))] * parts,
        compiler_params=pltpu.CompilerParams(vmem_limit_bytes=32 << 20),
        cost_estimate=pl.CostEstimate(
            flops=6 * rows * width * width, bytes_accessed=10 << 20, transcendentals=0
        ),
    )(normed, weight, bias, cos, sin)


def unproject_kernel(parts, *refs):
    d_refs, (x_ref, w_ref, dx_ref, gw_ref, gb_ref, turned) = refs[:parts], refs[parts:]
    s = pl.program_id(0)
    cols = w_ref.shape[2]

    @pl.when(s == 0)
    def _():
        turned[...] = x_ref[...].T
        dx_ref[...] = jnp.zeros_like(dx_ref)

    total = None
    for p in range(3):
        grad = jnp.concatenate([d_ref[p] for d_ref in d_refs], axis=1)
        product = lax.dot_general(grad, w_ref[p], NT, preferred_element_type=F32)
        total = product if total is None else total + product
        weight = jnp.dot(turned[...], grad, preferred_element_type=F32)
        gw_ref[:, p * cols : (p + 1) * cols] = weight.astype(BF)
        gb_ref[p : p + 1, :] = jnp.sum(grad.astype(F32), axis=0, keepdims=True)
    dx_ref[...] += total


def unproject(grads, normed, weight):
    rows = normed.shape[0]
    shards, _, width, cols = weight.shape
    parts = len(grads)
    return pl.pallas_call(
        partial(unproject_kernel, parts),
        out_shape=[
            jax.ShapeDtypeStruct((rows, width), F32),
            jax.ShapeDtypeStruct((width, shards * 3 * cols), BF),
            jax.ShapeDtypeStruct((shards, 3, cols), F32),
        ],
        grid=(shards,),
        in_specs=[pl.BlockSpec((None, 3, rows, LANES), lambda i: (i, 0, 0, 0))] * parts
        + [
            pl.BlockSpec((rows, width), lambda i: (0, 0)),
            pl.BlockSpec((None, 3, width, cols), lambda i: (i, 0, 0, 0)),
        ],
        out_specs=[
            pl.BlockSpec((rows, width), lambda i: (0, 0)),
            pl.BlockSpec((width, 3 * cols), lambda i: (0, i)),
            pl.BlockSpec((None, 3, cols), lambda i: (i, 0, 0)),
        ],
        scratch_shapes=[pltpu.VMEM((width, rows), BF)],
        compiler_params=pltpu.CompilerParams(vmem_limit_bytes=48 << 20),
        cost_estimate=pl.CostEstimate(
            flops=12 * rows * width * width, bytes_accessed=20 << 20, transcendentals=0
        ),
    )(*grads, normed, weight)


def head_masks(width):
    heads = width // HEAD_DIM
    lane = lax.broadcasted_iota(jnp.int32, (1, width), 1)
    half = HEAD_DIM // 2
    paired = [((lane % (width // 2)) // half) == h for h in range(heads)]
    plain = [(lane // HEAD_DIM) == h for h in range(heads)]
    return heads, paired, plain


def masked(values, masks):
    return [jnp.where(mask, values, jnp.zeros_like(values)) for mask in masks]


def attend_kernel(bounds, q_ref, k_ref, v_ref, sq_ref, sk_ref, o_ref, full_ref, lse_ref, vt_ref):
    i = pl.program_id(0)
    rows, width = q_ref.shape
    heads, paired, _ = head_masks(width)

    @pl.when(i == 0)
    def _():
        for b in range(v_ref.shape[0]):
            vt_ref[b] = v_ref[b].T

    q_heads = masked(q_ref[...] * jnp.asarray(HEAD_DIM**-0.5, BF), paired)
    sq = sq_ref[...]

    def step(kb, carry):
        k = k_ref[kb]
        same = sk_ref[kb] == sq
        new = []
        for h in range(heads):
            top_was, total, acc = carry[h]
            scores = lax.dot_general(k, q_heads[h], NT, preferred_element_type=F32)
            scores = jnp.where(same, scores, -1e30)
            top = jnp.maximum(top_was, jnp.max(scores, axis=0, keepdims=True))
            fade = jnp.exp(top_was - top)
            weight = jnp.exp(scores - top)
            total = fade * total + jnp.sum(weight, axis=0, keepdims=True)
            v_head = vt_ref[kb, h * HEAD_DIM : (h + 1) * HEAD_DIM, :]
            acc = acc * fade + jnp.dot(v_head, weight.astype(BF), preferred_element_type=F32)
            new.append((top, total, acc))
        return tuple(new)

    start = tuple(
        (jnp.full((1, rows), -1e30, F32), jnp.zeros((1, rows), F32), jnp.zeros((HEAD_DIM, rows), F32))
        for _ in range(heads)
    )
    done = lax.fori_loop(bounds[i, 0], bounds[i, 1], step, start)
    full = jnp.concatenate([acc * (1.0 / total) for _, total, acc in done], axis=0)
    full_ref[...] = full
    o_ref[...] = full.T.astype(BF)
    row = lax.broadcasted_iota(jnp.int32, lse_ref.shape, 0)
    logs = jnp.zeros(lse_ref.shape, F32)
    for h, (top, total, _) in enumerate(done):
        logs = jnp.where(row == h, top + jnp.log(total), logs)
    lse_ref[...] = logs


def attend(qkv, seg_rows, seg_columns, bounds, block):
    shards, _, rows, width = qkv.shape
    total = shards * rows
    per = rows // block
    grid_spec = pltpu.PrefetchScalarGridSpec(
        num_scalar_prefetch=1,
        grid=(total // block,),
        in_specs=[
            pl.BlockSpec((None, None, block, width), lambda i, b: (i // per, 0, i % per, 0)),
            pl.BlockSpec((shards, None, rows, width), lambda i, b: (0, 1, 0, 0)),
            pl.BlockSpec((shards, None, rows, width), lambda i, b: (0, 2, 0, 0)),
            pl.BlockSpec((1, block), lambda i, b: (0, i)),
            pl.BlockSpec((shards, rows, 1), lambda i, b: (0, 0, 0)),
        ],
        out_specs=[
            pl.BlockSpec((block, width), lambda i, b: (i, 0)),
            pl.BlockSpec((width, block), lambda i, b: (0, i)),
            pl.BlockSpec((8, block), lambda i, b: (0, i)),
        ],
        scratch_shapes=[pltpu.VMEM((shards, width, rows), BF)],
    )
    return pl.pallas_call(
        attend_kernel,
        out_shape=[
            jax.ShapeDtypeStruct((total, width), BF),
            jax.ShapeDtypeStruct((width, total), F32),
            jax.ShapeDtypeStruct((8, total), F32),
        ],
        grid_spec=grid_spec,
        compiler_params=pltpu.CompilerParams(vmem_limit_bytes=48 << 20),
        cost_estimate=pl.CostEstimate(
            flops=4 * total * total * width, bytes_accessed=8 << 20, transcendentals=0
        ),
    )(bounds, qkv, qkv, qkv, seg_rows, seg_columns)


def unrotate(values, cos, sin):
    return values * cos - pltpu.roll(values, LANES // 2, 1) * sin


def attend_back_kernel(
    bounds, q_ref, k_ref, v_ref, full_ref, lse_ref, do_ref, sq_ref, sk_ref, cos_ref, sin_ref,
    out_ref, dk_ref, dv_ref, kt_ref,
):
    i = pl.program_id(0)
    rows, width = q_ref.shape
    shards, _, shard_rows, _ = out_ref.shape
    per = shard_rows // rows
    heads, paired, plain = head_masks(width)
    scale = HEAD_DIM**-0.5

    @pl.when(i == 0)
    def _():
        dk_ref[...] = jnp.zeros_like(dk_ref)
        dv_ref[...] = jnp.zeros_like(dv_ref)
        for b in range(shards):
            for h, k_head in enumerate(masked(k_ref[b], paired)):
                kt_ref[b, h] = k_head.T

    do = do_ref[...]
    q_heads = masked(q_ref[...] * jnp.asarray(scale, BF), paired)
    do_heads = masked(do, plain)
    product = do.astype(F32).T * full_ref[...]
    deltas = [
        jnp.sum(product[h * HEAD_DIM : (h + 1) * HEAD_DIM], axis=0, keepdims=True)
        for h in range(heads)
    ]
    logs = [lse_ref[h : h + 1, :] for h in range(heads)]
    sq = sq_ref[...]

    def step(kb, dq):
        k, v = k_ref[kb], v_ref[kb]
        same = sk_ref[kb] == sq
        dk, dv = dk_ref[kb], dv_ref[kb]
        for h in range(heads):
            scores = lax.dot_general(k, q_heads[h], NT, preferred_element_type=F32)
            weight = jnp.where(same, jnp.exp(scores - logs[h]), 0.0)
            dp = lax.dot_general(v, do_heads[h], NT, preferred_element_type=F32)
            ds = (weight * (dp - deltas[h])).astype(BF)
            dv = dv + jnp.dot(weight.astype(BF), do_heads[h], preferred_element_type=F32)
            dk = dk + jnp.dot(ds, q_heads[h], preferred_element_type=F32)
            dq = dq + jnp.dot(kt_ref[kb, h], ds, preferred_element_type=F32)
        dk_ref[kb] = dk
        dv_ref[kb] = dv
        return dq

    dq = lax.fori_loop(bounds[i, 0], bounds[i, 1], step, jnp.zeros((width, rows), F32))
    dq = dq.T * scale
    here = pl.ds(pl.multiple_of(i * rows, rows), rows)
    inside = pl.ds(pl.multiple_of((i % per) * rows, rows), rows)
    out_ref[i // per, 0, inside, :] = unrotate(dq, cos_ref[here, :], sin_ref[here, :]).astype(BF)

    @pl.when(i == pl.num_programs(0) - 1)
    def _():
        for s in range(shards):
            own = slice(s * shard_rows, (s + 1) * shard_rows)
            out_ref[s, 1] = unrotate(dk_ref[s], cos_ref[own, :], sin_ref[own, :]).astype(BF)
            out_ref[s, 2] = dv_ref[s].astype(BF)


def attend_back(qkv, full, logs, grads, seg_rows, seg_columns, cos, sin, bounds, block):
    shards, _, rows, width = qkv.shape
    total = shards * rows
    per = rows // block
    heads = width // HEAD_DIM
    grid_spec = pltpu.PrefetchScalarGridSpec(
        num_scalar_prefetch=1,
        grid=(total // block,),
        in_specs=[
            pl.BlockSpec((None, None, block, width), lambda i, b: (i // per, 0, i % per, 0)),
            pl.BlockSpec((shards, None, rows, width), lambda i, b: (0, 1, 0, 0)),
            pl.BlockSpec((shards, None, rows, width), lambda i, b: (0, 2, 0, 0)),
            pl.BlockSpec((width, block), lambda i, b: (0, i)),
            pl.BlockSpec((8, block), lambda i, b: (0, i)),
            pl.BlockSpec((block, width), lambda i, b: (i, 0)),
            pl.BlockSpec((1, block), lambda i, b: (0, i)),
            pl.BlockSpec((shards, rows, 1), lambda i, b: (0, 0, 0)),
            pl.BlockSpec((total, width), lambda i, b: (0, 0)),
            pl.BlockSpec((total, width), lambda i, b: (0, 0)),
        ],
        out_specs=pl.BlockSpec((shards, 3, rows, width), lambda i, b: (0, 0, 0, 0)),
        scratch_shapes=[
            pltpu.VMEM((shards, rows, width), F32),
            pltpu.VMEM((shards, rows, width), F32),
            pltpu.VMEM((shards, heads, width, rows), BF),
        ],
    )
    return pl.pallas_call(
        attend_back_kernel,
        out_shape=jax.ShapeDtypeStruct((shards, 3, rows, width), BF),
        grid_spec=grid_spec,
        compiler_params=pltpu.CompilerParams(vmem_limit_bytes=48 << 20),
        cost_estimate=pl.CostEstimate(
            flops=10 * total * total * width, bytes_accessed=16 << 20, transcendentals=0
        ),
    )(bounds, qkv, qkv, qkv, full, logs, grads, seg_rows, seg_columns, cos, sin)


def middle_kernel(
    parts, clips, *refs,
):
    o_refs, refs = refs[:parts], refs[parts:]
    (x_ref, g_ref, seg_ref, mod_ref, wo_ref, bo_ref, w1_ref, b1_ref, w2_ref, b2_ref) = refs[:10]
    (out_ref, n_ref, r_ref, df_ref, dh_ref, da_ref, dx_ref, gb1_ref, gsum_ref) = refs[10:19]
    do_refs = refs[19:]
    rows, width = x_ref.shape
    shards = o_refs[0].shape[0]
    seg = seg_ref[...]

    @pl.when(pl.program_id(0) == 0)
    def _():
        gb1_ref[...] = jnp.zeros_like(gb1_ref)
        gsum_ref[...] = jnp.zeros_like(gsum_ref)

    def of_clip(part):
        columns = slice(part * width, (part + 1) * width)
        value = jnp.broadcast_to(mod_ref[0:1, columns], (rows, width))
        for c in range(1, clips):
            value = jnp.where(seg == c, mod_ref[c : c + 1, columns], value)
        return value

    def clip_sums(at, value):
        for c in range(clips):
            part = jnp.sum(jnp.where(seg == c, value, 0.0), axis=0, keepdims=True)
            gsum_ref[at + c : at + c + 1, :] += part

    def column_sum(at, value):
        gsum_ref[at : at + 1, :] += jnp.sum(value, axis=0, keepdims=True)

    def mean(value):
        return jnp.mean(value, axis=-1, keepdims=True)

    heads = [o_refs[p][s] for s in range(shards) for p in range(parts)]
    att = jnp.dot(jnp.concatenate(heads, axis=1), wo_ref[...], preferred_element_type=F32) + bo_ref[...]
    gate_a, gate_f, scale = of_clip(2), of_clip(5), 1.0 + of_clip(4)
    x2 = x_ref[...] + gate_a * att
    centred = x2 - mean(x2)
    under = lax.rsqrt(mean(centred * centred) + 1e-06)
    y = centred * under
    n2 = (y * scale + of_clip(3)).astype(BF)
    n_ref[...] = n2
    h = jnp.dot(n2, w1_ref[...], preferred_element_type=F32) + b1_ref[...]
    root = math.sqrt(2.0 / math.pi)
    square = h * h
    bent = jnp.tanh(root * h * (1.0 + 0.044715 * square))
    r = (0.5 * h * (1.0 + bent)).astype(BF)
    r_ref[...] = r
    slope = 0.5 * (1.0 + bent) + 0.5 * h * (1.0 - bent * bent) * root * (1.0 + 3 * 0.044715 * square)
    fo = jnp.dot(r, w2_ref[...], preferred_element_type=F32) + b2_ref[...]
    out_ref[...] = (x2 + gate_f * fo).astype(BF)

    g = g_ref[...].astype(F32)
    clip_sums(0, g * fo)
    gated = g * gate_f
    column_sum(4 * clips, gated)
    df = gated.astype(BF)
    df_ref[...] = df
    dh = (lax.dot_general(df, w2_ref[...], NT, preferred_element_type=F32) * slope).astype(BF)
    dh_ref[...] = dh
    gb1_ref[0:1, :] += jnp.sum(dh.astype(F32), axis=0, keepdims=True)
    dn2 = lax.dot_general(dh, w1_ref[...], NT, preferred_element_type=F32)
    clip_sums(clips, dn2)
    clip_sums(2 * clips, dn2 * y)
    z = dn2 * scale
    dx2 = g + (z - mean(z) - y * mean(z * y)) * under
    dx_ref[...] = dx2
    clip_sums(3 * clips, dx2 * att)
    gated = dx2 * gate_a
    column_sum(4 * clips + 1, gated)
    da = gated.astype(BF)
    da_ref[...] = da
    do = lax.dot_general(da, wo_ref[...], NT, preferred_element_type=F32).astype(BF)
    for s in range(shards):
        for p in range(parts):
            at = (s * parts + p) * LANES
            do_refs[p][s] = do[:, at : at + LANES]


def middle(o_parts, x1, grad, seg, mod, out_w, out_b, w1, b1, w2, b2):
    rows, width = x1.shape
    hidden = w1.shape[1]
    shards, parts, clips = o_parts[0].shape[0], len(o_parts), mod.shape[0]
    block = min(rows, 256)

    def row_block(columns):
        return pl.BlockSpec((block, columns), lambda i: (i, 0))

    def whole(shape):
        return pl.BlockSpec(shape, lambda i: (0, 0), pipeline_mode=pl.Buffered(1))

    def kept(shape):
        return pl.BlockSpec(shape, lambda i: (0, 0))

    by_shard = pl.BlockSpec((shards, block, LANES), lambda i: (0, i, 0))
    sums = -(-(4 * clips + 2) // 8) * 8
    shape = jax.ShapeDtypeStruct
    outs = [
        (shape((rows, width), BF), row_block(width)),
        (shape((rows, width), BF), row_block(width)),
        (shape((rows, hidden), BF), row_block(hidden)),
        (shape((rows, width), BF), row_block(width)),
        (shape((rows, hidden), BF), row_block(hidden)),
        (shape((rows, width), BF), row_block(width)),
        (shape((rows, width), F32), row_block(width)),
        (shape((8, hidden), F32), kept((8, hidden))),
        (shape((sums, width), F32), kept((sums, width))),
    ] + [(shape((shards, rows, LANES), BF), by_shard)] * parts
    return pl.pallas_call(
        partial(middle_kernel, parts, clips),
        out_shape=[o[0] for o in outs],
        grid=(rows // block,),
        in_specs=[by_shard] * parts
        + [
            row_block(width),
            row_block(width),
            row_block(1),
            whole(mod.shape),
            whole(out_w.shape),
            whole((1, width)),
            whole(w1.shape),
            whole((1, hidden)),
            whole(w2.shape),
            whole((1, width)),
        ],
        out_specs=[o[1] for o in outs],
        compiler_params=pltpu.CompilerParams(vmem_limit_bytes=56 << 20),
        cost_estimate=pl.CostEstimate(
            flops=2 * rows * width * (4 * hidden + 2 * width), bytes_accessed=20 << 20, transcendentals=0
        ),
    )(*o_parts, x1, grad, seg, mod, out_w, out_b[None], w1, b1[None], w2, b2[None])


def exchange(values, axis):
    return lax.all_to_all(values, axis, 0, 0)


def local(
    mel_pair, text_ids, clip_lengths, t_index,
    txt_table, txt_conv, txt_vec, txt_gain, txt_up, txt_hid, txt_down,
    emb_mel, emb_text, emb_bias, pos_conv, pos_bias,
    time_w1, time_bias, time_w2, ada_w, ada_b,
    qkv_w, qkv_b, out_w, out_b, ff_w1, ff_b1, ff_w2, ff_b2, out_grad,
):
    total = mel_pair.shape[0]
    width = emb_mel.shape[1]
    shards, groups = lax.axis_size("mp"), lax.axis_size("dp")
    rank, place = lax.axis_index("mp"), lax.axis_index("dp")
    rows = total // shards
    cols = width // shards
    clips = clip_lengths.shape[1]
    first = rank * rows
    taps = pos_conv.shape[1]
    group = pos_conv.shape[2]

    def spread_slice(weight, axis):
        piece = weight.shape[axis] // groups
        return lax.dynamic_slice_in_dim(weight, place * piece, piece, axis)

    def to_all(piece, axis_name="mp"):
        size = lax.axis_size(axis_name)
        return lax.all_to_all(jnp.broadcast_to(piece[None], (size,) + piece.shape), axis_name, 0, 0)

    def gather(piece, axis):
        return lax.all_gather(piece, "dp", axis=axis, tiled=True)

    def three(values):
        one = lax.reduce_precision(values, 8, 7)
        two = lax.reduce_precision(values - one, 8, 7)
        return jnp.concatenate([one, two, values - one - two], axis=0).astype(BF)

    qkv_piece = spread_slice(qkv_w, 1)
    qkv_piece = jnp.concatenate([pair_split(qkv_piece[:2]), qkv_piece[2:]], axis=0)
    in_rows = qkv_piece.shape[1]
    biases = jnp.concatenate(
        [pair_split(qkv_b[:2]), qkv_b[2:], ff_b1.reshape(-1, cols)], axis=0
    )
    bias_rows = biases.shape[0]
    biases = three(biases)
    biases = jnp.pad(biases, ((0, -biases.shape[0] % 16), (0, 0)))
    received = to_all(jnp.concatenate([qkv_piece.reshape(3 * in_rows, cols), biases], axis=0))
    qkv_full = gather(received[:, : 3 * in_rows].reshape(shards, 3, in_rows, cols), 2)
    biases = received[:, 3 * in_rows :].astype(F32)
    biases = sum(biases[:, i * bias_rows : (i + 1) * bias_rows] for i in range(3))
    qkv_bias = biases[:, :3]
    b1_full = biases[:, 3:].reshape(-1)
    out_piece, w2_piece, w1_piece = spread_slice(out_w, 0), spread_slice(ff_w2, 0), spread_slice(ff_w1, 0)
    w1_shape = w1_piece.shape
    cut = [out_piece.shape[0], out_piece.shape[0] + w2_piece.shape[0]]
    all_steps = lax.all_gather(t_index, "dp", tiled=True).reshape(-1)

    lengths = clip_lengths[0]
    clip_index = jnp.arange(clips, dtype=jnp.int32)
    ends = jnp.sum(jnp.where(clip_index[:, None] >= clip_index[None, :], lengths[None, :], 0), axis=1)
    starts = ends - lengths
    frames = jnp.arange(total, dtype=jnp.int32)
    member = (frames[:, None] >= starts[None, :]) & (frames[:, None] < ends[None, :])
    segment = jnp.sum(member * clip_index[None, :], axis=1).astype(jnp.int32)
    position = frames - jnp.sum(member * starts[None, :], axis=1)
    ext = rows + 2 * HALO
    ids = lax.dynamic_slice_in_dim(jnp.pad(text_ids, (HALO, HALO)), first, ext)
    seg_ext = lax.dynamic_slice_in_dim(jnp.pad(segment, (HALO, HALO), constant_values=-1), first, ext)
    hot_ext = (seg_ext[:, None] == clip_index[None, :]).astype(F32)
    ext_index = jnp.arange(ext, dtype=jnp.int32)
    inside = (ext_index >= HALO) & (ext_index < HALO + rows)
    own_ext = jnp.where(inside[:, None], hot_ext, 0.0)
    hot = hot_ext[HALO : HALO + rows]

    def time_path(steps):
        half = time_w1.shape[0] // 2
        frequency = jnp.exp(jnp.arange(half, dtype=F32) * (-math.log(10000.0) / (half - 1)))
        angles = steps.astype(F32)[:, None] * frequency[None, :]
        sinusoid = jnp.concatenate([jnp.sin(angles), jnp.cos(angles)], axis=-1)
        pre_one = precise(sinusoid, time_w1) + time_bias[0]
        act_one = jax.nn.silu(pre_one)
        time_vec = precise(act_one, time_w2) + time_bias[1]
        return sinusoid, pre_one, act_one, time_vec, jax.nn.silu(time_vec)

    mod = precise(time_path(t_index[0])[4], ada_w) + ada_b

    hidden = jnp.take(txt_table, ids, axis=0).astype(F32)
    kept = []
    blocks = txt_conv.shape[0]
    for b in range(blocks):
        hidden, saved = text_ahead(
            hidden, seg_ext, hot_ext, own_ext, txt_conv[b], txt_vec[b], txt_gain[b],
            txt_up[b], txt_hid[b], txt_down[b],
        )
        kept.append(saved)
    text = hidden[HALO : HALO + rows].astype(BF)

    mel = lax.dynamic_slice_in_dim(mel_pair, first, rows)
    x0 = dot(mel, emb_mel) + dot(text, emb_text) + emb_bias

    def to_channels(values):
        blocks_of = values.reshape(rows, shards, cols).transpose(1, 0, 2)
        return exchange(blocks_of, "mp").reshape(total, cols)

    def to_rows(values):
        return exchange(values.reshape(shards, rows, cols), "mp").transpose(1, 0, 2).reshape(rows, width)

    channels = to_channels(x0.astype(BF))
    pieces = jnp.concatenate([out_piece, w2_piece, w1_piece.reshape(-1, width)], axis=0)
    pieces, channels = lax.optimization_barrier((pieces, channels))
    spread_in = spread(channels.astype(F32), starts, ends)
    pre_a = apply_conv(spread_in, pos_conv[0], False) + pos_bias[0]
    received = to_all(pieces)
    received, pre_a = lax.optimization_barrier((received, pre_a))
    out_full = gather(received[:, : cut[0]], 1).reshape(width, width)
    w1_piece = received[:, cut[1] :].reshape((shards,) + w1_shape).transpose(1, 0, 2)
    w1_full = gather(w1_piece.reshape(w1_shape[0], -1), 0)
    w2_full = gather(received[:, cut[0] : cut[1]], 1).reshape(-1, width)
    y_a = jnp.pad(
        only_clips(mish(pre_a), starts, ends).astype(BF).astype(F32), ((GAP, GAP), (0, 0))
    )
    pre_b = apply_conv(y_a, pos_conv[1], False) + pos_bias[1]
    c_pos = to_rows(gather_back(mish(pre_b).astype(BF), starts, ends))
    x1 = x0 + c_pos.astype(F32)

    def modulate(state, mod_in, shift_part, scale_part):
        scale = expand(hot, mod_in[:, scale_part * width : (scale_part + 1) * width])
        shift = expand(hot, mod_in[:, shift_part * width : (shift_part + 1) * width])
        return layer_norm(state) * (1.0 + scale) + shift

    n1, n1_pull = jax.vjp(lambda s, m: modulate(s, m, 0, 1), x1, mod)
    n1 = n1.astype(BF)
    inverse = jnp.exp(jnp.arange(0, HEAD_DIM, 2, dtype=F32) * (-math.log(10000.0) / HEAD_DIM))
    angles = position.astype(F32)[:, None] * jnp.tile(inverse, LANES // inverse.shape[0])[None, :]
    cos = jnp.cos(angles)
    sin = jnp.sin(angles) * jnp.where(jnp.arange(LANES) < LANES // 2, -1.0, 1.0)
    cos_own = lax.dynamic_slice_in_dim(cos, first, rows)
    sin_own = lax.dynamic_slice_in_dim(sin, first, rows)
    parts = range(cols // LANES)
    qkv = [exchange(v, "mp") for v in project(n1, qkv_full, qkv_bias, cos_own, sin_own)]
    block = rows
    heads_of = segment[::block]
    tails_of = segment[block - 1 :: block]
    low_key = jnp.sum(jnp.where(heads_of[:, None] == clip_index, starts[None, :], 0), axis=1)
    high_key = jnp.sum(jnp.where(tails_of[:, None] == clip_index, ends[None, :], 0), axis=1)
    bounds = jnp.stack([low_key // rows, (high_key + rows - 1) // rows], axis=1).astype(jnp.int32)
    seg_rows = segment[None, :]
    seg_blocks = segment.reshape(shards, rows, 1)
    attended = [attend(qkv[h], seg_rows, seg_blocks, bounds, block) for h in parts]
    o_parts = [exchange(a[0].reshape(shards, rows, LANES), "mp") for a in attended]
    grad = lax.dynamic_slice_in_dim(out_grad, first, rows)
    seg_own = lax.dynamic_slice_in_dim(segment, first, rows)[:, None]
    out, n2, r, df, dh, da, dx2, g_ff_b1, sums, *do_parts = middle(
        o_parts, x1, grad, seg_own, mod, out_full, out_b, w1_full, b1_full, w2_full, ff_b2
    )
    g_ff_b1, g_ff_b2, g_out_b = g_ff_b1[0], sums[4 * clips], sums[4 * clips + 1]
    dmod_gate_f, dmod_shift_f, dmod_scale_f, dmod_gate_a = (
        sums[i * clips : (i + 1) * clips] for i in range(4)
    )
    g_ff_w2 = dot(df, r, TN)
    g_ff_w1 = dot(n2, dh, TN)
    o_rows = jnp.stack(o_parts).transpose(2, 1, 0, 3).reshape(rows, width)

    def for_dp(matrix):
        return matrix.astype(BF).reshape(groups, matrix.shape[0] // groups, matrix.shape[1])

    def by_rank(matrix):
        return matrix.reshape(matrix.shape[0], shards, -1).transpose(1, 0, 2)

    def scatter_dp(matrix):
        return lax.psum_scatter(matrix.astype(BF), "dp", scatter_dimension=0, tiled=True)

    sent_w1, sent_w2 = scatter_dp(g_ff_w1), scatter_dp(g_ff_w2)

    g_out_w = dot(da, o_rows, TN)
    dqkv = []
    for h in parts:
        do_part = exchange(do_parts[h], "mp").reshape(total, LANES)
        d_part = attend_back(
            qkv[h], attended[h][1], attended[h][2], do_part, seg_rows, seg_blocks, cos, sin, bounds, block
        )
        dqkv.append(exchange(d_part, "mp"))
    dn1, g_qkv_w, g_qkv_b = unproject(dqkv, n1, qkv_full)
    more, dmod_d = n1_pull(dn1)
    dx1 = dx2 + more
    sent_w1, sent_w2, dx1, out = lax.optimization_barrier((sent_w1, sent_w2, dx1, out))
    result = lax.all_gather(out, "mp", tiled=True)
    ff_pair = jnp.concatenate([by_rank(sent_w1), by_rank(sent_w2)], axis=2)
    sent_qkv, sent_out = scatter_dp(g_qkv_w), scatter_dp(g_out_w)

    dmod = dmod_d + jnp.concatenate(
        [
            jnp.zeros((clips, 2 * width), F32), dmod_gate_a, dmod_shift_f, dmod_scale_f, dmod_gate_f,
        ],
        axis=1,
    )

    slope_b = gather_back(mish_slope(pre_b), starts, ends)
    dy_b = to_channels(dx1.astype(BF)).astype(F32) * slope_b
    g_pos_b = jnp.sum(dy_b, axis=0)
    dy_b = spread(dy_b.astype(BF).astype(F32), starts, ends)
    dy_a = only_clips(apply_conv(dy_b, pos_conv[1], True) * mish_slope(pre_a), starts, ends)
    g_pos_a = jnp.sum(dy_a, axis=0)
    dy_a = jnp.pad(dy_a.astype(BF).astype(F32), ((GAP, GAP), (0, 0)))
    dc = gather_back(
        apply_conv(dy_a, pos_conv[0], True).astype(BF), starts, ends
    )
    ff_got, dc = lax.optimization_barrier((exchange(ff_pair, "mp"), dc))
    dx0_full = dx1 + to_rows(dc).astype(F32)
    g_conv = jnp.concatenate(
        [conv_grad(spread_in, dy_a[GAP:-GAP], taps, group), conv_grad(y_a, dy_b[GAP:-GAP], taps, group)],
        axis=1,
    )
    sent_qkv, sent_out, dx0_full = lax.optimization_barrier((sent_qkv, sent_out, dx0_full))
    at_pair = jnp.concatenate([by_rank(sent_qkv), by_rank(sent_out)], axis=2)
    sent_conv = scatter_dp(g_conv)

    g_emb_bias = jnp.sum(dx0_full, axis=0)
    dx0 = dx0_full.astype(BF)
    mel_grad = dot(dx0, emb_mel, NT).astype(BF)
    g_emb = jnp.concatenate([dot(dx0, text, TN), dot(dx0, mel, TN)], axis=1)
    sent_emb = scatter_dp(g_emb)
    text_width = text.shape[1]

    dtext = jnp.pad(dot(dx0, emb_text, NT), ((HALO, HALO), (0, 0)))
    text_grads = [None] * blocks
    extra = dmod
    at_got, result, dtext = lax.optimization_barrier((exchange(at_pair, "mp"), result, dtext))
    result = result.astype(F32)
    for b in reversed(range(blocks)):
        dtext, text_grads[b], summed = text_behind(kept[b], dtext, txt_up[b], txt_down[b], extra)
        if extra is not None:
            dmod_all = lax.all_gather(summed, "dp", tiled=True)
            sent_conv, dtext = lax.optimization_barrier((sent_conv, dtext))
        extra = None
    sent_emb, dtext = lax.optimization_barrier((sent_emb, dtext))
    vocab = txt_table.shape[0]
    wide = -(-vocab // 128) * 128
    chosen = (ids[:, None] == jnp.arange(wide, dtype=jnp.int32)[None, :]).astype(BF)
    g_table = dot(dtext, chosen, TN)
    hidden_width = txt_up.shape[2]

    def placed(values):
        full = jnp.zeros((shards,) + values.shape, F32)
        return lax.dynamic_update_slice_in_dim(full, values[None], rank, 0)

    g_pos_bias = placed(jnp.stack([g_pos_a, g_pos_b])).transpose(1, 0, 2).reshape(2, width)
    g_qkv_b = jnp.concatenate([pair_merge(g_qkv_b[:, :2]), g_qkv_b[:, 2:]], axis=1)
    g_qkv_b = g_qkv_b.transpose(1, 0, 2).reshape(3, width)
    small = [
        (jnp.stack([g[0] for g in text_grads]), "both"),
        (jnp.stack([g[1] for g in text_grads]), "both"),
        (jnp.stack([g[2] for g in text_grads]), "both"),
        (jnp.stack([g[4] for g in text_grads]), "both"),
        (g_emb_bias, "dp"),
        (g_pos_bias, "crossed"),
        (g_qkv_b, "crossed"),
        (g_out_b, "dp"),
        (g_ff_b1, "crossed"),
        (g_ff_b2, "dp"),
    ]
    packed = []
    for value, kind in small:
        lead = value.size // value.shape[-1]
        if kind == "crossed":
            value = value.reshape(lead, shards, groups, -1).transpose(2, 0, 1, 3)
        else:
            value = value.reshape(lead, groups, -1).transpose(1, 0, 2)
        packed.append(value.reshape(groups, -1))
    packed = jnp.concatenate(packed, axis=1)
    length = packed.shape[1]
    packed = jnp.pad(packed, ((0, 0), (0, -length % 1024))).reshape(groups, -1, 128)
    table_sum, up0, up1, down0, down1, packed, g_emb, mel_grad = last_sums(
        [for_dp(g_table)]
        + [for_dp(text_grads[b][3]) for b in range(blocks)]
        + [for_dp(text_grads[b][5]) for b in range(blocks)],
        packed,
        [],
        [sent_emb],
        [mel_grad],
    )
    mel_grad = mel_grad.reshape(total, -1)
    packed = packed.reshape(-1)
    unpacked, at = [], 0
    for value, kind in small:
        size = value.size // groups
        piece = packed[at : at + size]
        at += size
        if kind == "dp":
            unpacked.append(piece.reshape(value.shape[:-1] + (-1,)))
        else:
            piece = piece.reshape(value.size // value.shape[-1], shards, -1)
            piece = lax.dynamic_slice_in_dim(piece, rank, 1, 1)
            unpacked.append(piece.reshape(value.shape[:-1] + (-1,)))
    o_table = table_sum[:, :vocab].T
    o_up = jnp.stack([up0.T, up1.T])
    o_down = jnp.stack([down0.T, down1.T])
    ff_pair, at_pair = (jnp.sum(v.astype(F32), axis=0) for v in (ff_got, at_got))
    ff_cols = ff_w1.shape[1]
    o_ff_w1, o_ff_w2 = ff_pair[:, :ff_cols], ff_pair[:, ff_cols:].T
    g_qkv = at_pair[:, : 3 * cols].reshape(-1, 3, cols).transpose(1, 0, 2)
    o_qkv_w = jnp.concatenate([pair_merge(g_qkv[:2]), g_qkv[2:]], axis=0)
    o_out_w = at_pair[:, 3 * cols :].T
    o_pos_conv = sent_conv.astype(F32).T.reshape(2, taps, group, -1)
    o_emb_text, o_emb_mel = g_emb[:, :text_width].T, g_emb[:, text_width:].T

    def own(values, index, parts):
        piece = values.shape[-1] // parts
        return lax.dynamic_slice_in_dim(values, index * piece, piece, values.ndim - 1)

    sinusoid, pre_one, act_one, time_vec, act_two = time_path(all_steps)
    de = precise(dmod_all, ada_w, NT) * silu_slope(time_vec)
    dpre = precise(de, time_w2, NT) * silu_slope(pre_one)

    def outer(left, right):
        return lax.dot_general(left, own(right, place, groups), TN, precision=highest)

    return (
        result,
        mel_grad,
        o_table,
        unpacked[0],
        unpacked[1],
        unpacked[2],
        o_up,
        unpacked[3],
        o_down,
        o_emb_mel,
        o_emb_text,
        unpacked[4],
        o_pos_conv,
        unpacked[5],
        outer(sinusoid, dpre),
        own(jnp.stack([jnp.sum(dpre, axis=0), jnp.sum(de, axis=0)]), place, groups),
        outer(act_one, de),
        outer(act_two, dmod_all),
        own(jnp.sum(dmod_all, axis=0), place, groups),
        o_qkv_w,
        unpacked[6],
        o_out_w,
        unpacked[7],
        o_ff_w1,
        unpacked[8],
        o_ff_w2,
        unpacked[9],
    )


def solution(mesh):
    both, crossed = ("dp", "mp"), ("mp", "dp")
    placed = (
        P("dp", None), P("dp"), P("dp", None), P("dp", None),
        P(), P(), P(), P(), P(), P(), P(), P(), P(), P(),
        P(None, None, None, "mp"), P(None, "mp"),
        P(), P(), P(), P(), P(),
        P(None, None, "mp"), P(None, "mp"), P("mp", None), P(),
        P(None, "mp"), P("mp"), P("mp", None), P(),
        P("dp", None),
    )
    given = (
        P("dp", None), P("dp", None),
        P(None, both), P(None, None, both), P(None, None, both), P(None, both),
        P(None, None, both), P(None, None, both), P(None, None, both),
        P(None, "dp"), P(None, "dp"), P("dp"),
        P(None, None, None, crossed), P(None, crossed),
        P(None, "dp"), P(None, "dp"), P(None, "dp"), P(None, "dp"), P("dp"),
        P(None, "dp", "mp"), P(None, crossed), P("mp", "dp"), P("dp"),
        P("dp", "mp"), P(crossed), P("mp", "dp"), P("dp"),
    )
    return jax.shard_map(local, mesh=mesh, in_specs=placed, out_specs=given, check_vma=False)
```

```python
from functools import partial
import math

import jax
import jax.numpy as jnp
from jax import lax
from jax.experimental import pallas as pl
from jax.experimental.pallas import tpu as pltpu
from jax.sharding import PartitionSpec as P

HEAD_DIM = 64
GAP = 16
HALO = 8
BF = jnp.bfloat16
F32 = jnp.float32
highest = lax.Precision.HIGHEST
NN = (((1,), (0,)), ((), ()))
NT = (((1,), (1,)), ((), ()))
TN = (((0,), (0,)), ((), ()))


def dot(left, right, dims=NN):
    return lax.dot_general(left.astype(BF), right.astype(BF), dims, preferred_element_type=F32)


def precise(left, right, dims=NN):
    one = lax.reduce_precision(left, 8, 7)
    two = lax.reduce_precision(left - one, 8, 7)
    three = left - one - two
    rows = left.shape[0]
    stacked = jnp.concatenate([one, two, three], axis=0).astype(BF)
    product = lax.dot_general(stacked, right, dims, preferred_element_type=F32)
    return product[:rows] + product[rows : 2 * rows] + product[2 * rows :]


@jax.custom_vjp
def expand(onehot, parts):
    return sum(onehot[:, c : c + 1] * parts[c : c + 1] for c in range(parts.shape[0]))


def expand_ahead(onehot, parts):
    return expand(onehot, parts), onehot


def expand_behind(onehot, grad):
    return None, jnp.dot(onehot.T, grad, precision=highest)


expand.defvjp(expand_ahead, expand_behind)


def silu_slope(values):
    sigmoid_val = jax.nn.sigmoid(values)
    return sigmoid_val * (1.0 + values * (1.0 - sigmoid_val))


def layer_norm(values):
    centred = values - jnp.mean(values, axis=-1, keepdims=True)
    variance = jnp.mean(centred * centred, axis=-1, keepdims=True)
    return centred * lax.rsqrt(variance + 1e-06)


def mish(values):
    grown = jnp.exp(jnp.minimum(values, 20.0))
    wide = grown * (grown + 2.0)
    return values * (wide / (wide + 2.0))


def mish_slope(values):
    grown = jnp.exp(jnp.minimum(values, 20.0))
    wide = grown * (grown + 2.0)
    under = 1.0 / (wide + 2.0)
    return wide * under + values * (4.0 * grown * (1.0 + grown) * under * under)


def sum_kernel(axis, size, x_ref, o_ref, slots, send_sems, recv_sems):
    me = lax.axis_index(axis)
    barrier = pltpu.get_barrier_semaphore()
    peers = [lax.rem(me + step, size) for step in range(1, size)]
    for peer in peers:
        pl.semaphore_signal(
            barrier, inc=1, device_id={axis: peer}, device_id_type=pl.DeviceIdType.MESH
        )
    pl.semaphore_wait(barrier, size - 1)
    for step, peer in enumerate(peers):
        pltpu.make_async_remote_copy(
            src_ref=x_ref,
            dst_ref=slots.at[me],
            send_sem=send_sems.at[step],
            recv_sem=recv_sems.at[me],
            device_id={axis: peer},
            device_id_type=pl.DeviceIdType.MESH,
        ).start()
    slots[me] = x_ref[...]
    for step, peer in enumerate(peers):
        copy = pltpu.make_async_remote_copy(
            src_ref=x_ref,
            dst_ref=slots.at[peer],
            send_sem=send_sems.at[step],
            recv_sem=recv_sems.at[peer],
            device_id={axis: peer},
            device_id_type=pl.DeviceIdType.MESH,
        )
        copy.wait_send()
        copy.wait_recv()
    total = slots[0]
    for device in range(1, size):
        total = total + slots[device]
    o_ref[...] = total


def small_sum(values, axis, name):
    size = lax.axis_size(axis)
    whole = pl.BlockSpec(memory_space=pltpu.VMEM)
    return pl.pallas_call(
        partial(sum_kernel, axis, size),
        out_shape=jax.ShapeDtypeStruct(values.shape, F32),
        in_specs=[whole],
        out_specs=whole,
        scratch_shapes=[
            pltpu.VMEM((size,) + values.shape, F32),
            pltpu.SemaphoreType.DMA((size - 1,)),
            pltpu.SemaphoreType.DMA((size,)),
        ],
        compiler_params=pltpu.CompilerParams(
            collective_id=name, has_side_effects=True, vmem_limit_bytes=16 << 20
        ),
    )(values)


def last_kernel(dp, mp, n_all, n_mp, n_both, n_gather, *refs):
    n_in = n_all + n_mp + n_both + n_gather
    ins, outs, rest = refs[:n_in], refs[n_in : 2 * n_in], list(refs[2 * n_in :])

    def take(count):
        return [rest.pop(0) for _ in range(count)]

    own, pair, joint, chip_slots, middle, slots = (
        take(n_all), take(n_all), take(n_all), take(n_all), take(n_all), take(n_in)
    )
    pair_send, pair_recv, chip_send, chip_recv, mp_send, mp_recv, own_sems = rest
    me, z = lax.axis_index("dp"), lax.axis_index("mp")
    chips = dp // 2
    core, chip = lax.rem(me, 2), me // 2
    partner = me + 1 - 2 * core
    other_chips = [lax.rem(chip + step, chips) for step in range(1, chips)]
    other_z = [lax.rem(z + step, mp) for step in range(1, mp)]
    mesh_id = pl.DeviceIdType.MESH
    barrier = pltpu.get_barrier_semaphore()
    greeted = (
        [{"dp": partner}]
        + [{"dp": 2 * q + core} for q in other_chips]
        + [{"mp": peer} for peer in other_z]
    )
    for device in greeted:
        pl.semaphore_signal(barrier, inc=1, device_id=device, device_id_type=mesh_id)
    pl.semaphore_wait(barrier, chips + mp - 1)

    def to_partner(t):
        return pltpu.make_async_remote_copy(
            src_ref=ins[t].at[:, 1 - core],
            dst_ref=pair[t],
            send_sem=pair_send.at[t],
            recv_sem=pair_recv.at[t],
            device_id={"dp": partner},
            device_id_type=mesh_id,
        )

    def to_chip(t, step, mine):
        q = other_chips[step]
        return pltpu.make_async_remote_copy(
            src_ref=joint[t].at[q],
            dst_ref=chip_slots[t].at[mine],
            send_sem=chip_send.at[t, step],
            recv_sem=chip_recv.at[t, mine],
            device_id={"dp": 2 * q + core},
            device_id_type=mesh_id,
        )

    def to_z(t, step, mine):
        peer = other_z[step]
        if t < n_all - 1:
            source = middle[t].at[peer]
        elif t == n_all - 1:
            source = middle[t]
        else:
            source = ins[t].at[peer] if t < n_all + n_mp else ins[t]
        return pltpu.make_async_remote_copy(
            src_ref=source,
            dst_ref=slots[t].at[mine],
            send_sem=mp_send.at[t, step],
            recv_sem=mp_recv.at[t, mine],
            device_id={"mp": peer},
            device_id_type=mesh_id,
        )

    local = []
    for t in range(n_all):
        to_partner(t).start()
        copy = pltpu.make_async_copy(ins[t].at[:, core], own[t], own_sems.at[t])
        copy.start()
        local.append(copy)
    for t in range(n_all, n_in):
        for step in range(mp - 1):
            to_z(t, step, z).start()
        source = ins[t].at[z] if t < n_all + n_mp else ins[t]
        copy = pltpu.make_async_copy(source, slots[t].at[z], own_sems.at[t])
        copy.start()
        local.append(copy)

    def total(ref, size):
        value = ref[0].astype(F32)
        for device in range(1, size):
            value = value + ref[device].astype(F32)
        return value

    for t in range(n_all):
        local[t].wait()
        copy = to_partner(t)
        copy.wait_send()
        copy.wait_recv()
        for q in range(chips):
            value = own[t][q].astype(F32) + pair[t][q].astype(F32)
            joint[t][q] = value.astype(joint[t].dtype)
        for step in range(chips - 1):
            to_chip(t, step, chip).start()
        chip_slots[t][chip] = joint[t][chip]
    for t in range(n_all):
        for step in range(chips - 1):
            copy = to_chip(t, step, other_chips[step])
            copy.wait_send()
            copy.wait_recv()
        value = total(chip_slots[t], chips)
        if t < n_all - 1:
            rows = value.shape[0] // mp
            for device in range(mp):
                part = value[device * rows : (device + 1) * rows]
                middle[t][device] = part.astype(middle[t].dtype)
            slots[t][z] = middle[t][z]
        else:
            middle[t][...] = value
            slots[t][z] = value
        for step in range(mp - 1):
            to_z(t, step, z).start()
    for t in list(range(n_all, n_in)) + list(range(n_all)):
        if t >= n_all:
            local[t].wait()
        for step in range(mp - 1):
            copy = to_z(t, step, other_z[step])
            copy.wait_send()
            copy.wait_recv()
        if t < n_in - n_gather:
            outs[t][...] = total(slots[t], mp)
        else:
            outs[t][...] = slots[t][...].astype(F32)


def last_sums(over_all, small, over_mp, both, gathered):
    dp, mp = lax.axis_size("dp"), lax.axis_size("mp")
    chips = dp // 2
    everywhere = [v.reshape((chips, 2) + v.shape[1:]) for v in list(over_all) + [small]]
    ins = everywhere + list(over_mp) + list(both) + list(gathered)
    n_all, n_mp, n_both, n_gather = len(everywhere), len(over_mp), len(both), len(gathered)
    halves = [pltpu.VMEM((chips,) + v.shape[2:], v.dtype) for v in everywhere]
    outs, middle, slots = [], [], []
    for t, value in enumerate(ins):
        if t < n_all - 1:
            shape = (value.shape[2] // mp, value.shape[3])
            middle.append(pltpu.VMEM((mp,) + shape, value.dtype))
        elif t == n_all - 1:
            shape = value.shape[2:]
            middle.append(pltpu.VMEM(shape, value.dtype))
        else:
            shape = value.shape[1:] if t < n_all + n_mp else value.shape
        slots.append(pltpu.VMEM((mp,) + shape, value.dtype))
        outs.append((mp,) + shape if t >= len(ins) - n_gather else shape)
    dma = pltpu.SemaphoreType.DMA
    return pl.pallas_call(
        partial(last_kernel, dp, mp, n_all, n_mp, n_both, n_gather),
        out_shape=[jax.ShapeDtypeStruct(shape, F32) for shape in outs],
        in_specs=[pl.BlockSpec(memory_space=pl.ANY)] * len(ins),
        out_specs=[pl.BlockSpec(memory_space=pltpu.VMEM)] * len(ins),
        scratch_shapes=halves * 4
        + middle
        + slots
        + [
            dma((n_all,)),
            dma((n_all,)),
            dma((n_all, chips)),
            dma((n_all, chips)),
            dma((len(ins), mp)),
            dma((len(ins), mp)),
            dma((len(ins),)),
        ],
        compiler_params=pltpu.CompilerParams(
            collective_id=3, has_side_effects=True, vmem_limit_bytes=56 << 20
        ),
    )(*ins)


def conv_norm(hidden, segment, conv, vec, gain):
    taps = conv.shape[0]
    reach = taps // 2
    rows = hidden.shape[0]
    padded = jnp.pad(hidden, ((reach, reach), (0, 0)))
    seg_padded = jnp.pad(segment, (reach, reach), constant_values=-1)
    mixture = vec[0]
    for tap in range(taps):
        keep = (seg_padded[tap : tap + rows] == segment) & (segment >= 0)
        mixture = mixture + conv[tap] * jnp.where(keep[:, None], padded[tap : tap + rows], 0.0)
    return layer_norm(mixture) * gain + vec[1]


def activate(pre, bias):
    return jax.nn.gelu(pre + bias, approximate=False)


def clip_squares(own, active):
    return jnp.dot(own.T, active * active, precision=highest)


def respond(active, squares, onehot, scale, shift):
    norms = jnp.sqrt(jnp.maximum(squares, 1.0))
    ratio = norms / (jnp.mean(norms, axis=-1, keepdims=True) + 1e-06)
    return scale * (active * expand(onehot, ratio)) + shift + active


def text_ahead(hidden, segment, onehot, own, conv, vec, gain, up, hid, down):
    normed, norm_pull = jax.vjp(
        lambda h, c, v, g: conv_norm(h, segment, c, v, g), hidden, conv, vec, gain
    )
    normed = normed.astype(BF)
    active, act_pull = jax.vjp(activate, dot(normed, up), hid[0])
    squares, square_pull = jax.vjp(lambda a: clip_squares(own, a), active)
    squares = small_sum(squares, "mp", 1)
    grown, respond_pull = jax.vjp(
        lambda a, s, g, b: respond(a, s, onehot, g, b), active, squares, hid[1], hid[2]
    )
    grown = grown.astype(BF)
    result = hidden + dot(grown, down) + vec[2]
    return result, (norm_pull, normed, act_pull, square_pull, respond_pull, grown)


def text_behind(kept, grad, up, down, extra, waiting):
    norm_pull, normed, act_pull, square_pull, respond_pull, grown = kept
    grad_low = grad.astype(BF)
    g_out = jnp.sum(grad, axis=0)
    g_down = dot(grad_low, grown, TN)
    grad_active, grad_squares, g_scale, g_shift = respond_pull(dot(grad_low, down, NT))
    grad_squares, waiting = lax.optimization_barrier((grad_squares, waiting))
    if extra is None:
        grad_squares = small_sum(grad_squares, "mp", 1)
    else:
        joined = small_sum(jnp.concatenate([grad_squares, extra], axis=1), "mp", 2)
        grad_squares, extra = joined[:, : grad_squares.shape[1]], joined[:, grad_squares.shape[1] :]
    grad_active = grad_active + square_pull(grad_squares)[0]
    grad_pre, g_bias = act_pull(grad_active)
    pre_low = grad_pre.astype(BF)
    g_up = dot(pre_low, normed, TN)
    grad_hidden, g_conv, g_vec, g_gain = norm_pull(dot(pre_low, up, NT))
    g_vec = g_vec.at[2].add(g_out)
    return (
        grad + grad_hidden,
        (g_conv, g_vec, g_gain, g_up, jnp.stack([g_bias, g_scale, g_shift]), g_down),
        extra,
        waiting,
    )


def spread(values, starts, ends):
    rows = values.shape[0]
    clips = starts.shape[0]
    at = lax.broadcasted_iota(jnp.int32, values.shape, 0)
    total = rows + GAP * clips + 2 * GAP
    out = None
    for c in range(clips):
        part = jnp.where((at >= starts[c]) & (at < ends[c]), values, 0)
        lead = GAP + GAP * c
        part = jnp.pad(part, ((lead, total - lead - rows), (0, 0)))
        out = part if out is None else out + part
    return out


def only_clips(values, starts, ends):
    at = lax.broadcasted_iota(jnp.int32, values.shape, 0)
    keep = None
    for c in range(starts.shape[0]):
        inside = (at >= starts[c] + GAP * c) & (at < ends[c] + GAP * c)
        keep = inside if keep is None else keep | inside
    return jnp.where(keep, values, 0.0)


def gather_back(values, starts, ends):
    clips = starts.shape[0]
    rows = values.shape[0] - GAP * clips
    at = lax.broadcasted_iota(jnp.int32, (rows, values.shape[1]), 0)
    out = values[:rows]
    for c in range(1, clips):
        out = jnp.where(at >= starts[c], values[GAP * c : GAP * c + rows], out)
    return out


def conv_kernel(taps, turned, x_ref, w_ref, o_ref, full_ref):
    rows, width = o_ref.shape
    group = w_ref.shape[1]
    first = GAP - taps // 2

    @pl.when(pl.program_id(0) == 0)
    def _():
        lane = lax.broadcasted_iota(jnp.int32, (group, width), 1) // group
        for k in range(taps):
            tap = w_ref[taps - 1 - k if turned else k]
            for g in range(width // group):
                piece = jnp.where(lane == g, tap, jnp.zeros_like(tap))
                if turned:
                    full_ref[g * group : (g + 1) * group, k * width : (k + 1) * width] = piece
                else:
                    full_ref[k * width + g * group : k * width + (g + 1) * group, :] = piece

    columns = [x_ref[first + k : first + k + rows, :].astype(BF) for k in range(taps)]
    o_ref[...] = lax.dot_general(
        jnp.concatenate(columns, axis=1),
        full_ref[...],
        NT if turned else NN,
        preferred_element_type=F32,
    )


def conv_chunk(rows):
    for size in (528, 352, 256, 128, 64, 32, 16):
        if rows % size == 0:
            return size
    return rows


def apply_conv(spread_rows, weight, turned):
    rows = spread_rows.shape[0] - 2 * GAP
    width = spread_rows.shape[1]
    taps, group = weight.shape[:2]
    chunk = conv_chunk(rows)
    return pl.pallas_call(
        partial(conv_kernel, taps, turned),
        out_shape=jax.ShapeDtypeStruct((rows, width), F32),
        grid=(rows // chunk,),
        in_specs=[
            pl.BlockSpec((pl.Element(chunk + 2 * GAP), pl.Element(width)), lambda i: (i * chunk, 0)),
            pl.BlockSpec(weight.shape, lambda i: (0, 0, 0), pipeline_mode=pl.Buffered(1)),
        ],
        out_specs=pl.BlockSpec((chunk, width), lambda i: (i, 0)),
        scratch_shapes=[
            pltpu.VMEM((width, taps * width) if turned else (taps * width, width), BF)
        ],
        compiler_params=pltpu.CompilerParams(vmem_limit_bytes=48 << 20),
        cost_estimate=pl.CostEstimate(
            flops=2 * rows * taps * width * width, bytes_accessed=8 << 20, transcendentals=0
        ),
    )(spread_rows, weight)


def conv_grad_kernel(taps, group, x_ref, g_ref, o_ref):
    rows, width = g_ref.shape
    first = GAP - taps // 2
    turned = g_ref[...].T.astype(BF)

    @pl.when(pl.program_id(0) == 0)
    def _():
        o_ref[...] = jnp.zeros_like(o_ref)

    for k in range(taps):
        window = x_ref[first + k : first + k + rows, :].astype(BF)
        product = jnp.dot(turned, window, preferred_element_type=F32)
        for g in range(width // group):
            own = slice(g * group, (g + 1) * group)
            o_ref[own, k * group : (k + 1) * group] += product[own, own]


def conv_grad(spread_rows, grads, taps, group):
    rows, width = grads.shape
    chunk = conv_chunk(rows)
    return pl.pallas_call(
        partial(conv_grad_kernel, taps, group),
        out_shape=jax.ShapeDtypeStruct((width, taps * group), F32),
        grid=(rows // chunk,),
        in_specs=[
            pl.BlockSpec((pl.Element(chunk + 2 * GAP), pl.Element(width)), lambda i: (i * chunk, 0)),
            pl.BlockSpec((chunk, width), lambda i: (i, 0)),
        ],
        out_specs=pl.BlockSpec((width, taps * group), lambda i: (0, 0)),
        compiler_params=pltpu.CompilerParams(vmem_limit_bytes=48 << 20),
        cost_estimate=pl.CostEstimate(
            flops=2 * rows * taps * width * width, bytes_accessed=8 << 20, transcendentals=0
        ),
    )(spread_rows, grads)


LANES = 128


def pair_split(columns):
    pairs = columns.reshape(*columns.shape[:-1], -1, LANES // 2, 2)
    return jnp.swapaxes(pairs, -1, -2).reshape(columns.shape)


def pair_merge(columns):
    pairs = columns.reshape(*columns.shape[:-1], -1, 2, LANES // 2)
    return jnp.swapaxes(pairs, -1, -2).reshape(columns.shape)


def project_kernel(x_ref, w_ref, b_ref, cos_ref, sin_ref, *out_refs):
    cos, sin = cos_ref[...], sin_ref[...]
    for p in range(3):
        value = jnp.dot(x_ref[...], w_ref[p], preferred_element_type=F32) + b_ref[p : p + 1, :]
        for at, out_ref in enumerate(out_refs):
            piece = value[:, at * LANES : (at + 1) * LANES]
            if p < 2:
                piece = piece * cos + pltpu.roll(piece, LANES // 2, 1) * sin
            out_ref[p] = piece.astype(BF)


def project(normed, weight, bias, cos, sin):
    rows = normed.shape[0]
    shards, _, width, cols = weight.shape
    parts = cols // LANES
    return pl.pallas_call(
        project_kernel,
        out_shape=[jax.ShapeDtypeStruct((shards, 3, rows, LANES), BF)] * parts,
        grid=(shards,),
        in_specs=[
            pl.BlockSpec((rows, width), lambda i: (0, 0)),
            pl.BlockSpec((None, 3, width, cols), lambda i: (i, 0, 0, 0)),
            pl.BlockSpec((None, 3, cols), lambda i: (i, 0, 0)),
            pl.BlockSpec((rows, LANES), lambda i: (0, 0)),
            pl.BlockSpec((rows, LANES), lambda i: (0, 0)),
        ],
        out_specs=[pl.BlockSpec((None, 3, rows, LANES), lambda i: (i, 0, 0, 0))] * parts,
        compiler_params=pltpu.CompilerParams(vmem_limit_bytes=32 << 20),
        cost_estimate=pl.CostEstimate(
            flops=6 * rows * width * width, bytes_accessed=10 << 20, transcendentals=0
        ),
    )(normed, weight, bias, cos, sin)


def unproject_kernel(parts, *refs):
    d_refs, (x_ref, w_ref, dx_ref, gw_ref, gb_ref, turned) = refs[:parts], refs[parts:]
    s = pl.program_id(0)
    cols = w_ref.shape[2]

    @pl.when(s == 0)
    def _():
        turned[...] = x_ref[...].T
        dx_ref[...] = jnp.zeros_like(dx_ref)

    total = None
    for p in range(3):
        grad = jnp.concatenate([d_ref[p] for d_ref in d_refs], axis=1)
        product = lax.dot_general(grad, w_ref[p], NT, preferred_element_type=F32)
        total = product if total is None else total + product
        weight = jnp.dot(turned[...], grad, preferred_element_type=F32)
        gw_ref[:, p * cols : (p + 1) * cols] = weight.astype(BF)
        gb_ref[p : p + 1, :] = jnp.sum(grad.astype(F32), axis=0, keepdims=True)
    dx_ref[...] += total


def unproject(grads, normed, weight):
    rows = normed.shape[0]
    shards, _, width, cols = weight.shape
    parts = len(grads)
    return pl.pallas_call(
        partial(unproject_kernel, parts),
        out_shape=[
            jax.ShapeDtypeStruct((rows, width), F32),
            jax.ShapeDtypeStruct((width, shards * 3 * cols), BF),
            jax.ShapeDtypeStruct((shards, 3, cols), F32),
        ],
        grid=(shards,),
        in_specs=[pl.BlockSpec((None, 3, rows, LANES), lambda i: (i, 0, 0, 0))] * parts
        + [
            pl.BlockSpec((rows, width), lambda i: (0, 0)),
            pl.BlockSpec((None, 3, width, cols), lambda i: (i, 0, 0, 0)),
        ],
        out_specs=[
            pl.BlockSpec((rows, width), lambda i: (0, 0)),
            pl.BlockSpec((width, 3 * cols), lambda i: (0, i)),
            pl.BlockSpec((None, 3, cols), lambda i: (i, 0, 0)),
        ],
        scratch_shapes=[pltpu.VMEM((width, rows), BF)],
        compiler_params=pltpu.CompilerParams(vmem_limit_bytes=48 << 20),
        cost_estimate=pl.CostEstimate(
            flops=12 * rows * width * width, bytes_accessed=20 << 20, transcendentals=0
        ),
    )(*grads, normed, weight)


def head_masks(width):
    heads = width // HEAD_DIM
    lane = lax.broadcasted_iota(jnp.int32, (1, width), 1)
    half = HEAD_DIM // 2
    paired = [((lane % (width // 2)) // half) == h for h in range(heads)]
    plain = [(lane // HEAD_DIM) == h for h in range(heads)]
    return heads, paired, plain


def masked(values, masks):
    return [jnp.where(mask, values, jnp.zeros_like(values)) for mask in masks]


def attend_kernel(bounds, q_ref, k_ref, v_ref, sq_ref, sk_ref, o_ref, full_ref, lse_ref, vt_ref):
    i = pl.program_id(0)
    rows, width = q_ref.shape
    heads, paired, _ = head_masks(width)

    @pl.when(i == 0)
    def _():
        for b in range(v_ref.shape[0]):
            vt_ref[b] = v_ref[b].T

    q_heads = masked(q_ref[...] * jnp.asarray(HEAD_DIM**-0.5, BF), paired)
    sq = sq_ref[...]

    def step(kb, carry):
        k = k_ref[kb]
        same = sk_ref[kb] == sq
        new = []
        for h in range(heads):
            top_was, total, acc = carry[h]
            scores = lax.dot_general(k, q_heads[h], NT, preferred_element_type=F32)
            scores = jnp.where(same, scores, -1e30)
            top = jnp.maximum(top_was, jnp.max(scores, axis=0, keepdims=True))
            fade = jnp.exp(top_was - top)
            weight = jnp.exp(scores - top)
            total = fade * total + jnp.sum(weight, axis=0, keepdims=True)
            v_head = vt_ref[kb, h * HEAD_DIM : (h + 1) * HEAD_DIM, :]
            acc = acc * fade + jnp.dot(v_head, weight.astype(BF), preferred_element_type=F32)
            new.append((top, total, acc))
        return tuple(new)

    start = tuple(
        (jnp.full((1, rows), -1e30, F32), jnp.zeros((1, rows), F32), jnp.zeros((HEAD_DIM, rows), F32))
        for _ in range(heads)
    )
    done = lax.fori_loop(bounds[i, 0], bounds[i, 1], step, start)
    full = jnp.concatenate([acc * (1.0 / total) for _, total, acc in done], axis=0)
    full_ref[...] = full
    o_ref[...] = full.T.astype(BF)
    row = lax.broadcasted_iota(jnp.int32, lse_ref.shape, 0)
    logs = jnp.zeros(lse_ref.shape, F32)
    for h, (top, total, _) in enumerate(done):
        logs = jnp.where(row == h, top + jnp.log(total), logs)
    lse_ref[...] = logs


def attend(qkv, seg_rows, seg_columns, bounds, block):
    shards, _, rows, width = qkv.shape
    total = shards * rows
    per = rows // block
    grid_spec = pltpu.PrefetchScalarGridSpec(
        num_scalar_prefetch=1,
        grid=(total // block,),
        in_specs=[
            pl.BlockSpec((None, None, block, width), lambda i, b: (i // per, 0, i % per, 0)),
            pl.BlockSpec((shards, None, rows, width), lambda i, b: (0, 1, 0, 0)),
            pl.BlockSpec((shards, None, rows, width), lambda i, b: (0, 2, 0, 0)),
            pl.BlockSpec((1, block), lambda i, b: (0, i)),
            pl.BlockSpec((shards, rows, 1), lambda i, b: (0, 0, 0)),
        ],
        out_specs=[
            pl.BlockSpec((block, width), lambda i, b: (i, 0)),
            pl.BlockSpec((width, block), lambda i, b: (0, i)),
            pl.BlockSpec((8, block), lambda i, b: (0, i)),
        ],
        scratch_shapes=[pltpu.VMEM((shards, width, rows), BF)],
    )
    return pl.pallas_call(
        attend_kernel,
        out_shape=[
            jax.ShapeDtypeStruct((total, width), BF),
            jax.ShapeDtypeStruct((width, total), F32),
            jax.ShapeDtypeStruct((8, total), F32),
        ],
        grid_spec=grid_spec,
        compiler_params=pltpu.CompilerParams(vmem_limit_bytes=48 << 20),
        cost_estimate=pl.CostEstimate(
            flops=4 * total * total * width, bytes_accessed=8 << 20, transcendentals=0
        ),
    )(bounds, qkv, qkv, qkv, seg_rows, seg_columns)


def unrotate(values, cos, sin):
    return values * cos - pltpu.roll(values, LANES // 2, 1) * sin


def attend_back_kernel(
    bounds, q_ref, k_ref, v_ref, full_ref, lse_ref, do_ref, sq_ref, sk_ref, cos_ref, sin_ref,
    out_ref, dk_ref, dv_ref, kt_ref,
):
    i = pl.program_id(0)
    rows, width = q_ref.shape
    shards, _, shard_rows, _ = out_ref.shape
    per = shard_rows // rows
    heads, paired, plain = head_masks(width)
    scale = HEAD_DIM**-0.5

    @pl.when(i == 0)
    def _():
        dk_ref[...] = jnp.zeros_like(dk_ref)
        dv_ref[...] = jnp.zeros_like(dv_ref)
        for b in range(shards):
            for h, k_head in enumerate(masked(k_ref[b], paired)):
                kt_ref[b, h] = k_head.T

    do = do_ref[...]
    q_heads = masked(q_ref[...] * jnp.asarray(scale, BF), paired)
    do_heads = masked(do, plain)
    product = do.astype(F32).T * full_ref[...]
    deltas = [
        jnp.sum(product[h * HEAD_DIM : (h + 1) * HEAD_DIM], axis=0, keepdims=True)
        for h in range(heads)
    ]
    logs = [lse_ref[h : h + 1, :] for h in range(heads)]
    sq = sq_ref[...]

    def step(kb, dq):
        k, v = k_ref[kb], v_ref[kb]
        same = sk_ref[kb] == sq
        dk, dv = dk_ref[kb], dv_ref[kb]
        for h in range(heads):
            scores = lax.dot_general(k, q_heads[h], NT, preferred_element_type=F32)
            weight = jnp.where(same, jnp.exp(scores - logs[h]), 0.0)
            dp = lax.dot_general(v, do_heads[h], NT, preferred_element_type=F32)
            ds = (weight * (dp - deltas[h])).astype(BF)
            dv = dv + jnp.dot(weight.astype(BF), do_heads[h], preferred_element_type=F32)
            dk = dk + jnp.dot(ds, q_heads[h], preferred_element_type=F32)
            dq = dq + jnp.dot(kt_ref[kb, h], ds, preferred_element_type=F32)
        dk_ref[kb] = dk
        dv_ref[kb] = dv
        return dq

    dq = lax.fori_loop(bounds[i, 0], bounds[i, 1], step, jnp.zeros((width, rows), F32))
    dq = dq.T * scale
    here = pl.ds(pl.multiple_of(i * rows, rows), rows)
    inside = pl.ds(pl.multiple_of((i % per) * rows, rows), rows)
    out_ref[i // per, 0, inside, :] = unrotate(dq, cos_ref[here, :], sin_ref[here, :]).astype(BF)

    @pl.when(i == pl.num_programs(0) - 1)
    def _():
        for s in range(shards):
            own = slice(s * shard_rows, (s + 1) * shard_rows)
            out_ref[s, 1] = unrotate(dk_ref[s], cos_ref[own, :], sin_ref[own, :]).astype(BF)
            out_ref[s, 2] = dv_ref[s].astype(BF)


def attend_back(qkv, full, logs, grads, seg_rows, seg_columns, cos, sin, bounds, block):
    shards, _, rows, width = qkv.shape
    total = shards * rows
    per = rows // block
    heads = width // HEAD_DIM
    grid_spec = pltpu.PrefetchScalarGridSpec(
        num_scalar_prefetch=1,
        grid=(total // block,),
        in_specs=[
            pl.BlockSpec((None, None, block, width), lambda i, b: (i // per, 0, i % per, 0)),
            pl.BlockSpec((shards, None, rows, width), lambda i, b: (0, 1, 0, 0)),
            pl.BlockSpec((shards, None, rows, width), lambda i, b: (0, 2, 0, 0)),
            pl.BlockSpec((width, block), lambda i, b: (0, i)),
            pl.BlockSpec((8, block), lambda i, b: (0, i)),
            pl.BlockSpec((block, width), lambda i, b: (i, 0)),
            pl.BlockSpec((1, block), lambda i, b: (0, i)),
            pl.BlockSpec((shards, rows, 1), lambda i, b: (0, 0, 0)),
            pl.BlockSpec((total, width), lambda i, b: (0, 0)),
            pl.BlockSpec((total, width), lambda i, b: (0, 0)),
        ],
        out_specs=pl.BlockSpec((shards, 3, rows, width), lambda i, b: (0, 0, 0, 0)),
        scratch_shapes=[
            pltpu.VMEM((shards, rows, width), F32),
            pltpu.VMEM((shards, rows, width), F32),
            pltpu.VMEM((shards, heads, width, rows), BF),
        ],
    )
    return pl.pallas_call(
        attend_back_kernel,
        out_shape=jax.ShapeDtypeStruct((shards, 3, rows, width), BF),
        grid_spec=grid_spec,
        compiler_params=pltpu.CompilerParams(vmem_limit_bytes=48 << 20),
        cost_estimate=pl.CostEstimate(
            flops=10 * total * total * width, bytes_accessed=16 << 20, transcendentals=0
        ),
    )(bounds, qkv, qkv, qkv, full, logs, grads, seg_rows, seg_columns, cos, sin)


def middle_kernel(
    parts, clips, *refs,
):
    o_refs, refs = refs[:parts], refs[parts:]
    (x_ref, g_ref, seg_ref, mod_ref, wo_ref, bo_ref, w1_ref, b1_ref, w2_ref, b2_ref) = refs[:10]
    (out_ref, n_ref, r_ref, df_ref, dh_ref, da_ref, dx_ref, gb1_ref, gsum_ref) = refs[10:19]
    do_refs = refs[19:]
    rows, width = x_ref.shape
    shards = o_refs[0].shape[0]
    seg = seg_ref[...]

    @pl.when(pl.program_id(0) == 0)
    def _():
        gb1_ref[...] = jnp.zeros_like(gb1_ref)
        gsum_ref[...] = jnp.zeros_like(gsum_ref)

    def of_clip(part):
        columns = slice(part * width, (part + 1) * width)
        value = jnp.broadcast_to(mod_ref[0:1, columns], (rows, width))
        for c in range(1, clips):
            value = jnp.where(seg == c, mod_ref[c : c + 1, columns], value)
        return value

    def clip_sums(at, value):
        for c in range(clips):
            part = jnp.sum(jnp.where(seg == c, value, 0.0), axis=0, keepdims=True)
            gsum_ref[at + c : at + c + 1, :] += part

    def column_sum(at, value):
        gsum_ref[at : at + 1, :] += jnp.sum(value, axis=0, keepdims=True)

    def mean(value):
        return jnp.mean(value, axis=-1, keepdims=True)

    heads = [o_refs[p][s] for s in range(shards) for p in range(parts)]
    att = jnp.dot(jnp.concatenate(heads, axis=1), wo_ref[...], preferred_element_type=F32) + bo_ref[...]
    gate_a, gate_f, scale = of_clip(2), of_clip(5), 1.0 + of_clip(4)
    x2 = x_ref[...] + gate_a * att
    centred = x2 - mean(x2)
    under = lax.rsqrt(mean(centred * centred) + 1e-06)
    y = centred * under
    n2 = (y * scale + of_clip(3)).astype(BF)
    n_ref[...] = n2
    h = jnp.dot(n2, w1_ref[...], preferred_element_type=F32) + b1_ref[...]
    root = math.sqrt(2.0 / math.pi)
    square = h * h
    bent = jnp.tanh(root * h * (1.0 + 0.044715 * square))
    r = (0.5 * h * (1.0 + bent)).astype(BF)
    r_ref[...] = r
    slope = 0.5 * (1.0 + bent) + 0.5 * h * (1.0 - bent * bent) * root * (1.0 + 3 * 0.044715 * square)
    fo = jnp.dot(r, w2_ref[...], preferred_element_type=F32) + b2_ref[...]
    out_ref[...] = (x2 + gate_f * fo).astype(BF)

    g = g_ref[...].astype(F32)
    clip_sums(0, g * fo)
    gated = g * gate_f
    column_sum(4 * clips, gated)
    df = gated.astype(BF)
    df_ref[...] = df
    dh = (lax.dot_general(df, w2_ref[...], NT, preferred_element_type=F32) * slope).astype(BF)
    dh_ref[...] = dh
    gb1_ref[0:1, :] += jnp.sum(dh.astype(F32), axis=0, keepdims=True)
    dn2 = lax.dot_general(dh, w1_ref[...], NT, preferred_element_type=F32)
    clip_sums(clips, dn2)
    clip_sums(2 * clips, dn2 * y)
    z = dn2 * scale
    dx2 = g + (z - mean(z) - y * mean(z * y)) * under
    dx_ref[...] = dx2
    clip_sums(3 * clips, dx2 * att)
    gated = dx2 * gate_a
    column_sum(4 * clips + 1, gated)
    da = gated.astype(BF)
    da_ref[...] = da
    do = lax.dot_general(da, wo_ref[...], NT, preferred_element_type=F32).astype(BF)
    for s in range(shards):
        for p in range(parts):
            at = (s * parts + p) * LANES
            do_refs[p][s] = do[:, at : at + LANES]


def middle(o_parts, x1, grad, seg, mod, out_w, out_b, w1, b1, w2, b2):
    rows, width = x1.shape
    hidden = w1.shape[1]
    shards, parts, clips = o_parts[0].shape[0], len(o_parts), mod.shape[0]
    block = min(rows, 256)

    def row_block(columns):
        return pl.BlockSpec((block, columns), lambda i: (i, 0))

    def whole(shape):
        return pl.BlockSpec(shape, lambda i: (0, 0), pipeline_mode=pl.Buffered(1))

    def kept(shape):
        return pl.BlockSpec(shape, lambda i: (0, 0))

    by_shard = pl.BlockSpec((shards, block, LANES), lambda i: (0, i, 0))
    sums = -(-(4 * clips + 2) // 8) * 8
    shape = jax.ShapeDtypeStruct
    outs = [
        (shape((rows, width), BF), row_block(width)),
        (shape((rows, width), BF), row_block(width)),
        (shape((rows, hidden), BF), row_block(hidden)),
        (shape((rows, width), BF), row_block(width)),
        (shape((rows, hidden), BF), row_block(hidden)),
        (shape((rows, width), BF), row_block(width)),
        (shape((rows, width), F32), row_block(width)),
        (shape((8, hidden), F32), kept((8, hidden))),
        (shape((sums, width), F32), kept((sums, width))),
    ] + [(shape((shards, rows, LANES), BF), by_shard)] * parts
    return pl.pallas_call(
        partial(middle_kernel, parts, clips),
        out_shape=[o[0] for o in outs],
        grid=(rows // block,),
        in_specs=[by_shard] * parts
        + [
            row_block(width),
            row_block(width),
            row_block(1),
            whole(mod.shape),
            whole(out_w.shape),
            whole((1, width)),
            whole(w1.shape),
            whole((1, hidden)),
            whole(w2.shape),
            whole((1, width)),
        ],
        out_specs=[o[1] for o in outs],
        compiler_params=pltpu.CompilerParams(vmem_limit_bytes=56 << 20),
        cost_estimate=pl.CostEstimate(
            flops=2 * rows * width * (4 * hidden + 2 * width), bytes_accessed=20 << 20, transcendentals=0
        ),
    )(*o_parts, x1, grad, seg, mod, out_w, out_b[None], w1, b1[None], w2, b2[None])


def exchange(values, axis):
    return lax.all_to_all(values, axis, 0, 0)


def local(
    mel_pair, text_ids, clip_lengths, t_index,
    txt_table, txt_conv, txt_vec, txt_gain, txt_up, txt_hid, txt_down,
    emb_mel, emb_text, emb_bias, pos_conv, pos_bias,
    time_w1, time_bias, time_w2, ada_w, ada_b,
    qkv_w, qkv_b, out_w, out_b, ff_w1, ff_b1, ff_w2, ff_b2, out_grad,
):
    total = mel_pair.shape[0]
    width = emb_mel.shape[1]
    shards, groups = lax.axis_size("mp"), lax.axis_size("dp")
    rank, place = lax.axis_index("mp"), lax.axis_index("dp")
    rows = total // shards
    cols = width // shards
    clips = clip_lengths.shape[1]
    first = rank * rows
    taps = pos_conv.shape[1]
    group = pos_conv.shape[2]

    def spread_slice(weight, axis):
        piece = weight.shape[axis] // groups
        return lax.dynamic_slice_in_dim(weight, place * piece, piece, axis)

    def to_all(piece, axis_name="mp"):
        size = lax.axis_size(axis_name)
        return lax.all_to_all(jnp.broadcast_to(piece[None], (size,) + piece.shape), axis_name, 0, 0)

    def gather(piece, axis):
        return lax.all_gather(piece, "dp", axis=axis, tiled=True)

    def three(values):
        one = lax.reduce_precision(values, 8, 7)
        two = lax.reduce_precision(values - one, 8, 7)
        return jnp.concatenate([one, two, values - one - two], axis=0).astype(BF)

    qkv_piece = spread_slice(qkv_w, 1)
    qkv_piece = jnp.concatenate([pair_split(qkv_piece[:2]), qkv_piece[2:]], axis=0)
    in_rows = qkv_piece.shape[1]
    biases = jnp.concatenate(
        [pair_split(qkv_b[:2]), qkv_b[2:], ff_b1.reshape(-1, cols)], axis=0
    )
    bias_rows = biases.shape[0]
    biases = three(biases)
    biases = jnp.pad(biases, ((0, -biases.shape[0] % 16), (0, 0)))
    received = to_all(jnp.concatenate([qkv_piece.reshape(3 * in_rows, cols), biases], axis=0))
    qkv_full = gather(received[:, : 3 * in_rows].reshape(shards, 3, in_rows, cols), 2)
    biases = received[:, 3 * in_rows :].astype(F32)
    biases = sum(biases[:, i * bias_rows : (i + 1) * bias_rows] for i in range(3))
    qkv_bias = biases[:, :3]
    b1_full = biases[:, 3:].reshape(-1)
    out_piece, w2_piece, w1_piece = spread_slice(out_w, 0), spread_slice(ff_w2, 0), spread_slice(ff_w1, 0)
    w1_shape = w1_piece.shape
    cut = [out_piece.shape[0], out_piece.shape[0] + w2_piece.shape[0]]

    lengths = clip_lengths[0]
    clip_index = jnp.arange(clips, dtype=jnp.int32)
    ends = jnp.sum(jnp.where(clip_index[:, None] >= clip_index[None, :], lengths[None, :], 0), axis=1)
    starts = ends - lengths
    frames = jnp.arange(total, dtype=jnp.int32)
    member = (frames[:, None] >= starts[None, :]) & (frames[:, None] < ends[None, :])
    segment = jnp.sum(member * clip_index[None, :], axis=1).astype(jnp.int32)
    position = frames - jnp.sum(member * starts[None, :], axis=1)
    ext = rows + 2 * HALO
    ids = lax.dynamic_slice_in_dim(jnp.pad(text_ids, (HALO, HALO)), first, ext)
    seg_ext = lax.dynamic_slice_in_dim(jnp.pad(segment, (HALO, HALO), constant_values=-1), first, ext)
    hot_ext = (seg_ext[:, None] == clip_index[None, :]).astype(F32)
    ext_index = jnp.arange(ext, dtype=jnp.int32)
    inside = (ext_index >= HALO) & (ext_index < HALO + rows)
    own_ext = jnp.where(inside[:, None], hot_ext, 0.0)
    hot = hot_ext[HALO : HALO + rows]

    def time_path(steps):
        half = time_w1.shape[0] // 2
        frequency = jnp.exp(jnp.arange(half, dtype=F32) * (-math.log(10000.0) / (half - 1)))
        angles = steps.astype(F32)[:, None] * frequency[None, :]
        sinusoid = jnp.concatenate([jnp.sin(angles), jnp.cos(angles)], axis=-1)
        pre_one = precise(sinusoid, time_w1) + time_bias[0]
        act_one = jax.nn.silu(pre_one)
        time_vec = precise(act_one, time_w2) + time_bias[1]
        return sinusoid, pre_one, act_one, time_vec, jax.nn.silu(time_vec)

    mod = precise(time_path(t_index[0])[4], ada_w) + ada_b

    hidden = jnp.take(txt_table, ids, axis=0).astype(F32)
    kept = []
    blocks = txt_conv.shape[0]
    for b in range(blocks):
        hidden, saved = text_ahead(
            hidden, seg_ext, hot_ext, own_ext, txt_conv[b], txt_vec[b], txt_gain[b],
            txt_up[b], txt_hid[b], txt_down[b],
        )
        kept.append(saved)
    text = hidden[HALO : HALO + rows].astype(BF)

    mel = lax.dynamic_slice_in_dim(mel_pair, first, rows)
    x0 = dot(mel, emb_mel) + dot(text, emb_text) + emb_bias

    def to_channels(values):
        blocks_of = values.reshape(rows, shards, cols).transpose(1, 0, 2)
        return exchange(blocks_of, "mp").reshape(total, cols)

    def to_rows(values):
        return exchange(values.reshape(shards, rows, cols), "mp").transpose(1, 0, 2).reshape(rows, width)

    channels = to_channels(x0.astype(BF))
    pieces = jnp.concatenate([out_piece, w2_piece, w1_piece.reshape(-1, width)], axis=0)
    pieces, channels = lax.optimization_barrier((pieces, channels))
    spread_in = spread(channels.astype(F32), starts, ends)
    pre_a = apply_conv(spread_in, pos_conv[0], False) + pos_bias[0]
    y_a = jnp.pad(
        only_clips(mish(pre_a), starts, ends).astype(BF).astype(F32), ((GAP, GAP), (0, 0))
    )
    pre_b = apply_conv(y_a, pos_conv[1], False) + pos_bias[1]
    received = to_all(pieces)
    received, pre_b = lax.optimization_barrier((received, pre_b))
    out_full = gather(received[:, : cut[0]], 1).reshape(width, width)
    w1_piece = received[:, cut[1] :].reshape((shards,) + w1_shape).transpose(1, 0, 2)
    w1_full = gather(w1_piece.reshape(w1_shape[0], -1), 0)
    w2_full = gather(received[:, cut[0] : cut[1]], 1).reshape(-1, width)
    c_pos = to_rows(gather_back(mish(pre_b).astype(BF), starts, ends))
    x1 = x0 + c_pos.astype(F32)

    def modulate(state, mod_in, shift_part, scale_part):
        scale = expand(hot, mod_in[:, scale_part * width : (scale_part + 1) * width])
        shift = expand(hot, mod_in[:, shift_part * width : (shift_part + 1) * width])
        return layer_norm(state) * (1.0 + scale) + shift

    n1, n1_pull = jax.vjp(lambda s, m: modulate(s, m, 0, 1), x1, mod)
    n1 = n1.astype(BF)
    inverse = jnp.exp(jnp.arange(0, HEAD_DIM, 2, dtype=F32) * (-math.log(10000.0) / HEAD_DIM))
    angles = position.astype(F32)[:, None] * jnp.tile(inverse, LANES // inverse.shape[0])[None, :]
    cos = jnp.cos(angles)
    sin = jnp.sin(angles) * jnp.where(jnp.arange(LANES) < LANES // 2, -1.0, 1.0)
    cos_own = lax.dynamic_slice_in_dim(cos, first, rows)
    sin_own = lax.dynamic_slice_in_dim(sin, first, rows)
    parts = range(cols // LANES)
    qkv = [exchange(v, "mp") for v in project(n1, qkv_full, qkv_bias, cos_own, sin_own)]
    block = rows
    heads_of = segment[::block]
    tails_of = segment[block - 1 :: block]
    low_key = jnp.sum(jnp.where(heads_of[:, None] == clip_index, starts[None, :], 0), axis=1)
    high_key = jnp.sum(jnp.where(tails_of[:, None] == clip_index, ends[None, :], 0), axis=1)
    bounds = jnp.stack([low_key // rows, (high_key + rows - 1) // rows], axis=1).astype(jnp.int32)
    seg_rows = segment[None, :]
    seg_blocks = segment.reshape(shards, rows, 1)
    attended = [attend(qkv[h], seg_rows, seg_blocks, bounds, block) for h in parts]
    o_parts = [exchange(a[0].reshape(shards, rows, LANES), "mp") for a in attended]
    grad = lax.dynamic_slice_in_dim(out_grad, first, rows)
    seg_own = lax.dynamic_slice_in_dim(segment, first, rows)[:, None]
    out, n2, r, df, dh, da, dx2, g_ff_b1, sums, *do_parts = middle(
        o_parts, x1, grad, seg_own, mod, out_full, out_b, w1_full, b1_full, w2_full, ff_b2
    )
    g_ff_b1, g_ff_b2, g_out_b = g_ff_b1[0], sums[4 * clips], sums[4 * clips + 1]
    dmod_gate_f, dmod_shift_f, dmod_scale_f, dmod_gate_a = (
        sums[i * clips : (i + 1) * clips] for i in range(4)
    )
    g_ff_w2 = dot(df, r, TN)
    g_ff_w1 = dot(n2, dh, TN)
    o_rows = jnp.stack(o_parts).transpose(2, 1, 0, 3).reshape(rows, width)

    def for_dp(matrix):
        return matrix.astype(BF).reshape(groups, matrix.shape[0] // groups, matrix.shape[1])

    def by_rank(matrix):
        return matrix.reshape(matrix.shape[0], shards, -1).transpose(1, 0, 2)

    def scatter_dp(matrix):
        return lax.psum_scatter(matrix.astype(BF), "dp", scatter_dimension=0, tiled=True)

    sent_w1, sent_w2 = scatter_dp(g_ff_w1), scatter_dp(g_ff_w2)

    g_out_w = dot(da, o_rows, TN)
    dqkv = []
    for h in parts:
        do_part = exchange(do_parts[h], "mp").reshape(total, LANES)
        d_part = attend_back(
            qkv[h], attended[h][1], attended[h][2], do_part, seg_rows, seg_blocks, cos, sin, bounds, block
        )
        dqkv.append(exchange(d_part, "mp"))
    dn1, g_qkv_w, g_qkv_b = unproject(dqkv, n1, qkv_full)
    more, dmod_d = n1_pull(dn1)
    dx1 = dx2 + more
    sent_w1, sent_w2, dx1, out = lax.optimization_barrier((sent_w1, sent_w2, dx1, out))
    ff_pair = jnp.concatenate([by_rank(sent_w1), by_rank(sent_w2)], axis=2)
    sent_qkv, sent_out = scatter_dp(g_qkv_w), scatter_dp(g_out_w)

    dmod = dmod_d + jnp.concatenate(
        [
            jnp.zeros((clips, 2 * width), F32), dmod_gate_a, dmod_shift_f, dmod_scale_f, dmod_gate_f,
        ],
        axis=1,
    )

    slope_b = gather_back(mish_slope(pre_b), starts, ends)
    dy_b = to_channels(dx1.astype(BF)).astype(F32) * slope_b
    g_pos_b = jnp.sum(dy_b, axis=0)
    dy_b = spread(dy_b.astype(BF).astype(F32), starts, ends)
    dy_a = only_clips(apply_conv(dy_b, pos_conv[1], True) * mish_slope(pre_a), starts, ends)
    g_pos_a = jnp.sum(dy_a, axis=0)
    dy_a = jnp.pad(dy_a.astype(BF).astype(F32), ((GAP, GAP), (0, 0)))
    dc = gather_back(
        apply_conv(dy_a, pos_conv[0], True).astype(BF), starts, ends
    )
    ff_got, dc = lax.optimization_barrier((exchange(ff_pair, "mp"), dc))
    dx0_full = dx1 + to_rows(dc).astype(F32)
    g_conv = jnp.concatenate(
        [conv_grad(spread_in, dy_a[GAP:-GAP], taps, group), conv_grad(y_a, dy_b[GAP:-GAP], taps, group)],
        axis=1,
    )
    sent_qkv, sent_out, dx0_full = lax.optimization_barrier((sent_qkv, sent_out, dx0_full))
    at_pair = jnp.concatenate([by_rank(sent_qkv), by_rank(sent_out)], axis=2)
    sent_conv = scatter_dp(g_conv)

    g_emb_bias = jnp.sum(dx0_full, axis=0)
    dx0 = dx0_full.astype(BF)
    mel_grad = dot(dx0, emb_mel, NT).astype(BF)
    g_emb = jnp.concatenate([dot(dx0, text, TN), dot(dx0, mel, TN)], axis=1)
    sent_emb = scatter_dp(g_emb)
    text_width = text.shape[1]

    dtext = jnp.pad(dot(dx0, emb_text, NT), ((HALO, HALO), (0, 0)))
    text_grads = [None] * blocks
    extra = dmod
    at_got, out, dtext = lax.optimization_barrier((exchange(at_pair, "mp"), out, dtext))
    result = [
        lax.all_gather(half, "mp", tiled=True) for half in (out[:, : width // 2], out[:, width // 2 :])
    ]
    waiting = sent_conv
    for b in reversed(range(blocks)):
        dtext, text_grads[b], summed, waiting = text_behind(
            kept[b], dtext, txt_up[b], txt_down[b], extra, waiting
        )
        if extra is not None:
            stamps = jnp.broadcast_to(t_index[0].astype(F32)[:, None], (clips, 128))
            dmod_all = lax.all_gather(jnp.concatenate([summed, stamps], axis=1), "dp", tiled=True)
            sent_emb, dtext = lax.optimization_barrier((sent_emb, dtext))
            sent_conv, waiting = waiting, result[0]
            dmod_all, all_steps = dmod_all[:, : 6 * width], dmod_all[:, 6 * width]
        extra = None
    result = [waiting, result[1]]
    result[1], dtext = lax.optimization_barrier((result[1], dtext))
    result = jnp.concatenate(result, axis=1).astype(F32)
    vocab = txt_table.shape[0]
    wide = -(-vocab // 128) * 128
    chosen = (ids[:, None] == jnp.arange(wide, dtype=jnp.int32)[None, :]).astype(BF)
    g_table = dot(dtext, chosen, TN)
    hidden_width = txt_up.shape[2]

    def placed(values):
        full = jnp.zeros((shards,) + values.shape, F32)
        return lax.dynamic_update_slice_in_dim(full, values[None], rank, 0)

    g_pos_bias = placed(jnp.stack([g_pos_a, g_pos_b])).transpose(1, 0, 2).reshape(2, width)
    g_qkv_b = jnp.concatenate([pair_merge(g_qkv_b[:, :2]), g_qkv_b[:, 2:]], axis=1)
    g_qkv_b = g_qkv_b.transpose(1, 0, 2).reshape(3, width)
    small = [
        (jnp.stack([g[0] for g in text_grads]), "both"),
        (jnp.stack([g[1] for g in text_grads]), "both"),
        (jnp.stack([g[2] for g in text_grads]), "both"),
        (jnp.stack([g[4] for g in text_grads]), "both"),
        (g_emb_bias, "dp"),
        (g_pos_bias, "crossed"),
        (g_qkv_b, "crossed"),
        (g_out_b, "dp"),
        (g_ff_b1, "crossed"),
        (g_ff_b2, "dp"),
    ]
    packed = []
    for value, kind in small:
        lead = value.size // value.shape[-1]
        if kind == "crossed":
            value = value.reshape(lead, shards, groups, -1).transpose(2, 0, 1, 3)
        else:
            value = value.reshape(lead, groups, -1).transpose(1, 0, 2)
        packed.append(value.reshape(groups, -1))
    packed = jnp.concatenate(packed, axis=1)
    length = packed.shape[1]
    packed = jnp.pad(packed, ((0, 0), (0, -length % 1024))).reshape(groups, -1, 128)
    table_sum, up0, up1, down0, down1, packed, g_emb, mel_grad = last_sums(
        [for_dp(g_table)]
        + [for_dp(text_grads[b][3]) for b in range(blocks)]
        + [for_dp(text_grads[b][5]) for b in range(blocks)],
        packed,
        [],
        [sent_emb],
        [mel_grad],
    )
    mel_grad = mel_grad.reshape(total, -1)
    packed = packed.reshape(-1)
    unpacked, at = [], 0
    for value, kind in small:
        size = value.size // groups
        piece = packed[at : at + size]
        at += size
        if kind == "dp":
            unpacked.append(piece.reshape(value.shape[:-1] + (-1,)))
        else:
            piece = piece.reshape(value.size // value.shape[-1], shards, -1)
            piece = lax.dynamic_slice_in_dim(piece, rank, 1, 1)
            unpacked.append(piece.reshape(value.shape[:-1] + (-1,)))
    o_table = table_sum[:, :vocab].T
    o_up = jnp.stack([up0.T, up1.T])
    o_down = jnp.stack([down0.T, down1.T])
    ff_pair, at_pair = (jnp.sum(v.astype(F32), axis=0) for v in (ff_got, at_got))
    ff_cols = ff_w1.shape[1]
    o_ff_w1, o_ff_w2 = ff_pair[:, :ff_cols], ff_pair[:, ff_cols:].T
    g_qkv = at_pair[:, : 3 * cols].reshape(-1, 3, cols).transpose(1, 0, 2)
    o_qkv_w = jnp.concatenate([pair_merge(g_qkv[:2]), g_qkv[2:]], axis=0)
    o_out_w = at_pair[:, 3 * cols :].T
    o_pos_conv = sent_conv.astype(F32).T.reshape(2, taps, group, -1)
    o_emb_text, o_emb_mel = g_emb[:, :text_width].T, g_emb[:, text_width:].T

    def own(values, index, parts):
        piece = values.shape[-1] // parts
        return lax.dynamic_slice_in_dim(values, index * piece, piece, values.ndim - 1)

    sinusoid, pre_one, act_one, time_vec, act_two = time_path(all_steps)
    de = precise(dmod_all, ada_w, NT) * silu_slope(time_vec)
    dpre = precise(de, time_w2, NT) * silu_slope(pre_one)

    def outer(left, right):
        return lax.dot_general(left, own(right, place, groups), TN, precision=highest)

    return (
        result,
        mel_grad,
        o_table,
        unpacked[0],
        unpacked[1],
        unpacked[2],
        o_up,
        unpacked[3],
        o_down,
        o_emb_mel,
        o_emb_text,
        unpacked[4],
        o_pos_conv,
        unpacked[5],
        outer(sinusoid, dpre),
        own(jnp.stack([jnp.sum(dpre, axis=0), jnp.sum(de, axis=0)]), place, groups),
        outer(act_one, de),
        outer(act_two, dmod_all),
        own(jnp.sum(dmod_all, axis=0), place, groups),
        o_qkv_w,
        unpacked[6],
        o_out_w,
        unpacked[7],
        o_ff_w1,
        unpacked[8],
        o_ff_w2,
        unpacked[9],
    )


def solution(mesh):
    both, crossed = ("dp", "mp"), ("mp", "dp")
    placed = (
        P("dp", None), P("dp"), P("dp", None), P("dp", None),
        P(), P(), P(), P(), P(), P(), P(), P(), P(), P(),
        P(None, None, None, "mp"), P(None, "mp"),
        P(), P(), P(), P(), P(),
        P(None, None, "mp"), P(None, "mp"), P("mp", None), P(),
        P(None, "mp"), P("mp"), P("mp", None), P(),
        P("dp", None),
    )
    given = (
        P("dp", None), P("dp", None),
        P(None, both), P(None, None, both), P(None, None, both), P(None, both),
        P(None, None, both), P(None, None, both), P(None, None, both),
        P(None, "dp"), P(None, "dp"), P("dp"),
        P(None, None, None, crossed), P(None, crossed),
        P(None, "dp"), P(None, "dp"), P(None, "dp"), P(None, "dp"), P("dp"),
        P(None, "dp", "mp"), P(None, crossed), P("mp", "dp"), P("dp"),
        P("dp", "mp"), P(crossed), P("mp", "dp"), P("dp"),
    )
    return jax.shard_map(local, mesh=mesh, in_specs=placed, out_specs=given, check_vma=False)
```

```python
from functools import partial
import math

import jax
import jax.numpy as jnp
from jax import lax
from jax.experimental import pallas as pl
from jax.experimental.pallas import tpu as pltpu
from jax.sharding import PartitionSpec as P

HEAD_DIM = 64
GAP = 16
HALO = 8
BF = jnp.bfloat16
F32 = jnp.float32
highest = lax.Precision.HIGHEST
NN = (((1,), (0,)), ((), ()))
NT = (((1,), (1,)), ((), ()))
TN = (((0,), (0,)), ((), ()))


def dot(left, right, dims=NN):
    return lax.dot_general(left.astype(BF), right.astype(BF), dims, preferred_element_type=F32)


def precise(left, right, dims=NN):
    one = lax.reduce_precision(left, 8, 7)
    two = lax.reduce_precision(left - one, 8, 7)
    three = left - one - two
    rows = left.shape[0]
    stacked = jnp.concatenate([one, two, three], axis=0).astype(BF)
    product = lax.dot_general(stacked, right, dims, preferred_element_type=F32)
    return product[:rows] + product[rows : 2 * rows] + product[2 * rows :]


@jax.custom_vjp
def expand(onehot, parts):
    return sum(onehot[:, c : c + 1] * parts[c : c + 1] for c in range(parts.shape[0]))


def expand_ahead(onehot, parts):
    return expand(onehot, parts), onehot


def expand_behind(onehot, grad):
    return None, jnp.dot(onehot.T, grad, precision=highest)


expand.defvjp(expand_ahead, expand_behind)


def silu_slope(values):
    sigmoid_val = jax.nn.sigmoid(values)
    return sigmoid_val * (1.0 + values * (1.0 - sigmoid_val))


def layer_norm(values):
    centred = values - jnp.mean(values, axis=-1, keepdims=True)
    variance = jnp.mean(centred * centred, axis=-1, keepdims=True)
    return centred * lax.rsqrt(variance + 1e-06)


def mish(values):
    grown = jnp.exp(jnp.minimum(values, 20.0))
    wide = grown * (grown + 2.0)
    return values * (wide / (wide + 2.0))


def mish_slope(values):
    grown = jnp.exp(jnp.minimum(values, 20.0))
    wide = grown * (grown + 2.0)
    under = 1.0 / (wide + 2.0)
    return wide * under + values * (4.0 * grown * (1.0 + grown) * under * under)


def sum_kernel(axis, size, x_ref, o_ref, slots, send_sems, recv_sems):
    me = lax.axis_index(axis)
    barrier = pltpu.get_barrier_semaphore()
    peers = [lax.rem(me + step, size) for step in range(1, size)]
    for peer in peers:
        pl.semaphore_signal(
            barrier, inc=1, device_id={axis: peer}, device_id_type=pl.DeviceIdType.MESH
        )
    pl.semaphore_wait(barrier, size - 1)
    for step, peer in enumerate(peers):
        pltpu.make_async_remote_copy(
            src_ref=x_ref,
            dst_ref=slots.at[me],
            send_sem=send_sems.at[step],
            recv_sem=recv_sems.at[me],
            device_id={axis: peer},
            device_id_type=pl.DeviceIdType.MESH,
        ).start()
    slots[me] = x_ref[...]
    for step, peer in enumerate(peers):
        copy = pltpu.make_async_remote_copy(
            src_ref=x_ref,
            dst_ref=slots.at[peer],
            send_sem=send_sems.at[step],
            recv_sem=recv_sems.at[peer],
            device_id={axis: peer},
            device_id_type=pl.DeviceIdType.MESH,
        )
        copy.wait_send()
        copy.wait_recv()
    total = slots[0]
    for device in range(1, size):
        total = total + slots[device]
    o_ref[...] = total


def small_sum(values, axis, name):
    size = lax.axis_size(axis)
    whole = pl.BlockSpec(memory_space=pltpu.VMEM)
    return pl.pallas_call(
        partial(sum_kernel, axis, size),
        out_shape=jax.ShapeDtypeStruct(values.shape, F32),
        in_specs=[whole],
        out_specs=whole,
        scratch_shapes=[
            pltpu.VMEM((size,) + values.shape, F32),
            pltpu.SemaphoreType.DMA((size - 1,)),
            pltpu.SemaphoreType.DMA((size,)),
        ],
        compiler_params=pltpu.CompilerParams(
            collective_id=name, has_side_effects=True, vmem_limit_bytes=16 << 20
        ),
    )(values)


def places(dp, mp, width, kind):
    share = width // dp
    if kind in ("dp", "both"):
        return [(0, 0, share, 0, share, None)], 1
    count = share // mp
    found = []
    for z in range(mp):
        at = z * count
        column = z * dp * count if kind == "crossed" else 0
        found.append((at // LANES, at % LANES, count, column, count, z))
    return found, -(-share // LANES)


def pack_rows(dp, mp, pieces, sources, pack, z):
    pack[...] = jnp.zeros_like(pack)
    at = 0
    for source, first, rows, width, kind, _, _ in pieces:
        found, used = places(dp, mp, width, kind)
        for row, lane, count, column, step, device in found:
            for d in range(dp):
                start = column + d * step
                value = sources[source][first : first + rows, start : start + count]
                if kind == "mine":
                    value = jnp.where(z == device, value, 0.0)
                to = slice(at + row, at + row + rows)
                pack[d // 2, d % 2, to, lane : lane + count] = value
        at += rows * used


def unpack_rows(dp, mp, pieces, value, outs, z):
    at = 0
    for _, _, rows, width, kind, out, where in pieces:
        found, used = places(dp, mp, width, kind)
        if kind == "both":
            count = width // dp // mp
            found = [(0, device * count, count, 0, 0, device) for device in range(mp)]
        total = None
        for row, lane, count, _, _, device in found:
            part = value[at + row : at + row + rows, lane : lane + count]
            if device is not None:
                part = jnp.where(z == device, part, 0.0)
            total = part if total is None else total + part
        lead, row = where
        if lead is None:
            outs[out][row : row + rows, :] = total
        else:
            outs[out][lead, row : row + rows, :] = total
        at += rows * used


def last_kernel(dp, mp, n_all, n_mp, n_both, n_gather, n_sources, n_small, pieces, *refs):
    n_in = n_all + n_mp + n_both + n_gather
    ins, refs = list(refs[: n_in - 1]), refs[n_in - 1 :]
    sources, refs = refs[:n_sources], refs[n_sources:]
    outs, refs = list(refs[: n_in - 1]), refs[n_in - 1 :]
    small_outs, rest = refs[:n_small], list(refs[n_small:])
    ins.insert(n_all - 1, rest.pop(0))
    outs.insert(n_all - 1, None)

    def take(count):
        return [rest.pop(0) for _ in range(count)]

    own, pair, joint, chip_slots, middle, slots = (
        take(n_all), take(n_all), take(n_all), take(n_all), take(n_all), take(n_in)
    )
    pair_send, pair_recv, chip_send, chip_recv, mp_send, mp_recv, own_sems = rest
    me, z = lax.axis_index("dp"), lax.axis_index("mp")
    chips = dp // 2
    core, chip = lax.rem(me, 2), me // 2
    partner = me + 1 - 2 * core
    other_chips = [lax.rem(chip + step, chips) for step in range(1, chips)]
    other_z = [lax.rem(z + step, mp) for step in range(1, mp)]
    mesh_id = pl.DeviceIdType.MESH
    barrier = pltpu.get_barrier_semaphore()
    greeted = (
        [{"dp": partner}]
        + [{"dp": 2 * q + core} for q in other_chips]
        + [{"mp": peer} for peer in other_z]
    )
    for device in greeted:
        pl.semaphore_signal(barrier, inc=1, device_id=device, device_id_type=mesh_id)
    pl.semaphore_wait(barrier, chips + mp - 1)

    def to_partner(t):
        return pltpu.make_async_remote_copy(
            src_ref=ins[t].at[:, 1 - core],
            dst_ref=pair[t],
            send_sem=pair_send.at[t],
            recv_sem=pair_recv.at[t],
            device_id={"dp": partner},
            device_id_type=mesh_id,
        )

    def to_chip(t, step, mine):
        q = other_chips[step]
        return pltpu.make_async_remote_copy(
            src_ref=joint[t].at[q],
            dst_ref=chip_slots[t].at[mine],
            send_sem=chip_send.at[t, step],
            recv_sem=chip_recv.at[t, mine],
            device_id={"dp": 2 * q + core},
            device_id_type=mesh_id,
        )

    def to_z(t, step, mine):
        peer = other_z[step]
        if t < n_all - 1:
            source = middle[t].at[peer]
        elif t == n_all - 1:
            source = middle[t]
        else:
            source = ins[t].at[peer] if t < n_all + n_mp else ins[t]
        return pltpu.make_async_remote_copy(
            src_ref=source,
            dst_ref=slots[t].at[mine],
            send_sem=mp_send.at[t, step],
            recv_sem=mp_recv.at[t, mine],
            device_id={"mp": peer},
            device_id_type=mesh_id,
        )

    local = []
    for t in range(n_all):
        if t == n_all - 1:
            pack_rows(dp, mp, pieces, sources, ins[t], z)
        to_partner(t).start()
        copy = pltpu.make_async_copy(ins[t].at[:, core], own[t], own_sems.at[t])
        copy.start()
        local.append(copy)
    for t in range(n_all, n_in):
        for step in range(mp - 1):
            to_z(t, step, z).start()
        source = ins[t].at[z] if t < n_all + n_mp else ins[t]
        copy = pltpu.make_async_copy(source, slots[t].at[z], own_sems.at[t])
        copy.start()
        local.append(copy)

    def total(ref, size):
        value = ref[0].astype(F32)
        for device in range(1, size):
            value = value + ref[device].astype(F32)
        return value

    for t in range(n_all):
        local[t].wait()
        copy = to_partner(t)
        copy.wait_send()
        copy.wait_recv()
        for q in range(chips):
            value = own[t][q].astype(F32) + pair[t][q].astype(F32)
            joint[t][q] = value.astype(joint[t].dtype)
        for step in range(chips - 1):
            to_chip(t, step, chip).start()
        chip_slots[t][chip] = joint[t][chip]
    for t in range(n_all):
        for step in range(chips - 1):
            copy = to_chip(t, step, other_chips[step])
            copy.wait_send()
            copy.wait_recv()
        value = total(chip_slots[t], chips)
        if t < n_all - 1:
            rows = value.shape[0] // mp
            for device in range(mp):
                part = value[device * rows : (device + 1) * rows]
                middle[t][device] = part.astype(middle[t].dtype)
            slots[t][z] = middle[t][z]
        else:
            middle[t][...] = value
            slots[t][z] = value
        for step in range(mp - 1):
            to_z(t, step, z).start()
    for t in list(range(n_all, n_in)) + list(range(n_all)):
        if t >= n_all:
            local[t].wait()
        for step in range(mp - 1):
            copy = to_z(t, step, other_z[step])
            copy.wait_send()
            copy.wait_recv()
        if t == n_all - 1:
            unpack_rows(dp, mp, pieces, total(slots[t], mp), small_outs, z)
        elif t < n_in - n_gather:
            outs[t][...] = total(slots[t], mp)
        else:
            outs[t][...] = slots[t][...].astype(F32)


def last_sums(over_all, sources, pieces, small_shapes, over_mp, both, gathered):
    dp, mp = lax.axis_size("dp"), lax.axis_size("mp")
    chips = dp // 2
    rows = sum(p[2] * places(dp, mp, p[3], p[4])[1] for p in pieces)
    packed = jax.ShapeDtypeStruct((chips, 2, -(-rows // 8) * 8, LANES), F32)
    everywhere = [v.reshape((chips, 2) + v.shape[1:]) for v in over_all] + [packed]
    ins = everywhere + list(over_mp) + list(both) + list(gathered)
    n_all, n_mp, n_both, n_gather = len(everywhere), len(over_mp), len(both), len(gathered)
    halves = [pltpu.VMEM((chips,) + v.shape[2:], v.dtype) for v in everywhere]
    outs, middle, slots = [], [], []
    for t, value in enumerate(ins):
        if t < n_all - 1:
            shape = (value.shape[2] // mp, value.shape[3])
            middle.append(pltpu.VMEM((mp,) + shape, value.dtype))
        elif t == n_all - 1:
            shape = value.shape[2:]
            middle.append(pltpu.VMEM(shape, value.dtype))
        else:
            shape = value.shape[1:] if t < n_all + n_mp else value.shape
        slots.append(pltpu.VMEM((mp,) + shape, value.dtype))
        outs.append((mp,) + shape if t >= len(ins) - n_gather else shape)
    dma = pltpu.SemaphoreType.DMA
    return pl.pallas_call(
        partial(
            last_kernel, dp, mp, n_all, n_mp, n_both, n_gather, len(sources), len(small_shapes), pieces
        ),
        out_shape=[
            jax.ShapeDtypeStruct(shape, F32)
            for shape in outs[: n_all - 1] + outs[n_all:] + list(small_shapes)
        ],
        in_specs=[pl.BlockSpec(memory_space=pl.ANY)] * (len(ins) - 1)
        + [pl.BlockSpec(memory_space=pltpu.VMEM)] * len(sources),
        out_specs=[pl.BlockSpec(memory_space=pltpu.VMEM)] * (len(ins) - 1 + len(small_shapes)),
        scratch_shapes=[pltpu.VMEM(packed.shape, F32)]
        + halves * 4
        + middle
        + slots
        + [
            dma((n_all,)),
            dma((n_all,)),
            dma((n_all, chips)),
            dma((n_all, chips)),
            dma((len(ins), mp)),
            dma((len(ins), mp)),
            dma((len(ins),)),
        ],
        compiler_params=pltpu.CompilerParams(
            collective_id=3, has_side_effects=True, vmem_limit_bytes=56 << 20
        ),
    )(*ins[: n_all - 1], *ins[n_all:], *sources)


def conv_norm(hidden, segment, conv, vec, gain):
    taps = conv.shape[0]
    reach = taps // 2
    rows = hidden.shape[0]
    padded = jnp.pad(hidden, ((reach, reach), (0, 0)))
    seg_padded = jnp.pad(segment, (reach, reach), constant_values=-1)
    mixture = vec[0]
    for tap in range(taps):
        keep = (seg_padded[tap : tap + rows] == segment) & (segment >= 0)
        mixture = mixture + conv[tap] * jnp.where(keep[:, None], padded[tap : tap + rows], 0.0)
    return layer_norm(mixture) * gain + vec[1]


def activate(pre, bias):
    return jax.nn.gelu(pre + bias, approximate=False)


def clip_squares(own, active):
    return jnp.dot(own.T, active * active, precision=highest)


def respond(active, squares, onehot, scale, shift):
    norms = jnp.sqrt(jnp.maximum(squares, 1.0))
    ratio = norms / (jnp.mean(norms, axis=-1, keepdims=True) + 1e-06)
    return scale * (active * expand(onehot, ratio)) + shift + active


def text_ahead(hidden, segment, onehot, own, conv, vec, gain, up, hid, down):
    normed, norm_pull = jax.vjp(
        lambda h, c, v, g: conv_norm(h, segment, c, v, g), hidden, conv, vec, gain
    )
    normed = normed.astype(BF)
    active, act_pull = jax.vjp(activate, dot(normed, up), hid[0])
    squares, square_pull = jax.vjp(lambda a: clip_squares(own, a), active)
    squares = small_sum(squares, "mp", 1)
    grown, respond_pull = jax.vjp(
        lambda a, s, g, b: respond(a, s, onehot, g, b), active, squares, hid[1], hid[2]
    )
    grown = grown.astype(BF)
    result = hidden + dot(grown, down) + vec[2]
    return result, (norm_pull, normed, act_pull, square_pull, respond_pull, grown)


def text_behind(kept, grad, up, down, extra, waiting):
    norm_pull, normed, act_pull, square_pull, respond_pull, grown = kept
    grad_low = grad.astype(BF)
    g_out = jnp.sum(grad, axis=0)
    g_down = dot(grad_low, grown, TN)
    grad_active, grad_squares, g_scale, g_shift = respond_pull(dot(grad_low, down, NT))
    grad_squares, waiting = lax.optimization_barrier((grad_squares, waiting))
    if extra is None:
        grad_squares = small_sum(grad_squares, "mp", 1)
    else:
        joined = small_sum(jnp.concatenate([grad_squares, extra], axis=1), "mp", 2)
        grad_squares, extra = joined[:, : grad_squares.shape[1]], joined[:, grad_squares.shape[1] :]
    grad_active = grad_active + square_pull(grad_squares)[0]
    grad_pre, g_bias = act_pull(grad_active)
    pre_low = grad_pre.astype(BF)
    g_up = dot(pre_low, normed, TN)
    grad_hidden, g_conv, g_vec, g_gain = norm_pull(dot(pre_low, up, NT))
    g_vec = g_vec.at[2].add(g_out)
    return (
        grad + grad_hidden,
        (g_conv, g_vec, g_gain, g_up, (g_bias, g_scale, g_shift), g_down),
        extra,
        waiting,
    )


def spread(values, starts, ends):
    rows = values.shape[0]
    clips = starts.shape[0]
    at = lax.broadcasted_iota(jnp.int32, values.shape, 0)
    total = rows + GAP * clips + 2 * GAP
    out = None
    for c in range(clips):
        part = jnp.where((at >= starts[c]) & (at < ends[c]), values, 0)
        lead = GAP + GAP * c
        part = jnp.pad(part, ((lead, total - lead - rows), (0, 0)))
        out = part if out is None else out + part
    return out


def only_clips(values, starts, ends):
    at = lax.broadcasted_iota(jnp.int32, values.shape, 0)
    keep = None
    for c in range(starts.shape[0]):
        inside = (at >= starts[c] + GAP * c) & (at < ends[c] + GAP * c)
        keep = inside if keep is None else keep | inside
    return jnp.where(keep, values, 0.0)


def gather_back(values, starts, ends):
    clips = starts.shape[0]
    rows = values.shape[0] - GAP * clips
    at = lax.broadcasted_iota(jnp.int32, (rows, values.shape[1]), 0)
    out = values[:rows]
    for c in range(1, clips):
        out = jnp.where(at >= starts[c], values[GAP * c : GAP * c + rows], out)
    return out


def conv_kernel(taps, turned, x_ref, w_ref, o_ref, full_ref):
    rows, width = o_ref.shape
    group = w_ref.shape[1]
    first = GAP - taps // 2

    @pl.when(pl.program_id(0) == 0)
    def _():
        lane = lax.broadcasted_iota(jnp.int32, (group, width), 1) // group
        for k in range(taps):
            tap = w_ref[taps - 1 - k if turned else k]
            for g in range(width // group):
                piece = jnp.where(lane == g, tap, jnp.zeros_like(tap))
                if turned:
                    full_ref[g * group : (g + 1) * group, k * width : (k + 1) * width] = piece
                else:
                    full_ref[k * width + g * group : k * width + (g + 1) * group, :] = piece

    columns = [x_ref[first + k : first + k + rows, :].astype(BF) for k in range(taps)]
    o_ref[...] = lax.dot_general(
        jnp.concatenate(columns, axis=1),
        full_ref[...],
        NT if turned else NN,
        preferred_element_type=F32,
    )


def conv_chunk(rows):
    for size in (528, 352, 256, 128, 64, 32, 16):
        if rows % size == 0:
            return size
    return rows


def apply_conv(spread_rows, weight, turned):
    rows = spread_rows.shape[0] - 2 * GAP
    width = spread_rows.shape[1]
    taps, group = weight.shape[:2]
    chunk = conv_chunk(rows)
    return pl.pallas_call(
        partial(conv_kernel, taps, turned),
        out_shape=jax.ShapeDtypeStruct((rows, width), F32),
        grid=(rows // chunk,),
        in_specs=[
            pl.BlockSpec((pl.Element(chunk + 2 * GAP), pl.Element(width)), lambda i: (i * chunk, 0)),
            pl.BlockSpec(weight.shape, lambda i: (0, 0, 0), pipeline_mode=pl.Buffered(1)),
        ],
        out_specs=pl.BlockSpec((chunk, width), lambda i: (i, 0)),
        scratch_shapes=[
            pltpu.VMEM((width, taps * width) if turned else (taps * width, width), BF)
        ],
        compiler_params=pltpu.CompilerParams(vmem_limit_bytes=48 << 20),
        cost_estimate=pl.CostEstimate(
            flops=2 * rows * taps * width * width, bytes_accessed=8 << 20, transcendentals=0
        ),
    )(spread_rows, weight)


def conv_grad_kernel(taps, group, x_ref, g_ref, o_ref):
    rows, width = g_ref.shape
    first = GAP - taps // 2
    turned = g_ref[...].T.astype(BF)

    @pl.when(pl.program_id(0) == 0)
    def _():
        o_ref[...] = jnp.zeros_like(o_ref)

    for k in range(taps):
        window = x_ref[first + k : first + k + rows, :].astype(BF)
        product = jnp.dot(turned, window, preferred_element_type=F32)
        for g in range(width // group):
            own = slice(g * group, (g + 1) * group)
            o_ref[own, k * group : (k + 1) * group] += product[own, own]


def conv_grad(spread_rows, grads, taps, group):
    rows, width = grads.shape
    chunk = conv_chunk(rows)
    return pl.pallas_call(
        partial(conv_grad_kernel, taps, group),
        out_shape=jax.ShapeDtypeStruct((width, taps * group), F32),
        grid=(rows // chunk,),
        in_specs=[
            pl.BlockSpec((pl.Element(chunk + 2 * GAP), pl.Element(width)), lambda i: (i * chunk, 0)),
            pl.BlockSpec((chunk, width), lambda i: (i, 0)),
        ],
        out_specs=pl.BlockSpec((width, taps * group), lambda i: (0, 0)),
        compiler_params=pltpu.CompilerParams(vmem_limit_bytes=48 << 20),
        cost_estimate=pl.CostEstimate(
            flops=2 * rows * taps * width * width, bytes_accessed=8 << 20, transcendentals=0
        ),
    )(spread_rows, grads)


LANES = 128


def pair_split(columns):
    pairs = columns.reshape(*columns.shape[:-1], -1, LANES // 2, 2)
    return jnp.swapaxes(pairs, -1, -2).reshape(columns.shape)


def pair_merge(columns):
    pairs = columns.reshape(*columns.shape[:-1], -1, 2, LANES // 2)
    return jnp.swapaxes(pairs, -1, -2).reshape(columns.shape)


def project_kernel(x_ref, w_ref, b_ref, cos_ref, sin_ref, *out_refs):
    cos, sin = cos_ref[...], sin_ref[...]
    for p in range(3):
        value = jnp.dot(x_ref[...], w_ref[p], preferred_element_type=F32) + b_ref[p : p + 1, :]
        for at, out_ref in enumerate(out_refs):
            piece = value[:, at * LANES : (at + 1) * LANES]
            if p < 2:
                piece = piece * cos + pltpu.roll(piece, LANES // 2, 1) * sin
            out_ref[p] = piece.astype(BF)


def project(normed, weight, bias, cos, sin):
    rows = normed.shape[0]
    shards, _, width, cols = weight.shape
    parts = cols // LANES
    return pl.pallas_call(
        project_kernel,
        out_shape=[jax.ShapeDtypeStruct((shards, 3, rows, LANES), BF)] * parts,
        grid=(shards,),
        in_specs=[
            pl.BlockSpec((rows, width), lambda i: (0, 0)),
            pl.BlockSpec((None, 3, width, cols), lambda i: (i, 0, 0, 0)),
            pl.BlockSpec((None, 3, cols), lambda i: (i, 0, 0)),
            pl.BlockSpec((rows, LANES), lambda i: (0, 0)),
            pl.BlockSpec((rows, LANES), lambda i: (0, 0)),
        ],
        out_specs=[pl.BlockSpec((None, 3, rows, LANES), lambda i: (i, 0, 0, 0))] * parts,
        compiler_params=pltpu.CompilerParams(vmem_limit_bytes=32 << 20),
        cost_estimate=pl.CostEstimate(
            flops=6 * rows * width * width, bytes_accessed=10 << 20, transcendentals=0
        ),
    )(normed, weight, bias, cos, sin)


def unproject_kernel(parts, *refs):
    d_refs, (x_ref, w_ref, dx_ref, gw_ref, gb_ref, turned) = refs[:parts], refs[parts:]
    s = pl.program_id(0)
    cols = w_ref.shape[2]

    @pl.when(s == 0)
    def _():
        turned[...] = x_ref[...].T
        dx_ref[...] = jnp.zeros_like(dx_ref)

    total = None
    for p in range(3):
        grad = jnp.concatenate([d_ref[p] for d_ref in d_refs], axis=1)
        product = lax.dot_general(grad, w_ref[p], NT, preferred_element_type=F32)
        total = product if total is None else total + product
        weight = jnp.dot(turned[...], grad, preferred_element_type=F32)
        gw_ref[:, p * cols : (p + 1) * cols] = weight.astype(BF)
        gb_ref[p : p + 1, :] = jnp.sum(grad.astype(F32), axis=0, keepdims=True)
    dx_ref[...] += total


def unproject(grads, normed, weight):
    rows = normed.shape[0]
    shards, _, width, cols = weight.shape
    parts = len(grads)
    return pl.pallas_call(
        partial(unproject_kernel, parts),
        out_shape=[
            jax.ShapeDtypeStruct((rows, width), F32),
            jax.ShapeDtypeStruct((width, shards * 3 * cols), BF),
            jax.ShapeDtypeStruct((shards, 3, cols), F32),
        ],
        grid=(shards,),
        in_specs=[pl.BlockSpec((None, 3, rows, LANES), lambda i: (i, 0, 0, 0))] * parts
        + [
            pl.BlockSpec((rows, width), lambda i: (0, 0)),
            pl.BlockSpec((None, 3, width, cols), lambda i: (i, 0, 0, 0)),
        ],
        out_specs=[
            pl.BlockSpec((rows, width), lambda i: (0, 0)),
            pl.BlockSpec((width, 3 * cols), lambda i: (0, i)),
            pl.BlockSpec((None, 3, cols), lambda i: (i, 0, 0)),
        ],
        scratch_shapes=[pltpu.VMEM((width, rows), BF)],
        compiler_params=pltpu.CompilerParams(vmem_limit_bytes=48 << 20),
        cost_estimate=pl.CostEstimate(
            flops=12 * rows * width * width, bytes_accessed=20 << 20, transcendentals=0
        ),
    )(*grads, normed, weight)


def head_masks(width):
    heads = width // HEAD_DIM
    lane = lax.broadcasted_iota(jnp.int32, (1, width), 1)
    half = HEAD_DIM // 2
    paired = [((lane % (width // 2)) // half) == h for h in range(heads)]
    plain = [(lane // HEAD_DIM) == h for h in range(heads)]
    return heads, paired, plain


def masked(values, masks):
    return [jnp.where(mask, values, jnp.zeros_like(values)) for mask in masks]


def attend_kernel(bounds, q_ref, k_ref, v_ref, sq_ref, sk_ref, o_ref, full_ref, lse_ref, vt_ref):
    i = pl.program_id(0)
    rows, width = q_ref.shape
    heads, paired, _ = head_masks(width)

    @pl.when(i == 0)
    def _():
        for b in range(v_ref.shape[0]):
            vt_ref[b] = v_ref[b].T

    q_heads = masked(q_ref[...] * jnp.asarray(HEAD_DIM**-0.5, BF), paired)
    sq = sq_ref[...]

    def step(kb, carry):
        k = k_ref[kb]
        same = sk_ref[kb] == sq
        new = []
        for h in range(heads):
            top_was, total, acc = carry[h]
            scores = lax.dot_general(k, q_heads[h], NT, preferred_element_type=F32)
            scores = jnp.where(same, scores, -1e30)
            top = jnp.maximum(top_was, jnp.max(scores, axis=0, keepdims=True))
            fade = jnp.exp(top_was - top)
            weight = jnp.exp(scores - top)
            total = fade * total + jnp.sum(weight, axis=0, keepdims=True)
            v_head = vt_ref[kb, h * HEAD_DIM : (h + 1) * HEAD_DIM, :]
            acc = acc * fade + jnp.dot(v_head, weight.astype(BF), preferred_element_type=F32)
            new.append((top, total, acc))
        return tuple(new)

    start = tuple(
        (jnp.full((1, rows), -1e30, F32), jnp.zeros((1, rows), F32), jnp.zeros((HEAD_DIM, rows), F32))
        for _ in range(heads)
    )
    done = lax.fori_loop(bounds[i, 0], bounds[i, 1], step, start)
    full = jnp.concatenate([acc * (1.0 / total) for _, total, acc in done], axis=0)
    full_ref[...] = full
    o_ref[...] = full.T.astype(BF)
    row = lax.broadcasted_iota(jnp.int32, lse_ref.shape, 0)
    logs = jnp.zeros(lse_ref.shape, F32)
    for h, (top, total, _) in enumerate(done):
        logs = jnp.where(row == h, top + jnp.log(total), logs)
    lse_ref[...] = logs


def attend(qkv, seg_rows, seg_columns, bounds, block):
    shards, _, rows, width = qkv.shape
    total = shards * rows
    per = rows // block
    grid_spec = pltpu.PrefetchScalarGridSpec(
        num_scalar_prefetch=1,
        grid=(total // block,),
        in_specs=[
            pl.BlockSpec((None, None, block, width), lambda i, b: (i // per, 0, i % per, 0)),
            pl.BlockSpec((shards, None, rows, width), lambda i, b: (0, 1, 0, 0)),
            pl.BlockSpec((shards, None, rows, width), lambda i, b: (0, 2, 0, 0)),
            pl.BlockSpec((1, block), lambda i, b: (0, i)),
            pl.BlockSpec((shards, rows, 1), lambda i, b: (0, 0, 0)),
        ],
        out_specs=[
            pl.BlockSpec((block, width), lambda i, b: (i, 0)),
            pl.BlockSpec((width, block), lambda i, b: (0, i)),
            pl.BlockSpec((8, block), lambda i, b: (0, i)),
        ],
        scratch_shapes=[pltpu.VMEM((shards, width, rows), BF)],
    )
    return pl.pallas_call(
        attend_kernel,
        out_shape=[
            jax.ShapeDtypeStruct((total, width), BF),
            jax.ShapeDtypeStruct((width, total), F32),
            jax.ShapeDtypeStruct((8, total), F32),
        ],
        grid_spec=grid_spec,
        compiler_params=pltpu.CompilerParams(vmem_limit_bytes=48 << 20),
        cost_estimate=pl.CostEstimate(
            flops=4 * total * total * width, bytes_accessed=8 << 20, transcendentals=0
        ),
    )(bounds, qkv, qkv, qkv, seg_rows, seg_columns)


def unrotate(values, cos, sin):
    return values * cos - pltpu.roll(values, LANES // 2, 1) * sin


def attend_back_kernel(
    bounds, q_ref, k_ref, v_ref, full_ref, lse_ref, do_ref, sq_ref, sk_ref, cos_ref, sin_ref,
    out_ref, dk_ref, dv_ref, kt_ref,
):
    i = pl.program_id(0)
    rows, width = q_ref.shape
    shards, _, shard_rows, _ = out_ref.shape
    per = shard_rows // rows
    heads, paired, plain = head_masks(width)
    scale = HEAD_DIM**-0.5

    @pl.when(i == 0)
    def _():
        dk_ref[...] = jnp.zeros_like(dk_ref)
        dv_ref[...] = jnp.zeros_like(dv_ref)
        for b in range(shards):
            for h, k_head in enumerate(masked(k_ref[b], paired)):
                kt_ref[b, h] = k_head.T

    do = do_ref[...]
    q_heads = masked(q_ref[...] * jnp.asarray(scale, BF), paired)
    do_heads = masked(do, plain)
    product = do.astype(F32).T * full_ref[...]
    deltas = [
        jnp.sum(product[h * HEAD_DIM : (h + 1) * HEAD_DIM], axis=0, keepdims=True)
        for h in range(heads)
    ]
    logs = [lse_ref[h : h + 1, :] for h in range(heads)]
    sq = sq_ref[...]

    def step(kb, dq):
        k, v = k_ref[kb], v_ref[kb]
        same = sk_ref[kb] == sq
        dk, dv = dk_ref[kb], dv_ref[kb]
        for h in range(heads):
            scores = lax.dot_general(k, q_heads[h], NT, preferred_element_type=F32)
            weight = jnp.where(same, jnp.exp(scores - logs[h]), 0.0)
            dp = lax.dot_general(v, do_heads[h], NT, preferred_element_type=F32)
            ds = (weight * (dp - deltas[h])).astype(BF)
            dv = dv + jnp.dot(weight.astype(BF), do_heads[h], preferred_element_type=F32)
            dk = dk + jnp.dot(ds, q_heads[h], preferred_element_type=F32)
            dq = dq + jnp.dot(kt_ref[kb, h], ds, preferred_element_type=F32)
        dk_ref[kb] = dk
        dv_ref[kb] = dv
        return dq

    dq = lax.fori_loop(bounds[i, 0], bounds[i, 1], step, jnp.zeros((width, rows), F32))
    dq = dq.T * scale
    here = pl.ds(pl.multiple_of(i * rows, rows), rows)
    inside = pl.ds(pl.multiple_of((i % per) * rows, rows), rows)
    out_ref[i // per, 0, inside, :] = unrotate(dq, cos_ref[here, :], sin_ref[here, :]).astype(BF)

    @pl.when(i == pl.num_programs(0) - 1)
    def _():
        for s in range(shards):
            own = slice(s * shard_rows, (s + 1) * shard_rows)
            out_ref[s, 1] = unrotate(dk_ref[s], cos_ref[own, :], sin_ref[own, :]).astype(BF)
            out_ref[s, 2] = dv_ref[s].astype(BF)


def attend_back(qkv, full, logs, grads, seg_rows, seg_columns, cos, sin, bounds, block):
    shards, _, rows, width = qkv.shape
    total = shards * rows
    per = rows // block
    heads = width // HEAD_DIM
    grid_spec = pltpu.PrefetchScalarGridSpec(
        num_scalar_prefetch=1,
        grid=(total // block,),
        in_specs=[
            pl.BlockSpec((None, None, block, width), lambda i, b: (i // per, 0, i % per, 0)),
            pl.BlockSpec((shards, None, rows, width), lambda i, b: (0, 1, 0, 0)),
            pl.BlockSpec((shards, None, rows, width), lambda i, b: (0, 2, 0, 0)),
            pl.BlockSpec((width, block), lambda i, b: (0, i)),
            pl.BlockSpec((8, block), lambda i, b: (0, i)),
            pl.BlockSpec((block, width), lambda i, b: (i, 0)),
            pl.BlockSpec((1, block), lambda i, b: (0, i)),
            pl.BlockSpec((shards, rows, 1), lambda i, b: (0, 0, 0)),
            pl.BlockSpec((total, width), lambda i, b: (0, 0)),
            pl.BlockSpec((total, width), lambda i, b: (0, 0)),
        ],
        out_specs=pl.BlockSpec((shards, 3, rows, width), lambda i, b: (0, 0, 0, 0)),
        scratch_shapes=[
            pltpu.VMEM((shards, rows, width), F32),
            pltpu.VMEM((shards, rows, width), F32),
            pltpu.VMEM((shards, heads, width, rows), BF),
        ],
    )
    return pl.pallas_call(
        attend_back_kernel,
        out_shape=jax.ShapeDtypeStruct((shards, 3, rows, width), BF),
        grid_spec=grid_spec,
        compiler_params=pltpu.CompilerParams(vmem_limit_bytes=48 << 20),
        cost_estimate=pl.CostEstimate(
            flops=10 * total * total * width, bytes_accessed=16 << 20, transcendentals=0
        ),
    )(bounds, qkv, qkv, qkv, full, logs, grads, seg_rows, seg_columns, cos, sin)


def middle_kernel(
    parts, clips, *refs,
):
    o_refs, refs = refs[:parts], refs[parts:]
    (x_ref, g_ref, seg_ref, mod_ref, wo_ref, bo_ref, w1_ref, b1_ref, w2_ref, b2_ref) = refs[:10]
    (out_ref, n_ref, r_ref, df_ref, dh_ref, da_ref, dx_ref, gb1_ref, gsum_ref) = refs[10:19]
    do_refs = refs[19:]
    rows, width = x_ref.shape
    shards = o_refs[0].shape[0]
    seg = seg_ref[...]

    @pl.when(pl.program_id(0) == 0)
    def _():
        gb1_ref[...] = jnp.zeros_like(gb1_ref)
        gsum_ref[...] = jnp.zeros_like(gsum_ref)

    def of_clip(part):
        columns = slice(part * width, (part + 1) * width)
        value = jnp.broadcast_to(mod_ref[0:1, columns], (rows, width))
        for c in range(1, clips):
            value = jnp.where(seg == c, mod_ref[c : c + 1, columns], value)
        return value

    def clip_sums(at, value):
        for c in range(clips):
            part = jnp.sum(jnp.where(seg == c, value, 0.0), axis=0, keepdims=True)
            gsum_ref[at + c : at + c + 1, :] += part

    def column_sum(at, value):
        gsum_ref[at : at + 1, :] += jnp.sum(value, axis=0, keepdims=True)

    def mean(value):
        return jnp.mean(value, axis=-1, keepdims=True)

    heads = [o_refs[p][s] for s in range(shards) for p in range(parts)]
    att = jnp.dot(jnp.concatenate(heads, axis=1), wo_ref[...], preferred_element_type=F32) + bo_ref[...]
    gate_a, gate_f, scale = of_clip(2), of_clip(5), 1.0 + of_clip(4)
    x2 = x_ref[...] + gate_a * att
    centred = x2 - mean(x2)
    under = lax.rsqrt(mean(centred * centred) + 1e-06)
    y = centred * under
    n2 = (y * scale + of_clip(3)).astype(BF)
    n_ref[...] = n2
    h = jnp.dot(n2, w1_ref[...], preferred_element_type=F32) + b1_ref[...]
    root = math.sqrt(2.0 / math.pi)
    square = h * h
    bent = jnp.tanh(root * h * (1.0 + 0.044715 * square))
    r = (0.5 * h * (1.0 + bent)).astype(BF)
    r_ref[...] = r
    slope = 0.5 * (1.0 + bent) + 0.5 * h * (1.0 - bent * bent) * root * (1.0 + 3 * 0.044715 * square)
    fo = jnp.dot(r, w2_ref[...], preferred_element_type=F32) + b2_ref[...]
    out_ref[...] = (x2 + gate_f * fo).astype(BF)

    g = g_ref[...].astype(F32)
    clip_sums(0, g * fo)
    gated = g * gate_f
    column_sum(4 * clips, gated)
    df = gated.astype(BF)
    df_ref[...] = df
    dh = (lax.dot_general(df, w2_ref[...], NT, preferred_element_type=F32) * slope).astype(BF)
    dh_ref[...] = dh
    gb1_ref[0:1, :] += jnp.sum(dh.astype(F32), axis=0, keepdims=True)
    dn2 = lax.dot_general(dh, w1_ref[...], NT, preferred_element_type=F32)
    clip_sums(clips, dn2)
    clip_sums(2 * clips, dn2 * y)
    z = dn2 * scale
    dx2 = g + (z - mean(z) - y * mean(z * y)) * under
    dx_ref[...] = dx2
    clip_sums(3 * clips, dx2 * att)
    gated = dx2 * gate_a
    column_sum(4 * clips + 1, gated)
    da = gated.astype(BF)
    da_ref[...] = da
    do = lax.dot_general(da, wo_ref[...], NT, preferred_element_type=F32).astype(BF)
    for s in range(shards):
        for p in range(parts):
            at = (s * parts + p) * LANES
            do_refs[p][s] = do[:, at : at + LANES]


def middle(o_parts, x1, grad, seg, mod, out_w, out_b, w1, b1, w2, b2):
    rows, width = x1.shape
    hidden = w1.shape[1]
    shards, parts, clips = o_parts[0].shape[0], len(o_parts), mod.shape[0]
    block = min(rows, 256)

    def row_block(columns):
        return pl.BlockSpec((block, columns), lambda i: (i, 0))

    def whole(shape):
        return pl.BlockSpec(shape, lambda i: (0, 0), pipeline_mode=pl.Buffered(1))

    def kept(shape):
        return pl.BlockSpec(shape, lambda i: (0, 0))

    by_shard = pl.BlockSpec((shards, block, LANES), lambda i: (0, i, 0))
    sums = -(-(4 * clips + 2) // 8) * 8
    shape = jax.ShapeDtypeStruct
    outs = [
        (shape((rows, width), BF), row_block(width)),
        (shape((rows, width), BF), row_block(width)),
        (shape((rows, hidden), BF), row_block(hidden)),
        (shape((rows, width), BF), row_block(width)),
        (shape((rows, hidden), BF), row_block(hidden)),
        (shape((rows, width), BF), row_block(width)),
        (shape((rows, width), F32), row_block(width)),
        (shape((8, hidden), F32), kept((8, hidden))),
        (shape((sums, width), F32), kept((sums, width))),
    ] + [(shape((shards, rows, LANES), BF), by_shard)] * parts
    return pl.pallas_call(
        partial(middle_kernel, parts, clips),
        out_shape=[o[0] for o in outs],
        grid=(rows // block,),
        in_specs=[by_shard] * parts
        + [
            row_block(width),
            row_block(width),
            row_block(1),
            whole(mod.shape),
            whole(out_w.shape),
            whole((1, width)),
            whole(w1.shape),
            whole((1, hidden)),
            whole(w2.shape),
            whole((1, width)),
        ],
        out_specs=[o[1] for o in outs],
        compiler_params=pltpu.CompilerParams(vmem_limit_bytes=56 << 20),
        cost_estimate=pl.CostEstimate(
            flops=2 * rows * width * (4 * hidden + 2 * width), bytes_accessed=20 << 20, transcendentals=0
        ),
    )(*o_parts, x1, grad, seg, mod, out_w, out_b[None], w1, b1[None], w2, b2[None])


def exchange(values, axis):
    return lax.all_to_all(values, axis, 0, 0)


def local(
    mel_pair, text_ids, clip_lengths, t_index,
    txt_table, txt_conv, txt_vec, txt_gain, txt_up, txt_hid, txt_down,
    emb_mel, emb_text, emb_bias, pos_conv, pos_bias,
    time_w1, time_bias, time_w2, ada_w, ada_b,
    qkv_w, qkv_b, out_w, out_b, ff_w1, ff_b1, ff_w2, ff_b2, out_grad,
):
    total = mel_pair.shape[0]
    width = emb_mel.shape[1]
    shards, groups = lax.axis_size("mp"), lax.axis_size("dp")
    rank, place = lax.axis_index("mp"), lax.axis_index("dp")
    rows = total // shards
    cols = width // shards
    clips = clip_lengths.shape[1]
    first = rank * rows
    taps = pos_conv.shape[1]
    group = pos_conv.shape[2]

    def spread_slice(weight, axis):
        piece = weight.shape[axis] // groups
        return lax.dynamic_slice_in_dim(weight, place * piece, piece, axis)

    def to_all(piece, axis_name="mp"):
        size = lax.axis_size(axis_name)
        return lax.all_to_all(jnp.broadcast_to(piece[None], (size,) + piece.shape), axis_name, 0, 0)

    def gather(piece, axis):
        return lax.all_gather(piece, "dp", axis=axis, tiled=True)

    def three(values):
        one = lax.reduce_precision(values, 8, 7)
        two = lax.reduce_precision(values - one, 8, 7)
        return jnp.concatenate([one, two, values - one - two], axis=0).astype(BF)

    qkv_piece = spread_slice(qkv_w, 1)
    qkv_piece = jnp.concatenate([pair_split(qkv_piece[:2]), qkv_piece[2:]], axis=0)
    in_rows = qkv_piece.shape[1]
    biases = jnp.concatenate(
        [pair_split(qkv_b[:2]), qkv_b[2:], ff_b1.reshape(-1, cols)], axis=0
    )
    bias_rows = biases.shape[0]
    biases = three(biases)
    biases = jnp.pad(biases, ((0, -biases.shape[0] % 16), (0, 0)))
    received = to_all(jnp.concatenate([qkv_piece.reshape(3 * in_rows, cols), biases], axis=0))
    qkv_full = gather(received[:, : 3 * in_rows].reshape(shards, 3, in_rows, cols), 2)
    biases = received[:, 3 * in_rows :].astype(F32)
    biases = sum(biases[:, i * bias_rows : (i + 1) * bias_rows] for i in range(3))
    qkv_bias = biases[:, :3]
    b1_full = biases[:, 3:].reshape(-1)
    out_piece, w2_piece, w1_piece = spread_slice(out_w, 0), spread_slice(ff_w2, 0), spread_slice(ff_w1, 0)
    w1_shape = w1_piece.shape
    cut = [out_piece.shape[0], out_piece.shape[0] + w2_piece.shape[0]]

    lengths = clip_lengths[0]
    clip_index = jnp.arange(clips, dtype=jnp.int32)
    ends = jnp.sum(jnp.where(clip_index[:, None] >= clip_index[None, :], lengths[None, :], 0), axis=1)
    starts = ends - lengths
    frames = jnp.arange(total, dtype=jnp.int32)
    member = (frames[:, None] >= starts[None, :]) & (frames[:, None] < ends[None, :])
    segment = jnp.sum(member * clip_index[None, :], axis=1).astype(jnp.int32)
    position = frames - jnp.sum(member * starts[None, :], axis=1)
    ext = rows + 2 * HALO
    ids = lax.dynamic_slice_in_dim(jnp.pad(text_ids, (HALO, HALO)), first, ext)
    seg_ext = lax.dynamic_slice_in_dim(jnp.pad(segment, (HALO, HALO), constant_values=-1), first, ext)
    hot_ext = (seg_ext[:, None] == clip_index[None, :]).astype(F32)
    ext_index = jnp.arange(ext, dtype=jnp.int32)
    inside = (ext_index >= HALO) & (ext_index < HALO + rows)
    own_ext = jnp.where(inside[:, None], hot_ext, 0.0)
    hot = hot_ext[HALO : HALO + rows]

    def time_path(steps):
        half = time_w1.shape[0] // 2
        frequency = jnp.exp(jnp.arange(half, dtype=F32) * (-math.log(10000.0) / (half - 1)))
        angles = steps.astype(F32)[:, None] * frequency[None, :]
        sinusoid = jnp.concatenate([jnp.sin(angles), jnp.cos(angles)], axis=-1)
        pre_one = precise(sinusoid, time_w1) + time_bias[0]
        act_one = jax.nn.silu(pre_one)
        time_vec = precise(act_one, time_w2) + time_bias[1]
        return sinusoid, pre_one, act_one, time_vec, jax.nn.silu(time_vec)

    mod = precise(time_path(t_index[0])[4], ada_w) + ada_b

    hidden = jnp.take(txt_table, ids, axis=0).astype(F32)
    kept = []
    blocks = txt_conv.shape[0]
    for b in range(blocks):
        hidden, saved = text_ahead(
            hidden, seg_ext, hot_ext, own_ext, txt_conv[b], txt_vec[b], txt_gain[b],
            txt_up[b], txt_hid[b], txt_down[b],
        )
        kept.append(saved)
    text = hidden[HALO : HALO + rows].astype(BF)

    mel = lax.dynamic_slice_in_dim(mel_pair, first, rows)
    x0 = dot(mel, emb_mel) + dot(text, emb_text) + emb_bias

    def to_channels(values):
        blocks_of = values.reshape(rows, shards, cols).transpose(1, 0, 2)
        return exchange(blocks_of, "mp").reshape(total, cols)

    def to_rows(values):
        return exchange(values.reshape(shards, rows, cols), "mp").transpose(1, 0, 2).reshape(rows, width)

    channels = to_channels(x0.astype(BF))
    pieces = jnp.concatenate([out_piece, w2_piece, w1_piece.reshape(-1, width)], axis=0)
    pieces, channels = lax.optimization_barrier((pieces, channels))
    spread_in = spread(channels.astype(F32), starts, ends)
    pre_a = apply_conv(spread_in, pos_conv[0], False) + pos_bias[0]
    y_a = jnp.pad(
        only_clips(mish(pre_a), starts, ends).astype(BF).astype(F32), ((GAP, GAP), (0, 0))
    )
    pre_b = apply_conv(y_a, pos_conv[1], False) + pos_bias[1]
    received = to_all(pieces)
    received, pre_b = lax.optimization_barrier((received, pre_b))
    out_full = gather(received[:, : cut[0]], 1).reshape(width, width)
    w1_piece = received[:, cut[1] :].reshape((shards,) + w1_shape).transpose(1, 0, 2)
    w1_full = gather(w1_piece.reshape(w1_shape[0], -1), 0)
    w2_full = gather(received[:, cut[0] : cut[1]], 1).reshape(-1, width)
    c_pos = to_rows(gather_back(mish(pre_b).astype(BF), starts, ends))
    x1 = x0 + c_pos.astype(F32)

    def modulate(state, mod_in, shift_part, scale_part):
        scale = expand(hot, mod_in[:, scale_part * width : (scale_part + 1) * width])
        shift = expand(hot, mod_in[:, shift_part * width : (shift_part + 1) * width])
        return layer_norm(state) * (1.0 + scale) + shift

    n1, n1_pull = jax.vjp(lambda s, m: modulate(s, m, 0, 1), x1, mod)
    n1 = n1.astype(BF)
    inverse = jnp.exp(jnp.arange(0, HEAD_DIM, 2, dtype=F32) * (-math.log(10000.0) / HEAD_DIM))
    angles = position.astype(F32)[:, None] * jnp.tile(inverse, LANES // inverse.shape[0])[None, :]
    cos = jnp.cos(angles)
    sin = jnp.sin(angles) * jnp.where(jnp.arange(LANES) < LANES // 2, -1.0, 1.0)
    cos_own = lax.dynamic_slice_in_dim(cos, first, rows)
    sin_own = lax.dynamic_slice_in_dim(sin, first, rows)
    parts = range(cols // LANES)
    qkv = [exchange(v, "mp") for v in project(n1, qkv_full, qkv_bias, cos_own, sin_own)]
    block = rows
    heads_of = segment[::block]
    tails_of = segment[block - 1 :: block]
    low_key = jnp.sum(jnp.where(heads_of[:, None] == clip_index, starts[None, :], 0), axis=1)
    high_key = jnp.sum(jnp.where(tails_of[:, None] == clip_index, ends[None, :], 0), axis=1)
    bounds = jnp.stack([low_key // rows, (high_key + rows - 1) // rows], axis=1).astype(jnp.int32)
    seg_rows = segment[None, :]
    seg_blocks = segment.reshape(shards, rows, 1)
    attended = [attend(qkv[h], seg_rows, seg_blocks, bounds, block) for h in parts]
    o_parts = [exchange(a[0].reshape(shards, rows, LANES), "mp") for a in attended]
    grad = lax.dynamic_slice_in_dim(out_grad, first, rows)
    seg_own = lax.dynamic_slice_in_dim(segment, first, rows)[:, None]
    out, n2, r, df, dh, da, dx2, ff_sums, sums, *do_parts = middle(
        o_parts, x1, grad, seg_own, mod, out_full, out_b, w1_full, b1_full, w2_full, ff_b2
    )
    dmod_gate_f, dmod_shift_f, dmod_scale_f, dmod_gate_a = (
        sums[i * clips : (i + 1) * clips] for i in range(4)
    )
    g_ff_w2 = dot(df, r, TN)
    g_ff_w1 = dot(n2, dh, TN)
    o_rows = jnp.stack(o_parts).transpose(2, 1, 0, 3).reshape(rows, width)

    def for_dp(matrix):
        return matrix.astype(BF).reshape(groups, matrix.shape[0] // groups, matrix.shape[1])

    def by_rank(matrix):
        return matrix.reshape(matrix.shape[0], shards, -1).transpose(1, 0, 2)

    def scatter_dp(matrix):
        return lax.psum_scatter(matrix.astype(BF), "dp", scatter_dimension=0, tiled=True)

    sent_w1, sent_w2 = scatter_dp(g_ff_w1), scatter_dp(g_ff_w2)

    g_out_w = dot(da, o_rows, TN)
    dqkv = []
    for h in parts:
        do_part = exchange(do_parts[h], "mp").reshape(total, LANES)
        d_part = attend_back(
            qkv[h], attended[h][1], attended[h][2], do_part, seg_rows, seg_blocks, cos, sin, bounds, block
        )
        dqkv.append(exchange(d_part, "mp"))
    dn1, g_qkv_w, g_qkv_b = unproject(dqkv, n1, qkv_full)
    more, dmod_d = n1_pull(dn1)
    dx1 = dx2 + more
    sent_w1, sent_w2, dx1, out = lax.optimization_barrier((sent_w1, sent_w2, dx1, out))
    ff_pair = jnp.concatenate([by_rank(sent_w1), by_rank(sent_w2)], axis=2)
    sent_qkv, sent_out = scatter_dp(g_qkv_w), scatter_dp(g_out_w)

    dmod = dmod_d + jnp.concatenate(
        [
            jnp.zeros((clips, 2 * width), F32), dmod_gate_a, dmod_shift_f, dmod_scale_f, dmod_gate_f,
        ],
        axis=1,
    )

    slope_b = gather_back(mish_slope(pre_b), starts, ends)
    dy_b = to_channels(dx1.astype(BF)).astype(F32) * slope_b
    g_pos_b = jnp.sum(dy_b, axis=0)
    dy_b = spread(dy_b.astype(BF).astype(F32), starts, ends)
    dy_a = only_clips(apply_conv(dy_b, pos_conv[1], True) * mish_slope(pre_a), starts, ends)
    g_pos_a = jnp.sum(dy_a, axis=0)
    dy_a = jnp.pad(dy_a.astype(BF).astype(F32), ((GAP, GAP), (0, 0)))
    dc = gather_back(
        apply_conv(dy_a, pos_conv[0], True).astype(BF), starts, ends
    )
    ff_got, dc = lax.optimization_barrier((exchange(ff_pair, "mp"), dc))
    dx0_full = dx1 + to_rows(dc).astype(F32)
    g_conv = jnp.concatenate(
        [conv_grad(spread_in, dy_a[GAP:-GAP], taps, group), conv_grad(y_a, dy_b[GAP:-GAP], taps, group)],
        axis=1,
    )
    sent_qkv, sent_out, dx0_full = lax.optimization_barrier((sent_qkv, sent_out, dx0_full))
    at_pair = jnp.concatenate([by_rank(sent_qkv), by_rank(sent_out)], axis=2)
    sent_conv = scatter_dp(g_conv)

    g_emb_bias = jnp.sum(dx0_full, axis=0)
    dx0 = dx0_full.astype(BF)
    mel_grad = dot(dx0, emb_mel, NT).astype(BF)
    g_emb = jnp.concatenate([dot(dx0, text, TN), dot(dx0, mel, TN)], axis=1)
    sent_emb = scatter_dp(g_emb)
    text_width = text.shape[1]

    dtext = jnp.pad(dot(dx0, emb_text, NT), ((HALO, HALO), (0, 0)))
    text_grads = [None] * blocks
    extra = dmod
    result = lax.all_gather(out[:, : width // 2], "mp", tiled=True)
    at_got, result, out, dtext = lax.optimization_barrier((exchange(at_pair, "mp"), result, out, dtext))
    result = [result, lax.all_gather(out[:, width // 2 :], "mp", tiled=True)]
    waiting = sent_conv
    for b in reversed(range(blocks)):
        dtext, text_grads[b], summed, waiting = text_behind(
            kept[b], dtext, txt_up[b], txt_down[b], extra, waiting
        )
        if extra is not None:
            stamps = jnp.broadcast_to(t_index[0].astype(F32)[:, None], (clips, 128))
            dmod_all = lax.all_gather(jnp.concatenate([summed, stamps], axis=1), "dp", tiled=True)
            sent_emb, dtext = lax.optimization_barrier((sent_emb, dtext))
            sent_conv, waiting = waiting, at_got
            dmod_all, all_steps = dmod_all[:, : 6 * width], dmod_all[:, 6 * width]
        extra = None
    at_got = waiting
    result[1], dtext = lax.optimization_barrier((result[1], dtext))
    result = jnp.concatenate(result, axis=1).astype(F32)
    vocab = txt_table.shape[0]
    wide = -(-vocab // 128) * 128
    chosen = (ids[:, None] == jnp.arange(wide, dtype=jnp.int32)[None, :]).astype(BF)
    g_table = dot(dtext, chosen, TN)
    hidden_width = txt_up.shape[2]

    g_qkv_b = jnp.concatenate([pair_merge(g_qkv_b[:, :2]), g_qkv_b[:, 2:]], axis=1)
    g_qkv_b = g_qkv_b.transpose(1, 0, 2).reshape(3, width)
    sources, pieces = [], []
    everyone = groups * shards

    def piece(value, kind, out, where, first=0, count=None):
        value = value if value.ndim == 2 else value[None]
        known = [i for i, have in enumerate(sources) if have is value]
        if not known:
            sources.append(value)
        index = known[0] if known else len(sources) - 1
        columns = value.shape[1] * (shards if kind == "mine" else 1)
        pieces.append((index, first, count or value.shape[0], columns, kind, out, where))

    for b, (g_conv_b, g_vec, g_gain, _, g_hid, _) in enumerate(text_grads):
        piece(g_conv_b, "both", 0, (b, 0))
        piece(g_vec, "both", 1, (b, 0))
        piece(g_gain, "both", 2, (None, b))
        for i, value in enumerate(g_hid):
            piece(value, "both", 3, (b, i))
    piece(g_emb_bias, "dp", 4, (None, 0))
    piece(g_pos_a, "mine", 5, (None, 0))
    piece(g_pos_b, "mine", 5, (None, 1))
    piece(g_qkv_b, "crossed", 6, (None, 0))
    piece(sums, "dp", 7, (None, 0), 4 * clips + 1, 1)
    piece(ff_sums, "crossed", 8, (None, 0), 0, 1)
    piece(sums, "dp", 9, (None, 0), 4 * clips, 1)
    text_part, hid_part, part = text_width // everyone, hidden_width // everyone, width // everyone
    small_shapes = [
        (blocks, txt_conv.shape[1], text_part), (blocks, 3, text_part), (blocks, text_part),
        (blocks, 3, hid_part), (1, width // groups), (2, part), (3, part), (1, width // groups),
        (1, ff_sums.shape[1] // everyone), (1, width // groups),
    ]
    table_sum, up0, up1, down0, down1, g_emb, mel_grad, *unpacked = last_sums(
        [for_dp(g_table)]
        + [for_dp(text_grads[b][3]) for b in range(blocks)]
        + [for_dp(text_grads[b][5]) for b in range(blocks)],
        sources,
        pieces,
        small_shapes,
        [],
        [sent_emb],
        [mel_grad],
    )
    mel_grad = mel_grad.reshape(total, -1)
    for i in (4, 7, 8, 9):
        unpacked[i] = unpacked[i].reshape(-1)
    o_table = table_sum[:, :vocab].T
    o_up = jnp.stack([up0.T, up1.T])
    o_down = jnp.stack([down0.T, down1.T])
    ff_pair, at_pair = (jnp.sum(v.astype(F32), axis=0) for v in (ff_got, at_got))
    ff_cols = ff_w1.shape[1]
    o_ff_w1, o_ff_w2 = ff_pair[:, :ff_cols], ff_pair[:, ff_cols:].T
    g_qkv = at_pair[:, : 3 * cols].reshape(-1, 3, cols).transpose(1, 0, 2)
    o_qkv_w = jnp.concatenate([pair_merge(g_qkv[:2]), g_qkv[2:]], axis=0)
    o_out_w = at_pair[:, 3 * cols :].T
    o_pos_conv = sent_conv.astype(F32).T.reshape(2, taps, group, -1)
    o_emb_text, o_emb_mel = g_emb[:, :text_width].T, g_emb[:, text_width:].T

    def own(values, index, parts):
        piece = values.shape[-1] // parts
        return lax.dynamic_slice_in_dim(values, index * piece, piece, values.ndim - 1)

    sinusoid, pre_one, act_one, time_vec, act_two = time_path(all_steps)
    de = precise(dmod_all, ada_w, NT) * silu_slope(time_vec)
    dpre = precise(de, time_w2, NT) * silu_slope(pre_one)

    def outer(left, right):
        return lax.dot_general(left, own(right, place, groups), TN, precision=highest)

    return (
        result,
        mel_grad,
        o_table,
        unpacked[0],
        unpacked[1],
        unpacked[2],
        o_up,
        unpacked[3],
        o_down,
        o_emb_mel,
        o_emb_text,
        unpacked[4],
        o_pos_conv,
        unpacked[5],
        outer(sinusoid, dpre),
        own(jnp.stack([jnp.sum(dpre, axis=0), jnp.sum(de, axis=0)]), place, groups),
        outer(act_one, de),
        outer(act_two, dmod_all),
        own(jnp.sum(dmod_all, axis=0), place, groups),
        o_qkv_w,
        unpacked[6],
        o_out_w,
        unpacked[7],
        o_ff_w1,
        unpacked[8],
        o_ff_w2,
        unpacked[9],
    )


def solution(mesh):
    both, crossed = ("dp", "mp"), ("mp", "dp")
    placed = (
        P("dp", None), P("dp"), P("dp", None), P("dp", None),
        P(), P(), P(), P(), P(), P(), P(), P(), P(), P(),
        P(None, None, None, "mp"), P(None, "mp"),
        P(), P(), P(), P(), P(),
        P(None, None, "mp"), P(None, "mp"), P("mp", None), P(),
        P(None, "mp"), P("mp"), P("mp", None), P(),
        P("dp", None),
    )
    given = (
        P("dp", None), P("dp", None),
        P(None, both), P(None, None, both), P(None, None, both), P(None, both),
        P(None, None, both), P(None, None, both), P(None, None, both),
        P(None, "dp"), P(None, "dp"), P("dp"),
        P(None, None, None, crossed), P(None, crossed),
        P(None, "dp"), P(None, "dp"), P(None, "dp"), P(None, "dp"), P("dp"),
        P(None, "dp", "mp"), P(None, crossed), P("mp", "dp"), P("dp"),
        P("dp", "mp"), P(crossed), P("mp", "dp"), P("dp"),
    )
    return jax.shard_map(local, mesh=mesh, in_specs=placed, out_specs=given, check_vma=False)
```

```python
from functools import partial
import math

import jax
import jax.numpy as jnp
from jax import lax
from jax.experimental import pallas as pl
from jax.experimental.pallas import tpu as pltpu
from jax.sharding import PartitionSpec as P

HEAD_DIM = 64
GAP = 16
HALO = 8
BF = jnp.bfloat16
F32 = jnp.float32
highest = lax.Precision.HIGHEST
NN = (((1,), (0,)), ((), ()))
NT = (((1,), (1,)), ((), ()))
TN = (((0,), (0,)), ((), ()))


def dot(left, right, dims=NN):
    return lax.dot_general(left.astype(BF), right.astype(BF), dims, preferred_element_type=F32)


def precise(left, right, dims=NN):
    one = lax.reduce_precision(left, 8, 7)
    two = lax.reduce_precision(left - one, 8, 7)
    three = left - one - two
    rows = left.shape[0]
    stacked = jnp.concatenate([one, two, three], axis=0).astype(BF)
    product = lax.dot_general(stacked, right, dims, preferred_element_type=F32)
    return product[:rows] + product[rows : 2 * rows] + product[2 * rows :]


@jax.custom_vjp
def expand(onehot, parts):
    return sum(onehot[:, c : c + 1] * parts[c : c + 1] for c in range(parts.shape[0]))


def expand_ahead(onehot, parts):
    return expand(onehot, parts), onehot


def expand_behind(onehot, grad):
    return None, jnp.dot(onehot.T, grad, precision=highest)


expand.defvjp(expand_ahead, expand_behind)


def silu_slope(values):
    sigmoid_val = jax.nn.sigmoid(values)
    return sigmoid_val * (1.0 + values * (1.0 - sigmoid_val))


def layer_norm(values):
    centred = values - jnp.mean(values, axis=-1, keepdims=True)
    variance = jnp.mean(centred * centred, axis=-1, keepdims=True)
    return centred * lax.rsqrt(variance + 1e-06)


def mish(values):
    grown = jnp.exp(jnp.minimum(values, 20.0))
    wide = grown * (grown + 2.0)
    return values * (wide / (wide + 2.0))


def mish_slope(values):
    grown = jnp.exp(jnp.minimum(values, 20.0))
    wide = grown * (grown + 2.0)
    under = 1.0 / (wide + 2.0)
    return wide * under + values * (4.0 * grown * (1.0 + grown) * under * under)


def sum_kernel(axis, size, x_ref, o_ref, slots, send_sems, recv_sems):
    me = lax.axis_index(axis)
    barrier = pltpu.get_barrier_semaphore()
    peers = [lax.rem(me + step, size) for step in range(1, size)]
    for peer in peers:
        pl.semaphore_signal(
            barrier, inc=1, device_id={axis: peer}, device_id_type=pl.DeviceIdType.MESH
        )
    pl.semaphore_wait(barrier, size - 1)
    for step, peer in enumerate(peers):
        pltpu.make_async_remote_copy(
            src_ref=x_ref,
            dst_ref=slots.at[me],
            send_sem=send_sems.at[step],
            recv_sem=recv_sems.at[me],
            device_id={axis: peer},
            device_id_type=pl.DeviceIdType.MESH,
        ).start()
    slots[me] = x_ref[...]
    for step, peer in enumerate(peers):
        copy = pltpu.make_async_remote_copy(
            src_ref=x_ref,
            dst_ref=slots.at[peer],
            send_sem=send_sems.at[step],
            recv_sem=recv_sems.at[peer],
            device_id={axis: peer},
            device_id_type=pl.DeviceIdType.MESH,
        )
        copy.wait_send()
        copy.wait_recv()
    total = slots[0]
    for device in range(1, size):
        total = total + slots[device]
    o_ref[...] = total


def small_sum(values, axis, name):
    size = lax.axis_size(axis)
    whole = pl.BlockSpec(memory_space=pltpu.VMEM)
    return pl.pallas_call(
        partial(sum_kernel, axis, size),
        out_shape=jax.ShapeDtypeStruct(values.shape, F32),
        in_specs=[whole],
        out_specs=whole,
        scratch_shapes=[
            pltpu.VMEM((size,) + values.shape, F32),
            pltpu.SemaphoreType.DMA((size - 1,)),
            pltpu.SemaphoreType.DMA((size,)),
        ],
        compiler_params=pltpu.CompilerParams(
            collective_id=name, has_side_effects=True, vmem_limit_bytes=16 << 20
        ),
    )(values)


def places(dp, mp, width, kind):
    share = width // dp
    if kind in ("dp", "both"):
        return [(0, 0, share, 0, share, None)], 1
    count = share // mp
    found = []
    for z in range(mp):
        at = z * count
        column = z * dp * count if kind == "crossed" else 0
        found.append((at // LANES, at % LANES, count, column, count, z))
    return found, -(-share // LANES)


def pack_rows(dp, mp, pieces, sources, pack, z):
    pack[...] = jnp.zeros_like(pack)
    at = 0
    for source, first, rows, width, kind, _, _ in pieces:
        found, used = places(dp, mp, width, kind)
        for row, lane, count, column, step, device in found:
            for d in range(dp):
                start = column + d * step
                value = sources[source][first : first + rows, start : start + count]
                if kind == "mine":
                    value = jnp.where(z == device, value, 0.0)
                to = slice(at + row, at + row + rows)
                pack[d // 2, d % 2, to, lane : lane + count] = value
        at += rows * used


def unpack_rows(dp, mp, pieces, value, outs, z):
    at = 0
    for _, _, rows, width, kind, out, where in pieces:
        found, used = places(dp, mp, width, kind)
        if kind == "both":
            count = width // dp // mp
            found = [(0, device * count, count, 0, 0, device) for device in range(mp)]
        total = None
        for row, lane, count, _, _, device in found:
            part = value[at + row : at + row + rows, lane : lane + count]
            if device is not None:
                part = jnp.where(z == device, part, 0.0)
            total = part if total is None else total + part
        lead, row = where
        if lead is None:
            outs[out][row : row + rows, :] = total
        else:
            outs[out][lead, row : row + rows, :] = total
        at += rows * used


def last_kernel(dp, mp, n_all, n_mp, n_both, n_gather, n_sources, n_small, pieces, *refs):
    n_in = n_all + n_mp + n_both + n_gather
    ins, refs = list(refs[: n_in - 1]), refs[n_in - 1 :]
    sources, refs = refs[:n_sources], refs[n_sources:]
    outs, refs = list(refs[: n_in - 1]), refs[n_in - 1 :]
    small_outs, rest = refs[:n_small], list(refs[n_small:])
    ins.insert(n_all - 1, rest.pop(0))
    outs.insert(n_all - 1, None)

    def take(count):
        return [rest.pop(0) for _ in range(count)]

    own, pair, joint, chip_slots, middle, slots = (
        take(n_all), take(n_all), take(n_all), take(n_all), take(n_all), take(n_in)
    )
    pair_send, pair_recv, chip_send, chip_recv, mp_send, mp_recv, own_sems = rest
    me, z = lax.axis_index("dp"), lax.axis_index("mp")
    chips = dp // 2
    core, chip = lax.rem(me, 2), me // 2
    partner = me + 1 - 2 * core
    other_chips = [lax.rem(chip + step, chips) for step in range(1, chips)]
    other_z = [lax.rem(z + step, mp) for step in range(1, mp)]
    mesh_id = pl.DeviceIdType.MESH
    barrier = pltpu.get_barrier_semaphore()
    greeted = (
        [{"dp": partner}]
        + [{"dp": 2 * q + core} for q in other_chips]
        + [{"mp": peer} for peer in other_z]
    )
    for device in greeted:
        pl.semaphore_signal(barrier, inc=1, device_id=device, device_id_type=mesh_id)
    pl.semaphore_wait(barrier, chips + mp - 1)

    def to_partner(t):
        return pltpu.make_async_remote_copy(
            src_ref=ins[t].at[:, 1 - core],
            dst_ref=pair[t],
            send_sem=pair_send.at[t],
            recv_sem=pair_recv.at[t],
            device_id={"dp": partner},
            device_id_type=mesh_id,
        )

    def to_chip(t, step, mine):
        q = other_chips[step]
        return pltpu.make_async_remote_copy(
            src_ref=joint[t].at[q],
            dst_ref=chip_slots[t].at[mine],
            send_sem=chip_send.at[t, step],
            recv_sem=chip_recv.at[t, mine],
            device_id={"dp": 2 * q + core},
            device_id_type=mesh_id,
        )

    def to_z(t, step, mine):
        peer = other_z[step]
        if t < n_all - 1:
            source = middle[t].at[peer]
        elif t == n_all - 1:
            source = middle[t]
        else:
            source = ins[t].at[peer] if t < n_all + n_mp else ins[t]
        return pltpu.make_async_remote_copy(
            src_ref=source,
            dst_ref=slots[t].at[mine],
            send_sem=mp_send.at[t, step],
            recv_sem=mp_recv.at[t, mine],
            device_id={"mp": peer},
            device_id_type=mesh_id,
        )

    local = []
    for t in range(n_all):
        if t == n_all - 1:
            pack_rows(dp, mp, pieces, sources, ins[t], z)
        to_partner(t).start()
        copy = pltpu.make_async_copy(ins[t].at[:, core], own[t], own_sems.at[t])
        copy.start()
        local.append(copy)
    for t in range(n_all, n_in):
        for step in range(mp - 1):
            to_z(t, step, z).start()
        source = ins[t].at[z] if t < n_all + n_mp else ins[t]
        copy = pltpu.make_async_copy(source, slots[t].at[z], own_sems.at[t])
        copy.start()
        local.append(copy)

    def total(ref, size):
        value = ref[0].astype(F32)
        for device in range(1, size):
            value = value + ref[device].astype(F32)
        return value

    for t in range(n_all):
        local[t].wait()
        copy = to_partner(t)
        copy.wait_send()
        copy.wait_recv()
        for q in range(chips):
            value = own[t][q].astype(F32) + pair[t][q].astype(F32)
            joint[t][q] = value.astype(joint[t].dtype)
        for step in range(chips - 1):
            to_chip(t, step, chip).start()
        chip_slots[t][chip] = joint[t][chip]
    for t in range(n_all):
        for step in range(chips - 1):
            copy = to_chip(t, step, other_chips[step])
            copy.wait_send()
            copy.wait_recv()
        value = total(chip_slots[t], chips)
        if t < n_all - 1:
            rows = value.shape[0] // mp
            for device in range(mp):
                part = value[device * rows : (device + 1) * rows]
                middle[t][device] = part.astype(middle[t].dtype)
            slots[t][z] = middle[t][z]
        else:
            middle[t][...] = value
            slots[t][z] = value
        for step in range(mp - 1):
            to_z(t, step, z).start()
    for t in list(range(n_all, n_in)) + list(range(n_all)):
        if t >= n_all:
            local[t].wait()
        for step in range(mp - 1):
            copy = to_z(t, step, other_z[step])
            copy.wait_send()
            copy.wait_recv()
        if t == n_all - 1:
            unpack_rows(dp, mp, pieces, total(slots[t], mp), small_outs, z)
        elif t < n_in - n_gather:
            outs[t][...] = total(slots[t], mp)
        else:
            outs[t][...] = slots[t][...].astype(F32)


def last_sums(over_all, sources, pieces, small_shapes, over_mp, both, gathered):
    dp, mp = lax.axis_size("dp"), lax.axis_size("mp")
    chips = dp // 2
    rows = sum(p[2] * places(dp, mp, p[3], p[4])[1] for p in pieces)
    packed = jax.ShapeDtypeStruct((chips, 2, -(-rows // 8) * 8, LANES), F32)
    everywhere = [v.reshape((chips, 2) + v.shape[1:]) for v in over_all] + [packed]
    ins = everywhere + list(over_mp) + list(both) + list(gathered)
    n_all, n_mp, n_both, n_gather = len(everywhere), len(over_mp), len(both), len(gathered)
    halves = [pltpu.VMEM((chips,) + v.shape[2:], v.dtype) for v in everywhere]
    outs, middle, slots = [], [], []
    for t, value in enumerate(ins):
        if t < n_all - 1:
            shape = (value.shape[2] // mp, value.shape[3])
            middle.append(pltpu.VMEM((mp,) + shape, value.dtype))
        elif t == n_all - 1:
            shape = value.shape[2:]
            middle.append(pltpu.VMEM(shape, value.dtype))
        else:
            shape = value.shape[1:] if t < n_all + n_mp else value.shape
        slots.append(pltpu.VMEM((mp,) + shape, value.dtype))
        outs.append((mp,) + shape if t >= len(ins) - n_gather else shape)
    dma = pltpu.SemaphoreType.DMA
    return pl.pallas_call(
        partial(
            last_kernel, dp, mp, n_all, n_mp, n_both, n_gather, len(sources), len(small_shapes), pieces
        ),
        out_shape=[
            jax.ShapeDtypeStruct(shape, F32)
            for shape in outs[: n_all - 1] + outs[n_all:] + list(small_shapes)
        ],
        in_specs=[pl.BlockSpec(memory_space=pl.ANY)] * (len(ins) - 1)
        + [pl.BlockSpec(memory_space=pltpu.VMEM)] * len(sources),
        out_specs=[pl.BlockSpec(memory_space=pltpu.VMEM)] * (len(ins) - 1 + len(small_shapes)),
        scratch_shapes=[pltpu.VMEM(packed.shape, F32)]
        + halves * 4
        + middle
        + slots
        + [
            dma((n_all,)),
            dma((n_all,)),
            dma((n_all, chips)),
            dma((n_all, chips)),
            dma((len(ins), mp)),
            dma((len(ins), mp)),
            dma((len(ins),)),
        ],
        compiler_params=pltpu.CompilerParams(
            collective_id=3, has_side_effects=True, vmem_limit_bytes=56 << 20
        ),
    )(*ins[: n_all - 1], *ins[n_all:], *sources)


def conv_norm(hidden, segment, conv, vec, gain):
    taps = conv.shape[0]
    reach = taps // 2
    rows = hidden.shape[0]
    padded = jnp.pad(hidden, ((reach, reach), (0, 0)))
    seg_padded = jnp.pad(segment, (reach, reach), constant_values=-1)
    mixture = vec[0]
    for tap in range(taps):
        keep = (seg_padded[tap : tap + rows] == segment) & (segment >= 0)
        mixture = mixture + conv[tap] * jnp.where(keep[:, None], padded[tap : tap + rows], 0.0)
    return layer_norm(mixture) * gain + vec[1]


def activate(pre, bias):
    return jax.nn.gelu(pre + bias, approximate=False)


def clip_squares(own, active):
    return jnp.dot(own.T, active * active, precision=highest)


def respond(active, squares, onehot, scale, shift):
    norms = jnp.sqrt(jnp.maximum(squares, 1.0))
    ratio = norms / (jnp.mean(norms, axis=-1, keepdims=True) + 1e-06)
    return scale * (active * expand(onehot, ratio)) + shift + active


def text_ahead(hidden, segment, onehot, own, conv, vec, gain, up, hid, down):
    normed, norm_pull = jax.vjp(
        lambda h, c, v, g: conv_norm(h, segment, c, v, g), hidden, conv, vec, gain
    )
    normed = normed.astype(BF)
    active, act_pull = jax.vjp(activate, dot(normed, up), hid[0])
    squares, square_pull = jax.vjp(lambda a: clip_squares(own, a), active)
    squares = small_sum(squares, "mp", 1)
    grown, respond_pull = jax.vjp(
        lambda a, s, g, b: respond(a, s, onehot, g, b), active, squares, hid[1], hid[2]
    )
    grown = grown.astype(BF)
    result = hidden + dot(grown, down) + vec[2]
    return result, (norm_pull, normed, act_pull, square_pull, respond_pull, grown)


def text_behind(kept, grad, up, down, extra, waiting):
    norm_pull, normed, act_pull, square_pull, respond_pull, grown = kept
    grad_low = grad.astype(BF)
    g_out = jnp.sum(grad, axis=0)
    g_down = dot(grad_low, grown, TN)
    grad_active, grad_squares, g_scale, g_shift = respond_pull(dot(grad_low, down, NT))
    grad_squares, waiting = lax.optimization_barrier((grad_squares, waiting))
    if extra is None:
        grad_squares = small_sum(grad_squares, "mp", 1)
    else:
        joined = small_sum(jnp.concatenate([grad_squares, extra], axis=1), "mp", 2)
        grad_squares, extra = joined[:, : grad_squares.shape[1]], joined[:, grad_squares.shape[1] :]
    grad_active = grad_active + square_pull(grad_squares)[0]
    grad_pre, g_bias = act_pull(grad_active)
    pre_low = grad_pre.astype(BF)
    g_up = dot(pre_low, normed, TN)
    grad_hidden, g_conv, g_vec, g_gain = norm_pull(dot(pre_low, up, NT))
    g_vec = g_vec.at[2].add(g_out)
    return (
        grad + grad_hidden,
        (g_conv, g_vec, g_gain, g_up, (g_bias, g_scale, g_shift), g_down),
        extra,
        waiting,
    )


def spread(values, starts, ends):
    rows = values.shape[0]
    clips = starts.shape[0]
    at = lax.broadcasted_iota(jnp.int32, values.shape, 0)
    total = rows + GAP * clips + 2 * GAP
    out = None
    for c in range(clips):
        part = jnp.where((at >= starts[c]) & (at < ends[c]), values, 0)
        lead = GAP + GAP * c
        part = jnp.pad(part, ((lead, total - lead - rows), (0, 0)))
        out = part if out is None else out + part
    return out


def only_clips(values, starts, ends):
    at = lax.broadcasted_iota(jnp.int32, values.shape, 0)
    keep = None
    for c in range(starts.shape[0]):
        inside = (at >= starts[c] + GAP * c) & (at < ends[c] + GAP * c)
        keep = inside if keep is None else keep | inside
    return jnp.where(keep, values, 0.0)


def gather_back(values, starts, ends):
    clips = starts.shape[0]
    rows = values.shape[0] - GAP * clips
    at = lax.broadcasted_iota(jnp.int32, (rows, values.shape[1]), 0)
    out = values[:rows]
    for c in range(1, clips):
        out = jnp.where(at >= starts[c], values[GAP * c : GAP * c + rows], out)
    return out


def conv_kernel(taps, turned, x_ref, w_ref, o_ref, full_ref):
    rows, width = o_ref.shape
    group = w_ref.shape[1]
    first = GAP - taps // 2

    @pl.when(pl.program_id(0) == 0)
    def _():
        lane = lax.broadcasted_iota(jnp.int32, (group, width), 1) // group
        for k in range(taps):
            tap = w_ref[taps - 1 - k if turned else k]
            for g in range(width // group):
                piece = jnp.where(lane == g, tap, jnp.zeros_like(tap))
                if turned:
                    full_ref[g * group : (g + 1) * group, k * width : (k + 1) * width] = piece
                else:
                    full_ref[k * width + g * group : k * width + (g + 1) * group, :] = piece

    columns = [x_ref[first + k : first + k + rows, :].astype(BF) for k in range(taps)]
    o_ref[...] = lax.dot_general(
        jnp.concatenate(columns, axis=1),
        full_ref[...],
        NT if turned else NN,
        preferred_element_type=F32,
    )


def conv_chunk(rows):
    for size in (528, 352, 256, 128, 64, 32, 16):
        if rows % size == 0:
            return size
    return rows


def apply_conv(spread_rows, weight, turned):
    rows = spread_rows.shape[0] - 2 * GAP
    width = spread_rows.shape[1]
    taps, group = weight.shape[:2]
    chunk = conv_chunk(rows)
    return pl.pallas_call(
        partial(conv_kernel, taps, turned),
        out_shape=jax.ShapeDtypeStruct((rows, width), F32),
        grid=(rows // chunk,),
        in_specs=[
            pl.BlockSpec((pl.Element(chunk + 2 * GAP), pl.Element(width)), lambda i: (i * chunk, 0)),
            pl.BlockSpec(weight.shape, lambda i: (0, 0, 0), pipeline_mode=pl.Buffered(1)),
        ],
        out_specs=pl.BlockSpec((chunk, width), lambda i: (i, 0)),
        scratch_shapes=[
            pltpu.VMEM((width, taps * width) if turned else (taps * width, width), BF)
        ],
        compiler_params=pltpu.CompilerParams(vmem_limit_bytes=48 << 20),
        cost_estimate=pl.CostEstimate(
            flops=2 * rows * taps * width * width, bytes_accessed=8 << 20, transcendentals=0
        ),
    )(spread_rows, weight)


def conv_grad_kernel(taps, group, x_ref, g_ref, o_ref):
    rows, width = g_ref.shape
    first = GAP - taps // 2
    turned = g_ref[...].T.astype(BF)

    @pl.when(pl.program_id(0) == 0)
    def _():
        o_ref[...] = jnp.zeros_like(o_ref)

    for k in range(taps):
        window = x_ref[first + k : first + k + rows, :].astype(BF)
        product = jnp.dot(turned, window, preferred_element_type=F32)
        for g in range(width // group):
            own = slice(g * group, (g + 1) * group)
            o_ref[own, k * group : (k + 1) * group] += product[own, own]


def conv_grad(spread_rows, grads, taps, group):
    rows, width = grads.shape
    chunk = conv_chunk(rows)
    return pl.pallas_call(
        partial(conv_grad_kernel, taps, group),
        out_shape=jax.ShapeDtypeStruct((width, taps * group), F32),
        grid=(rows // chunk,),
        in_specs=[
            pl.BlockSpec((pl.Element(chunk + 2 * GAP), pl.Element(width)), lambda i: (i * chunk, 0)),
            pl.BlockSpec((chunk, width), lambda i: (i, 0)),
        ],
        out_specs=pl.BlockSpec((width, taps * group), lambda i: (0, 0)),
        compiler_params=pltpu.CompilerParams(vmem_limit_bytes=48 << 20),
        cost_estimate=pl.CostEstimate(
            flops=2 * rows * taps * width * width, bytes_accessed=8 << 20, transcendentals=0
        ),
    )(spread_rows, grads)


LANES = 128


def pair_split(columns):
    pairs = columns.reshape(*columns.shape[:-1], -1, LANES // 2, 2)
    return jnp.swapaxes(pairs, -1, -2).reshape(columns.shape)


def pair_merge(columns):
    pairs = columns.reshape(*columns.shape[:-1], -1, 2, LANES // 2)
    return jnp.swapaxes(pairs, -1, -2).reshape(columns.shape)


def project_kernel(x_ref, w_ref, b_ref, cos_ref, sin_ref, *out_refs):
    cos, sin = cos_ref[...], sin_ref[...]
    for p in range(3):
        value = jnp.dot(x_ref[...], w_ref[p], preferred_element_type=F32) + b_ref[p : p + 1, :]
        for at, out_ref in enumerate(out_refs):
            piece = value[:, at * LANES : (at + 1) * LANES]
            if p < 2:
                piece = piece * cos + pltpu.roll(piece, LANES // 2, 1) * sin
            out_ref[p] = piece.astype(BF)


def project(normed, weight, bias, cos, sin):
    rows = normed.shape[0]
    shards, _, width, cols = weight.shape
    parts = cols // LANES
    return pl.pallas_call(
        project_kernel,
        out_shape=[jax.ShapeDtypeStruct((shards, 3, rows, LANES), BF)] * parts,
        grid=(shards,),
        in_specs=[
            pl.BlockSpec((rows, width), lambda i: (0, 0)),
            pl.BlockSpec((None, 3, width, cols), lambda i: (i, 0, 0, 0)),
            pl.BlockSpec((None, 3, cols), lambda i: (i, 0, 0)),
            pl.BlockSpec((rows, LANES), lambda i: (0, 0)),
            pl.BlockSpec((rows, LANES), lambda i: (0, 0)),
        ],
        out_specs=[pl.BlockSpec((None, 3, rows, LANES), lambda i: (i, 0, 0, 0))] * parts,
        compiler_params=pltpu.CompilerParams(vmem_limit_bytes=32 << 20),
        cost_estimate=pl.CostEstimate(
            flops=6 * rows * width * width, bytes_accessed=10 << 20, transcendentals=0
        ),
    )(normed, weight, bias, cos, sin)


def unproject_kernel(parts, *refs):
    d_refs, (x_ref, w_ref, dx_ref, gw_ref, gb_ref, turned) = refs[:parts], refs[parts:]
    s = pl.program_id(0)
    cols = w_ref.shape[2]

    @pl.when(s == 0)
    def _():
        turned[...] = x_ref[...].T
        dx_ref[...] = jnp.zeros_like(dx_ref)

    total = None
    for p in range(3):
        grad = jnp.concatenate([d_ref[p] for d_ref in d_refs], axis=1)
        product = lax.dot_general(grad, w_ref[p], NT, preferred_element_type=F32)
        total = product if total is None else total + product
        weight = jnp.dot(turned[...], grad, preferred_element_type=F32)
        gw_ref[:, p * cols : (p + 1) * cols] = weight.astype(BF)
        gb_ref[p : p + 1, :] = jnp.sum(grad.astype(F32), axis=0, keepdims=True)
    dx_ref[...] += total


def unproject(grads, normed, weight):
    rows = normed.shape[0]
    shards, _, width, cols = weight.shape
    parts = len(grads)
    return pl.pallas_call(
        partial(unproject_kernel, parts),
        out_shape=[
            jax.ShapeDtypeStruct((rows, width), F32),
            jax.ShapeDtypeStruct((width, shards * 3 * cols), BF),
            jax.ShapeDtypeStruct((shards, 3, cols), F32),
        ],
        grid=(shards,),
        in_specs=[pl.BlockSpec((None, 3, rows, LANES), lambda i: (i, 0, 0, 0))] * parts
        + [
            pl.BlockSpec((rows, width), lambda i: (0, 0)),
            pl.BlockSpec((None, 3, width, cols), lambda i: (i, 0, 0, 0)),
        ],
        out_specs=[
            pl.BlockSpec((rows, width), lambda i: (0, 0)),
            pl.BlockSpec((width, 3 * cols), lambda i: (0, i)),
            pl.BlockSpec((None, 3, cols), lambda i: (i, 0, 0)),
        ],
        scratch_shapes=[pltpu.VMEM((width, rows), BF)],
        compiler_params=pltpu.CompilerParams(vmem_limit_bytes=48 << 20),
        cost_estimate=pl.CostEstimate(
            flops=12 * rows * width * width, bytes_accessed=20 << 20, transcendentals=0
        ),
    )(*grads, normed, weight)


def head_masks(width):
    heads = width // HEAD_DIM
    lane = lax.broadcasted_iota(jnp.int32, (1, width), 1)
    half = HEAD_DIM // 2
    paired = [((lane % (width // 2)) // half) == h for h in range(heads)]
    plain = [(lane // HEAD_DIM) == h for h in range(heads)]
    return heads, paired, plain


def masked(values, masks):
    return [jnp.where(mask, values, jnp.zeros_like(values)) for mask in masks]


def attend_kernel(bounds, q_ref, k_ref, v_ref, sq_ref, sk_ref, o_ref, full_ref, lse_ref, vt_ref):
    i = pl.program_id(0)
    rows, width = q_ref.shape
    heads, paired, _ = head_masks(width)

    @pl.when(i == 0)
    def _():
        for b in range(v_ref.shape[0]):
            vt_ref[b] = v_ref[b].T

    q_heads = masked(q_ref[...] * jnp.asarray(HEAD_DIM**-0.5, BF), paired)
    sq = sq_ref[...]

    def step(kb, carry):
        k = k_ref[kb]
        same = sk_ref[kb] == sq
        new = []
        for h in range(heads):
            top_was, total, acc = carry[h]
            scores = lax.dot_general(k, q_heads[h], NT, preferred_element_type=F32)
            scores = jnp.where(same, scores, -1e30)
            top = jnp.maximum(top_was, jnp.max(scores, axis=0, keepdims=True))
            fade = jnp.exp(top_was - top)
            weight = jnp.exp(scores - top)
            total = fade * total + jnp.sum(weight, axis=0, keepdims=True)
            v_head = vt_ref[kb, h * HEAD_DIM : (h + 1) * HEAD_DIM, :]
            acc = acc * fade + jnp.dot(v_head, weight.astype(BF), preferred_element_type=F32)
            new.append((top, total, acc))
        return tuple(new)

    start = tuple(
        (jnp.full((1, rows), -1e30, F32), jnp.zeros((1, rows), F32), jnp.zeros((HEAD_DIM, rows), F32))
        for _ in range(heads)
    )
    done = lax.fori_loop(bounds[i, 0], bounds[i, 1], step, start)
    full = jnp.concatenate([acc * (1.0 / total) for _, total, acc in done], axis=0)
    full_ref[...] = full
    o_ref[...] = full.T.astype(BF)
    row = lax.broadcasted_iota(jnp.int32, lse_ref.shape, 0)
    logs = jnp.zeros(lse_ref.shape, F32)
    for h, (top, total, _) in enumerate(done):
        logs = jnp.where(row == h, top + jnp.log(total), logs)
    lse_ref[...] = logs


def attend(qkv, seg_rows, seg_columns, bounds, block):
    shards, _, rows, width = qkv.shape
    total = shards * rows
    per = rows // block
    grid_spec = pltpu.PrefetchScalarGridSpec(
        num_scalar_prefetch=1,
        grid=(total // block,),
        in_specs=[
            pl.BlockSpec((None, None, block, width), lambda i, b: (i // per, 0, i % per, 0)),
            pl.BlockSpec((shards, None, rows, width), lambda i, b: (0, 1, 0, 0)),
            pl.BlockSpec((shards, None, rows, width), lambda i, b: (0, 2, 0, 0)),
            pl.BlockSpec((1, block), lambda i, b: (0, i)),
            pl.BlockSpec((shards, rows, 1), lambda i, b: (0, 0, 0)),
        ],
        out_specs=[
            pl.BlockSpec((block, width), lambda i, b: (i, 0)),
            pl.BlockSpec((width, block), lambda i, b: (0, i)),
            pl.BlockSpec((8, block), lambda i, b: (0, i)),
        ],
        scratch_shapes=[pltpu.VMEM((shards, width, rows), BF)],
    )
    return pl.pallas_call(
        attend_kernel,
        out_shape=[
            jax.ShapeDtypeStruct((total, width), BF),
            jax.ShapeDtypeStruct((width, total), F32),
            jax.ShapeDtypeStruct((8, total), F32),
        ],
        grid_spec=grid_spec,
        compiler_params=pltpu.CompilerParams(vmem_limit_bytes=48 << 20),
        cost_estimate=pl.CostEstimate(
            flops=4 * total * total * width, bytes_accessed=8 << 20, transcendentals=0
        ),
    )(bounds, qkv, qkv, qkv, seg_rows, seg_columns)


def unrotate(values, cos, sin):
    return values * cos - pltpu.roll(values, LANES // 2, 1) * sin


def attend_back_kernel(
    bounds, q_ref, k_ref, v_ref, full_ref, lse_ref, do_ref, sq_ref, sk_ref, cos_ref, sin_ref,
    out_ref, dk_ref, dv_ref, kt_ref,
):
    i = pl.program_id(0)
    rows, width = q_ref.shape
    shards, _, shard_rows, _ = out_ref.shape
    per = shard_rows // rows
    heads, paired, plain = head_masks(width)
    scale = HEAD_DIM**-0.5

    @pl.when(i == 0)
    def _():
        dk_ref[...] = jnp.zeros_like(dk_ref)
        dv_ref[...] = jnp.zeros_like(dv_ref)
        for b in range(shards):
            for h, k_head in enumerate(masked(k_ref[b], paired)):
                kt_ref[b, h] = k_head.T

    do = do_ref[...]
    q_heads = masked(q_ref[...] * jnp.asarray(scale, BF), paired)
    do_heads = masked(do, plain)
    product = do.astype(F32).T * full_ref[...]
    deltas = [
        jnp.sum(product[h * HEAD_DIM : (h + 1) * HEAD_DIM], axis=0, keepdims=True)
        for h in range(heads)
    ]
    logs = [lse_ref[h : h + 1, :] for h in range(heads)]
    sq = sq_ref[...]

    def step(kb, dq):
        k, v = k_ref[kb], v_ref[kb]
        same = sk_ref[kb] == sq
        dk, dv = dk_ref[kb], dv_ref[kb]
        for h in range(heads):
            scores = lax.dot_general(k, q_heads[h], NT, preferred_element_type=F32)
            weight = jnp.where(same, jnp.exp(scores - logs[h]), 0.0)
            dp = lax.dot_general(v, do_heads[h], NT, preferred_element_type=F32)
            ds = (weight * (dp - deltas[h])).astype(BF)
            dv = dv + jnp.dot(weight.astype(BF), do_heads[h], preferred_element_type=F32)
            dk = dk + jnp.dot(ds, q_heads[h], preferred_element_type=F32)
            dq = dq + jnp.dot(kt_ref[kb, h], ds, preferred_element_type=F32)
        dk_ref[kb] = dk
        dv_ref[kb] = dv
        return dq

    dq = lax.fori_loop(bounds[i, 0], bounds[i, 1], step, jnp.zeros((width, rows), F32))
    dq = dq.T * scale
    here = pl.ds(pl.multiple_of(i * rows, rows), rows)
    inside = pl.ds(pl.multiple_of((i % per) * rows, rows), rows)
    out_ref[i // per, 0, inside, :] = unrotate(dq, cos_ref[here, :], sin_ref[here, :]).astype(BF)

    @pl.when(i == pl.num_programs(0) - 1)
    def _():
        for s in range(shards):
            own = slice(s * shard_rows, (s + 1) * shard_rows)
            out_ref[s, 1] = unrotate(dk_ref[s], cos_ref[own, :], sin_ref[own, :]).astype(BF)
            out_ref[s, 2] = dv_ref[s].astype(BF)


def attend_back(qkv, full, logs, grads, seg_rows, seg_columns, cos, sin, bounds, block):
    shards, _, rows, width = qkv.shape
    total = shards * rows
    per = rows // block
    heads = width // HEAD_DIM
    grid_spec = pltpu.PrefetchScalarGridSpec(
        num_scalar_prefetch=1,
        grid=(total // block,),
        in_specs=[
            pl.BlockSpec((None, None, block, width), lambda i, b: (i // per, 0, i % per, 0)),
            pl.BlockSpec((shards, None, rows, width), lambda i, b: (0, 1, 0, 0)),
            pl.BlockSpec((shards, None, rows, width), lambda i, b: (0, 2, 0, 0)),
            pl.BlockSpec((width, block), lambda i, b: (0, i)),
            pl.BlockSpec((8, block), lambda i, b: (0, i)),
            pl.BlockSpec((block, width), lambda i, b: (i, 0)),
            pl.BlockSpec((1, block), lambda i, b: (0, i)),
            pl.BlockSpec((shards, rows, 1), lambda i, b: (0, 0, 0)),
            pl.BlockSpec((total, width), lambda i, b: (0, 0)),
            pl.BlockSpec((total, width), lambda i, b: (0, 0)),
        ],
        out_specs=pl.BlockSpec((shards, 3, rows, width), lambda i, b: (0, 0, 0, 0)),
        scratch_shapes=[
            pltpu.VMEM((shards, rows, width), F32),
            pltpu.VMEM((shards, rows, width), F32),
            pltpu.VMEM((shards, heads, width, rows), BF),
        ],
    )
    return pl.pallas_call(
        attend_back_kernel,
        out_shape=jax.ShapeDtypeStruct((shards, 3, rows, width), BF),
        grid_spec=grid_spec,
        compiler_params=pltpu.CompilerParams(vmem_limit_bytes=48 << 20),
        cost_estimate=pl.CostEstimate(
            flops=10 * total * total * width, bytes_accessed=16 << 20, transcendentals=0
        ),
    )(bounds, qkv, qkv, qkv, full, logs, grads, seg_rows, seg_columns, cos, sin)


def middle_kernel(
    parts, clips, *refs,
):
    o_refs, refs = refs[:parts], refs[parts:]
    (x_ref, g_ref, seg_ref, mod_ref, wo_ref, bo_ref, w1_ref, b1_ref, w2_ref, b2_ref) = refs[:10]
    (out_ref, n_ref, r_ref, df_ref, dh_ref, da_ref, dx_ref, gb1_ref, gsum_ref) = refs[10:19]
    do_refs = refs[19:]
    rows, width = x_ref.shape
    shards = o_refs[0].shape[0]
    seg = seg_ref[...]

    @pl.when(pl.program_id(0) == 0)
    def _():
        gb1_ref[...] = jnp.zeros_like(gb1_ref)
        gsum_ref[...] = jnp.zeros_like(gsum_ref)

    def of_clip(part):
        columns = slice(part * width, (part + 1) * width)
        value = jnp.broadcast_to(mod_ref[0:1, columns], (rows, width))
        for c in range(1, clips):
            value = jnp.where(seg == c, mod_ref[c : c + 1, columns], value)
        return value

    def clip_sums(at, value):
        for c in range(clips):
            part = jnp.sum(jnp.where(seg == c, value, 0.0), axis=0, keepdims=True)
            gsum_ref[at + c : at + c + 1, :] += part

    def column_sum(at, value):
        gsum_ref[at : at + 1, :] += jnp.sum(value, axis=0, keepdims=True)

    def mean(value):
        return jnp.mean(value, axis=-1, keepdims=True)

    heads = [o_refs[p][s] for s in range(shards) for p in range(parts)]
    att = jnp.dot(jnp.concatenate(heads, axis=1), wo_ref[...], preferred_element_type=F32) + bo_ref[...]
    gate_a, gate_f, scale = of_clip(2), of_clip(5), 1.0 + of_clip(4)
    x2 = x_ref[...] + gate_a * att
    centred = x2 - mean(x2)
    under = lax.rsqrt(mean(centred * centred) + 1e-06)
    y = centred * under
    n2 = (y * scale + of_clip(3)).astype(BF)
    n_ref[...] = n2
    h = jnp.dot(n2, w1_ref[...], preferred_element_type=F32) + b1_ref[...]
    root = math.sqrt(2.0 / math.pi)
    square = h * h
    bent = jnp.tanh(root * h * (1.0 + 0.044715 * square))
    r = (0.5 * h * (1.0 + bent)).astype(BF)
    r_ref[...] = r
    slope = 0.5 * (1.0 + bent) + 0.5 * h * (1.0 - bent * bent) * root * (1.0 + 3 * 0.044715 * square)
    fo = jnp.dot(r, w2_ref[...], preferred_element_type=F32) + b2_ref[...]
    out_ref[...] = (x2 + gate_f * fo).astype(BF)

    g = g_ref[...].astype(F32)
    clip_sums(0, g * fo)
    gated = g * gate_f
    column_sum(4 * clips, gated)
    df = gated.astype(BF)
    df_ref[...] = df
    dh = (lax.dot_general(df, w2_ref[...], NT, preferred_element_type=F32) * slope).astype(BF)
    dh_ref[...] = dh
    gb1_ref[0:1, :] += jnp.sum(dh.astype(F32), axis=0, keepdims=True)
    dn2 = lax.dot_general(dh, w1_ref[...], NT, preferred_element_type=F32)
    clip_sums(clips, dn2)
    clip_sums(2 * clips, dn2 * y)
    z = dn2 * scale
    dx2 = g + (z - mean(z) - y * mean(z * y)) * under
    dx_ref[...] = dx2
    clip_sums(3 * clips, dx2 * att)
    gated = dx2 * gate_a
    column_sum(4 * clips + 1, gated)
    da = gated.astype(BF)
    da_ref[...] = da
    do = lax.dot_general(da, wo_ref[...], NT, preferred_element_type=F32).astype(BF)
    for s in range(shards):
        for p in range(parts):
            at = (s * parts + p) * LANES
            do_refs[p][s] = do[:, at : at + LANES]


def middle(o_parts, x1, grad, seg, mod, out_w, out_b, w1, b1, w2, b2):
    rows, width = x1.shape
    hidden = w1.shape[1]
    shards, parts, clips = o_parts[0].shape[0], len(o_parts), mod.shape[0]
    block = min(rows, 256)

    def row_block(columns):
        return pl.BlockSpec((block, columns), lambda i: (i, 0))

    def whole(shape):
        return pl.BlockSpec(shape, lambda i: (0, 0), pipeline_mode=pl.Buffered(1))

    def kept(shape):
        return pl.BlockSpec(shape, lambda i: (0, 0))

    by_shard = pl.BlockSpec((shards, block, LANES), lambda i: (0, i, 0))
    sums = -(-(4 * clips + 2) // 8) * 8
    shape = jax.ShapeDtypeStruct
    outs = [
        (shape((rows, width), BF), row_block(width)),
        (shape((rows, width), BF), row_block(width)),
        (shape((rows, hidden), BF), row_block(hidden)),
        (shape((rows, width), BF), row_block(width)),
        (shape((rows, hidden), BF), row_block(hidden)),
        (shape((rows, width), BF), row_block(width)),
        (shape((rows, width), F32), row_block(width)),
        (shape((8, hidden), F32), kept((8, hidden))),
        (shape((sums, width), F32), kept((sums, width))),
    ] + [(shape((shards, rows, LANES), BF), by_shard)] * parts
    return pl.pallas_call(
        partial(middle_kernel, parts, clips),
        out_shape=[o[0] for o in outs],
        grid=(rows // block,),
        in_specs=[by_shard] * parts
        + [
            row_block(width),
            row_block(width),
            row_block(1),
            whole(mod.shape),
            whole(out_w.shape),
            whole((1, width)),
            whole(w1.shape),
            whole((1, hidden)),
            whole(w2.shape),
            whole((1, width)),
        ],
        out_specs=[o[1] for o in outs],
        compiler_params=pltpu.CompilerParams(vmem_limit_bytes=56 << 20),
        cost_estimate=pl.CostEstimate(
            flops=2 * rows * width * (4 * hidden + 2 * width), bytes_accessed=20 << 20, transcendentals=0
        ),
    )(*o_parts, x1, grad, seg, mod, out_w, out_b[None], w1, b1[None], w2, b2[None])


def exchange(values, axis):
    return lax.all_to_all(values, axis, 0, 0)


def local(
    mel_pair, text_ids, clip_lengths, t_index,
    txt_table, txt_conv, txt_vec, txt_gain, txt_up, txt_hid, txt_down,
    emb_mel, emb_text, emb_bias, pos_conv, pos_bias,
    time_w1, time_bias, time_w2, ada_w, ada_b,
    qkv_w, qkv_b, out_w, out_b, ff_w1, ff_b1, ff_w2, ff_b2, out_grad,
):
    total = mel_pair.shape[0]
    width = emb_mel.shape[1]
    shards, groups = lax.axis_size("mp"), lax.axis_size("dp")
    rank, place = lax.axis_index("mp"), lax.axis_index("dp")
    rows = total // shards
    cols = width // shards
    clips = clip_lengths.shape[1]
    first = rank * rows
    taps = pos_conv.shape[1]
    group = pos_conv.shape[2]

    def spread_slice(weight, axis):
        piece = weight.shape[axis] // groups
        return lax.dynamic_slice_in_dim(weight, place * piece, piece, axis)

    def to_all(piece, axis_name="mp"):
        size = lax.axis_size(axis_name)
        return lax.all_to_all(jnp.broadcast_to(piece[None], (size,) + piece.shape), axis_name, 0, 0)

    def gather(piece, axis):
        return lax.all_gather(piece, "dp", axis=axis, tiled=True)

    def three(values):
        one = lax.reduce_precision(values, 8, 7)
        two = lax.reduce_precision(values - one, 8, 7)
        return jnp.concatenate([one, two, values - one - two], axis=0).astype(BF)

    qkv_piece = spread_slice(qkv_w, 1)
    qkv_piece = jnp.concatenate([pair_split(qkv_piece[:2]), qkv_piece[2:]], axis=0)
    in_rows = qkv_piece.shape[1]
    biases = jnp.concatenate(
        [pair_split(qkv_b[:2]), qkv_b[2:], ff_b1.reshape(-1, cols)], axis=0
    )
    bias_rows = biases.shape[0]
    biases = three(biases)
    biases = jnp.pad(biases, ((0, -biases.shape[0] % 16), (0, 0)))
    received = to_all(jnp.concatenate([qkv_piece.reshape(3 * in_rows, cols), biases], axis=0))
    qkv_full = gather(received[:, : 3 * in_rows].reshape(shards, 3, in_rows, cols), 2)
    biases = received[:, 3 * in_rows :].astype(F32)
    biases = sum(biases[:, i * bias_rows : (i + 1) * bias_rows] for i in range(3))
    qkv_bias = biases[:, :3]
    b1_full = biases[:, 3:].reshape(-1)
    out_piece, w2_piece, w1_piece = spread_slice(out_w, 0), spread_slice(ff_w2, 0), spread_slice(ff_w1, 0)
    w1_shape = w1_piece.shape
    cut = [out_piece.shape[0], out_piece.shape[0] + w2_piece.shape[0]]

    lengths = clip_lengths[0]
    clip_index = jnp.arange(clips, dtype=jnp.int32)
    ends = jnp.sum(jnp.where(clip_index[:, None] >= clip_index[None, :], lengths[None, :], 0), axis=1)
    starts = ends - lengths
    frames = jnp.arange(total, dtype=jnp.int32)
    member = (frames[:, None] >= starts[None, :]) & (frames[:, None] < ends[None, :])
    segment = jnp.sum(member * clip_index[None, :], axis=1).astype(jnp.int32)
    position = frames - jnp.sum(member * starts[None, :], axis=1)
    ext = rows + 2 * HALO
    ids = lax.dynamic_slice_in_dim(jnp.pad(text_ids, (HALO, HALO)), first, ext)
    seg_ext = lax.dynamic_slice_in_dim(jnp.pad(segment, (HALO, HALO), constant_values=-1), first, ext)
    hot_ext = (seg_ext[:, None] == clip_index[None, :]).astype(F32)
    ext_index = jnp.arange(ext, dtype=jnp.int32)
    inside = (ext_index >= HALO) & (ext_index < HALO + rows)
    own_ext = jnp.where(inside[:, None], hot_ext, 0.0)
    hot = hot_ext[HALO : HALO + rows]

    def time_path(steps):
        half = time_w1.shape[0] // 2
        frequency = jnp.exp(jnp.arange(half, dtype=F32) * (-math.log(10000.0) / (half - 1)))
        angles = steps.astype(F32)[:, None] * frequency[None, :]
        sinusoid = jnp.concatenate([jnp.sin(angles), jnp.cos(angles)], axis=-1)
        pre_one = precise(sinusoid, time_w1) + time_bias[0]
        act_one = jax.nn.silu(pre_one)
        time_vec = precise(act_one, time_w2) + time_bias[1]
        return sinusoid, pre_one, act_one, time_vec, jax.nn.silu(time_vec)


    hidden = jnp.take(txt_table, ids, axis=0).astype(F32)
    kept = []
    blocks = txt_conv.shape[0]
    for b in range(blocks):
        hidden, saved = text_ahead(
            hidden, seg_ext, hot_ext, own_ext, txt_conv[b], txt_vec[b], txt_gain[b],
            txt_up[b], txt_hid[b], txt_down[b],
        )
        kept.append(saved)
    text = hidden[HALO : HALO + rows].astype(BF)

    mel = lax.dynamic_slice_in_dim(mel_pair, first, rows)
    x0 = dot(mel, emb_mel) + dot(text, emb_text) + emb_bias

    def to_channels(values):
        blocks_of = values.reshape(rows, shards, cols).transpose(1, 0, 2)
        return exchange(blocks_of, "mp").reshape(total, cols)

    def to_rows(values):
        return exchange(values.reshape(shards, rows, cols), "mp").transpose(1, 0, 2).reshape(rows, width)

    channels = to_channels(x0.astype(BF))
    pieces = jnp.concatenate([out_piece, w2_piece, w1_piece.reshape(-1, width)], axis=0)
    pieces, channels = lax.optimization_barrier((pieces, channels))
    spread_in = spread(channels.astype(F32), starts, ends)
    pre_a = apply_conv(spread_in, pos_conv[0], False) + pos_bias[0]
    y_a = jnp.pad(
        only_clips(mish(pre_a), starts, ends).astype(BF).astype(F32), ((GAP, GAP), (0, 0))
    )
    pre_b = apply_conv(y_a, pos_conv[1], False) + pos_bias[1]
    received = to_all(pieces)
    received, pre_b = lax.optimization_barrier((received, pre_b))
    out_full = gather(received[:, : cut[0]], 1).reshape(width, width)
    w1_piece = received[:, cut[1] :].reshape((shards,) + w1_shape).transpose(1, 0, 2)
    w1_full = gather(w1_piece.reshape(w1_shape[0], -1), 0)
    w2_full = gather(received[:, cut[0] : cut[1]], 1).reshape(-1, width)
    conv_out = gather_back(mish(pre_b).astype(BF), starts, ends)
    conv_out, steps, position = lax.optimization_barrier((conv_out, t_index[0], position))
    mod = precise(time_path(steps)[4], ada_w) + ada_b
    c_pos = to_rows(conv_out)
    x1 = x0 + c_pos.astype(F32)

    def modulate(state, mod_in, shift_part, scale_part):
        scale = expand(hot, mod_in[:, scale_part * width : (scale_part + 1) * width])
        shift = expand(hot, mod_in[:, shift_part * width : (shift_part + 1) * width])
        return layer_norm(state) * (1.0 + scale) + shift

    n1, n1_pull = jax.vjp(lambda s, m: modulate(s, m, 0, 1), x1, mod)
    n1 = n1.astype(BF)
    inverse = jnp.exp(jnp.arange(0, HEAD_DIM, 2, dtype=F32) * (-math.log(10000.0) / HEAD_DIM))
    angles = position.astype(F32)[:, None] * jnp.tile(inverse, LANES // inverse.shape[0])[None, :]
    cos = jnp.cos(angles)
    sin = jnp.sin(angles) * jnp.where(jnp.arange(LANES) < LANES // 2, -1.0, 1.0)
    cos_own = lax.dynamic_slice_in_dim(cos, first, rows)
    sin_own = lax.dynamic_slice_in_dim(sin, first, rows)
    parts = range(cols // LANES)
    qkv = [exchange(v, "mp") for v in project(n1, qkv_full, qkv_bias, cos_own, sin_own)]
    block = rows
    heads_of = segment[::block]
    tails_of = segment[block - 1 :: block]
    low_key = jnp.sum(jnp.where(heads_of[:, None] == clip_index, starts[None, :], 0), axis=1)
    high_key = jnp.sum(jnp.where(tails_of[:, None] == clip_index, ends[None, :], 0), axis=1)
    bounds = jnp.stack([low_key // rows, (high_key + rows - 1) // rows], axis=1).astype(jnp.int32)
    seg_rows = segment[None, :]
    seg_blocks = segment.reshape(shards, rows, 1)
    attended = [attend(qkv[h], seg_rows, seg_blocks, bounds, block) for h in parts]
    o_parts = [exchange(a[0].reshape(shards, rows, LANES), "mp") for a in attended]
    grad = lax.dynamic_slice_in_dim(out_grad, first, rows)
    seg_own = lax.dynamic_slice_in_dim(segment, first, rows)[:, None]
    out, n2, r, df, dh, da, dx2, ff_sums, sums, *do_parts = middle(
        o_parts, x1, grad, seg_own, mod, out_full, out_b, w1_full, b1_full, w2_full, ff_b2
    )
    dmod_gate_f, dmod_shift_f, dmod_scale_f, dmod_gate_a = (
        sums[i * clips : (i + 1) * clips] for i in range(4)
    )
    g_ff_w2 = dot(df, r, TN)
    g_ff_w1 = dot(n2, dh, TN)
    o_rows = jnp.stack(o_parts).transpose(2, 1, 0, 3).reshape(rows, width)

    def for_dp(matrix):
        return matrix.astype(BF).reshape(groups, matrix.shape[0] // groups, matrix.shape[1])

    def by_rank(matrix):
        return matrix.reshape(matrix.shape[0], shards, -1).transpose(1, 0, 2)

    def scatter_dp(matrix):
        return lax.psum_scatter(matrix.astype(BF), "dp", scatter_dimension=0, tiled=True)

    sent_w1, sent_w2 = scatter_dp(g_ff_w1), scatter_dp(g_ff_w2)

    g_out_w = dot(da, o_rows, TN)
    dqkv = []
    for h in parts:
        do_part = exchange(do_parts[h], "mp").reshape(total, LANES)
        d_part = attend_back(
            qkv[h], attended[h][1], attended[h][2], do_part, seg_rows, seg_blocks, cos, sin, bounds, block
        )
        dqkv.append(exchange(d_part, "mp"))
    dn1, g_qkv_w, g_qkv_b = unproject(dqkv, n1, qkv_full)
    more, dmod_d = n1_pull(dn1)
    dx1 = dx2 + more
    sent_w1, sent_w2, dx1, out = lax.optimization_barrier((sent_w1, sent_w2, dx1, out))
    ff_pair = jnp.concatenate([by_rank(sent_w1), by_rank(sent_w2)], axis=2)
    sent_qkv, sent_out = scatter_dp(g_qkv_w), scatter_dp(g_out_w)

    dmod = dmod_d + jnp.concatenate(
        [
            jnp.zeros((clips, 2 * width), F32), dmod_gate_a, dmod_shift_f, dmod_scale_f, dmod_gate_f,
        ],
        axis=1,
    )

    slope_b = gather_back(mish_slope(pre_b), starts, ends)
    dy_b = to_channels(dx1.astype(BF)).astype(F32) * slope_b
    g_pos_b = jnp.sum(dy_b, axis=0)
    dy_b = spread(dy_b.astype(BF).astype(F32), starts, ends)
    dy_a = only_clips(apply_conv(dy_b, pos_conv[1], True) * mish_slope(pre_a), starts, ends)
    g_pos_a = jnp.sum(dy_a, axis=0)
    dy_a = jnp.pad(dy_a.astype(BF).astype(F32), ((GAP, GAP), (0, 0)))
    dc = gather_back(
        apply_conv(dy_a, pos_conv[0], True).astype(BF), starts, ends
    )
    ff_got, dc = lax.optimization_barrier((exchange(ff_pair, "mp"), dc))
    dx0_full = dx1 + to_rows(dc).astype(F32)
    g_conv = jnp.concatenate(
        [conv_grad(spread_in, dy_a[GAP:-GAP], taps, group), conv_grad(y_a, dy_b[GAP:-GAP], taps, group)],
        axis=1,
    )
    sent_qkv, sent_out, dx0_full = lax.optimization_barrier((sent_qkv, sent_out, dx0_full))
    at_pair = jnp.concatenate([by_rank(sent_qkv), by_rank(sent_out)], axis=2)
    sent_conv = scatter_dp(g_conv)

    g_emb_bias = jnp.sum(dx0_full, axis=0)
    dx0 = dx0_full.astype(BF)
    mel_grad = dot(dx0, emb_mel, NT).astype(BF)
    g_emb = jnp.concatenate([dot(dx0, text, TN), dot(dx0, mel, TN)], axis=1)
    sent_emb = scatter_dp(g_emb)
    text_width = text.shape[1]

    dtext = jnp.pad(dot(dx0, emb_text, NT), ((HALO, HALO), (0, 0)))
    text_grads = [None] * blocks
    extra = dmod
    result = lax.all_gather(out[:, : width // 2], "mp", tiled=True)
    at_got, result, out, dtext = lax.optimization_barrier((exchange(at_pair, "mp"), result, out, dtext))
    result = [result, lax.all_gather(out[:, width // 2 :], "mp", tiled=True)]
    waiting = sent_conv
    for b in reversed(range(blocks)):
        dtext, text_grads[b], summed, waiting = text_behind(
            kept[b], dtext, txt_up[b], txt_down[b], extra, waiting
        )
        if extra is not None:
            stamps = jnp.broadcast_to(t_index[0].astype(F32)[:, None], (clips, 128))
            dmod_all = lax.all_gather(jnp.concatenate([summed, stamps], axis=1), "dp", tiled=True)
            sent_emb, dtext = lax.optimization_barrier((sent_emb, dtext))
            sent_conv, waiting = waiting, at_got
            dmod_all, all_steps = dmod_all[:, : 6 * width], dmod_all[:, 6 * width]
        extra = None
    at_got = waiting
    result[1], dtext = lax.optimization_barrier((result[1], dtext))
    result = jnp.concatenate(result, axis=1).astype(F32)
    vocab = txt_table.shape[0]
    wide = -(-vocab // 128) * 128
    chosen = (ids[:, None] == jnp.arange(wide, dtype=jnp.int32)[None, :]).astype(BF)
    g_table = dot(dtext, chosen, TN)
    hidden_width = txt_up.shape[2]

    g_qkv_b = jnp.concatenate([pair_merge(g_qkv_b[:, :2]), g_qkv_b[:, 2:]], axis=1)
    g_qkv_b = g_qkv_b.transpose(1, 0, 2).reshape(3, width)
    sources, pieces = [], []
    everyone = groups * shards

    def piece(value, kind, out, where, first=0, count=None):
        value = value if value.ndim == 2 else value[None]
        known = [i for i, have in enumerate(sources) if have is value]
        if not known:
            sources.append(value)
        index = known[0] if known else len(sources) - 1
        columns = value.shape[1] * (shards if kind == "mine" else 1)
        pieces.append((index, first, count or value.shape[0], columns, kind, out, where))

    for b, (g_conv_b, g_vec, g_gain, _, g_hid, _) in enumerate(text_grads):
        piece(g_conv_b, "both", 0, (b, 0))
        piece(g_vec, "both", 1, (b, 0))
        piece(g_gain, "both", 2, (None, b))
        for i, value in enumerate(g_hid):
            piece(value, "both", 3, (b, i))
    piece(g_emb_bias, "dp", 4, (None, 0))
    piece(g_pos_a, "mine", 5, (None, 0))
    piece(g_pos_b, "mine", 5, (None, 1))
    piece(g_qkv_b, "crossed", 6, (None, 0))
    piece(sums, "dp", 7, (None, 0), 4 * clips + 1, 1)
    piece(ff_sums, "crossed", 8, (None, 0), 0, 1)
    piece(sums, "dp", 9, (None, 0), 4 * clips, 1)
    text_part, hid_part, part = text_width // everyone, hidden_width // everyone, width // everyone
    small_shapes = [
        (blocks, txt_conv.shape[1], text_part), (blocks, 3, text_part), (blocks, text_part),
        (blocks, 3, hid_part), (1, width // groups), (2, part), (3, part), (1, width // groups),
        (1, ff_sums.shape[1] // everyone), (1, width // groups),
    ]
    table_sum, up0, up1, down0, down1, g_emb, mel_grad, *unpacked = last_sums(
        [for_dp(g_table)]
        + [for_dp(text_grads[b][3]) for b in range(blocks)]
        + [for_dp(text_grads[b][5]) for b in range(blocks)],
        sources,
        pieces,
        small_shapes,
        [],
        [sent_emb],
        [mel_grad],
    )
    mel_grad = mel_grad.reshape(total, -1)
    for i in (4, 7, 8, 9):
        unpacked[i] = unpacked[i].reshape(-1)
    o_table = table_sum[:, :vocab].T
    o_up = jnp.stack([up0.T, up1.T])
    o_down = jnp.stack([down0.T, down1.T])
    ff_pair, at_pair = (jnp.sum(v.astype(F32), axis=0) for v in (ff_got, at_got))
    ff_cols = ff_w1.shape[1]
    o_ff_w1, o_ff_w2 = ff_pair[:, :ff_cols], ff_pair[:, ff_cols:].T
    g_qkv = at_pair[:, : 3 * cols].reshape(-1, 3, cols).transpose(1, 0, 2)
    o_qkv_w = jnp.concatenate([pair_merge(g_qkv[:2]), g_qkv[2:]], axis=0)
    o_out_w = at_pair[:, 3 * cols :].T
    o_pos_conv = sent_conv.astype(F32).T.reshape(2, taps, group, -1)
    o_emb_text, o_emb_mel = g_emb[:, :text_width].T, g_emb[:, text_width:].T

    def own(values, index, parts):
        piece = values.shape[-1] // parts
        return lax.dynamic_slice_in_dim(values, index * piece, piece, values.ndim - 1)

    sinusoid, pre_one, act_one, time_vec, act_two = time_path(all_steps)
    de = precise(dmod_all, ada_w, NT) * silu_slope(time_vec)
    dpre = precise(de, time_w2, NT) * silu_slope(pre_one)

    def outer(left, right):
        return lax.dot_general(left, own(right, place, groups), TN, precision=highest)

    return (
        result,
        mel_grad,
        o_table,
        unpacked[0],
        unpacked[1],
        unpacked[2],
        o_up,
        unpacked[3],
        o_down,
        o_emb_mel,
        o_emb_text,
        unpacked[4],
        o_pos_conv,
        unpacked[5],
        outer(sinusoid, dpre),
        own(jnp.stack([jnp.sum(dpre, axis=0), jnp.sum(de, axis=0)]), place, groups),
        outer(act_one, de),
        outer(act_two, dmod_all),
        own(jnp.sum(dmod_all, axis=0), place, groups),
        o_qkv_w,
        unpacked[6],
        o_out_w,
        unpacked[7],
        o_ff_w1,
        unpacked[8],
        o_ff_w2,
        unpacked[9],
    )


def solution(mesh):
    both, crossed = ("dp", "mp"), ("mp", "dp")
    placed = (
        P("dp", None), P("dp"), P("dp", None), P("dp", None),
        P(), P(), P(), P(), P(), P(), P(), P(), P(), P(),
        P(None, None, None, "mp"), P(None, "mp"),
        P(), P(), P(), P(), P(),
        P(None, None, "mp"), P(None, "mp"), P("mp", None), P(),
        P(None, "mp"), P("mp"), P("mp", None), P(),
        P("dp", None),
    )
    given = (
        P("dp", None), P("dp", None),
        P(None, both), P(None, None, both), P(None, None, both), P(None, both),
        P(None, None, both), P(None, None, both), P(None, None, both),
        P(None, "dp"), P(None, "dp"), P("dp"),
        P(None, None, None, crossed), P(None, crossed),
        P(None, "dp"), P(None, "dp"), P(None, "dp"), P(None, "dp"), P("dp"),
        P(None, "dp", "mp"), P(None, crossed), P("mp", "dp"), P("dp"),
        P("dp", "mp"), P(crossed), P("mp", "dp"), P("dp"),
    )
    return jax.shard_map(local, mesh=mesh, in_specs=placed, out_specs=given, check_vma=False)
```
